32 devices in a mesh: section: 2 (over x), dp: 16 (over z, y, core).
Axes of the slice: x: 2, y: 2, z: 4, core: 2. Of those that a mesh axis runs over, the one named last changes fastest.
Arguments:
- states_in: bfloat16 [3072, 1536], P('dp'), may hold values from -6 to 6
- out_grad: bfloat16 [3072, 1536], P('dp'), may hold values from -6 to 6
- counts: int32 [32], P('dp'), may hold values from 24 to 96
- segments: int32 [32, 96], P('dp'), may hold values from 0 to 3, never falling along the last dimension, each value on 1 to 48 neighbouring positions
- mixing: float32 [2, 2, 2], P('section'), may hold values from -2.5 to 2.5
- correction: float32 [2, 2], P('section'), may hold values from 0.5 to 1.5
- gain_attn: float32 [2, 768], P('section'), may hold values from 0.1 to 1.9
- w_query: bfloat16 [2, 768, 768], P('section'), may hold values from -0.3125 to 0.3125
- w_key: bfloat16 [2, 768, 768], P('section'), may hold values from -0.3125 to 0.3125
- w_value: bfloat16 [2, 768, 768], P('section'), may hold values from -0.21875 to 0.21875
- w_attn_out: bfloat16 [2, 768, 768], P('section'), may hold values from -0.4375 to 0.4375
- gain_ffn: float32 [2, 768], P('section'), may hold values from 0.1 to 1.9
- w_gate: bfloat16 [2, 768, 3072], P('section'), may hold values from -0.21875 to 0.21875
- w_up: bfloat16 [2, 768, 3072], P('section'), may hold values from -0.21875 to 0.21875
- w_down: bfloat16 [2, 3072, 768], P('section'), may hold values from -0.15625 to 0.15625
Outputs:
- states: bfloat16 [2, 3072, 1536], P('section', 'dp')
- state_grads: bfloat16 [2, 3072, 1536], P('section', 'dp')
- grad_mixing: float32 [2, 2, 2], P('section')
- grad_correction: float32 [2, 2], P('section')
- grad_gain_attn: float32 [2, 768], P('section', 'dp')
- grad_query: float32 [2, 768, 768], P('section', 'dp')
- grad_key: float32 [2, 768, 768], P('section', 'dp')
- grad_value: float32 [2, 768, 768], P('section', 'dp')
- grad_attn_out: float32 [2, 768, 768], P('section', 'dp')
- grad_gain_ffn: float32 [2, 768], P('section', 'dp')
- grad_gate: float32 [2, 768, 3072], P('section', 'dp')
- grad_up: float32 [2, 768, 3072], P('section', 'dp')
- grad_down: float32 [2, 3072, 768], P('section', 'dp')
The draws below stay inside these ranges and needn't reach their ends.
Inputs may be any that keep to these rules, and one draw needn't show every extreme that they name: Positions below counts of a row hold real tokens, the rest is padding. `segments`: document numbers never fall along a row.
All inputs are finite; a program needn't handle non-finite values.
Results may differ from the reference program's by a relative error of at most 0.03.
The reference program's roundings to bfloat16 on the way count: a program that leaves them out, or rounds other values in their place, can miss the bound.
Values may be sent and summed in bfloat16 or wider, within the bound.
No kernel may reach another device: no remote copies, remote signals or barrier semaphores. Data moves between devices by JAX's collectives and lax.ppermute only.
A program may use at most 256 MiB of HBM per device.

```python
import math
import jax
import jax.numpy as jnp
import numpy as np
from jax import lax

D = 768
HEADS = 12
HEAD_DIM = 64
FF = 3072
LEN = 96
DOCS = 4
ROWS = 32
TOKENS = 3072


def set_ends(entries, rng, smallest, top_value):
    longest = entries.shape.index(max(entries.shape))
    spots = []
    for shift in (0, 1):
        where = [jax.random.randint(jax.random.fold_in(rng, axis), (), 0, length) for axis, length in enumerate(entries.shape)]
        where[longest] = (where[longest] + shift) % entries.shape[longest]
        spots.append(tuple(where))
    return entries.at[spots[0]].set(smallest).at[spots[1]].set(top_value)


def steps_of(own_key, extent, shards, least, largest):
    level = 1.0
    for dim, shards_of in shards:
        heights = jax.random.uniform(jax.random.fold_in(jax.random.fold_in(own_key, 6), dim), (shards_of,), jnp.float32, least / len(shards), largest / len(shards))
        level = level * jnp.repeat(jnp.exp(heights), extent[dim] // shards_of).reshape((-1,) + (1,) * (len(extent) - 1 - dim))
    return level


def profile(number_of, total, bound, slope):
    loads = [(1 << 20) // math.isqrt(rank ** slope) + 1 for rank in range(2, number_of + 1)]
    surplus, given = total - bound - (number_of - 1), [1] * (number_of - 1)
    while surplus > 0:
        free = [i for i in range(number_of - 1) if given[i] < bound]
        whole, left = sum([loads[i] for i in free]), surplus
        for i in free:
            addition = min(bound - given[i], max(1, left * loads[i] // whole), surplus)
            given[i] = given[i] + addition
            surplus = surplus - addition
    return np.array([bound] + given)


def uneven(own_key, amount, total, bound, skew):
    if amount == 2:
        one = jax.random.randint(own_key, (), max(1, total - bound), min(bound, total - 1) + 1)
        return jnp.stack([one, total - one])
    sizes = jnp.asarray(profile(amount, total, bound, skew), jnp.int32)
    couples = (amount - 1) // 2
    donor, receiver = sizes[1:1 + 2 * couples:2], sizes[2:2 + 2 * couples:2]
    slack = jnp.minimum(donor - 1, bound - receiver)
    shifted = jax.random.randint(jax.random.fold_in(own_key, 1), (couples,), 0, 1 << 20) % (slack + 1)
    sizes = sizes.at[1:1 + 2 * couples:2].set(donor - shifted).at[2:2 + 2 * couples:2].set(receiver + shifted)
    return sizes[jax.random.permutation(jax.random.fold_in(own_key, 2), amount)]


def noise(stream_key, dims, spread, reach, cuts=(), kind=jnp.bfloat16):
    array = jax.random.normal(stream_key, dims, jnp.float32) * spread
    if len(cuts) > 0:
        array = steps_of(stream_key, dims, cuts, -0.22, 0.18) * array
    return jnp.clip(array, min=-reach, max=reach).astype(kind)


def setup_inputs(seed: int = 0) -> dict:
    seeds = jax.random.split(jax.random.key(seed), 16)
    states_in = noise(seeds[0], (TOKENS, 2 * D), 1.0, 6.0, ((0, 16),))
    out_grad = noise(seeds[1], (TOKENS, 2 * D), 1.0, 6.0, ((0, 16),))
    counts = set_ends(jax.random.randint(seeds[2], (ROWS,), LEN // 4, LEN + 1), jax.random.fold_in(seeds[2], 1), LEN // 4, LEN).astype(jnp.int32)
    segments = jax.vmap(lambda own: jnp.searchsorted(jnp.cumsum(uneven(own, DOCS, LEN, LEN // 2, 0)), jnp.arange(LEN), side="right"))(jax.random.split(seeds[3], ROWS)).reshape((ROWS, LEN)).astype(jnp.int32)
    mixing = noise(seeds[4], (2, 2, 2), 0.4, 2.5, ((0, 2),), jnp.float32)
    correction = jnp.clip(0.5 + 1.0 * jax.random.uniform(seeds[5], (2, 2), jnp.float32) ** steps_of(seeds[5], (2, 2), ((0, 2),), -0.2, 0.2), 0.5, 1.5)
    gain_attn = jnp.clip(1.0 + 0.18 * jax.random.normal(seeds[6], (2, D), jnp.float32), 0.1, 1.9)
    w_query = noise(seeds[7], (2, D, D), (D // 2) ** -0.5, 0.3125, ((0, 2),))
    w_key = noise(seeds[8], (2, D, D), (D // 2) ** -0.5, 0.3125, ((0, 2),))
    w_value = noise(seeds[9], (2, D, D), D ** -0.5, 0.21875, ((0, 2),))
    w_attn_out = noise(seeds[10], (2, D, D), (D // 4) ** -0.5, 0.4375, ((0, 2),))
    gain_ffn = jnp.clip(1.0 + 0.18 * jax.random.normal(seeds[11], (2, D), jnp.float32), 0.1, 1.9)
    w_gate = noise(seeds[12], (2, D, FF), D ** -0.5, 0.21875, ((0, 2),))
    w_up = noise(seeds[13], (2, D, FF), D ** -0.5, 0.21875, ((0, 2),))
    w_down = noise(seeds[14], (2, FF, D), (FF // 2) ** -0.5, 0.15625, ((0, 2),))
    return {"states_in": states_in, "out_grad": out_grad, "counts": counts, "segments": segments, "mixing": mixing, "correction": correction, "gain_attn": gain_attn, "w_query": w_query, "w_key": w_key, "w_value": w_value, "w_attn_out": w_attn_out, "gain_ffn": gain_ffn, "w_gate": w_gate, "w_up": w_up, "w_down": w_down}


epsilon = 1e-06
highest = lax.Precision.HIGHEST

@jax.custom_vjp
def low(v):
    return lax.optimization_barrier(v.astype(jnp.bfloat16)).astype(jnp.float32)

@jax.custom_vjp
def low_back(v):
    return v

def low_keep(v):
    return (low(v), None)

def low_pass(kept, grad):
    return (grad,)

def back_keep(v):
    return (v, None)

def back_low(kept, grad):
    return (low(grad),)
low.defvjp(low_keep, low_pass)
low_back.defvjp(back_keep, back_low)

def matmul(earlier, later):
    return jnp.dot(earlier, later, precision=highest, preferred_element_type=jnp.float32)

def normalize(values, gain_vector):
    return values * lax.rsqrt(lax.optimization_barrier(jnp.mean(values * values, axis=-1, keepdims=True)) + epsilon) * gain_vector

def attend(queries, key_rows, value_rows, segments):
    groups = segments.shape[0]
    length = segments.shape[1]

    def shaped(member):
        return member.reshape(groups, length, HEADS, HEAD_DIM)
    raw_scores = jnp.einsum('gqhd,gkhd->ghqk', shaped(queries), shaped(key_rows), precision=highest)
    scores = low_back(raw_scores * HEAD_DIM ** (-0.5))
    places = jnp.arange(length, dtype=jnp.int32)
    causal = places[None, :] <= places[:, None]
    allowed = causal[None] & (segments[:, :, None] == segments[:, None, :])
    masked = jnp.where(allowed[:, None], scores, -1e+30)
    attn_probs = low(jax.nn.softmax(masked, axis=-1))
    mixed_heads = jnp.einsum('ghqk,gkhd->gqhd', attn_probs, shaped(value_rows), precision=highest)
    return mixed_heads.reshape(groups * length, HEADS * HEAD_DIM)

def layer_forward(state_now, weights, active_index, segments):
    mixing, correction, gain_attn, w_query, w_key, w_value, w_attn_out, gain_ffn, w_gate, w_up, w_down = weights
    row_count = state_now.shape[0]
    blocks = state_now.reshape(row_count, 2, D)
    predicted = blocks + jnp.einsum('tjd,ij->tid', blocks, mixing, precision=highest)
    active = predicted[:, active_index]
    normed = low(normalize(active, gain_attn))
    queries = low(low_back(matmul(normed, w_query)))
    key_rows = low(low_back(matmul(normed, w_key)))
    value_rows = low(low_back(matmul(normed, w_value)))
    attended = low(low_back(attend(queries, key_rows, value_rows, segments)))
    middle = active + low_back(matmul(attended, w_attn_out))
    normed_ffn = low(normalize(middle, gain_ffn))
    gate_pre = low_back(matmul(normed_ffn, w_gate))
    upward = low_back(matmul(normed_ffn, w_up))
    hidden = low(jax.nn.gelu(gate_pre, approximate=True) * upward)
    block_out = middle + low_back(matmul(hidden, w_down))
    updated = predicted + correction[None, :, None] * (block_out - active)[:, None, :]
    return updated.reshape(row_count, 2 * D)

def reference(states_in, out_grad, counts, segments, mixing, correction, gain_attn, w_query, w_key, w_value, w_attn_out, gain_ffn, w_gate, w_up, w_down):
    stacked = tuple((member.astype(jnp.float32) for member in (mixing, correction, gain_attn, w_query, w_key, w_value, w_attn_out, gain_ffn, w_gate, w_up, w_down)))
    params = tuple((tuple((member[layer_index] for member in stacked)) for layer_index in range(2)))
    row_total = counts.shape[0]
    length = segments.shape[1]
    state_width = states_in.shape[1]
    group_rows = max([choice_rows for choice_rows in range(1, row_total + 1) if row_total % choice_rows == 0 and choice_rows * length <= 4096] + [1])
    group_count = row_total // group_rows
    inputs = states_in.astype(jnp.float32).reshape(group_count, group_rows * length, state_width)
    targets = out_grad.astype(jnp.float32).reshape(group_count, group_rows * length, state_width)
    places = jnp.arange(length, dtype=jnp.int32)
    valid_all = (places[None, :] < counts[:, None]).astype(jnp.float32).reshape(group_count, group_rows * length)
    seg_groups = segments.reshape(group_count, group_rows, length)

    def group_loss(weights, state_now, probe_in, seg_group, valid_rows, target):
        first_out = layer_forward(state_now, weights[0], 0, seg_group)
        sent_state = low(low_back(first_out)) + probe_in
        second_out = layer_forward(sent_state, weights[1], 1, seg_group)
        return (jnp.sum(valid_rows[:, None] * second_out * target), (first_out, second_out))

    def step_group(totals, batch_item):
        state_now, target, valid_rows, seg_group = batch_item
        probe_zero = jnp.zeros_like(state_now)

        def wrapped(weights, start_state, probe_in):
            return group_loss(weights, start_state, probe_in, seg_group, valid_rows, target)
        objective, pullback, outputs = jax.vjp(wrapped, params, state_now, probe_zero, has_aux=True)
        grads_w, grads_x, grads_sent = pullback(jnp.ones_like(objective))
        totals = jax.tree.map(lambda earlier, later: earlier + later, totals, grads_w)
        return (totals, (outputs[0].astype(jnp.bfloat16), outputs[1].astype(jnp.bfloat16), grads_x.astype(jnp.bfloat16), grads_sent.astype(jnp.bfloat16)))
    zero_totals = jax.tree.map(jnp.zeros_like, params)
    totals, pieces = lax.scan(step_group, zero_totals, (inputs, targets, valid_all, seg_groups))
    token_total = row_total * length
    states = jnp.stack([pieces[0].reshape(token_total, state_width), pieces[1].reshape(token_total, state_width)])
    state_grads = jnp.stack([pieces[2].reshape(token_total, state_width), pieces[3].reshape(token_total, state_width)])
    grads = tuple((jnp.stack([totals[0][position], totals[1][position]]) for position in range(11)))
    return (states, state_grads, grads[0], grads[1], grads[2], grads[3], grads[4], grads[5], grads[6], grads[7], grads[8], grads[9], grads[10])
```

```python
import functools

import jax
import jax.numpy as jnp
from jax import lax
from jax.experimental import pallas as pl
from jax.experimental.pallas import tpu as pltpu
from jax.sharding import PartitionSpec as P

HEAD_DIM = 64
PAIR = 2 * HEAD_DIM
EPSILON = 1e-06
MASKED = -1e30
SCALE = HEAD_DIM ** (-0.5)
GELU_A = 0.7978845608028654
GELU_B = 0.044715
EXTRA = 16
bfloat = jnp.bfloat16
floating = jnp.float32

VMEM = pl.BlockSpec(memory_space=pltpu.VMEM)
SMEM = pl.BlockSpec(memory_space=pltpu.SMEM)
ANY = pl.BlockSpec(memory_space=pl.ANY)


def dot(a, b):
    return jnp.dot(a, b, preferred_element_type=floating)


def dot_t(a, b):
    return lax.dot_general(a, b, (((1,), (1,)), ((), ())), preferred_element_type=floating)


def t_dot(a, b):
    return lax.dot_general(a, b, (((0,), (0,)), ((), ())), preferred_element_type=floating)


def params(mebibytes):
    return pltpu.CompilerParams(vmem_limit_bytes=mebibytes * 1024 * 1024)


def cost(flops, moved):
    return pl.CostEstimate(flops=flops, bytes_accessed=moved, transcendentals=0)


def scalar_rows(values, rows, width):
    lane = lax.broadcasted_iota(jnp.int32, (rows, width), 1)
    row = lax.broadcasted_iota(jnp.int32, (rows, width), 0)
    whole = jnp.zeros((rows, width), floating)
    for place, value in enumerate(values):
        whole = jnp.where(lane == place, value, whole)
    high = whole.astype(bfloat).astype(floating)
    middle = (whole - high).astype(bfloat).astype(floating)
    low = whole - high - middle
    part = jnp.where(row == 0, high, jnp.where(row == 1, middle, jnp.where(row == 2, low, 0.0)))
    return part.astype(bfloat)


def read_scalars(block, count):
    lane = lax.broadcasted_iota(jnp.int32, block.shape, 1)
    return [jnp.sum(jnp.where(lane == place, block, 0.0)) for place in range(count)]


def rms_scale(values):
    return lax.rsqrt(jnp.mean(values * values, axis=-1, keepdims=True) + EPSILON)


def lane_mask(length):
    return lax.broadcasted_iota(jnp.int32, (length, PAIR), 1) < HEAD_DIM


def stack_heads(block, first):
    zero = jnp.zeros_like(block)
    return jnp.concatenate([jnp.where(first, block, zero), jnp.where(first, zero, block)], axis=0)


def gelu_wave(gate):
    return jnp.tanh(GELU_A * (gate + GELU_B * gate * gate * gate))


def relative(blocks, index):
    low = (index & 1) == 1
    high = (index >> 1) == 1
    once = [jnp.where(low, blocks[place ^ 1], blocks[place]) for place in range(4)]
    return [jnp.where(high, once[place ^ 2], once[place]) for place in range(4)]


def forward_body(full, fast, refs):
    if full:
        (x_in, message, seg_ref, mix_ref, cor_ref, ga_ref, gf_ref, wq, wk, wv, wo, wg, wu, wd) = refs[:14]
        outs = refs[14:29]
        (x_ref, out_ref, q_ref, k_ref, v_ref, p_ref, act_ref, mid_ref, one_ref, two_ref, chg_ref, *kept) = refs[29:44]
        (nrm_ref, att_ref, nf_ref, acc, wq_s, wk_s, wv_s, wo_s, wg_s, wu_s, wd_s, sem, out_sem) = refs[44:]
    else:
        (x_in, seg_ref, mix_ref, cor_ref, ga_ref, gf_ref, wq, wk, wv, wo, wg, wu, wd,
         out_ref,
         q_ref, k_ref, v_ref, act_ref, mid_ref,
         nrm_ref, att_ref, nf_ref, acc, wq_s, wk_s, wv_s, wo_s, wg_s, wu_s, wd_s, sem) = refs
    width = ga_ref.shape[1]
    length = seg_ref.shape[1]
    rows = x_in.shape[0] // length
    tokens = x_in.shape[0]
    chunk = width
    pieces = wg.shape[2] // chunk
    attn_copies = [
        pltpu.make_async_copy(source.at[0], target, sem.at[place])
        for place, (source, target) in enumerate(((wq, wq_s), (wk, wk_s), (wv, wv_s), (wo, wo_s)))
    ]
    ffn_copies = []
    for piece in range(pieces):
        span = pl.ds(piece * chunk, chunk)
        ffn_copies.append(
            [
                pltpu.make_async_copy(wg.at[0, :, span], wg_s.at[:, span], sem.at[4 + 3 * piece]),
                pltpu.make_async_copy(wu.at[0, :, span], wu_s.at[:, span], sem.at[5 + 3 * piece]),
                pltpu.make_async_copy(wd.at[0, span, :], wd_s.at[span, :], sem.at[6 + 3 * piece]),
            ]
        )
    queue = attn_copies + [copy for group in ffn_copies for copy in group]
    ahead = 3
    for copy in queue[:ahead]:
        copy.start()
    state = [0]

    def arrive(count=1):
        for _ in range(count):
            queue[state[0]].wait()
            if state[0] + ahead < len(queue):
                queue[state[0] + ahead].start()
            state[0] += 1

    leaving = []

    def leave(place):
        if full:
            copy = pltpu.make_async_copy(refs[29 + place], outs[place], out_sem.at[place])
            copy.start()
            leaving.append(copy)

    section = lax.axis_index("section")
    mix = [[mix_ref[0, i, j] for j in range(2)] for i in range(2)]
    cor = [cor_ref[0, i] for i in range(2)]
    xa = x_in[:, :width].astype(floating)
    xb = x_in[:, width:].astype(floating)
    if full:
        quarter = lax.axis_index("dp") & 3
        got = read_scalars(message[tokens : tokens + EXTRA, :PAIR].astype(floating), 6)
        moved = message[:tokens, :].astype(floating)
        sent_a = (xa + (got[0] * xa + got[1] * xb) + got[4] * moved).astype(bfloat)
        sent_b = (xb + (got[2] * xa + got[3] * xb) + got[5] * moved).astype(bfloat)
        x_ref[:, :width] = jnp.where(section == 0, x_in[:, :width], sent_a)
        x_ref[:, width:] = jnp.where(section == 0, x_in[:, width:], sent_b)
        xa = x_ref[:, :width].astype(floating)
        xb = x_ref[:, width:].astype(floating)
        leave(0)
    own_a = jnp.where(section == 0, mix[0][0], mix[1][0])
    own_b = jnp.where(section == 0, mix[0][1], mix[1][1])
    active = jnp.where(section == 0, xa, xb) + (own_a * xa + own_b * xb)
    act_ref[...] = active
    normed = (active * rms_scale(active) * ga_ref[...]).astype(bfloat)
    nrm_ref[...] = normed
    for weight, target in zip((wq_s, wk_s, wv_s), (q_ref, k_ref, v_ref)):
        arrive()
        target[...] = dot(nrm_ref[...], weight[...]).astype(bfloat)
    arrive()
    for place in (2, 3, 4, 6):
        leave(place)

    def keep_quarters(values, base):
        share = width // 16
        for far in range(4):
            blocks = [values[:, (4 * far + near) * share : (4 * far + near + 1) * share] for near in range(4)]
            for slot, block in enumerate(relative(blocks, quarter)):
                kept[slot][:, base + far * share : base + (far + 1) * share] = block

    first = lane_mask(length)
    later = lax.broadcasted_iota(jnp.int32, (length, length), 0)
    earlier = lax.broadcasted_iota(jnp.int32, (length, length), 1)
    pairs = width // PAIR
    for row in range(rows):
        documents = jnp.broadcast_to(seg_ref[row : row + 1, :], (length, length)).astype(floating)
        allowed = (earlier <= later) & (documents == documents.T)
        allowed = jnp.concatenate([allowed, allowed], axis=0)
        span = slice(row * length, (row + 1) * length)
        for pair in range(pairs):
            heads = slice(pair * PAIR, (pair + 1) * PAIR)
            stacked = stack_heads(q_ref[span, heads], first)
            scores = jnp.where(allowed, dot_t(stacked, k_ref[span, heads]) * SCALE, MASKED)
            powers = jnp.exp(scores - jnp.max(scores, axis=-1, keepdims=True))
            probs = powers / jnp.sum(powers, axis=-1, keepdims=True)
            if full:
                p_ref[row * pairs + pair] = probs
            mixed = dot(probs.astype(bfloat), v_ref[span, heads])
            att_ref[span, heads] = jnp.where(first, mixed[:length], mixed[length:]).astype(bfloat)
    leave(5)
    middle = act_ref[...] + dot(att_ref[...], wo_s[...])
    mid_ref[...] = middle
    leave(7)
    nf_ref[...] = (middle * rms_scale(middle) * gf_ref[...]).astype(bfloat)
    if full:
        if fast:
            keep_quarters(att_ref[...], 2 * width)
            keep_quarters(nrm_ref[...], 2 * width + width // 4)
            for slot in range(4):
                kept[slot][:, width : 2 * width] = nf_ref[...]
        else:
            kept[0][...] = nrm_ref[...]
            kept[1][...] = att_ref[...]
            kept[2][...] = nf_ref[...]
    for piece in range(pieces):
        span = slice(piece * chunk, (piece + 1) * chunk)
        arrive()
        gate = dot(nf_ref[...], wg_s[:, span])
        arrive()
        upward = dot(nf_ref[...], wu_s[:, span])
        wave = gelu_wave(gate)
        half = 0.5 * (1.0 + wave)
        value = gate * half
        hidden = (value * upward).astype(bfloat)
        if full:
            slope = half + 0.5 * gate * (1.0 - wave * wave) * (GELU_A * (1.0 + 3.0 * GELU_B * gate * gate))
            one_ref[piece] = upward * slope
            two_ref[piece] = value
            if fast:
                share = chunk // 4
                blocks = [hidden[:, near * share : (near + 1) * share] for near in range(4)]
                for slot, block in enumerate(relative(blocks, quarter)):
                    kept[slot][:, piece * share : (piece + 1) * share] = block
            else:
                kept[3][:, span] = hidden
        arrive()
        down = dot(hidden, wd_s[span, :])
        if piece == 0:
            acc[...] = down
        else:
            acc[...] += down
    leave(8)
    leave(9)
    for place in range(11, 15):
        leave(place)
    change = mid_ref[...] + acc[...] - act_ref[...]
    if full:
        chg_ref[...] = change
        leave(10)
        xa = x_ref[:, :width].astype(floating)
        xb = x_ref[:, width:].astype(floating)
        out_ref[0, :, :width] = (xa + (mix[0][0] * xa + mix[0][1] * xb) + cor[0] * change).astype(bfloat)
        out_ref[0, :, width:] = (xb + (mix[1][0] * xa + mix[1][1] * xb) + cor[1] * change).astype(bfloat)
        leave(1)
        for copy in leaving:
            copy.wait()
    else:
        out_ref[:tokens, :] = change.astype(bfloat)
        out_ref[tokens:, :] = scalar_rows(mix[0] + mix[1] + cor, EXTRA, width)


def forward(full, fast, x_in, message, segments, mixing, correction, gain_attn, gain_ffn, weights):
    tokens = x_in.shape[0]
    length = segments.shape[1]
    width = gain_attn.shape[1]
    hidden_width = weights[4].shape[2]
    pieces = hidden_width // width
    shape = jax.ShapeDtypeStruct
    narrow = ((tokens, width), bfloat)
    wide = ((tokens, width), floating)
    probs = ((tokens // length * (width // PAIR), 2 * length, length), floating)
    weight_scratch = [pltpu.VMEM(weight.shape[1:], bfloat) for weight in weights]
    common = [pltpu.VMEM(*narrow), pltpu.VMEM(*narrow), pltpu.VMEM(*narrow), pltpu.VMEM(*wide)]
    common += weight_scratch + [pltpu.SemaphoreType.DMA((4 + 3 * pieces,))]
    estimate = cost(2 * tokens * sum(weight.size for weight in weights), 2 * sum(weight.size for weight in weights))
    if full:
        if fast:
            kept = [((tokens, 2 * width + width // 2), bfloat)] * 4
        else:
            kept = [narrow, narrow, narrow, ((tokens, hidden_width), bfloat)]
        ffn = ((pieces, tokens, width), floating)
        outs = [((tokens, 2 * width), bfloat), ((1, tokens, 2 * width), bfloat), narrow, narrow, narrow, probs, wide, wide,
                ffn, ffn, wide] + kept
        args = (x_in, message, segments, mixing, correction, gain_attn, gain_ffn) + weights
        in_specs = [VMEM, VMEM, VMEM, SMEM, SMEM, VMEM, VMEM] + [ANY] * 7
        scratch = [pltpu.VMEM(*one) for one in outs] + common + [pltpu.SemaphoreType.DMA((len(outs),))]
        out_specs = [ANY] * len(outs)
    else:
        outs = [((tokens + EXTRA, width), bfloat)]
        args = (x_in, segments, mixing, correction, gain_attn, gain_ffn) + weights
        in_specs = [VMEM, VMEM, SMEM, SMEM, VMEM, VMEM] + [ANY] * 7
        scratch = [pltpu.VMEM(*narrow)] * 3 + [pltpu.VMEM(*wide)] * 2 + common
        out_specs = [VMEM]
    return pl.pallas_call(
        lambda *refs: forward_body(full, fast, refs),
        out_shape=[shape(*one) for one in outs],
        in_specs=in_specs,
        out_specs=out_specs,
        scratch_shapes=scratch,
        compiler_params=params(52),
        cost_estimate=estimate,
        name="forward_full" if full else "forward_lite",
    )(*args)


def start_rows(message, grad_ref, counts_ref, cor_ref, g_ref, low_ref):
    tokens, width = low_ref.shape
    rows = counts_ref.shape[0]
    length = tokens // rows
    section = lax.axis_index("section")
    if message is not None:
        got = read_scalars(message[tokens : tokens + EXTRA, :PAIR].astype(floating), 4)
    place = lax.broadcasted_iota(jnp.int32, (length, width), 0)
    for row in range(rows):
        span = slice(row * length, (row + 1) * length)
        valid = place < counts_ref[row]
        own_a = jnp.where(valid, grad_ref[span, :width].astype(floating), 0.0)
        own_b = jnp.where(valid, grad_ref[span, width:].astype(floating), 0.0)
        if message is not None:
            later_b = own_b + message[span, :].astype(floating)
            far_a = own_a + (got[0] * own_a + got[2] * later_b)
            far_b = later_b + (got[1] * own_a + got[3] * later_b)
            own_a = jnp.where(section == 0, far_a, own_a).astype(bfloat).astype(floating)
            own_b = jnp.where(section == 0, far_b, own_b).astype(bfloat).astype(floating)
        g_ref[span, :width] = own_a.astype(bfloat)
        g_ref[span, width:] = own_b.astype(bfloat)
        low_ref[span, :] = (cor_ref[0, 0] * own_a + cor_ref[0, 1] * own_b).astype(bfloat)


def start(message, out_grad, counts, correction):
    tokens = out_grad.shape[0]
    width = message.shape[1]
    shape = jax.ShapeDtypeStruct
    return pl.pallas_call(
        start_rows,
        out_shape=[shape((tokens, 2 * width), bfloat), shape((tokens, width), bfloat)],
        in_specs=[VMEM, VMEM, SMEM, SMEM],
        out_specs=[VMEM, VMEM],
        compiler_params=params(16),
        cost_estimate=cost(tokens * width * 20, tokens * width * 12),
        name="backward_start",
    )(message, out_grad, counts, correction)


def norm_backward(values, gain, grad_normed, with_gain):
    inverse = rms_scale(values)
    grad_gain = jnp.sum(grad_normed * values * inverse, axis=0, keepdims=True) if with_gain else None
    weighted = grad_normed * gain
    grad_values = inverse * weighted - values * inverse**3 * jnp.mean(weighted * values, axis=-1, keepdims=True)
    return grad_gain, grad_values


class FfnLoads:
    def __init__(self, wg, wu, wd, one, two, wg_s, wu_s, wd_s, one_s, two_s, sem):
        width = wd.shape[2]
        quarter = lax.axis_index("dp") & 3
        self.groups = []
        for step in range(4):
            slot = 3 - step
            piece = slot ^ quarter
            span = pl.ds(pl.multiple_of(piece * width, width), width)
            self.groups.append(
                [
                    pltpu.make_async_copy(wd.at[0, span, :], wd_s.at[step], sem.at[5 * step]),
                    pltpu.make_async_copy(one.at[piece], one_s.at[step], sem.at[5 * step + 1]),
                    pltpu.make_async_copy(two.at[piece], two_s.at[step], sem.at[5 * step + 2]),
                    pltpu.make_async_copy(wg.at[0, :, span], wg_s.at[step], sem.at[5 * step + 3]),
                    pltpu.make_async_copy(wu.at[0, :, span], wu_s.at[step], sem.at[5 * step + 4]),
                ]
            )

    def start(self, step):
        for copy in self.groups[step]:
            copy.start()


def ffn_steps(loads, low_ref, acc, wg_s, wu_s, wd_s, one_s, two_s, emit):
    for step in range(4):
        group = loads.groups[step]
        for copy in group[:3]:
            copy.wait()
        grad_hidden = dot_t(low_ref[...], wd_s[step])
        dgate = (grad_hidden * one_s[step]).astype(bfloat)
        dup = (grad_hidden * two_s[step]).astype(bfloat)
        emit(step, dgate, dup)
        for copy in group[3:]:
            copy.wait()
        if step + 2 < 4:
            loads.start(step + 2)
        total = dot_t(dgate, wg_s[step]) + dot_t(dup, wu_s[step])
        if step == 0:
            acc[...] = total
        else:
            acc[...] += total


def ffn_scratch(tokens, width):
    return [
        pltpu.VMEM((tokens, width), floating),
        pltpu.VMEM((4, width, width), bfloat),
        pltpu.VMEM((4, width, width), bfloat),
        pltpu.VMEM((4, width, width), bfloat),
        pltpu.VMEM((4, tokens, width), floating),
        pltpu.VMEM((4, tokens, width), floating),
        pltpu.SemaphoreType.DMA((20,)),
    ]


def ffn_kernel(g_in, low_ref, cor_ref, gf_ref, mid_ref, one, two, wg, wu, wd, *refs):
    slots = refs[:8]
    dmid_ref, datt_ref, gain_ref = refs[8:11]
    acc, wg_s, wu_s, wd_s, one_s, two_s, sem, dgate_s, dup_s, out_sem = refs[11:]
    width = gf_ref.shape[1]
    loads = FfnLoads(wg, wu, wd, one, two, wg_s, wu_s, wd_s, one_s, two_s, sem)
    loads.start(0)
    loads.start(1)
    leaving = []

    def emit(step, dgate, dup):
        slot = 3 - step
        dgate_s[step] = dgate
        dup_s[step] = dup
        for copy in (
            pltpu.make_async_copy(dgate_s.at[step], slots[slot], out_sem.at[slot]),
            pltpu.make_async_copy(dup_s.at[step], slots[4 + slot], out_sem.at[4 + slot]),
        ):
            copy.start()
            leaving.append(copy)

    ffn_steps(loads, low_ref, acc, wg_s, wu_s, wd_s, one_s, two_s, emit)
    grad_gain, grad_values = norm_backward(mid_ref[...], gf_ref[...], acc[...], True)
    block = cor_ref[0, 0] * g_in[:, :width].astype(floating) + cor_ref[0, 1] * g_in[:, width:].astype(floating)
    grad_middle = block + grad_values
    dmid_ref[...] = grad_middle
    datt_ref[...] = grad_middle.astype(bfloat)
    gain_ref[...] = grad_gain
    for copy in leaving:
        copy.wait()


def ffn_backward(g_in, low, correction, gain_ffn, middle, one, two, weights):
    tokens = g_in.shape[0]
    width = gain_ffn.shape[1]
    shape = jax.ShapeDtypeStruct
    return pl.pallas_call(
        ffn_kernel,
        out_shape=[shape((tokens, width), bfloat)] * 8
        + [shape((tokens, width), floating), shape((tokens, width), bfloat), shape((1, width), floating)],
        in_specs=[VMEM, VMEM, SMEM, VMEM, VMEM] + [ANY] * 5,
        out_specs=[ANY] * 8 + [VMEM] * 3,
        scratch_shapes=ffn_scratch(tokens, width)
        + [pltpu.VMEM((4, tokens, width), bfloat)] * 2
        + [pltpu.SemaphoreType.DMA((8,))],
        compiler_params=params(36),
        cost_estimate=cost(2 * tokens * 3 * weights[4].size, 2 * 3 * weights[4].size),
        name="backward_ffn",
    )(g_in, low, correction, gain_ffn, middle, one, two, *weights[4:])


def attn_steps(q_ref, k_ref, v_ref, p_ref, do_ref, dqkv_ref, base):
    tokens, width = do_ref.shape
    length = p_ref.shape[2]
    rows = tokens // length
    pairs = width // PAIR
    first = lane_mask(length)
    for row in range(rows):
        span = slice(row * length, (row + 1) * length)
        for pair in range(pairs):
            heads = slice(pair * PAIR, (pair + 1) * PAIR)
            probs = p_ref[row * pairs + pair]
            grad_out = stack_heads(do_ref[span, heads], first)
            grad_value = t_dot(probs.astype(bfloat), grad_out)
            grad_probs = dot_t(grad_out, v_ref[span, heads])
            carried = jnp.sum(probs * grad_probs, axis=-1, keepdims=True)
            grad_scores = (probs * (grad_probs - carried)).astype(bfloat)
            grad_query = dot(grad_scores, k_ref[span, heads])
            grad_query = jnp.where(first, grad_query[:length], grad_query[length:])
            grad_key = t_dot(grad_scores, stack_heads(q_ref[span, heads], first))
            at = base + pair * PAIR
            dqkv_ref[span, at : at + PAIR] = (grad_query * SCALE).astype(bfloat)
            dqkv_ref[span, at + width : at + width + PAIR] = (grad_key * SCALE).astype(bfloat)
            dqkv_ref[span, at + 2 * width : at + 2 * width + PAIR] = grad_value.astype(bfloat)


def normed_grad(dqkv_ref, base, width, wq_s, wk_s, wv_s):
    return (
        dot_t(dqkv_ref[:, base : base + width], wq_s[...])
        + dot_t(dqkv_ref[:, base + width : base + 2 * width], wk_s[...])
        + dot_t(dqkv_ref[:, base + 2 * width : base + 3 * width], wv_s[...])
    )


def attn_kernel(datt_ref, q_ref, k_ref, v_ref, p_ref, gfg_ref, ga_ref, mix_ref, cor_ref,
                x_any, g_any, dmid_any, act_any, chg_any, wq, wk, wv, wo,
                grad_ref, right_ref, small_ref,
                do_ref, wq_s, wk_s, wv_s, wo_s, x_ref, g_in, dmid_ref, act_ref, chg_ref, sem, right_s, right_sem):
    tokens, width = datt_ref.shape
    copies = [
        pltpu.make_async_copy(source, target, sem.at[place])
        for place, (source, target) in enumerate(
            (
                (wo.at[0], wo_s), (wq.at[0], wq_s), (wk.at[0], wk_s), (wv.at[0], wv_s), (act_any, act_ref), (g_any, g_in),
                (dmid_any, dmid_ref), (x_any, x_ref), (chg_any, chg_ref),
            )
        )
    ]
    for copy in copies:
        copy.start()
    right_s[:, :width] = datt_ref[...]
    copies[0].wait()
    do_ref[...] = dot_t(datt_ref[...], wo_s[...]).astype(bfloat)
    attn_steps(q_ref, k_ref, v_ref, p_ref, do_ref, right_s, width)
    right_copy = pltpu.make_async_copy(right_s, right_ref, right_sem)
    right_copy.start()
    for copy in copies[1:]:
        copy.wait()
    grad_normed = normed_grad(right_s, width, width, wq_s, wk_s, wv_s)
    grad_gain, grad_values = norm_backward(act_ref[...], ga_ref[...], grad_normed, True)
    section = lax.axis_index("section")
    mix = [[mix_ref[0, i, j] for j in range(2)] for i in range(2)]
    cor = [cor_ref[0, i] for i in range(2)]
    out_a = g_in[:, :width].astype(floating)
    out_b = g_in[:, width:].astype(floating)
    grad_active = dmid_ref[...] + grad_values - (cor[0] * out_a + cor[1] * out_b)
    pred_a = out_a + jnp.where(section == 0, grad_active, 0.0)
    pred_b = out_b + jnp.where(section == 0, 0.0, grad_active)
    grad_ref[0, :, :width] = (pred_a + (mix[0][0] * pred_a + mix[1][0] * pred_b)).astype(bfloat)
    grad_ref[0, :, width:] = (pred_b + (mix[0][1] * pred_a + mix[1][1] * pred_b)).astype(bfloat)
    xa = x_ref[:, :width].astype(floating)
    xb = x_ref[:, width:].astype(floating)
    small_ref[0:1, :] = grad_gain
    small_ref[1:2, :] = gfg_ref[...]
    place = 2
    for pred in (pred_a, pred_b):
        for state in (xa, xb):
            small_ref[place : place + 1, :] = jnp.sum(pred * state, axis=0, keepdims=True)
            place += 1
    for out in (out_a, out_b):
        small_ref[place : place + 1, :] = jnp.sum(out * chg_ref[...], axis=0, keepdims=True)
        place += 1
    right_copy.wait()


def attn_backward(x, g_in, grad_middle, grad_att, active, change, queries, key_rows, value_rows, probs, ffn_gain, gain_attn,
                  mixing, correction, weights):
    tokens, width = active.shape
    shape = jax.ShapeDtypeStruct
    wide = pltpu.VMEM((tokens, width), floating)
    return pl.pallas_call(
        attn_kernel,
        out_shape=[shape((1, tokens, 2 * width), bfloat), shape((tokens, 4 * width), bfloat), shape((8, width), floating)],
        in_specs=[VMEM] * 7 + [SMEM] * 2 + [ANY] * 9,
        out_specs=[VMEM, ANY, VMEM],
        scratch_shapes=[pltpu.VMEM((tokens, width), bfloat)]
        + [pltpu.VMEM((width, width), bfloat)] * 4
        + [pltpu.VMEM((tokens, 2 * width), bfloat)] * 2
        + [wide] * 3
        + [pltpu.SemaphoreType.DMA((9,)), pltpu.VMEM((tokens, 4 * width), bfloat), pltpu.SemaphoreType.DMA],
        compiler_params=params(32),
        cost_estimate=cost(2 * tokens * 5 * weights[0].size, 2 * 4 * weights[0].size),
        name="backward_attn",
    )(grad_att, queries, key_rows, value_rows, probs, ffn_gain, gain_attn, mixing, correction,
      x, g_in, grad_middle, active, change, *weights[:4])


def relay_kernel(grad_in, counts_ref, cor_ref, mix_ref, gf_ref, ga_ref,
                 one, two, mid_any, q_any, k_any, v_any, p_any, act_any, wq, wk, wv, wo, wg, wu, wd,
                 msg_ref,
                 acc, wg_s, wu_s, wd_s, one_s, two_s, sem,
                 g_in, low_ref, mid_ref, q_ref, k_ref, v_ref, p_ref, act_ref, do_ref, dqkv_ref, wq_s, wk_s, wv_s, wo_s, more):
    tokens, width = low_ref.shape
    loads = FfnLoads(wg, wu, wd, one, two, wg_s, wu_s, wd_s, one_s, two_s, sem)
    loads.start(0)
    loads.start(1)
    start_rows(None, grad_in, counts_ref, cor_ref, g_in, low_ref)
    copies = [
        pltpu.make_async_copy(source, target, more.at[place])
        for place, (source, target) in enumerate(
            (
                (mid_any, mid_ref), (wo.at[0], wo_s), (q_any, q_ref), (k_any, k_ref), (v_any, v_ref), (p_any, p_ref),
                (wq.at[0], wq_s), (wk.at[0], wk_s), (wv.at[0], wv_s), (act_any, act_ref),
            )
        )
    ]

    def emit(step, dgate, dup):
        if step == 2:
            for copy in copies[:6]:
                copy.start()
        if step == 3:
            for copy in copies[6:]:
                copy.start()

    ffn_steps(loads, low_ref, acc, wg_s, wu_s, wd_s, one_s, two_s, emit)
    copies[0].wait()
    grad_values = norm_backward(mid_ref[...], gf_ref[...], acc[...], False)[1]
    cor = [cor_ref[0, i] for i in range(2)]
    block = cor[0] * g_in[:, :width].astype(floating) + cor[1] * g_in[:, width:].astype(floating)
    acc[...] = block + grad_values
    copies[1].wait()
    do_ref[...] = dot_t(acc[...].astype(bfloat), wo_s[...]).astype(bfloat)
    for copy in copies[2:6]:
        copy.wait()
    attn_steps(q_ref, k_ref, v_ref, p_ref, do_ref, dqkv_ref, 0)
    for copy in copies[6:]:
        copy.wait()
    grad_normed = normed_grad(dqkv_ref, 0, width, wq_s, wk_s, wv_s)
    grad_values = norm_backward(act_ref[...], ga_ref[...], grad_normed, False)[1]
    block = cor[0] * g_in[:, :width].astype(floating) + cor[1] * g_in[:, width:].astype(floating)
    msg_ref[:tokens, :] = (acc[...] + grad_values - block).astype(bfloat)
    mix = [[mix_ref[0, i, j] for j in range(2)] for i in range(2)]
    msg_ref[tokens:, :] = scalar_rows(mix[0] + mix[1], EXTRA, width)


def relay_backward(out_grad, counts, correction, mixing, gain_ffn, gain_attn, one, two, middle, queries, key_rows, value_rows,
                   probs, active, weights):
    tokens, width = active.shape
    shape = jax.ShapeDtypeStruct
    narrow = pltpu.VMEM((tokens, width), bfloat)
    wide = pltpu.VMEM((tokens, width), floating)
    size = sum(weight.size for weight in weights)
    return pl.pallas_call(
        relay_kernel,
        out_shape=shape((tokens + EXTRA, width), bfloat),
        in_specs=[VMEM, SMEM, SMEM, SMEM, VMEM, VMEM] + [ANY] * 15,
        out_specs=VMEM,
        scratch_shapes=ffn_scratch(tokens, width)
        + [pltpu.VMEM((tokens, 2 * width), bfloat), narrow, wide, narrow, narrow, narrow, pltpu.VMEM(probs.shape, floating), wide,
           narrow, pltpu.VMEM((tokens, 3 * width), bfloat)]
        + [pltpu.VMEM((width, width), bfloat)] * 4
        + [pltpu.SemaphoreType.DMA((10,))],
        compiler_params=params(44),
        cost_estimate=cost(2 * tokens * size, 2 * size),
        name="backward_relay",
    )(out_grad, counts, correction, mixing, gain_ffn, gain_attn, one, two, middle, queries, key_rows, value_rows, probs, active,
      *weights)


def quarter_kernel(parts, block, refs):
    count = 4
    lefts = refs[:count]
    rights = refs[count : 2 * count]
    send_ref, keep_ref, left_s, right_s, sem = refs[2 * count :]
    tokens = lefts[0].shape[0]
    first, columns = parts[0]
    copies = []
    for place in range(count):
        span = pl.ds(place * tokens, tokens)
        copies.append(pltpu.make_async_copy(lefts[place].at[:, pl.ds(first, columns)], left_s.at[span, :], sem.at[2 * place]))
        copies.append(pltpu.make_async_copy(rights[place], right_s.at[span, :], sem.at[2 * place + 1]))
    for copy in copies:
        copy.start()
    for copy in copies:
        copy.wait()
    index = lax.axis_index("dp")
    near = (index >> 2) & 1
    far = (index >> 3) & 1
    products = parts[1]
    for left_at, left_wide, right_at, right_wide in products:
        total = t_dot(left_s[:, left_at : left_at + left_wide], right_s[:, right_at : right_at + right_wide])
        for place in range(4):
            part = total[place * block : (place + 1) * block, :]
            slot = (place >> 1) ^ far
            mine = (place & 1) == near

            @pl.when(mine)
            def _():
                keep_ref[slot, :, right_at : right_at + right_wide] = part

            @pl.when(jnp.logical_not(mine))
            def _():
                send_ref[slot, :, right_at : right_at + right_wide] = part.astype(bfloat)


def quarter_product(lefts, first, columns, rights, products, block, name):
    tokens = lefts[0].shape[0]
    right_wide = rights[0].shape[1]
    shape = jax.ShapeDtypeStruct
    flops = sum(2 * 4 * tokens * one[1] * one[3] for one in products)
    return pl.pallas_call(
        lambda *refs: quarter_kernel(((first, columns), products), block, refs),
        out_shape=[shape((2, block, right_wide), bfloat), shape((2, block, right_wide), floating)],
        in_specs=[ANY] * 8,
        out_specs=[VMEM, VMEM],
        scratch_shapes=[
            pltpu.VMEM((4 * tokens, columns), bfloat), pltpu.VMEM((4 * tokens, right_wide), bfloat), pltpu.SemaphoreType.DMA((8,))
        ],
        compiler_params=params(24),
        cost_estimate=cost(flops, 8 * tokens * (columns + right_wide) + 12 * block * right_wide),
        name=name,
    )(*lefts, *rights)


def assemble_kernel(own, one, two, three, gate_ref, up_ref):
    quarter = lax.axis_index("dp") & 3
    width = own.shape[1] // 2
    for slot, piece in enumerate((own, one, two, three)):
        span = pl.ds(pl.multiple_of((slot ^ quarter) * width, width), width)
        gate_ref[0, :, span] = piece[:, :width].astype(floating)
        up_ref[0, :, span] = piece[:, width:].astype(floating)


def assemble(pieces):
    share, double = pieces[0].shape
    shape = jax.ShapeDtypeStruct((1, share, 2 * double), floating)
    return pl.pallas_call(
        assemble_kernel,
        out_shape=[shape, shape],
        in_specs=[VMEM] * 4,
        out_specs=[VMEM] * 2,
        compiler_params=params(16),
        cost_estimate=cost(share * double * 4, share * double * 24),
        name="assemble",
    )(*pieces)


def exchange(value, flips):
    count = lax.axis_size("dp")
    return lax.ppermute(value, "dp", [(source, source ^ flips) for source in range(count)])


def relative_rows(matrix, order, index):
    bits = len(order)
    block = matrix.shape[0] >> bits
    split = matrix.reshape((2,) * bits + (block, matrix.shape[1]))
    axes = [bits - 1 - bit for bit in order]
    split = jnp.transpose(split, axes + [bits, bits + 1])
    for axis, bit in enumerate(order):
        split = jnp.where((index >> bit) & 1 == 1, jnp.flip(split, axis), split)
    return split.reshape(matrix.shape)


def scatter_sum(left, right, order):
    total = left.shape[0]
    arrived = []
    for step in range(len(order) + 1):
        low = total >> (step + 1) if step < len(order) else 0
        high = total >> step
        part = dot(left[low:high], right)
        for other in arrived:
            part = part + other[low:high].astype(floating)
        if step == len(order):
            return part
        arrived.append(exchange(part.astype(bfloat), 1 << order[step]))


def halving_grads(kept, low, slots, right, index, count):
    width = low.shape[1]
    order = list(range(count.bit_length() - 1))
    normed, attended, normed_ffn, hidden = (relative_rows(one.T, order, index) for one in kept)
    quarter = index & 3
    places = jnp.arange(4) ^ quarter
    dgate = jnp.concatenate(list(jnp.stack(slots[:4])[places]), axis=1)
    dup = jnp.concatenate(list(jnp.stack(slots[4:])[places]), axis=1)
    grad_down = scatter_sum(hidden, low, order)
    grad_gate = scatter_sum(normed_ffn, dgate, order)
    grad_up = scatter_sum(normed_ffn, dup, order)
    grad_out = scatter_sum(attended, right[:, :width], order)
    grad_qkv = scatter_sum(normed, right[:, width:], order)
    return grad_down[None], grad_gate[None], grad_up[None], grad_out[None], grad_qkv[None]


def gathered(value):
    across = exchange(value, 2)
    beside = exchange(value, 1)
    return [value, beside, across, exchange(across, 1)]


def swapped(pieces):
    return [pieces[0]] + [exchange(pieces[flips], flips) for flips in (1, 2, 3)]


def sum_on(pair):
    send, keep = pair
    arrived = exchange(send, 4)
    passed = (keep[1] + arrived[1].astype(floating)).astype(bfloat)
    held = keep[0] + arrived[0].astype(floating)
    return held, exchange(passed, 8)


def quarter_grads(kept, low, slots, right, index):
    width = low.shape[1]
    share = width // 16
    block = 4 * share
    lows = gathered(low)
    down_pair = quarter_product(kept, 0, width, lows, [(0, width, 0, width)], block, "product_down")
    gates = swapped(slots[:4])
    ups = swapped(slots[4:])
    gate_pair = quarter_product(kept, width, width, gates, [(0, width, 0, width)], block, "product_gate")
    up_pair = quarter_product(kept, width, width, ups, [(0, width, 0, width)], block, "product_up")
    rights = gathered(right)
    attn_products = [(0, block, 0, width), (block, block, width, 3 * width)]
    attn_pair = quarter_product(kept, 2 * width, 2 * block, rights, attn_products, share, "product_attn")
    held, passed = sum_on(down_pair)
    grad_down = held + passed.astype(floating)
    tiles = []
    for pair in (gate_pair, up_pair):
        held, passed = sum_on(pair)
        tiles.append((held + passed.astype(floating)).astype(bfloat))
    quarter = index & 3
    pieces = [
        jnp.concatenate([lax.dynamic_slice_in_dim(tile, (slot ^ quarter) * share, share, axis=0) for tile in tiles], axis=1)
        for slot in range(4)
    ]
    grad_gate, grad_up = assemble(swapped(pieces))
    held, passed = sum_on(attn_pair)
    total = held + passed.astype(floating)
    return grad_down[None], grad_gate, grad_up, total[None, :, :width], total[None, :, width:]


def local(states_in, out_grad, counts, segments, mixing, correction, gain_attn, w_query, w_key, w_value, w_attn_out, gain_ffn,
          w_gate, w_up, w_down):
    weights = (w_query, w_key, w_value, w_attn_out, w_gate, w_up, w_down)
    width = gain_attn.shape[1]
    index = lax.axis_index("dp")
    count = lax.axis_size("dp")
    fast = count == 16
    (message,) = forward(False, fast, states_in, None, segments, mixing, correction, gain_attn, gain_ffn, weights)
    message = lax.ppermute(message, "section", [(0, 1), (1, 0)])
    (x, states, queries, key_rows, value_rows, probs, active, middle, one, two, change, *kept) = forward(
        True, fast, states_in, message, segments, mixing, correction, gain_attn, gain_ffn, weights)
    if fast:
        kept = swapped(kept)
    message = relay_backward(out_grad, counts, correction, mixing, gain_ffn, gain_attn, one, two, middle, queries, key_rows,
                             value_rows, probs, active, weights)
    message = lax.ppermute(message, "section", [(0, 1), (1, 0)])
    g_in, low = start(message, out_grad, counts, correction)
    *slots, grad_middle, grad_att, ffn_gain = ffn_backward(g_in, low, correction, gain_ffn, middle, one, two, weights)
    state_grads, right, small = attn_backward(x, g_in, grad_middle, grad_att, active, change, queries, key_rows, value_rows, probs,
                                              ffn_gain, gain_attn, mixing, correction, weights)
    if fast:
        grad_down, grad_gate, grad_up, grad_out, grad_qkv = quarter_grads(kept, low, slots, right, index)
    else:
        grad_down, grad_gate, grad_up, grad_out, grad_qkv = halving_grads(kept, low, slots, right, index, count)
    for bit in range(count.bit_length() - 1):
        small = small + exchange(small, 1 << bit)
    share = width // count
    gains = lax.dynamic_slice(small, (0, index * share), (2, share))
    sums = jnp.sum(small[2:], axis=1)
    return (
        states,
        state_grads,
        sums[:4].reshape(1, 2, 2),
        sums[4:].reshape(1, 2),
        gains[0:1],
        grad_qkv[:, :, :width],
        grad_qkv[:, :, width : 2 * width],
        grad_qkv[:, :, 2 * width :],
        grad_out,
        gains[1:2],
        grad_gate,
        grad_up,
        grad_down,
    )


def solution(mesh):
    rows = P("dp", None)
    matrix = P("section", None, None)
    vector = P("section", None)
    share = P("section", "dp", None)
    gain_share = P("section", "dp")
    in_specs = (rows, rows, P("dp"), rows, matrix, vector, vector, matrix, matrix, matrix, matrix, vector, matrix, matrix, matrix)
    out_specs = (share, share, matrix, vector, gain_share, share, share, share, share, gain_share, share, share, share)
    return jax.shard_map(local, mesh=mesh, in_specs=in_specs, out_specs=out_specs, check_vma=False)
```

```python
import functools

import jax
import jax.numpy as jnp
from jax import lax
from jax.experimental import pallas as pl
from jax.experimental.pallas import tpu as pltpu
from jax.sharding import PartitionSpec as P

HEAD_DIM = 64
PAIR = 2 * HEAD_DIM
EPSILON = 1e-06
MASKED = -1e30
SCALE = HEAD_DIM ** (-0.5)
GELU_A = 0.7978845608028654
GELU_B = 0.044715
EXTRA = 16
AHEAD = 3
SCOPED = 12
bfloat = jnp.bfloat16
floating = jnp.float32

VMEM = pl.BlockSpec(memory_space=pltpu.VMEM)
SMEM = pl.BlockSpec(memory_space=pltpu.SMEM)
ANY = pl.BlockSpec(memory_space=pltpu.MemorySpace.HBM)


def dot(a, b):
    return jnp.dot(a, b, preferred_element_type=floating)


def dot_t(a, b):
    return lax.dot_general(a, b, (((1,), (1,)), ((), ())), preferred_element_type=floating)


def t_dot(a, b):
    return lax.dot_general(a, b, (((0,), (0,)), ((), ())), preferred_element_type=floating)


def params(mebibytes):
    return pltpu.CompilerParams(vmem_limit_bytes=mebibytes * 1024 * 1024)


def cost(flops, moved):
    return pl.CostEstimate(flops=flops // 1000, bytes_accessed=moved // 1000, transcendentals=0)


def scalar_rows(values, rows, width):
    lane = lax.broadcasted_iota(jnp.int32, (rows, width), 1)
    row = lax.broadcasted_iota(jnp.int32, (rows, width), 0)
    whole = jnp.zeros((rows, width), floating)
    for place, value in enumerate(values):
        whole = jnp.where(lane == place, value, whole)
    high = whole.astype(bfloat).astype(floating)
    middle = (whole - high).astype(bfloat).astype(floating)
    low = whole - high - middle
    part = jnp.where(row == 0, high, jnp.where(row == 1, middle, jnp.where(row == 2, low, 0.0)))
    return part.astype(bfloat)


def read_scalars(block, count):
    lane = lax.broadcasted_iota(jnp.int32, block.shape, 1)
    return [jnp.sum(jnp.where(lane == place, block, 0.0)) for place in range(count)]


def rms_scale(values):
    return lax.rsqrt(jnp.mean(values * values, axis=-1, keepdims=True) + EPSILON)


def lane_mask(length):
    return lax.broadcasted_iota(jnp.int32, (length, PAIR), 1) < HEAD_DIM


def stack_heads(block, first):
    zero = jnp.zeros_like(block)
    return jnp.concatenate([jnp.where(first, block, zero), jnp.where(first, zero, block)], axis=0)


def gelu_wave(gate):
    return jnp.tanh(GELU_A * (gate + GELU_B * gate * gate * gate))


def relative(blocks, index):
    low = (index & 1) == 1
    high = (index >> 1) == 1
    once = [jnp.where(low, blocks[place ^ 1], blocks[place]) for place in range(4)]
    return [jnp.where(high, once[place ^ 2], once[place]) for place in range(4)]


def attention(q_ref, k_ref, v_ref, seg_ref, att_ref, p_ref):
    length = seg_ref.shape[1]
    rows = q_ref.shape[0] // length
    pairs = q_ref.shape[1] // PAIR
    first = lane_mask(length)
    later = lax.broadcasted_iota(jnp.int32, (length, length), 0)
    earlier = lax.broadcasted_iota(jnp.int32, (length, length), 1)
    for row in range(rows):
        documents = jnp.broadcast_to(seg_ref[row : row + 1, :], (length, length)).astype(floating)
        allowed = (earlier <= later) & (documents == documents.T)
        allowed = jnp.concatenate([allowed, allowed], axis=0)
        span = slice(row * length, (row + 1) * length)
        for pair in range(pairs):
            heads = slice(pair * PAIR, (pair + 1) * PAIR)
            stacked = stack_heads(q_ref[span, heads], first)
            scores = jnp.where(allowed, dot_t(stacked, k_ref[span, heads]) * SCALE, MASKED)
            powers = jnp.exp(scores - jnp.max(scores, axis=-1, keepdims=True))
            probs = powers / jnp.sum(powers, axis=-1, keepdims=True)
            if p_ref is not None:
                p_ref[row * pairs + pair] = probs
            mixed = dot(probs.astype(bfloat), v_ref[span, heads])
            att_ref[span, heads] = jnp.where(first, mixed[:length], mixed[length:]).astype(bfloat)


def in_hbm(value):
    return pltpu.with_memory_space_constraint(value, pltpu.MemorySpace.HBM)


def forward_lite_kernel(x_any, seg_any, mix_any, cor_any, ga_any, gf_any, wq, wk, wv, wo, wg, wu, wd,
                        out_ref, wq_s, wk_s, wv_s, wo_s, wg_s, wu_s, wd_s,
                        x_in, seg_ref, mix_ref, cor_ref, ga_ref, gf_ref, q_ref, k_ref, v_ref, act_ref,
                        nrm_ref, att_ref, nf_ref, acc, sem, small_sem):
    tokens, width = act_ref.shape
    chunk = width
    pieces = wg.shape[2] // chunk
    small = [
        pltpu.make_async_copy(source, target, small_sem.at[place])
        for place, (source, target) in enumerate(
            ((x_any, x_in), (mix_any, mix_ref), (ga_any, ga_ref), (seg_any, seg_ref), (gf_any, gf_ref), (cor_any, cor_ref))
        )
    ]
    pairs = [(wq, wq_s), (wk, wk_s), (wv, wv_s), (wo, wo_s)]
    for piece in range(pieces):
        span = pl.ds(piece * chunk, chunk)
        pairs += [
            (wg.at[:, :, span], wg_s.at[:, :, span]), (wu.at[:, :, span], wu_s.at[:, :, span]), (wd.at[:, span, :], wd_s.at[:, span, :])
        ]
    queue = [pltpu.make_async_copy(source, target, sem.at[place]) for place, (source, target) in enumerate(pairs)]
    for copy in small + queue[:AHEAD]:
        copy.start()
    state = [0]

    def arrive():
        queue[state[0]].wait()
        if state[0] + AHEAD < len(queue):
            queue[state[0] + AHEAD].start()
        state[0] += 1

    for copy in small:
        copy.wait()
    section = lax.axis_index("section")
    mix = [[mix_ref[0, i, j] for j in range(2)] for i in range(2)]
    cor = [cor_ref[0, i] for i in range(2)]
    xa = x_in[:, :width].astype(floating)
    xb = x_in[:, width:].astype(floating)
    own_a = jnp.where(section == 0, mix[0][0], mix[1][0])
    own_b = jnp.where(section == 0, mix[0][1], mix[1][1])
    active = jnp.where(section == 0, xa, xb) + (own_a * xa + own_b * xb)
    act_ref[...] = active
    nrm_ref[...] = (active * rms_scale(active) * ga_ref[...]).astype(bfloat)
    for weight, target in zip((wq_s, wk_s, wv_s), (q_ref, k_ref, v_ref)):
        arrive()
        target[...] = dot(nrm_ref[...], weight[0]).astype(bfloat)
    attention(q_ref, k_ref, v_ref, seg_ref, att_ref, None)
    arrive()
    middle = act_ref[...] + dot(att_ref[...], wo_s[0])
    acc[...] = middle - act_ref[...]
    nf_ref[...] = (middle * rms_scale(middle) * gf_ref[...]).astype(bfloat)
    for piece in range(pieces):
        span = slice(piece * chunk, (piece + 1) * chunk)
        arrive()
        gate = dot(nf_ref[...], wg_s[0, :, span])
        arrive()
        upward = dot(nf_ref[...], wu_s[0, :, span])
        hidden = (0.5 * gate * (1.0 + gelu_wave(gate)) * upward).astype(bfloat)
        arrive()
        acc[...] += dot(hidden, wd_s[0, span, :])
    out_ref[:tokens, :] = acc[...].astype(bfloat)
    out_ref[tokens:, :] = scalar_rows(mix[0] + mix[1] + cor, EXTRA, width)


def forward_lite(x_in, segments, mixing, correction, gain_attn, gain_ffn, weights):
    tokens = x_in.shape[0]
    width = gain_attn.shape[1]
    size = sum(weight.size for weight in weights)
    narrow = pltpu.VMEM((tokens, width), bfloat)
    wide = pltpu.VMEM((tokens, width), floating)
    args = (x_in, segments, mixing, correction, gain_attn, gain_ffn) + weights
    scratch = [
        pltpu.VMEM(x_in.shape, bfloat), pltpu.VMEM(segments.shape, jnp.int32), pltpu.SMEM(mixing.shape, floating),
        pltpu.SMEM(correction.shape, floating), pltpu.VMEM(gain_attn.shape, floating), pltpu.VMEM(gain_ffn.shape, floating),
        narrow, narrow, narrow, wide, narrow, narrow, narrow, wide,
    ]
    scratch += [pltpu.SemaphoreType.DMA((4 + 3 * (weights[4].shape[2] // width),)), pltpu.SemaphoreType.DMA((6,))]
    return pl.pallas_call(
        forward_lite_kernel,
        out_shape=[jax.ShapeDtypeStruct((tokens + EXTRA, width), bfloat)]
        + [jax.ShapeDtypeStruct(weight.shape, bfloat) for weight in weights],
        in_specs=[ANY] * len(args),
        out_specs=[VMEM] * 8,
        scratch_shapes=scratch,
        compiler_params=params(SCOPED),
        cost_estimate=cost(2 * tokens * size, 2 * size),
        name="forward_lite",
    )(*[in_hbm(one) for one in args])


def forward_kernel(fast, x_in, message, seg_ref, mix_ref, cor_ref, ga_ref, gf_ref, wq, wk, wv, wo, wg, wu, wd,
                   x_ref, out_ref, q_ref, k_ref, v_ref, p_ref, act_ref, mid_ref, one_ref, two_ref, chg_ref, *refs):
    kept = refs[:4]
    nearby = refs[4:8]
    nf_ref = refs[-4]
    nrm_ref, att_ref, acc = refs[-3:]
    tokens, width = act_ref.shape
    chunk = width
    pieces = wg.shape[2] // chunk
    section = lax.axis_index("section")
    quarter = lax.axis_index("dp") & 3
    mix = [[mix_ref[0, i, j] for j in range(2)] for i in range(2)]
    cor = [cor_ref[0, i] for i in range(2)]
    xa = x_in[:, :width].astype(floating)
    xb = x_in[:, width:].astype(floating)
    got = read_scalars(message[tokens : tokens + EXTRA, :PAIR].astype(floating), 6)
    moved = message[:tokens, :].astype(floating)
    sent_a = (xa + (got[0] * xa + got[1] * xb) + got[4] * moved).astype(bfloat)
    sent_b = (xb + (got[2] * xa + got[3] * xb) + got[5] * moved).astype(bfloat)
    x_ref[:, :width] = jnp.where(section == 0, x_in[:, :width], sent_a)
    x_ref[:, width:] = jnp.where(section == 0, x_in[:, width:], sent_b)
    xa = x_ref[:, :width].astype(floating)
    xb = x_ref[:, width:].astype(floating)
    own_a = jnp.where(section == 0, mix[0][0], mix[1][0])
    own_b = jnp.where(section == 0, mix[0][1], mix[1][1])
    active = jnp.where(section == 0, xa, xb) + (own_a * xa + own_b * xb)
    act_ref[...] = active
    nrm_ref[...] = (active * rms_scale(active) * ga_ref[...]).astype(bfloat)
    for weight, target in zip((wq, wk, wv), (q_ref, k_ref, v_ref)):
        target[...] = dot(nrm_ref[...], weight[0]).astype(bfloat)

    def keep_quarters(values, base):
        share = width // 16
        for far in range(4):
            blocks = [values[:, (4 * far + near) * share : (4 * far + near + 1) * share] for near in range(4)]
            for slot, block in enumerate(relative(blocks, quarter)):
                nearby[slot][:, base + far * share : base + (far + 1) * share] = block

    attention(q_ref, k_ref, v_ref, seg_ref, att_ref, p_ref)
    middle = act_ref[...] + dot(att_ref[...], wo[0])
    mid_ref[...] = middle
    nf_ref[...] = (middle * rms_scale(middle) * gf_ref[...]).astype(bfloat)
    if fast:
        keep_quarters(att_ref[...], 0)
        keep_quarters(nrm_ref[...], width // 4)
    else:
        kept[1][...] = nrm_ref[...]
        kept[2][...] = att_ref[...]
    for piece in range(pieces):
        span = slice(piece * chunk, (piece + 1) * chunk)
        gate = dot(nf_ref[...], wg[0, :, span])
        upward = dot(nf_ref[...], wu[0, :, span])
        wave = gelu_wave(gate)
        half = 0.5 * (1.0 + wave)
        value = gate * half
        hidden = (value * upward).astype(bfloat)
        slope = half + 0.5 * gate * (1.0 - wave * wave) * (GELU_A * (1.0 + 3.0 * GELU_B * gate * gate))
        one_ref[piece] = upward * slope
        two_ref[piece] = value
        if fast:
            share = chunk // 4
            blocks = [hidden[:, near * share : (near + 1) * share] for near in range(4)]
            for slot, block in enumerate(relative(blocks, quarter)):
                kept[slot][:, piece * share : (piece + 1) * share] = block
        else:
            kept[0][:, span] = hidden
        down = dot(hidden, wd[0, span, :])
        if piece == 0:
            acc[...] = down
        else:
            acc[...] += down
    change = mid_ref[...] + acc[...] - act_ref[...]
    chg_ref[...] = change
    xa = x_ref[:, :width].astype(floating)
    xb = x_ref[:, width:].astype(floating)
    out_ref[0, :, :width] = (xa + (mix[0][0] * xa + mix[0][1] * xb) + cor[0] * change).astype(bfloat)
    out_ref[0, :, width:] = (xb + (mix[1][0] * xa + mix[1][1] * xb) + cor[1] * change).astype(bfloat)


def forward(fast, x_in, message, segments, mixing, correction, gain_attn, gain_ffn, weights):
    tokens = x_in.shape[0]
    length = segments.shape[1]
    width = gain_attn.shape[1]
    hidden_width = weights[4].shape[2]
    size = sum(weight.size for weight in weights)
    shape = jax.ShapeDtypeStruct
    narrow = ((tokens, width), bfloat)
    wide = ((tokens, width), floating)
    probs = ((tokens // length * (width // PAIR), 2 * length, length), floating)
    if fast:
        kept = [narrow] * 4 + [((tokens, width // 2), bfloat)] * 4 + [narrow]
    else:
        kept = [((tokens, hidden_width), bfloat), narrow, narrow, narrow]
    ffn = ((hidden_width // width, tokens, width), floating)
    outs = [((tokens, 2 * width), bfloat), ((1, tokens, 2 * width), bfloat), narrow, narrow, narrow, probs, wide, wide,
            ffn, ffn, wide] + kept
    return pl.pallas_call(
        lambda *refs: forward_kernel(fast, *refs),
        out_shape=[shape(*one) for one in outs],
        in_specs=[VMEM, VMEM, VMEM, SMEM, SMEM, VMEM, VMEM] + [VMEM] * 7,
        out_specs=[VMEM] * len(outs),
        scratch_shapes=[pltpu.VMEM(*narrow)] * 2 + [pltpu.VMEM(*wide)],
        compiler_params=params(SCOPED),
        cost_estimate=cost(2 * tokens * size, 2 * size),
        name="forward_full",
    )(x_in, message, segments, mixing, correction, gain_attn, gain_ffn, *weights)


def start_rows(message, grad_ref, counts_ref, cor_ref, g_ref, low_ref):
    tokens, width = low_ref.shape
    rows = counts_ref.shape[0]
    length = tokens // rows
    section = lax.axis_index("section")
    if message is not None:
        got = read_scalars(message[tokens : tokens + EXTRA, :PAIR].astype(floating), 4)
    place = lax.broadcasted_iota(jnp.int32, (length, width), 0)
    for row in range(rows):
        span = slice(row * length, (row + 1) * length)
        valid = place < counts_ref[row]
        own_a = jnp.where(valid, grad_ref[span, :width].astype(floating), 0.0)
        own_b = jnp.where(valid, grad_ref[span, width:].astype(floating), 0.0)
        if message is not None:
            later_b = own_b + message[span, :].astype(floating)
            far_a = own_a + (got[0] * own_a + got[2] * later_b)
            far_b = later_b + (got[1] * own_a + got[3] * later_b)
            own_a = jnp.where(section == 0, far_a, own_a).astype(bfloat).astype(floating)
            own_b = jnp.where(section == 0, far_b, own_b).astype(bfloat).astype(floating)
        g_ref[span, :width] = own_a.astype(bfloat)
        g_ref[span, width:] = own_b.astype(bfloat)
        low_ref[span, :] = (cor_ref[0, 0] * own_a + cor_ref[0, 1] * own_b).astype(bfloat)


def start(message, out_grad, counts, correction):
    tokens = out_grad.shape[0]
    width = message.shape[1]
    shape = jax.ShapeDtypeStruct
    return pl.pallas_call(
        start_rows,
        out_shape=[shape((tokens, 2 * width), bfloat), shape((tokens, width), bfloat)],
        in_specs=[VMEM, VMEM, SMEM, SMEM],
        out_specs=[VMEM, VMEM],
        compiler_params=params(SCOPED),
        cost_estimate=cost(tokens * width * 20, tokens * width * 12),
        name="backward_start",
    )(message, out_grad, counts, correction)


def norm_backward(values, gain, grad_normed, with_gain):
    inverse = rms_scale(values)
    grad_gain = jnp.sum(grad_normed * values * inverse, axis=0, keepdims=True) if with_gain else None
    weighted = grad_normed * gain
    grad_values = inverse * weighted - values * inverse**3 * jnp.mean(weighted * values, axis=-1, keepdims=True)
    return grad_gain, grad_values


def ffn_steps(low_ref, one, two, wg, wu, wd, acc, emit):
    width = wd.shape[2]
    quarter = lax.axis_index("dp") & 3
    for step in range(4):
        piece = (3 - step) ^ quarter
        span = pl.ds(pl.multiple_of(piece * width, width), width)
        grad_hidden = dot_t(low_ref[...], wd[0, span, :])
        dgate = (grad_hidden * one[piece]).astype(bfloat)
        dup = (grad_hidden * two[piece]).astype(bfloat)
        emit(3 - step, dgate, dup)
        total = dot_t(dgate, wg[0, :, span]) + dot_t(dup, wu[0, :, span])
        if step == 0:
            acc[...] = total
        else:
            acc[...] += total


def ffn_kernel(g_in, low_ref, cor_ref, gf_ref, mid_ref, one, two, wg, wu, wd, *refs):
    slots = refs[-8:-4]
    dmid_ref, datt_ref, gain_ref, acc = refs[-4:]
    width = gf_ref.shape[1]

    def emit(slot, dgate, dup):
        slots[slot][:, :width] = dgate
        slots[slot][:, width:] = dup

    ffn_steps(low_ref, one, two, wg, wu, wd, acc, emit)
    grad_gain, grad_values = norm_backward(mid_ref[...], gf_ref[...], acc[...], True)
    block = cor_ref[0, 0] * g_in[:, :width].astype(floating) + cor_ref[0, 1] * g_in[:, width:].astype(floating)
    grad_middle = block + grad_values
    dmid_ref[...] = grad_middle
    datt_ref[...] = grad_middle.astype(bfloat)
    gain_ref[...] = grad_gain


def ffn_backward(g_in, low, correction, gain_ffn, middle, one, two, before, weights):
    tokens = g_in.shape[0]
    width = gain_ffn.shape[1]
    shape = jax.ShapeDtypeStruct
    return pl.pallas_call(
        ffn_kernel,
        out_shape=[shape((tokens, 2 * width), bfloat)] * 4
        + [shape((tokens, width), floating), shape((tokens, width), bfloat), shape((1, width), floating)],
        in_specs=[VMEM, VMEM, SMEM] + [VMEM] * 7 + [ANY] * len(before),
        out_specs=[VMEM] * 7,
        scratch_shapes=[pltpu.VMEM((tokens, width), floating)],
        compiler_params=params(SCOPED),
        cost_estimate=cost(2 * tokens * 3 * weights[4].size, 2 * 3 * weights[4].size),
        name="backward_ffn",
    )(g_in, low, correction, gain_ffn, middle, one, two, *weights[4:], *before)


def attn_steps(q_ref, k_ref, v_ref, p_ref, do_ref, dqkv_ref, base):
    tokens, width = do_ref.shape
    length = p_ref.shape[2]
    rows = tokens // length
    pairs = width // PAIR
    first = lane_mask(length)
    for row in range(rows):
        span = slice(row * length, (row + 1) * length)
        for pair in range(pairs):
            heads = slice(pair * PAIR, (pair + 1) * PAIR)
            probs = p_ref[row * pairs + pair]
            grad_out = stack_heads(do_ref[span, heads], first)
            grad_value = t_dot(probs.astype(bfloat), grad_out)
            grad_probs = dot_t(grad_out, v_ref[span, heads])
            carried = jnp.sum(probs * grad_probs, axis=-1, keepdims=True)
            grad_scores = (probs * (grad_probs - carried)).astype(bfloat)
            grad_query = dot(grad_scores, k_ref[span, heads])
            grad_query = jnp.where(first, grad_query[:length], grad_query[length:])
            grad_key = t_dot(grad_scores, stack_heads(q_ref[span, heads], first))
            at = base + pair * PAIR
            dqkv_ref[span, at : at + PAIR] = (grad_query * SCALE).astype(bfloat)
            dqkv_ref[span, at + width : at + width + PAIR] = (grad_key * SCALE).astype(bfloat)
            dqkv_ref[span, at + 2 * width : at + 2 * width + PAIR] = grad_value.astype(bfloat)


def normed_grad(dqkv_ref, base, width, wq, wk, wv):
    return (
        dot_t(dqkv_ref[:, base : base + width], wq[0])
        + dot_t(dqkv_ref[:, base + width : base + 2 * width], wk[0])
        + dot_t(dqkv_ref[:, base + 2 * width : base + 3 * width], wv[0])
    )


def attn_kernel(datt_ref, q_ref, k_ref, v_ref, p_ref, gfg_ref, ga_ref, x_ref, g_in, dmid_ref, act_ref, chg_ref, mix_ref, cor_ref,
                wq, wk, wv, wo, before,
                grad_ref, right_ref, small_ref, do_ref):
    tokens, width = datt_ref.shape
    right_ref[:, :width] = datt_ref[...]
    do_ref[...] = dot_t(datt_ref[...], wo[0]).astype(bfloat)
    attn_steps(q_ref, k_ref, v_ref, p_ref, do_ref, right_ref, width)
    grad_normed = normed_grad(right_ref, width, width, wq, wk, wv)
    grad_gain, grad_values = norm_backward(act_ref[...], ga_ref[...], grad_normed, True)
    section = lax.axis_index("section")
    mix = [[mix_ref[0, i, j] for j in range(2)] for i in range(2)]
    cor = [cor_ref[0, i] for i in range(2)]
    out_a = g_in[:, :width].astype(floating)
    out_b = g_in[:, width:].astype(floating)
    grad_active = dmid_ref[...] + grad_values - (cor[0] * out_a + cor[1] * out_b)
    pred_a = out_a + jnp.where(section == 0, grad_active, 0.0)
    pred_b = out_b + jnp.where(section == 0, 0.0, grad_active)
    grad_ref[0, :, :width] = (pred_a + (mix[0][0] * pred_a + mix[1][0] * pred_b)).astype(bfloat)
    grad_ref[0, :, width:] = (pred_b + (mix[0][1] * pred_a + mix[1][1] * pred_b)).astype(bfloat)
    xa = x_ref[:, :width].astype(floating)
    xb = x_ref[:, width:].astype(floating)
    small_ref[0:1, :] = grad_gain
    small_ref[1:2, :] = gfg_ref[...]
    place = 2
    for pred in (pred_a, pred_b):
        for state in (xa, xb):
            small_ref[place : place + 1, :] = jnp.sum(pred * state, axis=0, keepdims=True)
            place += 1
    for out in (out_a, out_b):
        small_ref[place : place + 1, :] = jnp.sum(out * chg_ref[...], axis=0, keepdims=True)
        place += 1


def attn_backward(x, g_in, grad_middle, grad_att, active, change, queries, key_rows, value_rows, probs, ffn_gain, gain_attn,
                  mixing, correction, before, weights):
    tokens, width = active.shape
    shape = jax.ShapeDtypeStruct
    return pl.pallas_call(
        attn_kernel,
        out_shape=[shape((1, tokens, 2 * width), bfloat), shape((tokens, 4 * width), bfloat), shape((8, width), floating)],
        in_specs=[VMEM] * 12 + [SMEM] * 2 + [VMEM] * 4 + [ANY],
        out_specs=[VMEM] * 3,
        scratch_shapes=[pltpu.VMEM((tokens, width), bfloat)],
        compiler_params=params(SCOPED),
        cost_estimate=cost(2 * tokens * 5 * weights[0].size, 2 * 4 * weights[0].size),
        name="backward_attn",
    )(grad_att, queries, key_rows, value_rows, probs, ffn_gain, gain_attn, x, g_in, grad_middle, active, change,
      mixing, correction, *weights[:4], before)


def relay_kernel(grad_in, counts_ref, cor_ref, mix_ref, gf_ref, ga_ref, one, two, mid_ref, q_ref, k_ref, v_ref, p_ref, act_ref,
                 wq, wk, wv, wo, wg, wu, wd,
                 msg_ref,
                 acc, g_in, low_ref, do_ref, dqkv_ref):
    tokens, width = low_ref.shape
    start_rows(None, grad_in, counts_ref, cor_ref, g_in, low_ref)
    ffn_steps(low_ref, one, two, wg, wu, wd, acc, lambda *parts: None)
    grad_values = norm_backward(mid_ref[...], gf_ref[...], acc[...], False)[1]
    cor = [cor_ref[0, i] for i in range(2)]
    block = cor[0] * g_in[:, :width].astype(floating) + cor[1] * g_in[:, width:].astype(floating)
    acc[...] = block + grad_values
    do_ref[...] = dot_t(acc[...].astype(bfloat), wo[0]).astype(bfloat)
    attn_steps(q_ref, k_ref, v_ref, p_ref, do_ref, dqkv_ref, 0)
    grad_normed = normed_grad(dqkv_ref, 0, width, wq, wk, wv)
    grad_values = norm_backward(act_ref[...], ga_ref[...], grad_normed, False)[1]
    block = cor[0] * g_in[:, :width].astype(floating) + cor[1] * g_in[:, width:].astype(floating)
    msg_ref[:tokens, :] = (acc[...] + grad_values - block).astype(bfloat)
    mix = [[mix_ref[0, i, j] for j in range(2)] for i in range(2)]
    msg_ref[tokens:, :] = scalar_rows(mix[0] + mix[1], EXTRA, width)


def relay_backward(out_grad, counts, correction, mixing, gain_ffn, gain_attn, one, two, middle, queries, key_rows, value_rows,
                   probs, active, weights):
    tokens, width = active.shape
    shape = jax.ShapeDtypeStruct
    narrow = pltpu.VMEM((tokens, width), bfloat)
    wide = pltpu.VMEM((tokens, width), floating)
    size = sum(weight.size for weight in weights)
    return pl.pallas_call(
        relay_kernel,
        out_shape=shape((tokens + EXTRA, width), bfloat),
        in_specs=[VMEM, SMEM, SMEM, SMEM] + [VMEM] * 17,
        out_specs=VMEM,
        scratch_shapes=[wide, pltpu.VMEM((tokens, 2 * width), bfloat), narrow, narrow, pltpu.VMEM((tokens, 3 * width), bfloat)],
        compiler_params=params(SCOPED),
        cost_estimate=cost(2 * tokens * size, 2 * size),
        name="backward_relay",
    )(out_grad, counts, correction, mixing, gain_ffn, gain_attn, one, two, middle, queries, key_rows, value_rows, probs, active,
      *weights)


def quarter_kernel(first, products, block, refs):
    count = 4
    lefts = refs[:count]
    rights = refs[count : 2 * count]
    send_ref, keep_ref = refs[-2:]
    index = lax.axis_index("dp")
    near = (index >> 2) & 1
    far = (index >> 3) & 1
    for left_at, left_wide, right_at, right_wide in products:
        columns = slice(first + left_at, first + left_at + left_wide)
        span = slice(right_at, right_at + right_wide)
        total = sum(t_dot(left[:, columns], right[:, span]) for left, right in zip(lefts, rights))
        for place in range(4):
            part = total[place * block : (place + 1) * block, :]
            slot = (place >> 1) ^ far
            mine = (place & 1) == near

            @pl.when(mine)
            def _():
                keep_ref[slot, :, span] = part

            @pl.when(jnp.logical_not(mine))
            def _():
                send_ref[slot, :, span] = part.astype(bfloat)


def quarter_product(lefts, first, rights, products, block, before, name):
    tokens = lefts[0].shape[0]
    right_wide = rights[0].shape[1]
    shape = jax.ShapeDtypeStruct
    flops = sum(2 * 4 * tokens * one[1] * one[3] for one in products)
    return pl.pallas_call(
        lambda *refs: quarter_kernel(first, products, block, refs),
        out_shape=[shape((2, block, right_wide), bfloat), shape((2, block, right_wide), floating)],
        in_specs=[VMEM] * 8 + [ANY] * len(before),
        out_specs=[VMEM, VMEM],
        compiler_params=params(SCOPED),
        cost_estimate=cost(flops, 8 * tokens * right_wide),
        name=name,
    )(*lefts, *rights, *before)


def assemble_kernel(own, one, two, three, gate_ref, up_ref):
    quarter = lax.axis_index("dp") & 3
    width = own.shape[1] // 2
    for slot, piece in enumerate((own, one, two, three)):
        span = pl.ds(pl.multiple_of((slot ^ quarter) * width, width), width)
        gate_ref[0, :, span] = piece[:, :width].astype(floating)
        up_ref[0, :, span] = piece[:, width:].astype(floating)


def assemble(pieces):
    share, double = pieces[0].shape
    shape = jax.ShapeDtypeStruct((1, share, 2 * double), floating)
    return pl.pallas_call(
        assemble_kernel,
        out_shape=[shape, shape],
        in_specs=[VMEM] * 4,
        out_specs=[VMEM] * 2,
        compiler_params=params(SCOPED),
        cost_estimate=cost(share * double * 4, share * double * 24),
        name="assemble",
    )(*pieces)


def exchange(value, flips):
    count = lax.axis_size("dp")
    return lax.ppermute(value, "dp", [(source, source ^ flips) for source in range(count)])


def relative_rows(matrix, order, index):
    bits = len(order)
    block = matrix.shape[0] >> bits
    split = matrix.reshape((2,) * bits + (block, matrix.shape[1]))
    axes = [bits - 1 - bit for bit in order]
    split = jnp.transpose(split, axes + [bits, bits + 1])
    for axis, bit in enumerate(order):
        split = jnp.where((index >> bit) & 1 == 1, jnp.flip(split, axis), split)
    return split.reshape(matrix.shape)


def scatter_sum(left, right, order):
    total = left.shape[0]
    arrived = []
    for step in range(len(order) + 1):
        low = total >> (step + 1) if step < len(order) else 0
        high = total >> step
        part = dot(left[low:high], right)
        for other in arrived:
            part = part + other[low:high].astype(floating)
        if step == len(order):
            return part
        arrived.append(exchange(part.astype(bfloat), 1 << order[step]))


def halving_grads(kept, low, slots, right, index, count):
    width = low.shape[1]
    order = list(range(count.bit_length() - 1))
    hidden, normed, attended, normed_ffn = (relative_rows(one.T, order, index) for one in kept)
    quarter = index & 3
    places = jnp.arange(4) ^ quarter
    ordered = jnp.stack(slots)[places]
    dgate = jnp.concatenate([one[:, :width] for one in ordered], axis=1)
    dup = jnp.concatenate([one[:, width:] for one in ordered], axis=1)
    grad_down = scatter_sum(hidden, low, order)
    grad_gate = scatter_sum(normed_ffn, dgate, order)
    grad_up = scatter_sum(normed_ffn, dup, order)
    grad_out = scatter_sum(attended, right[:, :width], order)
    grad_qkv = scatter_sum(normed, right[:, width:], order)
    return grad_down[None], grad_gate[None], grad_up[None], grad_out[None], grad_qkv[None]


def after(values, *earlier):
    return lax.optimization_barrier((values, earlier))[0]


def gather_start(value):
    return [value, exchange(value, 1), exchange(value, 2)]


def gather_end(pieces, earlier):
    return pieces + [exchange(after(pieces[2], earlier), 1)]


def swapped(pieces):
    return [pieces[0]] + [exchange(pieces[flips], flips) for flips in (1, 2, 3)]


def sum_once(pair):
    send, keep = pair
    arrived = exchange(send, 4)
    return keep[0] + arrived[0].astype(floating), (keep[1] + arrived[1].astype(floating)).astype(bfloat)


def sum_twice(held, passed):
    return held + exchange(passed, 8).astype(floating)


def quarter_grads(normed_ffn, nearby, slots, right, down_pair, index):
    width = normed_ffn[0].shape[1]
    share = width // 16
    block = 4 * share
    ffns = swapped(slots)
    down_sums = sum_once(down_pair)
    ffn_products = [(0, width, 0, 2 * width)]
    ffn_pair = quarter_product(normed_ffn, 0, ffns, ffn_products, block, [right, down_sums[1]], "product_ffn")
    right, nearby = after((right, nearby), ffn_pair[0])
    rights = gather_end(gather_start(right), ffn_pair[0])
    nearby = swapped(list(nearby))
    grad_down = sum_twice(*down_sums)
    ffn_sums = sum_once(ffn_pair)
    attn_products = [(0, block, 0, width), (block, block, width, 3 * width)]
    attn_pair = quarter_product(nearby, 0, rights, attn_products, share, [grad_down, ffn_sums[1]], "product_attn")
    tile = sum_twice(*ffn_sums).astype(bfloat)
    quarter = index & 3
    pieces = [lax.dynamic_slice_in_dim(tile, (slot ^ quarter) * share, share, axis=0) for slot in range(4)]
    grad_gate, grad_up = assemble(swapped(pieces))
    total = sum_twice(*sum_once(attn_pair))
    return grad_down[None], grad_gate, grad_up, total[None, :, :width], total[None, :, width:], attn_pair[0]


def local(states_in, out_grad, counts, segments, mixing, correction, gain_attn, w_query, w_key, w_value, w_attn_out, gain_ffn,
          w_gate, w_up, w_down):
    weights = (w_query, w_key, w_value, w_attn_out, w_gate, w_up, w_down)
    width = gain_attn.shape[1]
    index = lax.axis_index("dp")
    count = lax.axis_size("dp")
    fast = count == 16
    message, *weights = forward_lite(states_in, segments, mixing, correction, gain_attn, gain_ffn, weights)
    message = lax.ppermute(message, "section", [(0, 1), (1, 0)])
    (x, states, queries, key_rows, value_rows, probs, active, middle, one, two, change, *kept) = forward(
        fast, states_in, message, segments, mixing, correction, gain_attn, gain_ffn, weights)
    if fast:
        hidden, nearby, normed_ffn = kept[:4], kept[4:8], gather_start(kept[8])
    message = relay_backward(out_grad, counts, correction, mixing, gain_ffn, gain_attn, one, two, middle, queries, key_rows,
                             value_rows, probs, active, weights)
    if fast:
        message, hidden, normed_ffn = after((message, hidden, normed_ffn), message)
        hidden = swapped(list(hidden))
        normed_ffn = gather_end(list(normed_ffn), message)
    message = lax.ppermute(message, "section", [(0, 1), (1, 0)])
    g_in, low = start(message, out_grad, counts, correction)
    before = []
    if fast:
        lows = gather_start(low)
        before = hidden[1:] + normed_ffn[3:]
    *slots, grad_middle, grad_att, ffn_gain = ffn_backward(g_in, low, correction, gain_ffn, middle, one, two, before, weights)
    before = slots[0]
    if fast:
        lows = gather_end(lows, before)
        down_pair = quarter_product(hidden, 0, lows, [(0, width, 0, width)], width // 4, [before], "product_down")
        before = down_pair[0]
    state_grads, right, small = attn_backward(x, g_in, grad_middle, grad_att, active, change, queries, key_rows, value_rows, probs,
                                              ffn_gain, gain_attn, mixing, correction, before, weights)
    if fast:
        grad_down, grad_gate, grad_up, grad_out, grad_qkv, last = quarter_grads(normed_ffn, nearby, slots, right, down_pair, index)
        small = after(small, last)
    else:
        grad_down, grad_gate, grad_up, grad_out, grad_qkv = halving_grads(kept, low, slots, right, index, count)
    for bit in range(count.bit_length() - 1):
        small = small + exchange(small, 1 << bit)
    share = width // count
    gains = lax.dynamic_slice(small, (0, index * share), (2, share))
    sums = jnp.sum(small[2:], axis=1)
    return (
        states,
        state_grads,
        sums[:4].reshape(1, 2, 2),
        sums[4:].reshape(1, 2),
        gains[0:1],
        grad_qkv[:, :, :width],
        grad_qkv[:, :, width : 2 * width],
        grad_qkv[:, :, 2 * width :],
        grad_out,
        gains[1:2],
        grad_gate,
        grad_up,
        grad_down,
    )


def solution(mesh):
    rows = P("dp", None)
    matrix = P("section", None, None)
    vector = P("section", None)
    share = P("section", "dp", None)
    gain_share = P("section", "dp")
    in_specs = (rows, rows, P("dp"), rows, matrix, vector, vector, matrix, matrix, matrix, matrix, vector, matrix, matrix, matrix)
    out_specs = (share, share, matrix, vector, gain_share, share, share, share, share, gain_share, share, share, share)
    return jax.shard_map(local, mesh=mesh, in_specs=in_specs, out_specs=out_specs, check_vma=False)
```

```python
import functools

import jax
import jax.numpy as jnp
from jax import lax
from jax.experimental import pallas as pl
from jax.experimental.pallas import tpu as pltpu
from jax.sharding import PartitionSpec as P

HEAD_DIM = 64
PAIR = 2 * HEAD_DIM
EPSILON = 1e-06
MASKED = -1e30
SCALE = HEAD_DIM ** (-0.5)
GELU_A = 0.7978845608028654
GELU_B = 0.044715
EXTRA = 16
AHEAD = 3
SCOPED = 12
bfloat = jnp.bfloat16
floating = jnp.float32

VMEM = pl.BlockSpec(memory_space=pltpu.VMEM)
SMEM = pl.BlockSpec(memory_space=pltpu.SMEM)
ANY = pl.BlockSpec(memory_space=pltpu.MemorySpace.HBM)


def dot(a, b):
    return jnp.dot(a, b, preferred_element_type=floating)


def dot_t(a, b):
    return lax.dot_general(a, b, (((1,), (1,)), ((), ())), preferred_element_type=floating)


def t_dot(a, b):
    return lax.dot_general(a, b, (((0,), (0,)), ((), ())), preferred_element_type=floating)


def params(mebibytes):
    return pltpu.CompilerParams(vmem_limit_bytes=mebibytes * 1024 * 1024)


def cost(flops, moved):
    return pl.CostEstimate(flops=flops // 1000, bytes_accessed=moved // 1000, transcendentals=0)


def scalar_rows(values, rows, width):
    lane = lax.broadcasted_iota(jnp.int32, (rows, width), 1)
    row = lax.broadcasted_iota(jnp.int32, (rows, width), 0)
    whole = jnp.zeros((rows, width), floating)
    for place, value in enumerate(values):
        whole = jnp.where(lane == place, value, whole)
    high = whole.astype(bfloat).astype(floating)
    middle = (whole - high).astype(bfloat).astype(floating)
    low = whole - high - middle
    part = jnp.where(row == 0, high, jnp.where(row == 1, middle, jnp.where(row == 2, low, 0.0)))
    return part.astype(bfloat)


def read_scalars(block, count):
    lane = lax.broadcasted_iota(jnp.int32, block.shape, 1)
    return [jnp.sum(jnp.where(lane == place, block, 0.0)) for place in range(count)]


def rms_scale(values):
    return lax.rsqrt(jnp.mean(values * values, axis=-1, keepdims=True) + EPSILON)


def lane_mask(length):
    return lax.broadcasted_iota(jnp.int32, (length, PAIR), 1) < HEAD_DIM


def stack_heads(block, first):
    zero = jnp.zeros_like(block)
    return jnp.concatenate([jnp.where(first, block, zero), jnp.where(first, zero, block)], axis=0)


def gelu_wave(gate):
    return jnp.tanh(GELU_A * (gate + GELU_B * gate * gate * gate))


def relative(blocks, index):
    low = (index & 1) == 1
    high = (index >> 1) == 1
    once = [jnp.where(low, blocks[place ^ 1], blocks[place]) for place in range(4)]
    return [jnp.where(high, once[place ^ 2], once[place]) for place in range(4)]


def attention(q_ref, k_ref, v_ref, seg_ref, att_ref, p_ref):
    length = seg_ref.shape[1]
    rows = q_ref.shape[0] // length
    pairs = q_ref.shape[1] // PAIR
    first = lane_mask(length)
    later = lax.broadcasted_iota(jnp.int32, (length, length), 0)
    earlier = lax.broadcasted_iota(jnp.int32, (length, length), 1)
    for row in range(rows):
        documents = jnp.broadcast_to(seg_ref[row : row + 1, :], (length, length)).astype(floating)
        allowed = (earlier <= later) & (documents == documents.T)
        allowed = jnp.concatenate([allowed, allowed], axis=0)
        span = slice(row * length, (row + 1) * length)
        for pair in range(pairs):
            heads = slice(pair * PAIR, (pair + 1) * PAIR)
            stacked = stack_heads(q_ref[span, heads], first)
            scores = jnp.where(allowed, dot_t(stacked, k_ref[span, heads]) * SCALE, MASKED)
            powers = jnp.exp(scores - jnp.max(scores, axis=-1, keepdims=True))
            probs = powers / jnp.sum(powers, axis=-1, keepdims=True)
            if p_ref is not None:
                p_ref[row * pairs + pair] = probs
            mixed = dot(probs.astype(bfloat), v_ref[span, heads])
            att_ref[span, heads] = jnp.where(first, mixed[:length], mixed[length:]).astype(bfloat)


def in_hbm(value):
    return pltpu.with_memory_space_constraint(value, pltpu.MemorySpace.HBM)


def forward_lite_kernel(x_any, seg_any, mix_any, cor_any, ga_any, gf_any, wq, wk, wv, wo, wg, wu, wd,
                        out_ref, wq_s, wk_s, wv_s, wo_s, wg_s, wu_s, wd_s,
                        x_in, seg_ref, mix_ref, cor_ref, ga_ref, gf_ref, q_ref, k_ref, v_ref, act_ref,
                        nrm_ref, att_ref, nf_ref, acc, sem, small_sem):
    tokens, width = act_ref.shape
    chunk = width
    pieces = wg.shape[2] // chunk
    small = [
        pltpu.make_async_copy(source, target, small_sem.at[place])
        for place, (source, target) in enumerate(
            ((x_any, x_in), (mix_any, mix_ref), (ga_any, ga_ref), (seg_any, seg_ref), (gf_any, gf_ref), (cor_any, cor_ref))
        )
    ]
    pairs = [(wq, wq_s), (wk, wk_s), (wv, wv_s), (wo, wo_s)]
    for piece in range(pieces):
        span = pl.ds(piece * chunk, chunk)
        pairs += [
            (wg.at[:, :, span], wg_s.at[:, :, span]), (wu.at[:, :, span], wu_s.at[:, :, span]), (wd.at[:, span, :], wd_s.at[:, span, :])
        ]
    queue = [pltpu.make_async_copy(source, target, sem.at[place]) for place, (source, target) in enumerate(pairs)]
    for copy in small + queue[:AHEAD]:
        copy.start()
    state = [0]

    def arrive():
        queue[state[0]].wait()
        if state[0] + AHEAD < len(queue):
            queue[state[0] + AHEAD].start()
        state[0] += 1

    for copy in small:
        copy.wait()
    section = lax.axis_index("section")
    mix = [[mix_ref[0, i, j] for j in range(2)] for i in range(2)]
    cor = [cor_ref[0, i] for i in range(2)]
    xa = x_in[:, :width].astype(floating)
    xb = x_in[:, width:].astype(floating)
    own_a = jnp.where(section == 0, mix[0][0], mix[1][0])
    own_b = jnp.where(section == 0, mix[0][1], mix[1][1])
    active = jnp.where(section == 0, xa, xb) + (own_a * xa + own_b * xb)
    act_ref[...] = active
    nrm_ref[...] = (active * rms_scale(active) * ga_ref[...]).astype(bfloat)
    for weight, target in zip((wq_s, wk_s, wv_s), (q_ref, k_ref, v_ref)):
        arrive()
        target[...] = dot(nrm_ref[...], weight[0]).astype(bfloat)
    attention(q_ref, k_ref, v_ref, seg_ref, att_ref, None)
    arrive()
    middle = act_ref[...] + dot(att_ref[...], wo_s[0])
    acc[...] = middle - act_ref[...]
    nf_ref[...] = (middle * rms_scale(middle) * gf_ref[...]).astype(bfloat)
    for piece in range(pieces):
        span = slice(piece * chunk, (piece + 1) * chunk)
        arrive()
        gate = dot(nf_ref[...], wg_s[0, :, span])
        arrive()
        upward = dot(nf_ref[...], wu_s[0, :, span])
        hidden = (0.5 * gate * (1.0 + gelu_wave(gate)) * upward).astype(bfloat)
        arrive()
        acc[...] += dot(hidden, wd_s[0, span, :])
    out_ref[:tokens, :] = acc[...].astype(bfloat)
    out_ref[tokens:, :] = scalar_rows(mix[0] + mix[1] + cor, EXTRA, width)


def forward_lite(x_in, segments, mixing, correction, gain_attn, gain_ffn, weights):
    tokens = x_in.shape[0]
    width = gain_attn.shape[1]
    size = sum(weight.size for weight in weights)
    narrow = pltpu.VMEM((tokens, width), bfloat)
    wide = pltpu.VMEM((tokens, width), floating)
    args = (x_in, segments, mixing, correction, gain_attn, gain_ffn) + weights
    scratch = [
        pltpu.VMEM(x_in.shape, bfloat), pltpu.VMEM(segments.shape, jnp.int32), pltpu.SMEM(mixing.shape, floating),
        pltpu.SMEM(correction.shape, floating), pltpu.VMEM(gain_attn.shape, floating), pltpu.VMEM(gain_ffn.shape, floating),
        narrow, narrow, narrow, wide, narrow, narrow, narrow, wide,
    ]
    scratch += [pltpu.SemaphoreType.DMA((4 + 3 * (weights[4].shape[2] // width),)), pltpu.SemaphoreType.DMA((6,))]
    return pl.pallas_call(
        forward_lite_kernel,
        out_shape=[jax.ShapeDtypeStruct((tokens + EXTRA, width), bfloat)]
        + [jax.ShapeDtypeStruct(weight.shape, bfloat) for weight in weights],
        in_specs=[ANY] * len(args),
        out_specs=[VMEM] * 8,
        scratch_shapes=scratch,
        compiler_params=params(SCOPED),
        cost_estimate=cost(2 * tokens * size, 2 * size),
        name="forward_lite",
    )(*[in_hbm(one) for one in args])


def forward_kernel(fast, x_in, message, seg_ref, mix_ref, cor_ref, ga_ref, gf_ref, wq, wk, wv, wo, wg, wu, wd,
                   x_ref, out_ref, q_ref, k_ref, v_ref, p_ref, act_ref, mid_ref, one_ref, two_ref, chg_ref, *refs):
    kept = refs[:4]
    nf_ref = refs[-4]
    nrm_ref, att_ref, acc = refs[-3:]
    tokens, width = act_ref.shape
    chunk = width
    pieces = wg.shape[2] // chunk
    section = lax.axis_index("section")
    quarter = lax.axis_index("dp") & 3
    mix = [[mix_ref[0, i, j] for j in range(2)] for i in range(2)]
    cor = [cor_ref[0, i] for i in range(2)]
    xa = x_in[:, :width].astype(floating)
    xb = x_in[:, width:].astype(floating)
    got = read_scalars(message[tokens : tokens + EXTRA, :PAIR].astype(floating), 6)
    moved = message[:tokens, :].astype(floating)
    sent_a = (xa + (got[0] * xa + got[1] * xb) + got[4] * moved).astype(bfloat)
    sent_b = (xb + (got[2] * xa + got[3] * xb) + got[5] * moved).astype(bfloat)
    x_ref[:, :width] = jnp.where(section == 0, x_in[:, :width], sent_a)
    x_ref[:, width:] = jnp.where(section == 0, x_in[:, width:], sent_b)
    xa = x_ref[:, :width].astype(floating)
    xb = x_ref[:, width:].astype(floating)
    own_a = jnp.where(section == 0, mix[0][0], mix[1][0])
    own_b = jnp.where(section == 0, mix[0][1], mix[1][1])
    active = jnp.where(section == 0, xa, xb) + (own_a * xa + own_b * xb)
    act_ref[...] = active
    nrm_ref[...] = (active * rms_scale(active) * ga_ref[...]).astype(bfloat)
    for weight, target in zip((wq, wk, wv), (q_ref, k_ref, v_ref)):
        target[...] = dot(nrm_ref[...], weight[0]).astype(bfloat)

    def keep_quarters(values, base):
        share = width // 16
        for far in range(4):
            blocks = [values[:, (4 * far + near) * share : (4 * far + near + 1) * share] for near in range(4)]
            for slot, block in enumerate(relative(blocks, quarter)):
                kept[slot][:, base + far * share : base + (far + 1) * share] = block

    attention(q_ref, k_ref, v_ref, seg_ref, att_ref, p_ref)
    middle = act_ref[...] + dot(att_ref[...], wo[0])
    mid_ref[...] = middle
    nf_ref[...] = (middle * rms_scale(middle) * gf_ref[...]).astype(bfloat)
    if fast:
        keep_quarters(att_ref[...], width)
        keep_quarters(nrm_ref[...], width + width // 4)
        for slot in (1, 2):
            kept[slot][:, width + width // 2 :] = nf_ref[...]
    else:
        kept[1][...] = nrm_ref[...]
        kept[2][...] = att_ref[...]
    for piece in range(pieces):
        span = slice(piece * chunk, (piece + 1) * chunk)
        gate = dot(nf_ref[...], wg[0, :, span])
        upward = dot(nf_ref[...], wu[0, :, span])
        wave = gelu_wave(gate)
        half = 0.5 * (1.0 + wave)
        value = gate * half
        hidden = (value * upward).astype(bfloat)
        slope = half + 0.5 * gate * (1.0 - wave * wave) * (GELU_A * (1.0 + 3.0 * GELU_B * gate * gate))
        one_ref[piece] = upward * slope
        two_ref[piece] = value
        if fast:
            share = chunk // 4
            blocks = [hidden[:, near * share : (near + 1) * share] for near in range(4)]
            for slot, block in enumerate(relative(blocks, quarter)):
                kept[slot][:, piece * share : (piece + 1) * share] = block
        else:
            kept[0][:, span] = hidden
        down = dot(hidden, wd[0, span, :])
        if piece == 0:
            acc[...] = down
        else:
            acc[...] += down
    change = mid_ref[...] + acc[...] - act_ref[...]
    chg_ref[...] = change
    xa = x_ref[:, :width].astype(floating)
    xb = x_ref[:, width:].astype(floating)
    out_ref[0, :, :width] = (xa + (mix[0][0] * xa + mix[0][1] * xb) + cor[0] * change).astype(bfloat)
    out_ref[0, :, width:] = (xb + (mix[1][0] * xa + mix[1][1] * xb) + cor[1] * change).astype(bfloat)


def forward(fast, x_in, message, segments, mixing, correction, gain_attn, gain_ffn, weights):
    tokens = x_in.shape[0]
    length = segments.shape[1]
    width = gain_attn.shape[1]
    hidden_width = weights[4].shape[2]
    size = sum(weight.size for weight in weights)
    shape = jax.ShapeDtypeStruct
    narrow = ((tokens, width), bfloat)
    wide = ((tokens, width), floating)
    probs = ((tokens // length * (width // PAIR), 2 * length, length), floating)
    if fast:
        short, long = (((tokens, columns), bfloat) for columns in (width + width // 2, 2 * width + width // 2))
        kept = [short, long, long, short, narrow]
    else:
        kept = [((tokens, hidden_width), bfloat), narrow, narrow, narrow]
    ffn = ((hidden_width // width, tokens, width), floating)
    outs = [((tokens, 2 * width), bfloat), ((1, tokens, 2 * width), bfloat), narrow, narrow, narrow, probs, wide, wide,
            ffn, ffn, wide] + kept
    return pl.pallas_call(
        lambda *refs: forward_kernel(fast, *refs),
        out_shape=[shape(*one) for one in outs],
        in_specs=[VMEM, VMEM, VMEM, SMEM, SMEM, VMEM, VMEM] + [VMEM] * 7,
        out_specs=[VMEM] * len(outs),
        scratch_shapes=[pltpu.VMEM(*narrow)] * 2 + [pltpu.VMEM(*wide)],
        compiler_params=params(SCOPED),
        cost_estimate=cost(2 * tokens * size, 2 * size),
        name="forward_full",
    )(x_in, message, segments, mixing, correction, gain_attn, gain_ffn, *weights)


def start_rows(message, grad_ref, counts_ref, cor_ref, g_ref, low_ref):
    tokens, width = low_ref.shape
    rows = counts_ref.shape[0]
    length = tokens // rows
    section = lax.axis_index("section")
    if message is not None:
        got = read_scalars(message[tokens : tokens + EXTRA, :PAIR].astype(floating), 4)
    place = lax.broadcasted_iota(jnp.int32, (length, width), 0)
    for row in range(rows):
        span = slice(row * length, (row + 1) * length)
        valid = place < counts_ref[row]
        own_a = jnp.where(valid, grad_ref[span, :width].astype(floating), 0.0)
        own_b = jnp.where(valid, grad_ref[span, width:].astype(floating), 0.0)
        if message is not None:
            later_b = own_b + message[span, :].astype(floating)
            far_a = own_a + (got[0] * own_a + got[2] * later_b)
            far_b = later_b + (got[1] * own_a + got[3] * later_b)
            own_a = jnp.where(section == 0, far_a, own_a).astype(bfloat).astype(floating)
            own_b = jnp.where(section == 0, far_b, own_b).astype(bfloat).astype(floating)
        g_ref[span, :width] = own_a.astype(bfloat)
        g_ref[span, width:] = own_b.astype(bfloat)
        low_ref[span, :] = (cor_ref[0, 0] * own_a + cor_ref[0, 1] * own_b).astype(bfloat)


def start(message, out_grad, counts, correction, before):
    tokens = out_grad.shape[0]
    width = message.shape[1]
    shape = jax.ShapeDtypeStruct
    return pl.pallas_call(
        lambda *refs: start_rows(*refs[:4], *refs[-2:]),
        out_shape=[shape((tokens, 2 * width), bfloat), shape((tokens, width), bfloat)],
        in_specs=[VMEM, VMEM, SMEM, SMEM] + [ANY] * len(before),
        out_specs=[VMEM, VMEM],
        compiler_params=params(SCOPED),
        cost_estimate=cost(tokens * width * 20, tokens * width * 12),
        name="backward_start",
    )(message, out_grad, counts, correction, *before)


def norm_backward(values, gain, grad_normed, with_gain):
    inverse = rms_scale(values)
    grad_gain = jnp.sum(grad_normed * values * inverse, axis=0, keepdims=True) if with_gain else None
    weighted = grad_normed * gain
    grad_values = inverse * weighted - values * inverse**3 * jnp.mean(weighted * values, axis=-1, keepdims=True)
    return grad_gain, grad_values


def ffn_steps(low_ref, one, two, wg, wu, wd, acc, emit):
    width = wd.shape[2]
    quarter = lax.axis_index("dp") & 3
    for step in range(4):
        piece = (3 - step) ^ quarter
        span = pl.ds(pl.multiple_of(piece * width, width), width)
        grad_hidden = dot_t(low_ref[...], wd[0, span, :])
        dgate = (grad_hidden * one[piece]).astype(bfloat)
        dup = (grad_hidden * two[piece]).astype(bfloat)
        emit(3 - step, dgate, dup)
        total = dot_t(dgate, wg[0, :, span]) + dot_t(dup, wu[0, :, span])
        if step == 0:
            acc[...] = total
        else:
            acc[...] += total


def ffn_kernel(g_in, low_ref, cor_ref, gf_ref, mid_ref, one, two, wg, wu, wd, *refs):
    slots = refs[-12:-4]
    dmid_ref, datt_ref, gain_ref, acc = refs[-4:]
    width = gf_ref.shape[1]

    def emit(slot, dgate, dup):
        slots[slot][...] = dgate
        slots[4 + slot][...] = dup

    ffn_steps(low_ref, one, two, wg, wu, wd, acc, emit)
    grad_gain, grad_values = norm_backward(mid_ref[...], gf_ref[...], acc[...], True)
    block = cor_ref[0, 0] * g_in[:, :width].astype(floating) + cor_ref[0, 1] * g_in[:, width:].astype(floating)
    grad_middle = block + grad_values
    dmid_ref[...] = grad_middle
    datt_ref[...] = grad_middle.astype(bfloat)
    gain_ref[...] = grad_gain


def ffn_backward(g_in, low, correction, gain_ffn, middle, one, two, before, weights):
    tokens = g_in.shape[0]
    width = gain_ffn.shape[1]
    shape = jax.ShapeDtypeStruct
    return pl.pallas_call(
        ffn_kernel,
        out_shape=[shape((tokens, width), bfloat)] * 8
        + [shape((tokens, width), floating), shape((tokens, width), bfloat), shape((1, width), floating)],
        in_specs=[VMEM, VMEM, SMEM] + [VMEM] * 7 + [ANY] * len(before),
        out_specs=[VMEM] * 11,
        scratch_shapes=[pltpu.VMEM((tokens, width), floating)],
        compiler_params=params(SCOPED),
        cost_estimate=cost(2 * tokens * 3 * weights[4].size, 2 * 3 * weights[4].size),
        name="backward_ffn",
    )(g_in, low, correction, gain_ffn, middle, one, two, *weights[4:], *before)


def attn_steps(q_ref, k_ref, v_ref, p_ref, do_ref, parts):
    tokens, width = do_ref.shape
    length = p_ref.shape[2]
    rows = tokens // length
    pairs = width // PAIR
    first = lane_mask(length)
    for row in range(rows):
        span = slice(row * length, (row + 1) * length)
        for pair in range(pairs):
            heads = slice(pair * PAIR, (pair + 1) * PAIR)
            probs = p_ref[row * pairs + pair]
            grad_out = stack_heads(do_ref[span, heads], first)
            grad_value = t_dot(probs.astype(bfloat), grad_out)
            grad_probs = dot_t(grad_out, v_ref[span, heads])
            carried = jnp.sum(probs * grad_probs, axis=-1, keepdims=True)
            grad_scores = (probs * (grad_probs - carried)).astype(bfloat)
            grad_query = dot(grad_scores, k_ref[span, heads])
            grad_query = jnp.where(first, grad_query[:length], grad_query[length:])
            grad_key = t_dot(grad_scores, stack_heads(q_ref[span, heads], first))
            for (part, base), value in zip(parts, (grad_query * SCALE, grad_key * SCALE, grad_value)):
                part[span, base + pair * PAIR : base + (pair + 1) * PAIR] = value.astype(bfloat)


def normed_grad(parts, width, wq, wk, wv):
    return sum(dot_t(part[:, base : base + width], weight[0]) for (part, base), weight in zip(parts, (wq, wk, wv)))


def attn_kernel(datt_ref, q_ref, k_ref, v_ref, p_ref, gfg_ref, ga_ref, x_ref, g_in, dmid_ref, act_ref, chg_ref, mix_ref, cor_ref,
                wq, wk, wv, wo, before,
                grad_ref, right_a, right_b, small_ref, do_ref):
    tokens, width = datt_ref.shape
    right_a[:, :width] = datt_ref[...]
    do_ref[...] = dot_t(datt_ref[...], wo[0]).astype(bfloat)
    parts = (right_a, width), (right_b, 0), (right_b, width)
    attn_steps(q_ref, k_ref, v_ref, p_ref, do_ref, parts)
    grad_normed = normed_grad(parts, width, wq, wk, wv)
    grad_gain, grad_values = norm_backward(act_ref[...], ga_ref[...], grad_normed, True)
    section = lax.axis_index("section")
    mix = [[mix_ref[0, i, j] for j in range(2)] for i in range(2)]
    cor = [cor_ref[0, i] for i in range(2)]
    out_a = g_in[:, :width].astype(floating)
    out_b = g_in[:, width:].astype(floating)
    grad_active = dmid_ref[...] + grad_values - (cor[0] * out_a + cor[1] * out_b)
    pred_a = out_a + jnp.where(section == 0, grad_active, 0.0)
    pred_b = out_b + jnp.where(section == 0, 0.0, grad_active)
    grad_ref[0, :, :width] = (pred_a + (mix[0][0] * pred_a + mix[1][0] * pred_b)).astype(bfloat)
    grad_ref[0, :, width:] = (pred_b + (mix[0][1] * pred_a + mix[1][1] * pred_b)).astype(bfloat)
    xa = x_ref[:, :width].astype(floating)
    xb = x_ref[:, width:].astype(floating)
    small_ref[0:1, :] = grad_gain
    small_ref[1:2, :] = gfg_ref[...]
    place = 2
    for pred in (pred_a, pred_b):
        for state in (xa, xb):
            small_ref[place : place + 1, :] = jnp.sum(pred * state, axis=0, keepdims=True)
            place += 1
    for out in (out_a, out_b):
        small_ref[place : place + 1, :] = jnp.sum(out * chg_ref[...], axis=0, keepdims=True)
        place += 1


def attn_backward(x, g_in, grad_middle, grad_att, active, change, queries, key_rows, value_rows, probs, ffn_gain, gain_attn,
                  mixing, correction, before, weights):
    tokens, width = active.shape
    shape = jax.ShapeDtypeStruct
    return pl.pallas_call(
        attn_kernel,
        out_shape=[shape((1, tokens, 2 * width), bfloat)] + [shape((tokens, 2 * width), bfloat)] * 2 + [shape((8, width), floating)],
        in_specs=[VMEM] * 12 + [SMEM] * 2 + [VMEM] * 4 + [ANY],
        out_specs=[VMEM] * 4,
        scratch_shapes=[pltpu.VMEM((tokens, width), bfloat)],
        compiler_params=params(SCOPED),
        cost_estimate=cost(2 * tokens * 5 * weights[0].size, 2 * 4 * weights[0].size),
        name="backward_attn",
    )(grad_att, queries, key_rows, value_rows, probs, ffn_gain, gain_attn, x, g_in, grad_middle, active, change,
      mixing, correction, *weights[:4], before)


def relay_kernel(grad_in, counts_ref, cor_ref, mix_ref, gf_ref, ga_ref, one, two, mid_ref, q_ref, k_ref, v_ref, p_ref, act_ref,
                 wq, wk, wv, wo, wg, wu, wd,
                 msg_ref,
                 acc, g_in, low_ref, do_ref, dqkv_ref):
    tokens, width = low_ref.shape
    start_rows(None, grad_in, counts_ref, cor_ref, g_in, low_ref)
    ffn_steps(low_ref, one, two, wg, wu, wd, acc, lambda *parts: None)
    grad_values = norm_backward(mid_ref[...], gf_ref[...], acc[...], False)[1]
    cor = [cor_ref[0, i] for i in range(2)]
    block = cor[0] * g_in[:, :width].astype(floating) + cor[1] * g_in[:, width:].astype(floating)
    acc[...] = block + grad_values
    do_ref[...] = dot_t(acc[...].astype(bfloat), wo[0]).astype(bfloat)
    parts = (dqkv_ref, 0), (dqkv_ref, width), (dqkv_ref, 2 * width)
    attn_steps(q_ref, k_ref, v_ref, p_ref, do_ref, parts)
    grad_normed = normed_grad(parts, width, wq, wk, wv)
    grad_values = norm_backward(act_ref[...], ga_ref[...], grad_normed, False)[1]
    block = cor[0] * g_in[:, :width].astype(floating) + cor[1] * g_in[:, width:].astype(floating)
    msg_ref[:tokens, :] = (acc[...] + grad_values - block).astype(bfloat)
    mix = [[mix_ref[0, i, j] for j in range(2)] for i in range(2)]
    msg_ref[tokens:, :] = scalar_rows(mix[0] + mix[1], EXTRA, width)


def relay_backward(out_grad, counts, correction, mixing, gain_ffn, gain_attn, one, two, middle, queries, key_rows, value_rows,
                   probs, active, weights):
    tokens, width = active.shape
    shape = jax.ShapeDtypeStruct
    narrow = pltpu.VMEM((tokens, width), bfloat)
    wide = pltpu.VMEM((tokens, width), floating)
    size = sum(weight.size for weight in weights)
    return pl.pallas_call(
        relay_kernel,
        out_shape=shape((tokens + EXTRA, width), bfloat),
        in_specs=[VMEM, SMEM, SMEM, SMEM] + [VMEM] * 17,
        out_specs=VMEM,
        scratch_shapes=[wide, pltpu.VMEM((tokens, 2 * width), bfloat), narrow, narrow, pltpu.VMEM((tokens, 3 * width), bfloat)],
        compiler_params=params(SCOPED),
        cost_estimate=cost(2 * tokens * size, 2 * size),
        name="backward_relay",
    )(out_grad, counts, correction, mixing, gain_ffn, gain_attn, one, two, middle, queries, key_rows, value_rows, probs, active,
      *weights)


def quarter_kernel(base, products, block, refs):
    count = 4
    lefts = refs[:count]
    rights = refs[count : 2 * count]
    send_ref, keep_ref = refs[-2:]
    index = lax.axis_index("dp")
    near = (index >> 2) & 1
    far = (index >> 3) & 1
    for left_at, left_wide, right_at, right_wide in products:
        columns = slice(left_at, left_at + left_wide)
        total = sum(t_dot(left[:, columns], right[:, right_at : right_at + right_wide]) for left, right in zip(lefts, rights))
        span = slice(right_at - base, right_at - base + right_wide)
        for place in range(4):
            part = total[place * block : (place + 1) * block, :]
            slot = (place >> 1) ^ far
            mine = (place & 1) == near

            @pl.when(mine)
            def _():
                keep_ref[slot, :, span] = part

            @pl.when(jnp.logical_not(mine))
            def _():
                send_ref[slot, :, span] = part.astype(bfloat)


def quarter_product(lefts, rights, products, block, before, name):
    base = products[0][2]
    wide = sum(one[3] for one in products)
    shape = jax.ShapeDtypeStruct
    flops = sum(2 * 4 * lefts[0].shape[0] * one[1] * one[3] for one in products)
    return pl.pallas_call(
        lambda *refs: quarter_kernel(base, products, block, refs),
        out_shape=[shape((2, block, wide), bfloat), shape((2, block, wide), floating)],
        in_specs=[VMEM] * 8 + [ANY] * len(before),
        out_specs=[VMEM, VMEM],
        compiler_params=params(SCOPED),
        cost_estimate=cost(flops, 12 * block * wide),
        name=name,
    )(*lefts, *rights, *before)


def assemble_kernel(own, one, two, three, gate_ref, up_ref):
    quarter = lax.axis_index("dp") & 3
    width = own.shape[1] // 2
    for slot, piece in enumerate((own, one, two, three)):
        span = pl.ds(pl.multiple_of((slot ^ quarter) * width, width), width)
        gate_ref[0, :, span] = piece[:, :width].astype(floating)
        up_ref[0, :, span] = piece[:, width:].astype(floating)


def assemble(pieces):
    share, double = pieces[0].shape
    shape = jax.ShapeDtypeStruct((1, share, 2 * double), floating)
    return pl.pallas_call(
        assemble_kernel,
        out_shape=[shape, shape],
        in_specs=[VMEM] * 4,
        out_specs=[VMEM] * 2,
        compiler_params=params(SCOPED),
        cost_estimate=cost(share * double * 4, share * double * 24),
        name="assemble",
    )(*pieces)


def exchange(value, flips):
    count = lax.axis_size("dp")
    return lax.ppermute(value, "dp", [(source, source ^ flips) for source in range(count)])


def relative_rows(matrix, order, index):
    bits = len(order)
    block = matrix.shape[0] >> bits
    split = matrix.reshape((2,) * bits + (block, matrix.shape[1]))
    axes = [bits - 1 - bit for bit in order]
    split = jnp.transpose(split, axes + [bits, bits + 1])
    for axis, bit in enumerate(order):
        split = jnp.where((index >> bit) & 1 == 1, jnp.flip(split, axis), split)
    return split.reshape(matrix.shape)


def scatter_sum(left, right, order):
    total = left.shape[0]
    arrived = []
    for step in range(len(order) + 1):
        low = total >> (step + 1) if step < len(order) else 0
        high = total >> step
        part = dot(left[low:high], right)
        for other in arrived:
            part = part + other[low:high].astype(floating)
        if step == len(order):
            return part
        arrived.append(exchange(part.astype(bfloat), 1 << order[step]))


def halving_grads(kept, low, slots, right, index, count):
    width = low.shape[1]
    order = list(range(count.bit_length() - 1))
    hidden, normed, attended, normed_ffn = (relative_rows(one.T, order, index) for one in kept)
    quarter = index & 3
    places = jnp.arange(4) ^ quarter
    dgate = jnp.concatenate(list(jnp.stack(slots[:4])[places]), axis=1)
    dup = jnp.concatenate(list(jnp.stack(slots[4:])[places]), axis=1)
    grad_down = scatter_sum(hidden, low, order)
    grad_gate = scatter_sum(normed_ffn, dgate, order)
    grad_up = scatter_sum(normed_ffn, dup, order)
    grad_out = scatter_sum(attended, right[:, :width], order)
    grad_qkv = scatter_sum(normed, right[:, width:], order)
    return [grad_down, grad_gate, grad_up, grad_out] + [grad_qkv[:, place * width : (place + 1) * width] for place in range(3)]


def after(values, *earlier):
    return lax.optimization_barrier((values, earlier))[0]


def gather_start(value):
    return [value, exchange(value, 1), exchange(value, 2)]


def gather_end(pieces, *earlier):
    return pieces + [exchange(after(pieces[2], *earlier), 1)]


def swapped(pieces):
    return [pieces[0]] + [exchange(pieces[flips], flips) for flips in (1, 2, 3)]


def sum_once(pair, *earlier):
    send, keep = pair
    arrived = after(exchange(send, 4), *earlier)
    return keep[0] + arrived[0].astype(floating), (keep[1] + arrived[1].astype(floating)).astype(bfloat)


def sum_twice(held, passed, *earlier):
    return held + after(exchange(passed, 8), *earlier).astype(floating)


def sum_over(value, bits):
    for bit in range(bits):
        value = value + exchange(value, 1 << bit)
    return value


def sum_of_four(value, step):
    return value + exchange(value, step) + exchange(value, 2 * step) + exchange(value, 3 * step)


def quarter_grads(normed_ffn, kept, slots, rights, small, down_pair, index):
    width = normed_ffn[0].shape[1]
    share = width // 16
    block = 4 * share
    whole = [(0, width, 0, width)]
    gates = swapped(slots[:4])
    ups = swapped(list(after(slots[4:], rights[0])))
    down_sums = sum_once(down_pair, rights[0])
    gate_pair = quarter_product(normed_ffn, gates, whole, block, [rights[0], down_sums[1]], "product_gate")
    grad_down = sum_twice(*down_sums)
    up_pair = quarter_product(normed_ffn, ups, whole, block, [gate_pair[0], grad_down], "product_up")
    first, second, small = after((*rights, small), up_pair[0])
    first, second = gather_start(first), gather_start(second)
    gate_sums = sum_once(gate_pair, up_pair[0])
    first = gather_end(first, gate_sums[1])
    small = sum_of_four(after(small, gate_sums[1]), 1)
    up_sums = sum_once(up_pair)
    first_products = [(width, block, 0, width), (width + block, block, width, width)]
    first_pair = quarter_product(kept, first, first_products, share, [up_sums[1], small], "product_attn_first")
    small = sum_of_four(after(small, first_pair[0]), 4)
    gate_tile = sum_twice(*gate_sums).astype(bfloat)
    first_sums = sum_once(first_pair)
    second = gather_end(second, first_sums[1], gate_tile)
    second_products = [(width + block, block, 0, 2 * width)]
    second_pair = quarter_product(kept, second, second_products, share, [small, first_sums[1]], "product_attn_second")
    quarter = index & 3
    gate_tile = after(gate_tile, second_pair[0])
    up_tile = sum_twice(*up_sums, second_pair[0]).astype(bfloat)
    pieces = [
        jnp.concatenate(
            [lax.dynamic_slice_in_dim(tile, (slot ^ quarter) * share, share, axis=0) for tile in (gate_tile, up_tile)], axis=1)
        for slot in range(4)
    ]
    pieces = swapped(pieces)
    grads = [grad_down]
    first_grad = sum_twice(*first_sums)
    second_sums = sum_once(second_pair, first_grad)
    grad_gate, grad_up = assemble(list(after(pieces, second_sums[1])))
    second_grad = sum_twice(*second_sums)
    grads = [grad_down, grad_gate[0], grad_up[0]]
    for grad in (first_grad, second_grad):
        grads += [grad[:, :width], grad[:, width:]]
    return grads, small


def local(states_in, out_grad, counts, segments, mixing, correction, gain_attn, w_query, w_key, w_value, w_attn_out, gain_ffn,
          w_gate, w_up, w_down):
    weights = (w_query, w_key, w_value, w_attn_out, w_gate, w_up, w_down)
    width = gain_attn.shape[1]
    index = lax.axis_index("dp")
    count = lax.axis_size("dp")
    fast = count == 16
    message, *weights = forward_lite(states_in, segments, mixing, correction, gain_attn, gain_ffn, weights)
    message = lax.ppermute(message, "section", [(0, 1), (1, 0)])
    (x, states, queries, key_rows, value_rows, probs, active, middle, one, two, change, *kept) = forward(
        fast, states_in, message, segments, mixing, correction, gain_attn, gain_ffn, weights)
    before = []
    if fast:
        kept, normed_ffn = swapped(kept[:4]), kept[4]
        before = kept[1:]
    message = relay_backward(out_grad, counts, correction, mixing, gain_ffn, gain_attn, one, two, middle, queries, key_rows,
                             value_rows, probs, active, weights)
    message = lax.ppermute(message, "section", [(0, 1), (1, 0)])
    g_in, low = start(message, out_grad, counts, correction, [])
    *slots, grad_middle, grad_att, ffn_gain = ffn_backward(g_in, low, correction, gain_ffn, middle, one, two, before, weights)
    before = slots[0]
    if fast:
        lows = gather_end(gather_start(low), before)
        beside, across = (one[:, width + width // 2 :] for one in kept[1:3])
        normed_ffn = gather_end([normed_ffn, beside, across], before)
        down_pair = quarter_product(kept, lows, [(0, width, 0, width)], width // 4, [before], "product_down")
        before = down_pair[0]
    state_grads, *rights, small = attn_backward(x, g_in, grad_middle, grad_att, active, change, queries, key_rows, value_rows, probs,
                                                ffn_gain, gain_attn, mixing, correction, before, weights)
    if fast:
        grads, small = quarter_grads(normed_ffn, kept, slots, rights, small, down_pair, index)
    else:
        grads = halving_grads(kept, low, slots, jnp.concatenate(rights, axis=1), index, count)
        small = sum_over(small, count.bit_length() - 1)
    grad_down, grad_gate, grad_up, grad_out, grad_query, grad_key, grad_value = grads
    share = width // count
    gains = lax.dynamic_slice(small, (0, index * share), (2, share))
    sums = jnp.sum(small[2:], axis=1)
    return (
        states,
        state_grads,
        sums[:4].reshape(1, 2, 2),
        sums[4:].reshape(1, 2),
        gains[0:1],
        grad_query[None],
        grad_key[None],
        grad_value[None],
        grad_out[None],
        gains[1:2],
        grad_gate[None],
        grad_up[None],
        grad_down[None],
    )


def solution(mesh):
    rows = P("dp", None)
    matrix = P("section", None, None)
    vector = P("section", None)
    share = P("section", "dp", None)
    gain_share = P("section", "dp")
    in_specs = (rows, rows, P("dp"), rows, matrix, vector, vector, matrix, matrix, matrix, matrix, vector, matrix, matrix, matrix)
    out_specs = (share, share, matrix, vector, gain_share, share, share, share, share, gain_share, share, share, share)
    return jax.shard_map(local, mesh=mesh, in_specs=in_specs, out_specs=out_specs, check_vma=False)
```

```python
import functools

import jax
import jax.numpy as jnp
from jax import lax
from jax.experimental import pallas as pl
from jax.experimental.pallas import tpu as pltpu
from jax.sharding import PartitionSpec as P

HEAD_DIM = 64
PAIR = 2 * HEAD_DIM
EPSILON = 1e-06
MASKED = -1e30
SCALE = HEAD_DIM ** (-0.5)
GELU_A = 0.7978845608028654
GELU_B = 0.044715
EXTRA = 16
AHEAD = 3
SCOPED = 12
bfloat = jnp.bfloat16
floating = jnp.float32

VMEM = pl.BlockSpec(memory_space=pltpu.VMEM)
SMEM = pl.BlockSpec(memory_space=pltpu.SMEM)
ANY = pl.BlockSpec(memory_space=pltpu.MemorySpace.HBM)


def dot(a, b):
    return jnp.dot(a, b, preferred_element_type=floating)


def dot_t(a, b):
    return lax.dot_general(a, b, (((1,), (1,)), ((), ())), preferred_element_type=floating)


def t_dot(a, b):
    return lax.dot_general(a, b, (((0,), (0,)), ((), ())), preferred_element_type=floating)


def params(mebibytes):
    return pltpu.CompilerParams(vmem_limit_bytes=mebibytes * 1024 * 1024)


def cost(flops, moved):
    return pl.CostEstimate(flops=flops // 1000, bytes_accessed=moved // 1000, transcendentals=0)


def scalar_rows(values, rows, width):
    lane = lax.broadcasted_iota(jnp.int32, (rows, width), 1)
    row = lax.broadcasted_iota(jnp.int32, (rows, width), 0)
    whole = jnp.zeros((rows, width), floating)
    for place, value in enumerate(values):
        whole = jnp.where(lane == place, value, whole)
    high = whole.astype(bfloat).astype(floating)
    middle = (whole - high).astype(bfloat).astype(floating)
    low = whole - high - middle
    part = jnp.where(row == 0, high, jnp.where(row == 1, middle, jnp.where(row == 2, low, 0.0)))
    return part.astype(bfloat)


def spread(value):
    high = value.astype(bfloat).astype(floating)
    middle = (value - high).astype(bfloat).astype(floating)
    low = value - high - middle
    top = jnp.concatenate([high, middle], axis=1)
    bottom = jnp.concatenate([low, jnp.zeros_like(low)], axis=1)
    return jnp.concatenate([top, bottom], axis=0).astype(bfloat)


def gathered_parts(block):
    block = block.astype(floating)
    width = block.shape[1] // 2
    return block[:8, :width] + block[:8, width:] + block[8:, :width]


def read_scalars(block, count):
    lane = lax.broadcasted_iota(jnp.int32, block.shape, 1)
    return [jnp.sum(jnp.where(lane == place, block, 0.0)) for place in range(count)]


def rms_scale(values):
    return lax.rsqrt(jnp.mean(values * values, axis=-1, keepdims=True) + EPSILON)


def lane_mask(length):
    return lax.broadcasted_iota(jnp.int32, (length, PAIR), 1) < HEAD_DIM


def stack_heads(block, first):
    zero = jnp.zeros_like(block)
    return jnp.concatenate([jnp.where(first, block, zero), jnp.where(first, zero, block)], axis=0)


def gelu_wave(gate):
    return jnp.tanh(GELU_A * (gate + GELU_B * gate * gate * gate))


def relative(blocks, index):
    low = (index & 1) == 1
    high = (index >> 1) == 1
    once = [jnp.where(low, blocks[place ^ 1], blocks[place]) for place in range(4)]
    return [jnp.where(high, once[place ^ 2], once[place]) for place in range(4)]


def attention(q_ref, k_ref, v_ref, seg_ref, att_ref, p_ref):
    length = seg_ref.shape[1]
    rows = q_ref.shape[0] // length
    pairs = q_ref.shape[1] // PAIR
    first = lane_mask(length)
    later = lax.broadcasted_iota(jnp.int32, (length, length), 0)
    earlier = lax.broadcasted_iota(jnp.int32, (length, length), 1)
    for row in range(rows):
        documents = jnp.broadcast_to(seg_ref[row : row + 1, :], (length, length)).astype(floating)
        allowed = (earlier <= later) & (documents == documents.T)
        allowed = jnp.concatenate([allowed, allowed], axis=0)
        span = slice(row * length, (row + 1) * length)
        for pair in range(pairs):
            heads = slice(pair * PAIR, (pair + 1) * PAIR)
            stacked = stack_heads(q_ref[span, heads], first)
            scores = jnp.where(allowed, dot_t(stacked, k_ref[span, heads]) * SCALE, MASKED)
            powers = jnp.exp(scores - jnp.max(scores, axis=-1, keepdims=True))
            probs = powers / jnp.sum(powers, axis=-1, keepdims=True)
            if p_ref is not None:
                p_ref[row * pairs + pair] = probs
            mixed = dot(probs.astype(bfloat), v_ref[span, heads])
            att_ref[span, heads] = jnp.where(first, mixed[:length], mixed[length:]).astype(bfloat)


def in_hbm(value):
    return pltpu.with_memory_space_constraint(value, pltpu.MemorySpace.HBM)


def forward_lite_kernel(x_any, seg_any, mix_any, cor_any, ga_any, gf_any, wq, wk, wv, wo, wg, wu, wd,
                        out_ref, wq_s, wk_s, wv_s, wo_s, wg_s, wu_s, wd_s,
                        x_in, seg_ref, mix_ref, cor_ref, ga_ref, gf_ref, q_ref, k_ref, v_ref, act_ref,
                        nrm_ref, att_ref, nf_ref, acc, sem, small_sem):
    tokens, width = act_ref.shape
    chunk = width
    pieces = wg.shape[2] // chunk
    small = [
        pltpu.make_async_copy(source, target, small_sem.at[place])
        for place, (source, target) in enumerate(
            ((x_any, x_in), (mix_any, mix_ref), (ga_any, ga_ref), (seg_any, seg_ref), (gf_any, gf_ref), (cor_any, cor_ref))
        )
    ]
    pairs = [(wq, wq_s), (wk, wk_s), (wv, wv_s), (wo, wo_s)]
    for piece in range(pieces):
        span = pl.ds(piece * chunk, chunk)
        pairs += [
            (wg.at[:, :, span], wg_s.at[:, :, span]), (wu.at[:, :, span], wu_s.at[:, :, span]), (wd.at[:, span, :], wd_s.at[:, span, :])
        ]
    queue = [pltpu.make_async_copy(source, target, sem.at[place]) for place, (source, target) in enumerate(pairs)]
    for copy in small + queue[:AHEAD]:
        copy.start()
    state = [0]

    def arrive():
        queue[state[0]].wait()
        if state[0] + AHEAD < len(queue):
            queue[state[0] + AHEAD].start()
        state[0] += 1

    for copy in small:
        copy.wait()
    section = lax.axis_index("section")
    mix = [[mix_ref[0, i, j] for j in range(2)] for i in range(2)]
    cor = [cor_ref[0, i] for i in range(2)]
    xa = x_in[:, :width].astype(floating)
    xb = x_in[:, width:].astype(floating)
    own_a = jnp.where(section == 0, mix[0][0], mix[1][0])
    own_b = jnp.where(section == 0, mix[0][1], mix[1][1])
    active = jnp.where(section == 0, xa, xb) + (own_a * xa + own_b * xb)
    act_ref[...] = active
    nrm_ref[...] = (active * rms_scale(active) * ga_ref[...]).astype(bfloat)
    for weight, target in zip((wq_s, wk_s, wv_s), (q_ref, k_ref, v_ref)):
        arrive()
        target[...] = dot(nrm_ref[...], weight[0]).astype(bfloat)
    attention(q_ref, k_ref, v_ref, seg_ref, att_ref, None)
    arrive()
    middle = act_ref[...] + dot(att_ref[...], wo_s[0])
    acc[...] = middle - act_ref[...]
    nf_ref[...] = (middle * rms_scale(middle) * gf_ref[...]).astype(bfloat)
    for piece in range(pieces):
        span = slice(piece * chunk, (piece + 1) * chunk)
        arrive()
        gate = dot(nf_ref[...], wg_s[0, :, span])
        arrive()
        upward = dot(nf_ref[...], wu_s[0, :, span])
        hidden = (0.5 * gate * (1.0 + gelu_wave(gate)) * upward).astype(bfloat)
        arrive()
        acc[...] += dot(hidden, wd_s[0, span, :])
    out_ref[:tokens, :] = acc[...].astype(bfloat)
    out_ref[tokens:, :] = scalar_rows(mix[0] + mix[1] + cor, EXTRA, width)


def forward_lite(x_in, segments, mixing, correction, gain_attn, gain_ffn, weights):
    tokens = x_in.shape[0]
    width = gain_attn.shape[1]
    size = sum(weight.size for weight in weights)
    narrow = pltpu.VMEM((tokens, width), bfloat)
    wide = pltpu.VMEM((tokens, width), floating)
    args = (x_in, segments, mixing, correction, gain_attn, gain_ffn) + weights
    scratch = [
        pltpu.VMEM(x_in.shape, bfloat), pltpu.VMEM(segments.shape, jnp.int32), pltpu.SMEM(mixing.shape, floating),
        pltpu.SMEM(correction.shape, floating), pltpu.VMEM(gain_attn.shape, floating), pltpu.VMEM(gain_ffn.shape, floating),
        narrow, narrow, narrow, wide, narrow, narrow, narrow, wide,
    ]
    scratch += [pltpu.SemaphoreType.DMA((4 + 3 * (weights[4].shape[2] // width),)), pltpu.SemaphoreType.DMA((6,))]
    return pl.pallas_call(
        forward_lite_kernel,
        out_shape=[jax.ShapeDtypeStruct((tokens + EXTRA, width), bfloat)]
        + [jax.ShapeDtypeStruct(weight.shape, bfloat) for weight in weights],
        in_specs=[ANY] * len(args),
        out_specs=[VMEM] * 8,
        scratch_shapes=scratch,
        compiler_params=params(SCOPED),
        cost_estimate=cost(2 * tokens * size, 2 * size),
        name="forward_lite",
    )(*[in_hbm(one) for one in args])


def forward_kernel(fast, x_in, message, seg_ref, mix_ref, cor_ref, ga_ref, gf_ref, wq, wk, wv, wo, wg, wu, wd,
                   x_ref, out_ref, q_ref, k_ref, v_ref, p_ref, act_ref, mid_ref, one_ref, two_ref, chg_ref, *refs):
    kept = refs[:4]
    nf_ref = refs[-4]
    nrm_ref, att_ref, acc = refs[-3:]
    tokens, width = act_ref.shape
    chunk = width
    pieces = wg.shape[2] // chunk
    section = lax.axis_index("section")
    quarter = lax.axis_index("dp") & 3
    mix = [[mix_ref[0, i, j] for j in range(2)] for i in range(2)]
    cor = [cor_ref[0, i] for i in range(2)]
    xa = x_in[:, :width].astype(floating)
    xb = x_in[:, width:].astype(floating)
    got = read_scalars(message[tokens : tokens + EXTRA, :PAIR].astype(floating), 6)
    moved = message[:tokens, :].astype(floating)
    sent_a = (xa + (got[0] * xa + got[1] * xb) + got[4] * moved).astype(bfloat)
    sent_b = (xb + (got[2] * xa + got[3] * xb) + got[5] * moved).astype(bfloat)
    x_ref[:, :width] = jnp.where(section == 0, x_in[:, :width], sent_a)
    x_ref[:, width:] = jnp.where(section == 0, x_in[:, width:], sent_b)
    xa = x_ref[:, :width].astype(floating)
    xb = x_ref[:, width:].astype(floating)
    own_a = jnp.where(section == 0, mix[0][0], mix[1][0])
    own_b = jnp.where(section == 0, mix[0][1], mix[1][1])
    active = jnp.where(section == 0, xa, xb) + (own_a * xa + own_b * xb)
    act_ref[...] = active
    nrm_ref[...] = (active * rms_scale(active) * ga_ref[...]).astype(bfloat)
    for weight, target in zip((wq, wk, wv), (q_ref, k_ref, v_ref)):
        target[...] = dot(nrm_ref[...], weight[0]).astype(bfloat)

    def keep_quarters(values, base):
        share = width // 16
        for far in range(4):
            blocks = [values[:, (4 * far + near) * share : (4 * far + near + 1) * share] for near in range(4)]
            for slot, block in enumerate(relative(blocks, quarter)):
                kept[slot][:, base + far * share : base + (far + 1) * share] = block

    attention(q_ref, k_ref, v_ref, seg_ref, att_ref, p_ref)
    middle = act_ref[...] + dot(att_ref[...], wo[0])
    mid_ref[...] = middle
    nf_ref[...] = (middle * rms_scale(middle) * gf_ref[...]).astype(bfloat)
    if fast:
        keep_quarters(att_ref[...], width)
        keep_quarters(nrm_ref[...], width + width // 4)
        for slot in (1, 2):
            kept[slot][:, width + width // 2 :] = nf_ref[...]
    else:
        kept[1][...] = nrm_ref[...]
        kept[2][...] = att_ref[...]
    for piece in range(pieces):
        span = slice(piece * chunk, (piece + 1) * chunk)
        gate = dot(nf_ref[...], wg[0, :, span])
        upward = dot(nf_ref[...], wu[0, :, span])
        wave = gelu_wave(gate)
        half = 0.5 * (1.0 + wave)
        value = gate * half
        hidden = (value * upward).astype(bfloat)
        slope = half + 0.5 * gate * (1.0 - wave * wave) * (GELU_A * (1.0 + 3.0 * GELU_B * gate * gate))
        one_ref[piece] = upward * slope
        two_ref[piece] = value
        if fast:
            share = chunk // 4
            blocks = [hidden[:, near * share : (near + 1) * share] for near in range(4)]
            for slot, block in enumerate(relative(blocks, quarter)):
                kept[slot][:, piece * share : (piece + 1) * share] = block
        else:
            kept[0][:, span] = hidden
        down = dot(hidden, wd[0, span, :])
        if piece == 0:
            acc[...] = down
        else:
            acc[...] += down
    change = mid_ref[...] + acc[...] - act_ref[...]
    chg_ref[...] = change
    xa = x_ref[:, :width].astype(floating)
    xb = x_ref[:, width:].astype(floating)
    out_ref[0, :, :width] = (xa + (mix[0][0] * xa + mix[0][1] * xb) + cor[0] * change).astype(bfloat)
    out_ref[0, :, width:] = (xb + (mix[1][0] * xa + mix[1][1] * xb) + cor[1] * change).astype(bfloat)


def forward(fast, x_in, message, segments, mixing, correction, gain_attn, gain_ffn, weights):
    tokens = x_in.shape[0]
    length = segments.shape[1]
    width = gain_attn.shape[1]
    hidden_width = weights[4].shape[2]
    size = sum(weight.size for weight in weights)
    shape = jax.ShapeDtypeStruct
    narrow = ((tokens, width), bfloat)
    wide = ((tokens, width), floating)
    probs = ((tokens // length * (width // PAIR), 2 * length, length), floating)
    if fast:
        short, long = (((tokens, columns), bfloat) for columns in (width + width // 2, 2 * width + width // 2))
        kept = [short, long, long, short, narrow]
    else:
        kept = [((tokens, hidden_width), bfloat), narrow, narrow, narrow]
    ffn = ((hidden_width // width, tokens, width), floating)
    outs = [((tokens, 2 * width), bfloat), ((1, tokens, 2 * width), bfloat), narrow, narrow, narrow, probs, wide, wide,
            ffn, ffn, wide] + kept
    return pl.pallas_call(
        lambda *refs: forward_kernel(fast, *refs),
        out_shape=[shape(*one) for one in outs],
        in_specs=[VMEM, VMEM, VMEM, SMEM, SMEM, VMEM, VMEM] + [VMEM] * 7,
        out_specs=[VMEM] * len(outs),
        scratch_shapes=[pltpu.VMEM(*narrow)] * 2 + [pltpu.VMEM(*wide)],
        compiler_params=params(SCOPED),
        cost_estimate=cost(2 * tokens * size, 2 * size),
        name="forward_full",
    )(x_in, message, segments, mixing, correction, gain_attn, gain_ffn, *weights)


def start_rows(message, grad_ref, counts_ref, cor_ref, g_ref, low_ref):
    tokens, width = low_ref.shape
    rows = counts_ref.shape[0]
    length = tokens // rows
    section = lax.axis_index("section")
    if message is not None:
        got = read_scalars(message[tokens : tokens + EXTRA, :PAIR].astype(floating), 4)
    place = lax.broadcasted_iota(jnp.int32, (length, width), 0)
    for row in range(rows):
        span = slice(row * length, (row + 1) * length)
        valid = place < counts_ref[row]
        own_a = jnp.where(valid, grad_ref[span, :width].astype(floating), 0.0)
        own_b = jnp.where(valid, grad_ref[span, width:].astype(floating), 0.0)
        if message is not None:
            later_b = own_b + message[span, :].astype(floating)
            far_a = own_a + (got[0] * own_a + got[2] * later_b)
            far_b = later_b + (got[1] * own_a + got[3] * later_b)
            own_a = jnp.where(section == 0, far_a, own_a).astype(bfloat).astype(floating)
            own_b = jnp.where(section == 0, far_b, own_b).astype(bfloat).astype(floating)
        g_ref[span, :width] = own_a.astype(bfloat)
        g_ref[span, width:] = own_b.astype(bfloat)
        low_ref[span, :] = (cor_ref[0, 0] * own_a + cor_ref[0, 1] * own_b).astype(bfloat)


def start(message, out_grad, counts, correction, before):
    tokens = out_grad.shape[0]
    width = message.shape[1]
    shape = jax.ShapeDtypeStruct
    return pl.pallas_call(
        lambda *refs: start_rows(*refs[:4], *refs[-2:]),
        out_shape=[shape((tokens, 2 * width), bfloat), shape((tokens, width), bfloat)],
        in_specs=[VMEM, VMEM, SMEM, SMEM] + [ANY] * len(before),
        out_specs=[VMEM, VMEM],
        compiler_params=params(SCOPED),
        cost_estimate=cost(tokens * width * 20, tokens * width * 12),
        name="backward_start",
    )(message, out_grad, counts, correction, *before)


def norm_backward(values, gain, grad_normed, with_gain):
    inverse = rms_scale(values)
    grad_gain = jnp.sum(grad_normed * values * inverse, axis=0, keepdims=True) if with_gain else None
    weighted = grad_normed * gain
    grad_values = inverse * weighted - values * inverse**3 * jnp.mean(weighted * values, axis=-1, keepdims=True)
    return grad_gain, grad_values


def ffn_steps(low_ref, one, two, wg, wu, wd, acc, emit):
    width = wd.shape[2]
    quarter = lax.axis_index("dp") & 3
    for step in range(4):
        piece = (3 - step) ^ quarter
        span = pl.ds(pl.multiple_of(piece * width, width), width)
        grad_hidden = dot_t(low_ref[...], wd[0, span, :])
        dgate = (grad_hidden * one[piece]).astype(bfloat)
        dup = (grad_hidden * two[piece]).astype(bfloat)
        emit(3 - step, dgate, dup)
        total = dot_t(dgate, wg[0, :, span]) + dot_t(dup, wu[0, :, span])
        if step == 0:
            acc[...] = total
        else:
            acc[...] += total


def ffn_kernel(g_in, low_ref, cor_ref, gf_ref, mid_ref, one, two, wg, wu, wd, *refs):
    slots = refs[-12:-4]
    dmid_ref, datt_ref, gain_ref, acc = refs[-4:]
    width = gf_ref.shape[1]

    def emit(slot, dgate, dup):
        slots[slot][...] = dgate
        slots[4 + slot][...] = dup

    ffn_steps(low_ref, one, two, wg, wu, wd, acc, emit)
    grad_gain, grad_values = norm_backward(mid_ref[...], gf_ref[...], acc[...], True)
    block = cor_ref[0, 0] * g_in[:, :width].astype(floating) + cor_ref[0, 1] * g_in[:, width:].astype(floating)
    grad_middle = block + grad_values
    dmid_ref[...] = grad_middle
    datt_ref[...] = grad_middle.astype(bfloat)
    gain_ref[...] = grad_gain


def ffn_backward(g_in, low, correction, gain_ffn, middle, one, two, before, weights):
    tokens = g_in.shape[0]
    width = gain_ffn.shape[1]
    shape = jax.ShapeDtypeStruct
    return pl.pallas_call(
        ffn_kernel,
        out_shape=[shape((tokens, width), bfloat)] * 8
        + [shape((tokens, width), floating), shape((tokens, width), bfloat), shape((1, width), floating)],
        in_specs=[VMEM, VMEM, SMEM] + [VMEM] * 7 + [ANY] * len(before),
        out_specs=[VMEM] * 11,
        scratch_shapes=[pltpu.VMEM((tokens, width), floating)],
        compiler_params=params(SCOPED),
        cost_estimate=cost(2 * tokens * 3 * weights[4].size, 2 * 3 * weights[4].size),
        name="backward_ffn",
    )(g_in, low, correction, gain_ffn, middle, one, two, *weights[4:], *before)


def attn_steps(q_ref, k_ref, v_ref, p_ref, do_ref, parts):
    tokens, width = do_ref.shape
    length = p_ref.shape[2]
    rows = tokens // length
    pairs = width // PAIR
    first = lane_mask(length)
    for row in range(rows):
        span = slice(row * length, (row + 1) * length)
        for pair in range(pairs):
            heads = slice(pair * PAIR, (pair + 1) * PAIR)
            probs = p_ref[row * pairs + pair]
            grad_out = stack_heads(do_ref[span, heads], first)
            grad_value = t_dot(probs.astype(bfloat), grad_out)
            grad_probs = dot_t(grad_out, v_ref[span, heads])
            carried = jnp.sum(probs * grad_probs, axis=-1, keepdims=True)
            grad_scores = (probs * (grad_probs - carried)).astype(bfloat)
            grad_query = dot(grad_scores, k_ref[span, heads])
            grad_query = jnp.where(first, grad_query[:length], grad_query[length:])
            grad_key = t_dot(grad_scores, stack_heads(q_ref[span, heads], first))
            for (part, base), value in zip(parts, (grad_query * SCALE, grad_key * SCALE, grad_value)):
                part[span, base + pair * PAIR : base + (pair + 1) * PAIR] = value.astype(bfloat)


def normed_grad(parts, rows, width, wq, wk, wv):
    return sum(dot_t(part[:rows, base : base + width], weight[0]) for (part, base), weight in zip(parts, (wq, wk, wv)))


def attn_kernel(datt_ref, q_ref, k_ref, v_ref, p_ref, gfg_ref, ga_ref, x_ref, g_in, dmid_ref, act_ref, chg_ref, mix_ref, cor_ref,
                wq, wk, wv, wo, before,
                grad_ref, right_a, right_b, small_ref, do_ref):
    tokens, width = datt_ref.shape
    right_a[:tokens, :width] = datt_ref[...]
    do_ref[...] = dot_t(datt_ref[...], wo[0]).astype(bfloat)
    parts = (right_a, width), (right_b, 0), (right_b, width)
    attn_steps(q_ref, k_ref, v_ref, p_ref, do_ref, parts)
    grad_normed = normed_grad(parts, tokens, width, wq, wk, wv)
    grad_gain, grad_values = norm_backward(act_ref[...], ga_ref[...], grad_normed, True)
    section = lax.axis_index("section")
    mix = [[mix_ref[0, i, j] for j in range(2)] for i in range(2)]
    cor = [cor_ref[0, i] for i in range(2)]
    out_a = g_in[:, :width].astype(floating)
    out_b = g_in[:, width:].astype(floating)
    grad_active = dmid_ref[...] + grad_values - (cor[0] * out_a + cor[1] * out_b)
    pred_a = out_a + jnp.where(section == 0, grad_active, 0.0)
    pred_b = out_b + jnp.where(section == 0, 0.0, grad_active)
    grad_ref[0, :, :width] = (pred_a + (mix[0][0] * pred_a + mix[1][0] * pred_b)).astype(bfloat)
    grad_ref[0, :, width:] = (pred_b + (mix[0][1] * pred_a + mix[1][1] * pred_b)).astype(bfloat)
    xa = x_ref[:, :width].astype(floating)
    xb = x_ref[:, width:].astype(floating)
    small_ref[0:1, :] = grad_gain
    small_ref[1:2, :] = gfg_ref[...]
    place = 2
    for pred in (pred_a, pred_b):
        for state in (xa, xb):
            small_ref[place : place + 1, :] = jnp.sum(pred * state, axis=0, keepdims=True)
            place += 1
    for out in (out_a, out_b):
        small_ref[place : place + 1, :] = jnp.sum(out * chg_ref[...], axis=0, keepdims=True)
        place += 1
    right_a[tokens:, :] = spread(small_ref[...])


def attn_backward(x, g_in, grad_middle, grad_att, active, change, queries, key_rows, value_rows, probs, ffn_gain, gain_attn,
                  mixing, correction, before, weights):
    tokens, width = active.shape
    shape = jax.ShapeDtypeStruct
    return pl.pallas_call(
        attn_kernel,
        out_shape=[
            shape((1, tokens, 2 * width), bfloat), shape((tokens + EXTRA, 2 * width), bfloat), shape((tokens, 2 * width), bfloat),
            shape((8, width), floating),
        ],
        in_specs=[VMEM] * 12 + [SMEM] * 2 + [VMEM] * 4 + [ANY],
        out_specs=[VMEM] * 4,
        scratch_shapes=[pltpu.VMEM((tokens, width), bfloat)],
        compiler_params=params(SCOPED),
        cost_estimate=cost(2 * tokens * 5 * weights[0].size, 2 * 4 * weights[0].size),
        name="backward_attn",
    )(grad_att, queries, key_rows, value_rows, probs, ffn_gain, gain_attn, x, g_in, grad_middle, active, change,
      mixing, correction, *weights[:4], before)


def relay_kernel(grad_in, counts_ref, cor_ref, mix_ref, gf_ref, ga_ref, one, two, mid_ref, q_ref, k_ref, v_ref, p_ref, act_ref,
                 wq, wk, wv, wo, wg, wu, wd,
                 msg_ref,
                 acc, g_in, low_ref, do_ref, dqkv_ref):
    tokens, width = low_ref.shape
    start_rows(None, grad_in, counts_ref, cor_ref, g_in, low_ref)
    ffn_steps(low_ref, one, two, wg, wu, wd, acc, lambda *parts: None)
    grad_values = norm_backward(mid_ref[...], gf_ref[...], acc[...], False)[1]
    cor = [cor_ref[0, i] for i in range(2)]
    block = cor[0] * g_in[:, :width].astype(floating) + cor[1] * g_in[:, width:].astype(floating)
    acc[...] = block + grad_values
    do_ref[...] = dot_t(acc[...].astype(bfloat), wo[0]).astype(bfloat)
    parts = (dqkv_ref, 0), (dqkv_ref, width), (dqkv_ref, 2 * width)
    attn_steps(q_ref, k_ref, v_ref, p_ref, do_ref, parts)
    grad_normed = normed_grad(parts, tokens, width, wq, wk, wv)
    grad_values = norm_backward(act_ref[...], ga_ref[...], grad_normed, False)[1]
    block = cor[0] * g_in[:, :width].astype(floating) + cor[1] * g_in[:, width:].astype(floating)
    msg_ref[:tokens, :] = (acc[...] + grad_values - block).astype(bfloat)
    mix = [[mix_ref[0, i, j] for j in range(2)] for i in range(2)]
    msg_ref[tokens:, :] = scalar_rows(mix[0] + mix[1], EXTRA, width)


def relay_backward(out_grad, counts, correction, mixing, gain_ffn, gain_attn, one, two, middle, queries, key_rows, value_rows,
                   probs, active, weights):
    tokens, width = active.shape
    shape = jax.ShapeDtypeStruct
    narrow = pltpu.VMEM((tokens, width), bfloat)
    wide = pltpu.VMEM((tokens, width), floating)
    size = sum(weight.size for weight in weights)
    return pl.pallas_call(
        relay_kernel,
        out_shape=shape((tokens + EXTRA, width), bfloat),
        in_specs=[VMEM, SMEM, SMEM, SMEM] + [VMEM] * 17,
        out_specs=VMEM,
        scratch_shapes=[wide, pltpu.VMEM((tokens, 2 * width), bfloat), narrow, narrow, pltpu.VMEM((tokens, 3 * width), bfloat)],
        compiler_params=params(SCOPED),
        cost_estimate=cost(2 * tokens * size, 2 * size),
        name="backward_relay",
    )(out_grad, counts, correction, mixing, gain_ffn, gain_attn, one, two, middle, queries, key_rows, value_rows, probs, active,
      *weights)


def quarter_kernel(base, products, block, refs):
    count = 4
    lefts = refs[:count]
    rights = refs[count : 2 * count]
    send_ref, keep_ref = refs[-2:]
    quarter_parts(base, products, block, lefts, rights, send_ref, keep_ref)


def quarter_parts(base, products, block, lefts, rights, send_ref, keep_ref):
    tokens = lefts[0].shape[0]
    index = lax.axis_index("dp")
    near = (index >> 2) & 1
    far = (index >> 3) & 1
    for left_at, left_wide, right_at, right_wide in products:
        rows = slice(left_at, left_at + left_wide)
        columns = slice(right_at, right_at + right_wide)
        total = sum(t_dot(left[:, rows], right[:tokens, columns]) for left, right in zip(lefts, rights))
        span = slice(right_at - base, right_at - base + right_wide)
        for place in range(4):
            part = total[place * block : (place + 1) * block, :]
            slot = (place >> 1) ^ far
            mine = (place & 1) == near

            @pl.when(mine)
            def _():
                keep_ref[slot, :, span] = part

            @pl.when(jnp.logical_not(mine))
            def _():
                send_ref[slot, :, span] = part.astype(bfloat)


def first_kernel(products, block, refs):
    lefts, rights = refs[:4], refs[4:8]
    send_ref, keep_ref, small_ref, stage = refs[-4:]
    quarter_parts(0, products, block, lefts, rights, stage, keep_ref)
    tokens = lefts[0].shape[0]
    send_ref[:block, :] = stage[0]
    send_ref[block : 2 * block, :] = stage[1]
    small = sum(gathered_parts(right[tokens:, :]) for right in rights)
    small_ref[...] = small
    send_ref[2 * block :, :] = spread(small)


def first_product(lefts, rights, products, block, before):
    wide = rights[0].shape[1]
    shape = jax.ShapeDtypeStruct
    return pl.pallas_call(
        lambda *refs: first_kernel(products, block, refs),
        out_shape=[shape((2 * block + EXTRA, wide), bfloat), shape((2, block, wide), floating), shape((8, wide // 2), floating)],
        in_specs=[VMEM] * 8 + [ANY] * len(before),
        out_specs=[VMEM] * 3,
        scratch_shapes=[pltpu.VMEM((2, block, wide), bfloat)],
        compiler_params=params(SCOPED),
        cost_estimate=cost(wide, wide),
        name="product_attn_first",
    )(*lefts, *rights, *before)


def first_sum_kernel(keep_ref, came_ref, small_ref, held_ref, passed_ref, sums_ref):
    block = held_ref.shape[0]
    held_ref[...] = keep_ref[0] + came_ref[:block, :].astype(floating)
    passed_ref[:block, :] = (keep_ref[1] + came_ref[block : 2 * block, :].astype(floating)).astype(bfloat)
    small = small_ref[...] + gathered_parts(came_ref[2 * block :, :])
    sums_ref[...] = small
    passed_ref[block:, :] = spread(small)


def first_sum(keep, came, small):
    _, block, wide = keep.shape
    shape = jax.ShapeDtypeStruct
    return pl.pallas_call(
        first_sum_kernel,
        out_shape=[shape((block, wide), floating), shape((block + EXTRA, wide), bfloat), shape(small.shape, floating)],
        in_specs=[VMEM] * 3,
        out_specs=[VMEM] * 3,
        compiler_params=params(SCOPED),
        cost_estimate=cost(wide, wide),
        name="first_sum",
    )(keep, came, small)


def first_end_kernel(held_ref, came_ref, small_ref, left_ref, right_ref, sums_ref):
    block, wide = held_ref.shape
    left_ref[0] = held_ref[:, : wide // 2] + came_ref[:block, : wide // 2].astype(floating)
    right_ref[0] = held_ref[:, wide // 2 :] + came_ref[:block, wide // 2 :].astype(floating)
    sums_ref[...] = small_ref[...] + gathered_parts(came_ref[block:, :])


def first_end(held, came, small):
    block, wide = held.shape
    shape = jax.ShapeDtypeStruct
    return pl.pallas_call(
        first_end_kernel,
        out_shape=[shape((1, block, wide // 2), floating)] * 2 + [shape(small.shape, floating)],
        in_specs=[VMEM] * 3,
        out_specs=[VMEM] * 3,
        compiler_params=params(SCOPED),
        cost_estimate=cost(wide, wide),
        name="first_end",
    )(held, came, small)


def quarter_product(lefts, rights, products, block, before, name):
    base = products[0][2]
    wide = sum(one[3] for one in products)
    shape = jax.ShapeDtypeStruct
    flops = sum(2 * 4 * lefts[0].shape[0] * one[1] * one[3] for one in products)
    return pl.pallas_call(
        lambda *refs: quarter_kernel(base, products, block, refs),
        out_shape=[shape((2, block, wide), bfloat), shape((2, block, wide), floating)],
        in_specs=[VMEM] * 8 + [ANY] * len(before),
        out_specs=[VMEM, VMEM],
        compiler_params=params(SCOPED),
        cost_estimate=cost(flops, 12 * block * wide),
        name=name,
    )(*lefts, *rights, *before)


def assemble_kernel(own, one, two, three, gate_ref, up_ref):
    quarter = lax.axis_index("dp") & 3
    width = own.shape[1] // 2
    for slot, piece in enumerate((own, one, two, three)):
        span = pl.ds(pl.multiple_of((slot ^ quarter) * width, width), width)
        gate_ref[0, :, span] = piece[:, :width].astype(floating)
        up_ref[0, :, span] = piece[:, width:].astype(floating)


def assemble(pieces):
    share, double = pieces[0].shape
    shape = jax.ShapeDtypeStruct((1, share, 2 * double), floating)
    return pl.pallas_call(
        assemble_kernel,
        out_shape=[shape, shape],
        in_specs=[VMEM] * 4,
        out_specs=[VMEM] * 2,
        compiler_params=params(SCOPED),
        cost_estimate=cost(share * double * 4, share * double * 24),
        name="assemble",
    )(*pieces)


def exchange(value, flips):
    count = lax.axis_size("dp")
    return lax.ppermute(value, "dp", [(source, source ^ flips) for source in range(count)])


def relative_rows(matrix, order, index):
    bits = len(order)
    block = matrix.shape[0] >> bits
    split = matrix.reshape((2,) * bits + (block, matrix.shape[1]))
    axes = [bits - 1 - bit for bit in order]
    split = jnp.transpose(split, axes + [bits, bits + 1])
    for axis, bit in enumerate(order):
        split = jnp.where((index >> bit) & 1 == 1, jnp.flip(split, axis), split)
    return split.reshape(matrix.shape)


def scatter_sum(left, right, order):
    total = left.shape[0]
    arrived = []
    for step in range(len(order) + 1):
        low = total >> (step + 1) if step < len(order) else 0
        high = total >> step
        part = dot(left[low:high], right)
        for other in arrived:
            part = part + other[low:high].astype(floating)
        if step == len(order):
            return part
        arrived.append(exchange(part.astype(bfloat), 1 << order[step]))


def halving_grads(kept, low, slots, right, index, count):
    width = low.shape[1]
    order = list(range(count.bit_length() - 1))
    hidden, normed, attended, normed_ffn = (relative_rows(one.T, order, index) for one in kept)
    quarter = index & 3
    places = jnp.arange(4) ^ quarter
    dgate = jnp.concatenate(list(jnp.stack(slots[:4])[places]), axis=1)
    dup = jnp.concatenate(list(jnp.stack(slots[4:])[places]), axis=1)
    grad_down = scatter_sum(hidden, low, order)
    grad_gate = scatter_sum(normed_ffn, dgate, order)
    grad_up = scatter_sum(normed_ffn, dup, order)
    grad_out = scatter_sum(attended, right[:, :width], order)
    grad_qkv = scatter_sum(normed, right[:, width:], order)
    grads = [grad_down, grad_gate, grad_up, grad_out] + [grad_qkv[:, place * width : (place + 1) * width] for place in range(3)]
    return [one[None] for one in grads]


def after(values, *earlier):
    return lax.optimization_barrier((values, earlier))[0]


def gather_start(value):
    return [value, exchange(value, 1), exchange(value, 2)]


def gather_end(pieces, *earlier):
    return pieces + [exchange(after(pieces[2], *earlier), 1)]


def swapped(pieces):
    return [pieces[0]] + [exchange(pieces[flips], flips) for flips in (1, 2, 3)]


def sum_once(pair, *earlier):
    send, keep = pair
    arrived = after(exchange(send, 4), *earlier)
    return keep[0] + arrived[0].astype(floating), (keep[1] + arrived[1].astype(floating)).astype(bfloat)


def sum_twice(held, passed, *earlier):
    return held + after(exchange(passed, 8), *earlier).astype(floating)


def sum_over(value, bits):
    for bit in range(bits):
        value = value + exchange(value, 1 << bit)
    return value


def quarter_grads(normed_ffn, kept, slots, rights, down_pair, index):
    width = normed_ffn[0].shape[1]
    share = width // 16
    block = 4 * share
    whole = [(0, width, 0, width)]
    gates = swapped(slots[:4])
    ups = swapped(list(after(slots[4:], rights[0])))
    down_sums = sum_once(down_pair, rights[0])
    gate_pair = quarter_product(normed_ffn, gates, whole, block, [rights[0], down_sums[1]], "product_gate")
    grad_down = sum_twice(*down_sums)
    up_pair = quarter_product(normed_ffn, ups, whole, block, [gate_pair[0], grad_down], "product_up")
    first = gather_start(after(rights[0], up_pair[0]))
    second = gather_start(after(rights[1], first[2]))
    gate_sums = sum_once(gate_pair, up_pair[0])
    first = gather_end(first, gate_sums[1])
    up_sums = sum_once(up_pair)
    first_products = [(width, block, 0, width), (width + block, block, width, width)]
    first_send, first_keep, small = first_product(kept, first, first_products, share, [up_sums[1]])
    gate_tile = sum_twice(*gate_sums).astype(bfloat)
    held, passed, small = first_sum(first_keep, exchange(first_send, 4), small)
    second = gather_end(second, passed, gate_tile)
    second_products = [(width + block, block, 0, 2 * width)]
    second_pair = quarter_product(kept, second, second_products, share, [passed], "product_attn_second")
    quarter = index & 3
    gate_tile = after(gate_tile, second_pair[0])
    up_tile = sum_twice(*up_sums, second_pair[0]).astype(bfloat)
    pieces = [
        jnp.concatenate(
            [lax.dynamic_slice_in_dim(tile, (slot ^ quarter) * share, share, axis=0) for tile in (gate_tile, up_tile)], axis=1)
        for slot in range(4)
    ]
    pieces = swapped(pieces)
    grad_out, grad_query, small = first_end(held, exchange(passed, 8), small)
    second_sums = sum_once(second_pair, small)
    grad_gate, grad_up = assemble(list(after(pieces, second_sums[1])))
    held, passed = second_sums
    passed = exchange(passed, 8)
    grads = [grad_down[None], grad_gate, grad_up, grad_out, grad_query]
    for span in (slice(0, width), slice(width, 2 * width)):
        grads.append((held[:, span] + passed[:, span].astype(floating))[None])
    return grads, small


def local(states_in, out_grad, counts, segments, mixing, correction, gain_attn, w_query, w_key, w_value, w_attn_out, gain_ffn,
          w_gate, w_up, w_down):
    weights = (w_query, w_key, w_value, w_attn_out, w_gate, w_up, w_down)
    width = gain_attn.shape[1]
    index = lax.axis_index("dp")
    count = lax.axis_size("dp")
    fast = count == 16
    message, *weights = forward_lite(states_in, segments, mixing, correction, gain_attn, gain_ffn, weights)
    message = lax.ppermute(message, "section", [(0, 1), (1, 0)])
    (x, states, queries, key_rows, value_rows, probs, active, middle, one, two, change, *kept) = forward(
        fast, states_in, message, segments, mixing, correction, gain_attn, gain_ffn, weights)
    before = []
    if fast:
        kept, normed_ffn = swapped(kept[:4]), kept[4]
        before = kept[1:]
    message = relay_backward(out_grad, counts, correction, mixing, gain_ffn, gain_attn, one, two, middle, queries, key_rows,
                             value_rows, probs, active, weights)
    message = lax.ppermute(message, "section", [(0, 1), (1, 0)])
    g_in, low = start(message, out_grad, counts, correction, [])
    *slots, grad_middle, grad_att, ffn_gain = ffn_backward(g_in, low, correction, gain_ffn, middle, one, two, before, weights)
    before = slots[0]
    if fast:
        lows = gather_end(gather_start(low), before)
        beside, across = (one[:, width + width // 2 :] for one in kept[1:3])
        normed_ffn = gather_end([normed_ffn, beside, across], before)
        down_pair = quarter_product(kept, lows, [(0, width, 0, width)], width // 4, [before], "product_down")
        before = down_pair[0]
    state_grads, *rights, small = attn_backward(x, g_in, grad_middle, grad_att, active, change, queries, key_rows, value_rows, probs,
                                                ffn_gain, gain_attn, mixing, correction, before, weights)
    if fast:
        grads, small = quarter_grads(normed_ffn, kept, slots, rights, down_pair, index)
    else:
        rights[0] = rights[0][: low.shape[0]]
        grads = halving_grads(kept, low, slots, jnp.concatenate(rights, axis=1), index, count)
        small = sum_over(small, count.bit_length() - 1)
    grad_down, grad_gate, grad_up, grad_out, grad_query, grad_key, grad_value = grads
    share = width // count
    gains = lax.dynamic_slice(small, (0, index * share), (2, share))
    sums = jnp.sum(small[2:], axis=1)
    return (
        states,
        state_grads,
        sums[:4].reshape(1, 2, 2),
        sums[4:].reshape(1, 2),
        gains[0:1],
        grad_query,
        grad_key,
        grad_value,
        grad_out,
        gains[1:2],
        grad_gate,
        grad_up,
        grad_down,
    )


def solution(mesh):
    rows = P("dp", None)
    matrix = P("section", None, None)
    vector = P("section", None)
    share = P("section", "dp", None)
    gain_share = P("section", "dp")
    in_specs = (rows, rows, P("dp"), rows, matrix, vector, vector, matrix, matrix, matrix, matrix, vector, matrix, matrix, matrix)
    out_specs = (share, share, matrix, vector, gain_share, share, share, share, share, gain_share, share, share, share)
    return jax.shard_map(local, mesh=mesh, in_specs=in_specs, out_specs=out_specs, check_vma=False)
```

```python
import functools

import jax
import jax.numpy as jnp
from jax import lax
from jax.experimental import pallas as pl
from jax.experimental.pallas import tpu as pltpu
from jax.sharding import PartitionSpec as P

HEAD_DIM = 64
PAIR = 2 * HEAD_DIM
EPSILON = 1e-06
MASKED = -1e30
SCALE = HEAD_DIM ** (-0.5)
GELU_A = 0.7978845608028654
GELU_B = 0.044715
EXTRA = 16
AHEAD = 3
SCOPED = 12
bfloat = jnp.bfloat16
floating = jnp.float32

VMEM = pl.BlockSpec(memory_space=pltpu.VMEM)
SMEM = pl.BlockSpec(memory_space=pltpu.SMEM)
ANY = pl.BlockSpec(memory_space=pltpu.MemorySpace.HBM)


def dot(a, b):
    return jnp.dot(a, b, preferred_element_type=floating)


def dot_t(a, b):
    return lax.dot_general(a, b, (((1,), (1,)), ((), ())), preferred_element_type=floating)


def t_dot(a, b):
    return lax.dot_general(a, b, (((0,), (0,)), ((), ())), preferred_element_type=floating)


def params(mebibytes):
    return pltpu.CompilerParams(vmem_limit_bytes=mebibytes * 1024 * 1024)


def cost(flops, moved):
    return pl.CostEstimate(flops=flops // 1000, bytes_accessed=moved // 1000, transcendentals=0)


def scalar_rows(values, rows, width):
    lane = lax.broadcasted_iota(jnp.int32, (rows, width), 1)
    row = lax.broadcasted_iota(jnp.int32, (rows, width), 0)
    whole = jnp.zeros((rows, width), floating)
    for place, value in enumerate(values):
        whole = jnp.where(lane == place, value, whole)
    high = whole.astype(bfloat).astype(floating)
    middle = (whole - high).astype(bfloat).astype(floating)
    low = whole - high - middle
    part = jnp.where(row == 0, high, jnp.where(row == 1, middle, jnp.where(row == 2, low, 0.0)))
    return part.astype(bfloat)


def spread(value):
    high = value.astype(bfloat).astype(floating)
    middle = (value - high).astype(bfloat).astype(floating)
    low = value - high - middle
    top = jnp.concatenate([high, middle], axis=1)
    bottom = jnp.concatenate([low, jnp.zeros_like(low)], axis=1)
    return jnp.concatenate([top, bottom], axis=0).astype(bfloat)


def gathered_parts(block):
    block = block.astype(floating)
    width = block.shape[1] // 2
    return block[:8, :width] + block[:8, width:] + block[8:, :width]


def read_scalars(block, count):
    lane = lax.broadcasted_iota(jnp.int32, block.shape, 1)
    return [jnp.sum(jnp.where(lane == place, block, 0.0)) for place in range(count)]


def rms_scale(values):
    return lax.rsqrt(jnp.mean(values * values, axis=-1, keepdims=True) + EPSILON)


def lane_mask(length):
    return lax.broadcasted_iota(jnp.int32, (length, PAIR), 1) < HEAD_DIM


def stack_heads(block, first):
    zero = jnp.zeros_like(block)
    return jnp.concatenate([jnp.where(first, block, zero), jnp.where(first, zero, block)], axis=0)


def gelu_wave(gate):
    return jnp.tanh(GELU_A * (gate + GELU_B * gate * gate * gate))


def relative(blocks, index):
    low = (index & 1) == 1
    high = (index >> 1) == 1
    once = [jnp.where(low, blocks[place ^ 1], blocks[place]) for place in range(4)]
    return [jnp.where(high, once[place ^ 2], once[place]) for place in range(4)]


def attention(q_ref, k_ref, v_ref, seg_ref, att_ref, p_ref):
    length = seg_ref.shape[1]
    rows = q_ref.shape[0] // length
    pairs = q_ref.shape[1] // PAIR
    first = lane_mask(length)
    later = lax.broadcasted_iota(jnp.int32, (length, length), 0)
    earlier = lax.broadcasted_iota(jnp.int32, (length, length), 1)
    for row in range(rows):
        documents = jnp.broadcast_to(seg_ref[row : row + 1, :], (length, length)).astype(floating)
        allowed = (earlier <= later) & (documents == documents.T)
        allowed = jnp.concatenate([allowed, allowed], axis=0)
        span = slice(row * length, (row + 1) * length)
        for pair in range(pairs):
            heads = slice(pair * PAIR, (pair + 1) * PAIR)
            stacked = stack_heads(q_ref[span, heads], first)
            scores = jnp.where(allowed, dot_t(stacked, k_ref[span, heads]) * SCALE, MASKED)
            powers = jnp.exp(scores - jnp.max(scores, axis=-1, keepdims=True))
            probs = powers / jnp.sum(powers, axis=-1, keepdims=True)
            if p_ref is not None:
                p_ref[row * pairs + pair] = probs
            mixed = dot(probs.astype(bfloat), v_ref[span, heads])
            att_ref[span, heads] = jnp.where(first, mixed[:length], mixed[length:]).astype(bfloat)


def in_hbm(value):
    return pltpu.with_memory_space_constraint(value, pltpu.MemorySpace.HBM)


def forward_lite_kernel(x_any, seg_any, mix_any, cor_any, ga_any, gf_any, wq, wk, wv, wo, wg, wu, wd,
                        out_ref, wq_s, wk_s, wv_s, wo_s, wg_s, wu_s, wd_s,
                        x_in, seg_ref, mix_ref, cor_ref, ga_ref, gf_ref, q_ref, k_ref, v_ref, act_ref,
                        nrm_ref, att_ref, nf_ref, acc, sem, small_sem):
    tokens, width = act_ref.shape
    chunk = width
    pieces = wg.shape[2] // chunk
    small = [
        pltpu.make_async_copy(source, target, small_sem.at[place])
        for place, (source, target) in enumerate(
            ((x_any, x_in), (mix_any, mix_ref), (ga_any, ga_ref), (seg_any, seg_ref), (gf_any, gf_ref), (cor_any, cor_ref))
        )
    ]
    pairs = [(wq, wq_s), (wk, wk_s), (wv, wv_s), (wo, wo_s)]
    for piece in range(pieces):
        span = pl.ds(piece * chunk, chunk)
        pairs += [
            (wg.at[:, :, span], wg_s.at[:, :, span]), (wu.at[:, :, span], wu_s.at[:, :, span]), (wd.at[:, span, :], wd_s.at[:, span, :])
        ]
    queue = [pltpu.make_async_copy(source, target, sem.at[place]) for place, (source, target) in enumerate(pairs)]
    for copy in small + queue[:AHEAD]:
        copy.start()
    state = [0]

    def arrive():
        queue[state[0]].wait()
        if state[0] + AHEAD < len(queue):
            queue[state[0] + AHEAD].start()
        state[0] += 1

    for copy in small:
        copy.wait()
    section = lax.axis_index("section")
    mix = [[mix_ref[0, i, j] for j in range(2)] for i in range(2)]
    cor = [cor_ref[0, i] for i in range(2)]
    xa = x_in[:, :width].astype(floating)
    xb = x_in[:, width:].astype(floating)
    own_a = jnp.where(section == 0, mix[0][0], mix[1][0])
    own_b = jnp.where(section == 0, mix[0][1], mix[1][1])
    active = jnp.where(section == 0, xa, xb) + (own_a * xa + own_b * xb)
    act_ref[...] = active
    nrm_ref[...] = (active * rms_scale(active) * ga_ref[...]).astype(bfloat)
    for weight, target in zip((wq_s, wk_s, wv_s), (q_ref, k_ref, v_ref)):
        arrive()
        target[...] = dot(nrm_ref[...], weight[0]).astype(bfloat)
    attention(q_ref, k_ref, v_ref, seg_ref, att_ref, None)
    arrive()
    middle = act_ref[...] + dot(att_ref[...], wo_s[0])
    acc[...] = middle - act_ref[...]
    nf_ref[...] = (middle * rms_scale(middle) * gf_ref[...]).astype(bfloat)
    for piece in range(pieces):
        span = slice(piece * chunk, (piece + 1) * chunk)
        arrive()
        gate = dot(nf_ref[...], wg_s[0, :, span])
        arrive()
        upward = dot(nf_ref[...], wu_s[0, :, span])
        hidden = (0.5 * gate * (1.0 + gelu_wave(gate)) * upward).astype(bfloat)
        arrive()
        acc[...] += dot(hidden, wd_s[0, span, :])
    out_ref[:tokens, :] = acc[...].astype(bfloat)
    out_ref[tokens:, :] = scalar_rows(mix[0] + mix[1] + cor, EXTRA, width)


def forward_lite(x_in, segments, mixing, correction, gain_attn, gain_ffn, weights):
    tokens = x_in.shape[0]
    width = gain_attn.shape[1]
    size = sum(weight.size for weight in weights)
    narrow = pltpu.VMEM((tokens, width), bfloat)
    wide = pltpu.VMEM((tokens, width), floating)
    args = (x_in, segments, mixing, correction, gain_attn, gain_ffn) + weights
    scratch = [
        pltpu.VMEM(x_in.shape, bfloat), pltpu.VMEM(segments.shape, jnp.int32), pltpu.SMEM(mixing.shape, floating),
        pltpu.SMEM(correction.shape, floating), pltpu.VMEM(gain_attn.shape, floating), pltpu.VMEM(gain_ffn.shape, floating),
        narrow, narrow, narrow, wide, narrow, narrow, narrow, wide,
    ]
    scratch += [pltpu.SemaphoreType.DMA((4 + 3 * (weights[4].shape[2] // width),)), pltpu.SemaphoreType.DMA((6,))]
    return pl.pallas_call(
        forward_lite_kernel,
        out_shape=[jax.ShapeDtypeStruct((tokens + EXTRA, width), bfloat)]
        + [jax.ShapeDtypeStruct(weight.shape, bfloat) for weight in weights],
        in_specs=[ANY] * len(args),
        out_specs=[VMEM] * 8,
        scratch_shapes=scratch,
        compiler_params=params(SCOPED),
        cost_estimate=cost(2 * tokens * size, 2 * size),
        name="forward_lite",
    )(*[in_hbm(one) for one in args])


def forward_kernel(fast, x_in, message, seg_ref, mix_ref, cor_ref, ga_ref, gf_ref, wq, wk, wv, wo, wg, wu, wd,
                   x_ref, out_ref, q_ref, k_ref, v_ref, p_ref, act_ref, mid_ref, one_ref, two_ref, chg_ref, *refs):
    kept = refs[:4]
    nf_ref = refs[-4]
    nrm_ref, att_ref, acc = refs[-3:]
    tokens, width = act_ref.shape
    chunk = width
    pieces = wg.shape[2] // chunk
    section = lax.axis_index("section")
    quarter = lax.axis_index("dp") & 3
    mix = [[mix_ref[0, i, j] for j in range(2)] for i in range(2)]
    cor = [cor_ref[0, i] for i in range(2)]
    xa = x_in[:, :width].astype(floating)
    xb = x_in[:, width:].astype(floating)
    got = read_scalars(message[tokens : tokens + EXTRA, :PAIR].astype(floating), 6)
    moved = message[:tokens, :].astype(floating)
    sent_a = (xa + (got[0] * xa + got[1] * xb) + got[4] * moved).astype(bfloat)
    sent_b = (xb + (got[2] * xa + got[3] * xb) + got[5] * moved).astype(bfloat)
    x_ref[:, :width] = jnp.where(section == 0, x_in[:, :width], sent_a)
    x_ref[:, width:] = jnp.where(section == 0, x_in[:, width:], sent_b)
    xa = x_ref[:, :width].astype(floating)
    xb = x_ref[:, width:].astype(floating)
    own_a = jnp.where(section == 0, mix[0][0], mix[1][0])
    own_b = jnp.where(section == 0, mix[0][1], mix[1][1])
    active = jnp.where(section == 0, xa, xb) + (own_a * xa + own_b * xb)
    act_ref[...] = active
    nrm_ref[...] = (active * rms_scale(active) * ga_ref[...]).astype(bfloat)
    for weight, target in zip((wq, wk, wv), (q_ref, k_ref, v_ref)):
        target[...] = dot(nrm_ref[...], weight[0]).astype(bfloat)

    def keep_quarters(values, base):
        share = width // 16
        for far in range(4):
            blocks = [values[:, (4 * far + near) * share : (4 * far + near + 1) * share] for near in range(4)]
            for slot, block in enumerate(relative(blocks, quarter)):
                kept[slot][:, base + far * share : base + (far + 1) * share] = block

    attention(q_ref, k_ref, v_ref, seg_ref, att_ref, p_ref)
    middle = act_ref[...] + dot(att_ref[...], wo[0])
    mid_ref[...] = middle
    nf_ref[...] = (middle * rms_scale(middle) * gf_ref[...]).astype(bfloat)
    if fast:
        keep_quarters(att_ref[...], width)
        keep_quarters(nrm_ref[...], width + width // 4)
        for slot in (1, 2):
            kept[slot][:, width + width // 2 :] = nf_ref[...]
    else:
        kept[1][...] = nrm_ref[...]
        kept[2][...] = att_ref[...]
    for piece in range(pieces):
        span = slice(piece * chunk, (piece + 1) * chunk)
        gate = dot(nf_ref[...], wg[0, :, span])
        upward = dot(nf_ref[...], wu[0, :, span])
        wave = gelu_wave(gate)
        half = 0.5 * (1.0 + wave)
        value = gate * half
        hidden = (value * upward).astype(bfloat)
        slope = half + 0.5 * gate * (1.0 - wave * wave) * (GELU_A * (1.0 + 3.0 * GELU_B * gate * gate))
        one_ref[piece] = upward * slope
        two_ref[piece] = value
        if fast:
            share = chunk // 4
            blocks = [hidden[:, near * share : (near + 1) * share] for near in range(4)]
            for slot, block in enumerate(relative(blocks, quarter)):
                kept[slot][:, piece * share : (piece + 1) * share] = block
        else:
            kept[0][:, span] = hidden
        down = dot(hidden, wd[0, span, :])
        if piece == 0:
            acc[...] = down
        else:
            acc[...] += down
    change = mid_ref[...] + acc[...] - act_ref[...]
    chg_ref[...] = change
    xa = x_ref[:, :width].astype(floating)
    xb = x_ref[:, width:].astype(floating)
    out_ref[0, :, :width] = (xa + (mix[0][0] * xa + mix[0][1] * xb) + cor[0] * change).astype(bfloat)
    out_ref[0, :, width:] = (xb + (mix[1][0] * xa + mix[1][1] * xb) + cor[1] * change).astype(bfloat)


def forward(fast, x_in, message, segments, mixing, correction, gain_attn, gain_ffn, weights):
    tokens = x_in.shape[0]
    length = segments.shape[1]
    width = gain_attn.shape[1]
    hidden_width = weights[4].shape[2]
    size = sum(weight.size for weight in weights)
    shape = jax.ShapeDtypeStruct
    narrow = ((tokens, width), bfloat)
    wide = ((tokens, width), floating)
    probs = ((tokens // length * (width // PAIR), 2 * length, length), floating)
    if fast:
        short, long = (((tokens, columns), bfloat) for columns in (width + width // 2, 2 * width + width // 2))
        kept = [short, long, long, short, narrow]
    else:
        kept = [((tokens, hidden_width), bfloat), narrow, narrow, narrow]
    ffn = ((hidden_width // width, tokens, width), floating)
    outs = [((tokens, 2 * width), bfloat), ((1, tokens, 2 * width), bfloat), narrow, narrow, narrow, probs, wide, wide,
            ffn, ffn, wide] + kept
    return pl.pallas_call(
        lambda *refs: forward_kernel(fast, *refs),
        out_shape=[shape(*one) for one in outs],
        in_specs=[VMEM, VMEM, VMEM, SMEM, SMEM, VMEM, VMEM] + [VMEM] * 7,
        out_specs=[VMEM] * len(outs),
        scratch_shapes=[pltpu.VMEM(*narrow)] * 2 + [pltpu.VMEM(*wide)],
        compiler_params=params(SCOPED),
        cost_estimate=cost(2 * tokens * size, 2 * size),
        name="forward_full",
    )(x_in, message, segments, mixing, correction, gain_attn, gain_ffn, *weights)


def start_rows(message, grad_ref, counts_ref, cor_ref, g_ref, low_ref):
    tokens, width = low_ref.shape
    rows = counts_ref.shape[0]
    length = tokens // rows
    section = lax.axis_index("section")
    if message is not None:
        got = read_scalars(message[tokens : tokens + EXTRA, :PAIR].astype(floating), 4)
    place = lax.broadcasted_iota(jnp.int32, (length, width), 0)
    for row in range(rows):
        span = slice(row * length, (row + 1) * length)
        valid = place < counts_ref[row]
        own_a = jnp.where(valid, grad_ref[span, :width].astype(floating), 0.0)
        own_b = jnp.where(valid, grad_ref[span, width:].astype(floating), 0.0)
        if message is not None:
            later_b = own_b + message[span, :].astype(floating)
            far_a = own_a + (got[0] * own_a + got[2] * later_b)
            far_b = later_b + (got[1] * own_a + got[3] * later_b)
            own_a = jnp.where(section == 0, far_a, own_a).astype(bfloat).astype(floating)
            own_b = jnp.where(section == 0, far_b, own_b).astype(bfloat).astype(floating)
        g_ref[span, :width] = own_a.astype(bfloat)
        g_ref[span, width:] = own_b.astype(bfloat)
        low_ref[span, :] = (cor_ref[0, 0] * own_a + cor_ref[0, 1] * own_b).astype(bfloat)


def start(message, out_grad, counts, correction, before):
    tokens = out_grad.shape[0]
    width = message.shape[1]
    shape = jax.ShapeDtypeStruct
    return pl.pallas_call(
        lambda *refs: start_rows(*refs[:4], *refs[-2:]),
        out_shape=[shape((tokens, 2 * width), bfloat), shape((tokens, width), bfloat)],
        in_specs=[VMEM, VMEM, SMEM, SMEM] + [ANY] * len(before),
        out_specs=[VMEM, VMEM],
        compiler_params=params(SCOPED),
        cost_estimate=cost(tokens * width * 20, tokens * width * 12),
        name="backward_start",
    )(message, out_grad, counts, correction, *before)


def norm_backward(values, gain, grad_normed, with_gain):
    inverse = rms_scale(values)
    grad_gain = jnp.sum(grad_normed * values * inverse, axis=0, keepdims=True) if with_gain else None
    weighted = grad_normed * gain
    grad_values = inverse * weighted - values * inverse**3 * jnp.mean(weighted * values, axis=-1, keepdims=True)
    return grad_gain, grad_values


def ffn_steps(low_ref, one, two, wg, wu, wd, acc, emit):
    width = wd.shape[2]
    quarter = lax.axis_index("dp") & 3
    for step in range(4):
        piece = (3 - step) ^ quarter
        span = pl.ds(pl.multiple_of(piece * width, width), width)
        grad_hidden = dot_t(low_ref[...], wd[0, span, :])
        dgate = (grad_hidden * one[piece]).astype(bfloat)
        dup = (grad_hidden * two[piece]).astype(bfloat)
        emit(3 - step, dgate, dup)
        total = dot_t(dgate, wg[0, :, span]) + dot_t(dup, wu[0, :, span])
        if step == 0:
            acc[...] = total
        else:
            acc[...] += total


def ffn_kernel(g_in, low_ref, cor_ref, gf_ref, mid_ref, one, two, wg, wu, wd, *refs):
    slots = refs[-12:-4]
    dmid_ref, datt_ref, gain_ref, acc = refs[-4:]
    width = gf_ref.shape[1]

    def emit(slot, dgate, dup):
        slots[slot][...] = dgate
        slots[4 + slot][...] = dup

    ffn_steps(low_ref, one, two, wg, wu, wd, acc, emit)
    grad_gain, grad_values = norm_backward(mid_ref[...], gf_ref[...], acc[...], True)
    block = cor_ref[0, 0] * g_in[:, :width].astype(floating) + cor_ref[0, 1] * g_in[:, width:].astype(floating)
    grad_middle = block + grad_values
    dmid_ref[...] = grad_middle
    datt_ref[...] = grad_middle.astype(bfloat)
    gain_ref[...] = grad_gain


def ffn_backward(g_in, low, correction, gain_ffn, middle, one, two, before, weights):
    tokens = g_in.shape[0]
    width = gain_ffn.shape[1]
    shape = jax.ShapeDtypeStruct
    return pl.pallas_call(
        ffn_kernel,
        out_shape=[shape((tokens, width), bfloat)] * 8
        + [shape((tokens, width), floating), shape((tokens, width), bfloat), shape((1, width), floating)],
        in_specs=[VMEM, VMEM, SMEM] + [VMEM] * 7 + [ANY] * len(before),
        out_specs=[VMEM] * 11,
        scratch_shapes=[pltpu.VMEM((tokens, width), floating)],
        compiler_params=params(SCOPED),
        cost_estimate=cost(2 * tokens * 3 * weights[4].size, 2 * 3 * weights[4].size),
        name="backward_ffn",
    )(g_in, low, correction, gain_ffn, middle, one, two, *weights[4:], *before)


def attn_steps(q_ref, k_ref, v_ref, p_ref, do_ref, parts):
    tokens, width = do_ref.shape
    length = p_ref.shape[2]
    rows = tokens // length
    pairs = width // PAIR
    first = lane_mask(length)
    for row in range(rows):
        span = slice(row * length, (row + 1) * length)
        for pair in range(pairs):
            heads = slice(pair * PAIR, (pair + 1) * PAIR)
            probs = p_ref[row * pairs + pair]
            grad_out = stack_heads(do_ref[span, heads], first)
            grad_value = t_dot(probs.astype(bfloat), grad_out)
            grad_probs = dot_t(grad_out, v_ref[span, heads])
            carried = jnp.sum(probs * grad_probs, axis=-1, keepdims=True)
            grad_scores = (probs * (grad_probs - carried)).astype(bfloat)
            grad_query = dot(grad_scores, k_ref[span, heads])
            grad_query = jnp.where(first, grad_query[:length], grad_query[length:])
            grad_key = t_dot(grad_scores, stack_heads(q_ref[span, heads], first))
            for (part, base), value in zip(parts, (grad_query * SCALE, grad_key * SCALE, grad_value)):
                part[span, base + pair * PAIR : base + (pair + 1) * PAIR] = value.astype(bfloat)


def normed_grad(parts, rows, width, wq, wk, wv):
    return sum(dot_t(part[:rows, base : base + width], weight[0]) for (part, base), weight in zip(parts, (wq, wk, wv)))


def attn_kernel(datt_ref, q_ref, k_ref, v_ref, p_ref, gfg_ref, ga_ref, x_ref, g_in, dmid_ref, act_ref, chg_ref, mix_ref, cor_ref,
                wq, wk, wv, wo, before,
                grad_ref, right_ref, small_ref, do_ref):
    tokens, width = datt_ref.shape
    right_ref[:tokens, :width] = datt_ref[...]
    do_ref[...] = dot_t(datt_ref[...], wo[0]).astype(bfloat)
    parts = (right_ref, width), (right_ref, 2 * width), (right_ref, 3 * width)
    attn_steps(q_ref, k_ref, v_ref, p_ref, do_ref, parts)
    grad_normed = normed_grad(parts, tokens, width, wq, wk, wv)
    grad_gain, grad_values = norm_backward(act_ref[...], ga_ref[...], grad_normed, True)
    section = lax.axis_index("section")
    mix = [[mix_ref[0, i, j] for j in range(2)] for i in range(2)]
    cor = [cor_ref[0, i] for i in range(2)]
    out_a = g_in[:, :width].astype(floating)
    out_b = g_in[:, width:].astype(floating)
    grad_active = dmid_ref[...] + grad_values - (cor[0] * out_a + cor[1] * out_b)
    pred_a = out_a + jnp.where(section == 0, grad_active, 0.0)
    pred_b = out_b + jnp.where(section == 0, 0.0, grad_active)
    grad_ref[0, :, :width] = (pred_a + (mix[0][0] * pred_a + mix[1][0] * pred_b)).astype(bfloat)
    grad_ref[0, :, width:] = (pred_b + (mix[0][1] * pred_a + mix[1][1] * pred_b)).astype(bfloat)
    xa = x_ref[:, :width].astype(floating)
    xb = x_ref[:, width:].astype(floating)
    small_ref[0:1, :] = grad_gain
    small_ref[1:2, :] = gfg_ref[...]
    place = 2
    for pred in (pred_a, pred_b):
        for state in (xa, xb):
            small_ref[place : place + 1, :] = jnp.sum(pred * state, axis=0, keepdims=True)
            place += 1
    for out in (out_a, out_b):
        small_ref[place : place + 1, :] = jnp.sum(out * chg_ref[...], axis=0, keepdims=True)
        place += 1
    right_ref[tokens:, : 2 * width] = spread(small_ref[...])
    right_ref[tokens:, 2 * width :] = jnp.zeros((right_ref.shape[0] - tokens, 2 * width), bfloat)


def attn_backward(x, g_in, grad_middle, grad_att, active, change, queries, key_rows, value_rows, probs, ffn_gain, gain_attn,
                  mixing, correction, before, weights):
    tokens, width = active.shape
    shape = jax.ShapeDtypeStruct
    return pl.pallas_call(
        attn_kernel,
        out_shape=[
            shape((1, tokens, 2 * width), bfloat), shape((tokens + EXTRA, 4 * width), bfloat), shape((8, width), floating),
        ],
        in_specs=[VMEM] * 12 + [SMEM] * 2 + [VMEM] * 4 + [ANY],
        out_specs=[VMEM] * 3,
        scratch_shapes=[pltpu.VMEM((tokens, width), bfloat)],
        compiler_params=params(SCOPED),
        cost_estimate=cost(2 * tokens * 5 * weights[0].size, 2 * 4 * weights[0].size),
        name="backward_attn",
    )(grad_att, queries, key_rows, value_rows, probs, ffn_gain, gain_attn, x, g_in, grad_middle, active, change,
      mixing, correction, *weights[:4], before)


def relay_kernel(grad_in, counts_ref, cor_ref, mix_ref, gf_ref, ga_ref, one, two, mid_ref, q_ref, k_ref, v_ref, p_ref, act_ref,
                 wq, wk, wv, wo, wg, wu, wd,
                 msg_ref,
                 acc, g_in, low_ref, do_ref, dqkv_ref):
    tokens, width = low_ref.shape
    start_rows(None, grad_in, counts_ref, cor_ref, g_in, low_ref)
    ffn_steps(low_ref, one, two, wg, wu, wd, acc, lambda *parts: None)
    grad_values = norm_backward(mid_ref[...], gf_ref[...], acc[...], False)[1]
    cor = [cor_ref[0, i] for i in range(2)]
    block = cor[0] * g_in[:, :width].astype(floating) + cor[1] * g_in[:, width:].astype(floating)
    acc[...] = block + grad_values
    do_ref[...] = dot_t(acc[...].astype(bfloat), wo[0]).astype(bfloat)
    parts = (dqkv_ref, 0), (dqkv_ref, width), (dqkv_ref, 2 * width)
    attn_steps(q_ref, k_ref, v_ref, p_ref, do_ref, parts)
    grad_normed = normed_grad(parts, tokens, width, wq, wk, wv)
    grad_values = norm_backward(act_ref[...], ga_ref[...], grad_normed, False)[1]
    block = cor[0] * g_in[:, :width].astype(floating) + cor[1] * g_in[:, width:].astype(floating)
    msg_ref[:tokens, :] = (acc[...] + grad_values - block).astype(bfloat)
    mix = [[mix_ref[0, i, j] for j in range(2)] for i in range(2)]
    msg_ref[tokens:, :] = scalar_rows(mix[0] + mix[1], EXTRA, width)


def relay_backward(out_grad, counts, correction, mixing, gain_ffn, gain_attn, one, two, middle, queries, key_rows, value_rows,
                   probs, active, weights):
    tokens, width = active.shape
    shape = jax.ShapeDtypeStruct
    narrow = pltpu.VMEM((tokens, width), bfloat)
    wide = pltpu.VMEM((tokens, width), floating)
    size = sum(weight.size for weight in weights)
    return pl.pallas_call(
        relay_kernel,
        out_shape=shape((tokens + EXTRA, width), bfloat),
        in_specs=[VMEM, SMEM, SMEM, SMEM] + [VMEM] * 17,
        out_specs=VMEM,
        scratch_shapes=[wide, pltpu.VMEM((tokens, 2 * width), bfloat), narrow, narrow, pltpu.VMEM((tokens, 3 * width), bfloat)],
        compiler_params=params(SCOPED),
        cost_estimate=cost(2 * tokens * size, 2 * size),
        name="backward_relay",
    )(out_grad, counts, correction, mixing, gain_ffn, gain_attn, one, two, middle, queries, key_rows, value_rows, probs, active,
      *weights)


def quarter_kernel(base, products, block, refs):
    count = 4
    lefts = refs[:count]
    rights = refs[count : 2 * count]
    send_ref, keep_ref = refs[-2:]
    quarter_parts(base, products, block, lefts, rights, send_ref, keep_ref)


def quarter_parts(base, products, block, lefts, rights, send_ref, keep_ref):
    tokens = lefts[0].shape[0]
    index = lax.axis_index("dp")
    near = (index >> 2) & 1
    far = (index >> 3) & 1
    for left_at, left_wide, right_at, right_wide in products:
        rows = slice(left_at, left_at + left_wide)
        columns = slice(right_at, right_at + right_wide)
        total = sum(t_dot(left[:, rows], right[:tokens, columns]) for left, right in zip(lefts, rights))
        span = slice(right_at - base, right_at - base + right_wide)
        for place in range(4):
            part = total[place * block : (place + 1) * block, :]
            slot = (place >> 1) ^ far
            mine = (place & 1) == near

            @pl.when(mine)
            def _():
                keep_ref[slot, :, span] = part

            @pl.when(jnp.logical_not(mine))
            def _():
                send_ref[slot, :, span] = part.astype(bfloat)


def first_kernel(products, block, refs):
    lefts, rights = refs[:4], refs[4:8]
    send_ref, keep_ref, small_ref, stage = refs[-4:]
    quarter_parts(0, products, block, lefts, rights, stage, keep_ref)
    tokens = lefts[0].shape[0]
    send_ref[:block, :] = stage[0]
    send_ref[block : 2 * block, :] = stage[1]
    small = sum(gathered_parts(right[tokens:, : keep_ref.shape[2]]) for right in rights)
    small_ref[...] = small
    send_ref[2 * block :, :] = spread(small)


def first_product(lefts, rights, products, block, before):
    wide = rights[0].shape[1] // 2
    shape = jax.ShapeDtypeStruct
    return pl.pallas_call(
        lambda *refs: first_kernel(products, block, refs),
        out_shape=[shape((2 * block + EXTRA, wide), bfloat), shape((2, block, wide), floating), shape((8, wide // 2), floating)],
        in_specs=[VMEM] * 8 + [ANY] * len(before),
        out_specs=[VMEM] * 3,
        scratch_shapes=[pltpu.VMEM((2, block, wide), bfloat)],
        compiler_params=params(SCOPED),
        cost_estimate=cost(wide, wide),
        name="product_attn_first",
    )(*lefts, *rights, *before)


def first_sum_kernel(keep_ref, came_ref, small_ref, held_ref, passed_ref, sums_ref):
    block = held_ref.shape[0]
    held_ref[...] = keep_ref[0] + came_ref[:block, :].astype(floating)
    passed_ref[:block, :] = (keep_ref[1] + came_ref[block : 2 * block, :].astype(floating)).astype(bfloat)
    small = small_ref[...] + gathered_parts(came_ref[2 * block :, :])
    sums_ref[...] = small
    passed_ref[block:, :] = spread(small)


def first_sum(keep, came, small):
    _, block, wide = keep.shape
    shape = jax.ShapeDtypeStruct
    return pl.pallas_call(
        first_sum_kernel,
        out_shape=[shape((block, wide), floating), shape((block + EXTRA, wide), bfloat), shape(small.shape, floating)],
        in_specs=[VMEM] * 3,
        out_specs=[VMEM] * 3,
        compiler_params=params(SCOPED),
        cost_estimate=cost(wide, wide),
        name="first_sum",
    )(keep, came, small)


def first_end_kernel(held_ref, came_ref, small_ref, left_ref, right_ref, sums_ref):
    block, wide = held_ref.shape
    left_ref[0] = held_ref[:, : wide // 2] + came_ref[:block, : wide // 2].astype(floating)
    right_ref[0] = held_ref[:, wide // 2 :] + came_ref[:block, wide // 2 :].astype(floating)
    sums_ref[...] = small_ref[...] + gathered_parts(came_ref[block:, :])


def first_end(held, came, small):
    block, wide = held.shape
    shape = jax.ShapeDtypeStruct
    return pl.pallas_call(
        first_end_kernel,
        out_shape=[shape((1, block, wide // 2), floating)] * 2 + [shape(small.shape, floating)],
        in_specs=[VMEM] * 3,
        out_specs=[VMEM] * 3,
        compiler_params=params(SCOPED),
        cost_estimate=cost(wide, wide),
        name="first_end",
    )(held, came, small)


def quarter_product(lefts, rights, products, block, before, name):
    base = products[0][2]
    wide = sum(one[3] for one in products)
    shape = jax.ShapeDtypeStruct
    flops = sum(2 * 4 * lefts[0].shape[0] * one[1] * one[3] for one in products)
    return pl.pallas_call(
        lambda *refs: quarter_kernel(base, products, block, refs),
        out_shape=[shape((2, block, wide), bfloat), shape((2, block, wide), floating)],
        in_specs=[VMEM] * 8 + [ANY] * len(before),
        out_specs=[VMEM, VMEM],
        compiler_params=params(SCOPED),
        cost_estimate=cost(flops, 12 * block * wide),
        name=name,
    )(*lefts, *rights, *before)


def assemble_kernel(own, one, two, three, gate_ref, up_ref):
    quarter = lax.axis_index("dp") & 3
    width = own.shape[1] // 2
    for slot, piece in enumerate((own, one, two, three)):
        span = pl.ds(pl.multiple_of((slot ^ quarter) * width, width), width)
        gate_ref[0, :, span] = piece[:, :width].astype(floating)
        up_ref[0, :, span] = piece[:, width:].astype(floating)


def assemble(pieces):
    share, double = pieces[0].shape
    shape = jax.ShapeDtypeStruct((1, share, 2 * double), floating)
    return pl.pallas_call(
        assemble_kernel,
        out_shape=[shape, shape],
        in_specs=[VMEM] * 4,
        out_specs=[VMEM] * 2,
        compiler_params=params(SCOPED),
        cost_estimate=cost(share * double * 4, share * double * 24),
        name="assemble",
    )(*pieces)


def exchange(value, flips):
    count = lax.axis_size("dp")
    return lax.ppermute(value, "dp", [(source, source ^ flips) for source in range(count)])


def relative_rows(matrix, order, index):
    bits = len(order)
    block = matrix.shape[0] >> bits
    split = matrix.reshape((2,) * bits + (block, matrix.shape[1]))
    axes = [bits - 1 - bit for bit in order]
    split = jnp.transpose(split, axes + [bits, bits + 1])
    for axis, bit in enumerate(order):
        split = jnp.where((index >> bit) & 1 == 1, jnp.flip(split, axis), split)
    return split.reshape(matrix.shape)


def scatter_sum(left, right, order):
    total = left.shape[0]
    arrived = []
    for step in range(len(order) + 1):
        low = total >> (step + 1) if step < len(order) else 0
        high = total >> step
        part = dot(left[low:high], right)
        for other in arrived:
            part = part + other[low:high].astype(floating)
        if step == len(order):
            return part
        arrived.append(exchange(part.astype(bfloat), 1 << order[step]))


def halving_grads(kept, low, slots, right, index, count):
    width = low.shape[1]
    order = list(range(count.bit_length() - 1))
    hidden, normed, attended, normed_ffn = (relative_rows(one.T, order, index) for one in kept)
    quarter = index & 3
    places = jnp.arange(4) ^ quarter
    dgate = jnp.concatenate(list(jnp.stack(slots[:4])[places]), axis=1)
    dup = jnp.concatenate(list(jnp.stack(slots[4:])[places]), axis=1)
    grad_down = scatter_sum(hidden, low, order)
    grad_gate = scatter_sum(normed_ffn, dgate, order)
    grad_up = scatter_sum(normed_ffn, dup, order)
    grad_out = scatter_sum(attended, right[:, :width], order)
    grad_qkv = scatter_sum(normed, right[:, width:], order)
    grads = [grad_down, grad_gate, grad_up, grad_out] + [grad_qkv[:, place * width : (place + 1) * width] for place in range(3)]
    return [one[None] for one in grads]


def after(values, *earlier):
    return lax.optimization_barrier((values, earlier))[0]


def gather_start(value):
    return [value, exchange(value, 1), exchange(value, 2)]


def gather_end(pieces, *earlier):
    return pieces + [exchange(after(pieces[2], *earlier), 1)]


def swapped(pieces):
    return [pieces[0]] + [exchange(pieces[flips], flips) for flips in (1, 2, 3)]


def sum_once(pair, *earlier):
    send, keep = pair
    arrived = after(exchange(send, 4), *earlier)
    return keep[0] + arrived[0].astype(floating), (keep[1] + arrived[1].astype(floating)).astype(bfloat)


def sum_twice(held, passed, *earlier):
    return held + after(exchange(passed, 8), *earlier).astype(floating)


def sum_over(value, bits):
    for bit in range(bits):
        value = value + exchange(value, 1 << bit)
    return value


def quarter_grads(normed_ffn, kept, slots, right, down_pair, index):
    width = normed_ffn[0].shape[1]
    share = width // 16
    block = 4 * share
    whole = [(0, width, 0, width)]
    gates = swapped(slots[:4])
    ups = swapped(list(after(slots[4:], right)))
    down_sums = sum_once(down_pair, right)
    gate_pair = quarter_product(normed_ffn, gates, whole, block, [right, down_sums[1]], "product_gate")
    grad_down = sum_twice(*down_sums)
    rights = gather_start(after(right, gate_pair[0], grad_down, ups[1:]))
    gate_sums = sum_once(gate_pair)
    up_pair = quarter_product(normed_ffn, ups, whole, block, [gate_sums[1], grad_down], "product_up")
    up_sums = sum_once(up_pair)
    gate_tile = sum_twice(*gate_sums).astype(bfloat)
    rights = gather_end(rights, up_sums[1], gate_tile)
    first_products = [(width, block, 0, width), (width + block, block, width, width)]
    first_send, first_keep, small = first_product(kept, rights, first_products, share, [up_sums[1], gate_tile])
    up_tile = sum_twice(*up_sums).astype(bfloat)
    second_products = [(width + block, block, 2 * width, 2 * width)]
    second_pair = quarter_product(kept, rights, second_products, share, [first_keep, up_tile], "product_attn_second")
    held, passed, small = first_sum(first_keep, after(exchange(first_send, 4), second_pair[0]), small)
    quarter = index & 3
    gate_tile, up_tile = after((gate_tile, up_tile), passed)
    pieces = [
        jnp.concatenate(
            [lax.dynamic_slice_in_dim(tile, (slot ^ quarter) * share, share, axis=0) for tile in (gate_tile, up_tile)], axis=1)
        for slot in range(4)
    ]
    pieces = swapped(pieces)
    grad_out, grad_query, small = first_end(held, exchange(passed, 8), small)
    second_sums = sum_once(second_pair, small)
    grad_gate, grad_up = assemble(list(after(pieces, second_sums[1])))
    held, passed = second_sums
    passed = exchange(passed, 8)
    grads = [grad_down[None], grad_gate, grad_up, grad_out, grad_query]
    for span in (slice(0, width), slice(width, 2 * width)):
        grads.append((held[:, span] + passed[:, span].astype(floating))[None])
    return grads, small


def local(states_in, out_grad, counts, segments, mixing, correction, gain_attn, w_query, w_key, w_value, w_attn_out, gain_ffn,
          w_gate, w_up, w_down):
    weights = (w_query, w_key, w_value, w_attn_out, w_gate, w_up, w_down)
    width = gain_attn.shape[1]
    index = lax.axis_index("dp")
    count = lax.axis_size("dp")
    fast = count == 16
    message, *weights = forward_lite(states_in, segments, mixing, correction, gain_attn, gain_ffn, weights)
    message = lax.ppermute(message, "section", [(0, 1), (1, 0)])
    (x, states, queries, key_rows, value_rows, probs, active, middle, one, two, change, *kept) = forward(
        fast, states_in, message, segments, mixing, correction, gain_attn, gain_ffn, weights)
    before = []
    if fast:
        kept, normed_ffn = swapped(kept[:4]), kept[4]
        before = kept[1:]
    message = relay_backward(out_grad, counts, correction, mixing, gain_ffn, gain_attn, one, two, middle, queries, key_rows,
                             value_rows, probs, active, weights)
    message = lax.ppermute(message, "section", [(0, 1), (1, 0)])
    g_in, low = start(message, out_grad, counts, correction, [])
    *slots, grad_middle, grad_att, ffn_gain = ffn_backward(g_in, low, correction, gain_ffn, middle, one, two, before, weights)
    before = slots[0]
    if fast:
        lows = gather_end(gather_start(low), before)
        beside, across = (one[:, width + width // 2 :] for one in kept[1:3])
        normed_ffn = gather_end([normed_ffn, beside, across], before)
        down_pair = quarter_product(kept, lows, [(0, width, 0, width)], width // 4, [before], "product_down")
        before = down_pair[0]
    state_grads, right, small = attn_backward(x, g_in, grad_middle, grad_att, active, change, queries, key_rows, value_rows, probs,
                                              ffn_gain, gain_attn, mixing, correction, before, weights)
    if fast:
        grads, small = quarter_grads(normed_ffn, kept, slots, right, down_pair, index)
    else:
        grads = halving_grads(kept, low, slots, right[: low.shape[0]], index, count)
        small = sum_over(small, count.bit_length() - 1)
    grad_down, grad_gate, grad_up, grad_out, grad_query, grad_key, grad_value = grads
    share = width // count
    gains = lax.dynamic_slice(small, (0, index * share), (2, share))
    sums = jnp.sum(small[2:], axis=1)
    return (
        states,
        state_grads,
        sums[:4].reshape(1, 2, 2),
        sums[4:].reshape(1, 2),
        gains[0:1],
        grad_query,
        grad_key,
        grad_value,
        grad_out,
        gains[1:2],
        grad_gate,
        grad_up,
        grad_down,
    )


def solution(mesh):
    rows = P("dp", None)
    matrix = P("section", None, None)
    vector = P("section", None)
    share = P("section", "dp", None)
    gain_share = P("section", "dp")
    in_specs = (rows, rows, P("dp"), rows, matrix, vector, vector, matrix, matrix, matrix, matrix, vector, matrix, matrix, matrix)
    out_specs = (share, share, matrix, vector, gain_share, share, share, share, share, gain_share, share, share, share)
    return jax.shard_map(local, mesh=mesh, in_specs=in_specs, out_specs=out_specs, check_vma=False)
```

```python
import functools

import jax
import jax.numpy as jnp
from jax import lax
from jax.experimental import pallas as pl
from jax.experimental.pallas import tpu as pltpu
from jax.sharding import PartitionSpec as P

HEAD_DIM = 64
PAIR = 2 * HEAD_DIM
EPSILON = 1e-06
MASKED = -1e30
SCALE = HEAD_DIM ** (-0.5)
GELU_A = 0.7978845608028654
GELU_B = 0.044715
EXTRA = 16
AHEAD = 3
SCOPED = 12
bfloat = jnp.bfloat16
floating = jnp.float32

VMEM = pl.BlockSpec(memory_space=pltpu.VMEM)
SMEM = pl.BlockSpec(memory_space=pltpu.SMEM)
ANY = pl.BlockSpec(memory_space=pltpu.MemorySpace.HBM)


def dot(a, b):
    return jnp.dot(a, b, preferred_element_type=floating)


def dot_t(a, b):
    return lax.dot_general(a, b, (((1,), (1,)), ((), ())), preferred_element_type=floating)


def t_dot(a, b):
    return lax.dot_general(a, b, (((0,), (0,)), ((), ())), preferred_element_type=floating)


def params(mebibytes):
    return pltpu.CompilerParams(vmem_limit_bytes=mebibytes * 1024 * 1024)


def cost(flops, moved):
    return pl.CostEstimate(flops=flops // 1000, bytes_accessed=moved // 1000, transcendentals=0)


def scalar_rows(values, rows, width):
    lane = lax.broadcasted_iota(jnp.int32, (rows, width), 1)
    row = lax.broadcasted_iota(jnp.int32, (rows, width), 0)
    whole = jnp.zeros((rows, width), floating)
    for place, value in enumerate(values):
        whole = jnp.where(lane == place, value, whole)
    high = whole.astype(bfloat).astype(floating)
    middle = (whole - high).astype(bfloat).astype(floating)
    low = whole - high - middle
    part = jnp.where(row == 0, high, jnp.where(row == 1, middle, jnp.where(row == 2, low, 0.0)))
    return part.astype(bfloat)


def spread(value):
    high = value.astype(bfloat).astype(floating)
    middle = (value - high).astype(bfloat).astype(floating)
    low = value - high - middle
    top = jnp.concatenate([high, middle], axis=1)
    bottom = jnp.concatenate([low, jnp.zeros_like(low)], axis=1)
    return jnp.concatenate([top, bottom], axis=0).astype(bfloat)


def gathered_parts(block):
    block = block.astype(floating)
    width = block.shape[1] // 2
    return block[:8, :width] + block[:8, width:] + block[8:, :width]


def read_scalars(block, count):
    lane = lax.broadcasted_iota(jnp.int32, block.shape, 1)
    return [jnp.sum(jnp.where(lane == place, block, 0.0)) for place in range(count)]


def rms_scale(values):
    return lax.rsqrt(jnp.mean(values * values, axis=-1, keepdims=True) + EPSILON)


def lane_mask(length):
    return lax.broadcasted_iota(jnp.int32, (length, PAIR), 1) < HEAD_DIM


def stack_heads(block, first):
    zero = jnp.zeros_like(block)
    return jnp.concatenate([jnp.where(first, block, zero), jnp.where(first, zero, block)], axis=0)


def gelu_wave(gate):
    return jnp.tanh(GELU_A * (gate + GELU_B * gate * gate * gate))


def relative(blocks, index):
    low = (index & 1) == 1
    high = (index >> 1) == 1
    once = [jnp.where(low, blocks[place ^ 1], blocks[place]) for place in range(4)]
    return [jnp.where(high, once[place ^ 2], once[place]) for place in range(4)]


def attention(q_ref, k_ref, v_ref, seg_ref, att_ref, p_ref):
    length = seg_ref.shape[1]
    rows = q_ref.shape[0] // length
    pairs = q_ref.shape[1] // PAIR
    first = lane_mask(length)
    later = lax.broadcasted_iota(jnp.int32, (length, length), 0)
    earlier = lax.broadcasted_iota(jnp.int32, (length, length), 1)
    for row in range(rows):
        documents = jnp.broadcast_to(seg_ref[row : row + 1, :], (length, length)).astype(floating)
        allowed = (earlier <= later) & (documents == documents.T)
        allowed = jnp.concatenate([allowed, allowed], axis=0)
        span = slice(row * length, (row + 1) * length)
        for pair in range(pairs):
            heads = slice(pair * PAIR, (pair + 1) * PAIR)
            stacked = stack_heads(q_ref[span, heads], first)
            scores = jnp.where(allowed, dot_t(stacked, k_ref[span, heads]) * SCALE, MASKED)
            powers = jnp.exp(scores - jnp.max(scores, axis=-1, keepdims=True))
            probs = powers / jnp.sum(powers, axis=-1, keepdims=True)
            if p_ref is not None:
                p_ref[row * pairs + pair] = probs
            mixed = dot(probs.astype(bfloat), v_ref[span, heads])
            att_ref[span, heads] = jnp.where(first, mixed[:length], mixed[length:]).astype(bfloat)


def in_hbm(value):
    return pltpu.with_memory_space_constraint(value, pltpu.MemorySpace.HBM)


def forward_lite_kernel(x_any, seg_any, mix_any, cor_any, ga_any, gf_any, wq, wk, wv, wo, wg, wu, wd,
                        out_ref, wq_s, wk_s, wv_s, wo_s, wg_s, wu_s, wd_s,
                        x_in, seg_ref, mix_ref, cor_ref, ga_ref, gf_ref, q_ref, k_ref, v_ref, act_ref,
                        nrm_ref, att_ref, nf_ref, acc, sem, small_sem):
    tokens, width = act_ref.shape
    chunk = width
    pieces = wg.shape[2] // chunk
    small = [
        pltpu.make_async_copy(source, target, small_sem.at[place])
        for place, (source, target) in enumerate(
            ((x_any, x_in), (mix_any, mix_ref), (ga_any, ga_ref), (seg_any, seg_ref), (gf_any, gf_ref), (cor_any, cor_ref))
        )
    ]
    pairs = [(wq, wq_s), (wk, wk_s), (wv, wv_s), (wo, wo_s)]
    for piece in range(pieces):
        span = pl.ds(piece * chunk, chunk)
        pairs += [
            (wg.at[:, :, span], wg_s.at[:, :, span]), (wu.at[:, :, span], wu_s.at[:, :, span]), (wd.at[:, span, :], wd_s.at[:, span, :])
        ]
    queue = [pltpu.make_async_copy(source, target, sem.at[place]) for place, (source, target) in enumerate(pairs)]
    for copy in small + queue[:AHEAD]:
        copy.start()
    state = [0]

    def arrive():
        queue[state[0]].wait()
        if state[0] + AHEAD < len(queue):
            queue[state[0] + AHEAD].start()
        state[0] += 1

    for copy in small:
        copy.wait()
    section = lax.axis_index("section")
    mix = [[mix_ref[0, i, j] for j in range(2)] for i in range(2)]
    cor = [cor_ref[0, i] for i in range(2)]
    xa = x_in[:, :width].astype(floating)
    xb = x_in[:, width:].astype(floating)
    own_a = jnp.where(section == 0, mix[0][0], mix[1][0])
    own_b = jnp.where(section == 0, mix[0][1], mix[1][1])
    active = jnp.where(section == 0, xa, xb) + (own_a * xa + own_b * xb)
    act_ref[...] = active
    nrm_ref[...] = (active * rms_scale(active) * ga_ref[...]).astype(bfloat)
    for weight, target in zip((wq_s, wk_s, wv_s), (q_ref, k_ref, v_ref)):
        arrive()
        target[...] = dot(nrm_ref[...], weight[0]).astype(bfloat)
    attention(q_ref, k_ref, v_ref, seg_ref, att_ref, None)
    arrive()
    middle = act_ref[...] + dot(att_ref[...], wo_s[0])
    acc[...] = middle - act_ref[...]
    nf_ref[...] = (middle * rms_scale(middle) * gf_ref[...]).astype(bfloat)
    for piece in range(pieces):
        span = slice(piece * chunk, (piece + 1) * chunk)
        arrive()
        gate = dot(nf_ref[...], wg_s[0, :, span])
        arrive()
        upward = dot(nf_ref[...], wu_s[0, :, span])
        hidden = (0.5 * gate * (1.0 + gelu_wave(gate)) * upward).astype(bfloat)
        arrive()
        acc[...] += dot(hidden, wd_s[0, span, :])
    out_ref[:tokens, :] = acc[...].astype(bfloat)
    out_ref[tokens:, :] = scalar_rows(mix[0] + mix[1] + cor, EXTRA, width)


def forward_lite(x_in, segments, mixing, correction, gain_attn, gain_ffn, weights):
    tokens = x_in.shape[0]
    width = gain_attn.shape[1]
    size = sum(weight.size for weight in weights)
    narrow = pltpu.VMEM((tokens, width), bfloat)
    wide = pltpu.VMEM((tokens, width), floating)
    args = (x_in, segments, mixing, correction, gain_attn, gain_ffn) + weights
    scratch = [
        pltpu.VMEM(x_in.shape, bfloat), pltpu.VMEM(segments.shape, jnp.int32), pltpu.SMEM(mixing.shape, floating),
        pltpu.SMEM(correction.shape, floating), pltpu.VMEM(gain_attn.shape, floating), pltpu.VMEM(gain_ffn.shape, floating),
        narrow, narrow, narrow, wide, narrow, narrow, narrow, wide,
    ]
    scratch += [pltpu.SemaphoreType.DMA((4 + 3 * (weights[4].shape[2] // width),)), pltpu.SemaphoreType.DMA((6,))]
    return pl.pallas_call(
        forward_lite_kernel,
        out_shape=[jax.ShapeDtypeStruct((tokens + EXTRA, width), bfloat)]
        + [jax.ShapeDtypeStruct(weight.shape, bfloat) for weight in weights],
        in_specs=[ANY] * len(args),
        out_specs=[VMEM] * 8,
        scratch_shapes=scratch,
        compiler_params=params(SCOPED),
        cost_estimate=cost(2 * tokens * size, 2 * size),
        name="forward_lite",
    )(*[in_hbm(one) for one in args])


def forward_kernel(fast, x_in, message, seg_ref, mix_ref, cor_ref, ga_ref, gf_ref, wq, wk, wv, wo, wg, wu, wd,
                   x_ref, out_ref, q_ref, k_ref, v_ref, p_ref, act_ref, mid_ref, one_ref, two_ref, chg_ref, *refs):
    kept = refs[:4]
    nf_ref = refs[-4]
    nrm_ref, att_ref, acc = refs[-3:]
    tokens, width = act_ref.shape
    chunk = width
    pieces = wg.shape[2] // chunk
    section = lax.axis_index("section")
    quarter = lax.axis_index("dp") & 3
    mix = [[mix_ref[0, i, j] for j in range(2)] for i in range(2)]
    cor = [cor_ref[0, i] for i in range(2)]
    xa = x_in[:, :width].astype(floating)
    xb = x_in[:, width:].astype(floating)
    got = read_scalars(message[tokens : tokens + EXTRA, :PAIR].astype(floating), 6)
    moved = message[:tokens, :].astype(floating)
    sent_a = (xa + (got[0] * xa + got[1] * xb) + got[4] * moved).astype(bfloat)
    sent_b = (xb + (got[2] * xa + got[3] * xb) + got[5] * moved).astype(bfloat)
    x_ref[:, :width] = jnp.where(section == 0, x_in[:, :width], sent_a)
    x_ref[:, width:] = jnp.where(section == 0, x_in[:, width:], sent_b)
    xa = x_ref[:, :width].astype(floating)
    xb = x_ref[:, width:].astype(floating)
    own_a = jnp.where(section == 0, mix[0][0], mix[1][0])
    own_b = jnp.where(section == 0, mix[0][1], mix[1][1])
    active = jnp.where(section == 0, xa, xb) + (own_a * xa + own_b * xb)
    act_ref[...] = active
    nrm_ref[...] = (active * rms_scale(active) * ga_ref[...]).astype(bfloat)
    for weight, target in zip((wq, wk, wv), (q_ref, k_ref, v_ref)):
        target[...] = dot(nrm_ref[...], weight[0]).astype(bfloat)

    def keep_quarters(values, base):
        share = width // 16
        for far in range(4):
            blocks = [values[:, (4 * far + near) * share : (4 * far + near + 1) * share] for near in range(4)]
            for slot, block in enumerate(relative(blocks, quarter)):
                kept[slot][:, base + far * share : base + (far + 1) * share] = block

    attention(q_ref, k_ref, v_ref, seg_ref, att_ref, p_ref)
    middle = act_ref[...] + dot(att_ref[...], wo[0])
    mid_ref[...] = middle
    nf_ref[...] = (middle * rms_scale(middle) * gf_ref[...]).astype(bfloat)
    if fast:
        keep_quarters(att_ref[...], width)
        keep_quarters(nrm_ref[...], width + width // 4)
        for slot in (1, 2):
            kept[slot][:, width + width // 2 :] = nf_ref[...]
    else:
        kept[1][...] = nrm_ref[...]
        kept[2][...] = att_ref[...]
    for piece in range(pieces):
        span = slice(piece * chunk, (piece + 1) * chunk)
        gate = dot(nf_ref[...], wg[0, :, span])
        upward = dot(nf_ref[...], wu[0, :, span])
        wave = gelu_wave(gate)
        half = 0.5 * (1.0 + wave)
        value = gate * half
        hidden = (value * upward).astype(bfloat)
        slope = half + 0.5 * gate * (1.0 - wave * wave) * (GELU_A * (1.0 + 3.0 * GELU_B * gate * gate))
        one_ref[piece] = upward * slope
        two_ref[piece] = value
        if fast:
            share = chunk // 4
            blocks = [hidden[:, near * share : (near + 1) * share] for near in range(4)]
            for slot, block in enumerate(relative(blocks, quarter)):
                kept[slot][:, piece * share : (piece + 1) * share] = block
        else:
            kept[0][:, span] = hidden
        down = dot(hidden, wd[0, span, :])
        if piece == 0:
            acc[...] = down
        else:
            acc[...] += down
    change = mid_ref[...] + acc[...] - act_ref[...]
    chg_ref[...] = change
    xa = x_ref[:, :width].astype(floating)
    xb = x_ref[:, width:].astype(floating)
    out_ref[0, :, :width] = (xa + (mix[0][0] * xa + mix[0][1] * xb) + cor[0] * change).astype(bfloat)
    out_ref[0, :, width:] = (xb + (mix[1][0] * xa + mix[1][1] * xb) + cor[1] * change).astype(bfloat)


def forward(fast, x_in, message, segments, mixing, correction, gain_attn, gain_ffn, weights):
    tokens = x_in.shape[0]
    length = segments.shape[1]
    width = gain_attn.shape[1]
    hidden_width = weights[4].shape[2]
    size = sum(weight.size for weight in weights)
    shape = jax.ShapeDtypeStruct
    narrow = ((tokens, width), bfloat)
    wide = ((tokens, width), floating)
    probs = ((tokens // length * (width // PAIR), 2 * length, length), floating)
    if fast:
        short, long = (((tokens, columns), bfloat) for columns in (width + width // 2, 2 * width + width // 2))
        kept = [short, long, long, short, narrow]
    else:
        kept = [((tokens, hidden_width), bfloat), narrow, narrow, narrow]
    ffn = ((hidden_width // width, tokens, width), floating)
    outs = [((tokens, 2 * width), bfloat), ((1, tokens, 2 * width), bfloat), narrow, narrow, narrow, probs, wide, wide,
            ffn, ffn, wide] + kept
    return pl.pallas_call(
        lambda *refs: forward_kernel(fast, *refs),
        out_shape=[shape(*one) for one in outs],
        in_specs=[VMEM, VMEM, VMEM, SMEM, SMEM, VMEM, VMEM] + [VMEM] * 7,
        out_specs=[VMEM] * len(outs),
        scratch_shapes=[pltpu.VMEM(*narrow)] * 2 + [pltpu.VMEM(*wide)],
        compiler_params=params(SCOPED),
        cost_estimate=cost(2 * tokens * size, 2 * size),
        name="forward_full",
    )(x_in, message, segments, mixing, correction, gain_attn, gain_ffn, *weights)


def start_rows(message, grad_ref, counts_ref, cor_ref, g_ref, low_ref):
    tokens, width = low_ref.shape
    rows = counts_ref.shape[0]
    length = tokens // rows
    section = lax.axis_index("section")
    if message is not None:
        got = read_scalars(message[tokens : tokens + EXTRA, :PAIR].astype(floating), 4)
    place = lax.broadcasted_iota(jnp.int32, (length, width), 0)
    for row in range(rows):
        span = slice(row * length, (row + 1) * length)
        valid = place < counts_ref[row]
        own_a = jnp.where(valid, grad_ref[span, :width].astype(floating), 0.0)
        own_b = jnp.where(valid, grad_ref[span, width:].astype(floating), 0.0)
        if message is not None:
            later_b = own_b + message[span, :].astype(floating)
            far_a = own_a + (got[0] * own_a + got[2] * later_b)
            far_b = later_b + (got[1] * own_a + got[3] * later_b)
            own_a = jnp.where(section == 0, far_a, own_a).astype(bfloat).astype(floating)
            own_b = jnp.where(section == 0, far_b, own_b).astype(bfloat).astype(floating)
        g_ref[span, :width] = own_a.astype(bfloat)
        g_ref[span, width:] = own_b.astype(bfloat)
        low_ref[span, :] = (cor_ref[0, 0] * own_a + cor_ref[0, 1] * own_b).astype(bfloat)


def start(message, out_grad, counts, correction, before):
    tokens = out_grad.shape[0]
    width = message.shape[1]
    shape = jax.ShapeDtypeStruct
    return pl.pallas_call(
        lambda *refs: start_rows(*refs[:4], *refs[-2:]),
        out_shape=[shape((tokens, 2 * width), bfloat), shape((tokens, width), bfloat)],
        in_specs=[VMEM, VMEM, SMEM, SMEM] + [ANY] * len(before),
        out_specs=[VMEM, VMEM],
        compiler_params=params(SCOPED),
        cost_estimate=cost(tokens * width * 20, tokens * width * 12),
        name="backward_start",
    )(message, out_grad, counts, correction, *before)


def norm_backward(values, gain, grad_normed, with_gain):
    inverse = rms_scale(values)
    grad_gain = jnp.sum(grad_normed * values * inverse, axis=0, keepdims=True) if with_gain else None
    weighted = grad_normed * gain
    grad_values = inverse * weighted - values * inverse**3 * jnp.mean(weighted * values, axis=-1, keepdims=True)
    return grad_gain, grad_values


def ffn_steps(low_ref, one, two, wg, wu, wd, acc, emit):
    width = wd.shape[2]
    quarter = lax.axis_index("dp") & 3
    for step in range(4):
        piece = (3 - step) ^ quarter
        span = pl.ds(pl.multiple_of(piece * width, width), width)
        grad_hidden = dot_t(low_ref[...], wd[0, span, :])
        dgate = (grad_hidden * one[piece]).astype(bfloat)
        dup = (grad_hidden * two[piece]).astype(bfloat)
        emit(3 - step, dgate, dup)
        total = dot_t(dgate, wg[0, :, span]) + dot_t(dup, wu[0, :, span])
        if step == 0:
            acc[...] = total
        else:
            acc[...] += total


def ffn_kernel(g_in, low_ref, cor_ref, gf_ref, mid_ref, one, two, wg, wu, wd, *refs):
    slots = refs[-12:-4]
    dmid_ref, datt_ref, gain_ref, acc = refs[-4:]
    width = gf_ref.shape[1]

    def emit(slot, dgate, dup):
        slots[slot][...] = dgate
        slots[4 + slot][...] = dup

    ffn_steps(low_ref, one, two, wg, wu, wd, acc, emit)
    grad_gain, grad_values = norm_backward(mid_ref[...], gf_ref[...], acc[...], True)
    block = cor_ref[0, 0] * g_in[:, :width].astype(floating) + cor_ref[0, 1] * g_in[:, width:].astype(floating)
    grad_middle = block + grad_values
    dmid_ref[...] = grad_middle
    datt_ref[...] = grad_middle.astype(bfloat)
    gain_ref[...] = grad_gain


def ffn_backward(g_in, low, correction, gain_ffn, middle, one, two, before, weights):
    tokens = g_in.shape[0]
    width = gain_ffn.shape[1]
    shape = jax.ShapeDtypeStruct
    return pl.pallas_call(
        ffn_kernel,
        out_shape=[shape((tokens, width), bfloat)] * 8
        + [shape((tokens, width), floating), shape((tokens, width), bfloat), shape((1, width), floating)],
        in_specs=[VMEM, VMEM, SMEM] + [VMEM] * 7 + [ANY] * len(before),
        out_specs=[VMEM] * 11,
        scratch_shapes=[pltpu.VMEM((tokens, width), floating)],
        compiler_params=params(SCOPED),
        cost_estimate=cost(2 * tokens * 3 * weights[4].size, 2 * 3 * weights[4].size),
        name="backward_ffn",
    )(g_in, low, correction, gain_ffn, middle, one, two, *weights[4:], *before)


def attn_steps(q_ref, k_ref, v_ref, p_ref, do_ref, parts):
    tokens, width = do_ref.shape
    length = p_ref.shape[2]
    rows = tokens // length
    pairs = width // PAIR
    first = lane_mask(length)
    for row in range(rows):
        span = slice(row * length, (row + 1) * length)
        for pair in range(pairs):
            heads = slice(pair * PAIR, (pair + 1) * PAIR)
            probs = p_ref[row * pairs + pair]
            grad_out = stack_heads(do_ref[span, heads], first)
            grad_value = t_dot(probs.astype(bfloat), grad_out)
            grad_probs = dot_t(grad_out, v_ref[span, heads])
            carried = jnp.sum(probs * grad_probs, axis=-1, keepdims=True)
            grad_scores = (probs * (grad_probs - carried)).astype(bfloat)
            grad_query = dot(grad_scores, k_ref[span, heads])
            grad_query = jnp.where(first, grad_query[:length], grad_query[length:])
            grad_key = t_dot(grad_scores, stack_heads(q_ref[span, heads], first))
            for (part, base), value in zip(parts, (grad_query * SCALE, grad_key * SCALE, grad_value)):
                part[span, base + pair * PAIR : base + (pair + 1) * PAIR] = value.astype(bfloat)


def normed_grad(parts, rows, width, wq, wk, wv):
    return sum(dot_t(part[:rows, base : base + width], weight[0]) for (part, base), weight in zip(parts, (wq, wk, wv)))


def attn_kernel(datt_ref, q_ref, k_ref, v_ref, p_ref, gfg_ref, ga_ref, x_ref, g_in, dmid_ref, act_ref, chg_ref, mix_ref, cor_ref,
                wq, wk, wv, wo, before,
                grad_ref, right_ref, small_ref, do_ref):
    tokens, width = datt_ref.shape
    right_ref[:tokens, :width] = datt_ref[...]
    do_ref[...] = dot_t(datt_ref[...], wo[0]).astype(bfloat)
    parts = (right_ref, width), (right_ref, 2 * width), (right_ref, 3 * width)
    attn_steps(q_ref, k_ref, v_ref, p_ref, do_ref, parts)
    grad_normed = normed_grad(parts, tokens, width, wq, wk, wv)
    grad_gain, grad_values = norm_backward(act_ref[...], ga_ref[...], grad_normed, True)
    section = lax.axis_index("section")
    mix = [[mix_ref[0, i, j] for j in range(2)] for i in range(2)]
    cor = [cor_ref[0, i] for i in range(2)]
    out_a = g_in[:, :width].astype(floating)
    out_b = g_in[:, width:].astype(floating)
    grad_active = dmid_ref[...] + grad_values - (cor[0] * out_a + cor[1] * out_b)
    pred_a = out_a + jnp.where(section == 0, grad_active, 0.0)
    pred_b = out_b + jnp.where(section == 0, 0.0, grad_active)
    grad_ref[0, :, :width] = (pred_a + (mix[0][0] * pred_a + mix[1][0] * pred_b)).astype(bfloat)
    grad_ref[0, :, width:] = (pred_b + (mix[0][1] * pred_a + mix[1][1] * pred_b)).astype(bfloat)
    xa = x_ref[:, :width].astype(floating)
    xb = x_ref[:, width:].astype(floating)
    small_ref[0:1, :] = grad_gain
    small_ref[1:2, :] = gfg_ref[...]
    place = 2
    for pred in (pred_a, pred_b):
        for state in (xa, xb):
            small_ref[place : place + 1, :] = jnp.sum(pred * state, axis=0, keepdims=True)
            place += 1
    for out in (out_a, out_b):
        small_ref[place : place + 1, :] = jnp.sum(out * chg_ref[...], axis=0, keepdims=True)
        place += 1
    right_ref[tokens:, : 2 * width] = spread(small_ref[...])
    right_ref[tokens:, 2 * width :] = jnp.zeros((right_ref.shape[0] - tokens, 2 * width), bfloat)


def attn_backward(x, g_in, grad_middle, grad_att, active, change, queries, key_rows, value_rows, probs, ffn_gain, gain_attn,
                  mixing, correction, before, weights):
    tokens, width = active.shape
    shape = jax.ShapeDtypeStruct
    return pl.pallas_call(
        attn_kernel,
        out_shape=[
            shape((1, tokens, 2 * width), bfloat), shape((tokens + EXTRA, 4 * width), bfloat), shape((8, width), floating),
        ],
        in_specs=[VMEM] * 12 + [SMEM] * 2 + [VMEM] * 4 + [ANY],
        out_specs=[VMEM] * 3,
        scratch_shapes=[pltpu.VMEM((tokens, width), bfloat)],
        compiler_params=params(SCOPED),
        cost_estimate=cost(2 * tokens * 5 * weights[0].size, 2 * 4 * weights[0].size),
        name="backward_attn",
    )(grad_att, queries, key_rows, value_rows, probs, ffn_gain, gain_attn, x, g_in, grad_middle, active, change,
      mixing, correction, *weights[:4], before)


def relay_kernel(grad_in, counts_ref, cor_ref, mix_ref, gf_ref, ga_ref, one, two, mid_ref, q_ref, k_ref, v_ref, p_ref, act_ref,
                 wq, wk, wv, wo, wg, wu, wd,
                 msg_ref,
                 acc, g_in, low_ref, do_ref, dqkv_ref):
    tokens, width = low_ref.shape
    start_rows(None, grad_in, counts_ref, cor_ref, g_in, low_ref)
    ffn_steps(low_ref, one, two, wg, wu, wd, acc, lambda *parts: None)
    grad_values = norm_backward(mid_ref[...], gf_ref[...], acc[...], False)[1]
    cor = [cor_ref[0, i] for i in range(2)]
    block = cor[0] * g_in[:, :width].astype(floating) + cor[1] * g_in[:, width:].astype(floating)
    acc[...] = block + grad_values
    do_ref[...] = dot_t(acc[...].astype(bfloat), wo[0]).astype(bfloat)
    parts = (dqkv_ref, 0), (dqkv_ref, width), (dqkv_ref, 2 * width)
    attn_steps(q_ref, k_ref, v_ref, p_ref, do_ref, parts)
    grad_normed = normed_grad(parts, tokens, width, wq, wk, wv)
    grad_values = norm_backward(act_ref[...], ga_ref[...], grad_normed, False)[1]
    block = cor[0] * g_in[:, :width].astype(floating) + cor[1] * g_in[:, width:].astype(floating)
    msg_ref[:tokens, :] = (acc[...] + grad_values - block).astype(bfloat)
    mix = [[mix_ref[0, i, j] for j in range(2)] for i in range(2)]
    msg_ref[tokens:, :] = scalar_rows(mix[0] + mix[1], EXTRA, width)


def relay_backward(out_grad, counts, correction, mixing, gain_ffn, gain_attn, one, two, middle, queries, key_rows, value_rows,
                   probs, active, weights):
    tokens, width = active.shape
    shape = jax.ShapeDtypeStruct
    narrow = pltpu.VMEM((tokens, width), bfloat)
    wide = pltpu.VMEM((tokens, width), floating)
    size = sum(weight.size for weight in weights)
    return pl.pallas_call(
        relay_kernel,
        out_shape=shape((tokens + EXTRA, width), bfloat),
        in_specs=[VMEM, SMEM, SMEM, SMEM] + [VMEM] * 17,
        out_specs=VMEM,
        scratch_shapes=[wide, pltpu.VMEM((tokens, 2 * width), bfloat), narrow, narrow, pltpu.VMEM((tokens, 3 * width), bfloat)],
        compiler_params=params(SCOPED),
        cost_estimate=cost(2 * tokens * size, 2 * size),
        name="backward_relay",
    )(out_grad, counts, correction, mixing, gain_ffn, gain_attn, one, two, middle, queries, key_rows, value_rows, probs, active,
      *weights)


def quarter_kernel(base, products, block, refs):
    count = 4
    lefts = refs[:count]
    rights = refs[count : 2 * count]
    send_ref, keep_ref = refs[-2:]
    quarter_parts(base, products, block, lefts, rights, send_ref, keep_ref)


def quarter_parts(base, products, block, lefts, rights, send_ref, keep_ref):
    tokens = lefts[0].shape[0]
    index = lax.axis_index("dp")
    near = (index >> 2) & 1
    far = (index >> 3) & 1
    for left_at, left_wide, right_at, right_wide in products:
        rows = slice(left_at, left_at + left_wide)
        columns = slice(right_at, right_at + right_wide)
        total = sum(t_dot(left[:, rows], right[:tokens, columns]) for left, right in zip(lefts, rights))
        span = slice(right_at - base, right_at - base + right_wide)
        for place in range(4):
            part = total[place * block : (place + 1) * block, :]
            slot = (place >> 1) ^ far
            mine = (place & 1) == near

            @pl.when(mine)
            def _():
                keep_ref[slot, :, span] = part

            @pl.when(jnp.logical_not(mine))
            def _():
                send_ref[slot, :, span] = part.astype(bfloat)


def attn_product_kernel(halves, block, refs):
    lefts, rights = refs[:4], refs[4:8]
    first_send, first_keep, small_ref, second_send, second_keep, stage = refs[-6:]
    tokens = lefts[0].shape[0]
    wide = first_keep.shape[2]
    quarter_parts(0, halves[0], block, lefts, rights, stage, first_keep)
    first_send[:block, :] = stage[0]
    first_send[block : 2 * block, :] = stage[1]
    small = sum(gathered_parts(right[tokens:, :wide]) for right in rights)
    small_ref[...] = small
    first_send[2 * block :, :] = spread(small)
    quarter_parts(wide, halves[1], block, lefts, rights, second_send, second_keep)


def attn_product(lefts, rights, halves, block, before):
    wide = rights[0].shape[1] // 2
    shape = jax.ShapeDtypeStruct
    send, keep = shape((2, block, wide), bfloat), shape((2, block, wide), floating)
    return pl.pallas_call(
        lambda *refs: attn_product_kernel(halves, block, refs),
        out_shape=[shape((2 * block + EXTRA, wide), bfloat), keep, shape((8, wide // 2), floating), send, keep],
        in_specs=[VMEM] * 8 + [ANY] * len(before),
        out_specs=[VMEM] * 5,
        scratch_shapes=[pltpu.VMEM(send.shape, bfloat)],
        compiler_params=params(SCOPED),
        cost_estimate=cost(wide, wide),
        name="product_attn",
    )(*lefts, *rights, *before)


def first_sum_kernel(keep_ref, came_ref, small_ref, held_ref, passed_ref, sums_ref):
    block = held_ref.shape[0]
    held_ref[...] = keep_ref[0] + came_ref[:block, :].astype(floating)
    passed_ref[:block, :] = (keep_ref[1] + came_ref[block : 2 * block, :].astype(floating)).astype(bfloat)
    small = small_ref[...] + gathered_parts(came_ref[2 * block :, :])
    sums_ref[...] = small
    passed_ref[block:, :] = spread(small)


def first_sum(keep, came, small):
    _, block, wide = keep.shape
    shape = jax.ShapeDtypeStruct
    return pl.pallas_call(
        first_sum_kernel,
        out_shape=[shape((block, wide), floating), shape((block + EXTRA, wide), bfloat), shape(small.shape, floating)],
        in_specs=[VMEM] * 3,
        out_specs=[VMEM] * 3,
        compiler_params=params(SCOPED),
        cost_estimate=cost(wide, wide),
        name="first_sum",
    )(keep, came, small)


def first_end_kernel(held_ref, came_ref, small_ref, left_ref, right_ref, sums_ref):
    block, wide = held_ref.shape
    left_ref[0] = held_ref[:, : wide // 2] + came_ref[:block, : wide // 2].astype(floating)
    right_ref[0] = held_ref[:, wide // 2 :] + came_ref[:block, wide // 2 :].astype(floating)
    sums_ref[...] = small_ref[...] + gathered_parts(came_ref[block:, :])


def first_end(held, came, small):
    block, wide = held.shape
    shape = jax.ShapeDtypeStruct
    return pl.pallas_call(
        first_end_kernel,
        out_shape=[shape((1, block, wide // 2), floating)] * 2 + [shape(small.shape, floating)],
        in_specs=[VMEM] * 3,
        out_specs=[VMEM] * 3,
        compiler_params=params(SCOPED),
        cost_estimate=cost(wide, wide),
        name="first_end",
    )(held, came, small)


def quarter_product(lefts, rights, products, block, before, name):
    base = products[0][2]
    wide = sum(one[3] for one in products)
    shape = jax.ShapeDtypeStruct
    flops = sum(2 * 4 * lefts[0].shape[0] * one[1] * one[3] for one in products)
    return pl.pallas_call(
        lambda *refs: quarter_kernel(base, products, block, refs),
        out_shape=[shape((2, block, wide), bfloat), shape((2, block, wide), floating)],
        in_specs=[VMEM] * 8 + [ANY] * len(before),
        out_specs=[VMEM, VMEM],
        compiler_params=params(SCOPED),
        cost_estimate=cost(flops, 12 * block * wide),
        name=name,
    )(*lefts, *rights, *before)


def assemble_kernel(own, one, two, three, gate_ref, up_ref):
    quarter = lax.axis_index("dp") & 3
    width = own.shape[1] // 2
    for slot, piece in enumerate((own, one, two, three)):
        span = pl.ds(pl.multiple_of((slot ^ quarter) * width, width), width)
        gate_ref[0, :, span] = piece[:, :width].astype(floating)
        up_ref[0, :, span] = piece[:, width:].astype(floating)


def assemble(pieces):
    share, double = pieces[0].shape
    shape = jax.ShapeDtypeStruct((1, share, 2 * double), floating)
    return pl.pallas_call(
        assemble_kernel,
        out_shape=[shape, shape],
        in_specs=[VMEM] * 4,
        out_specs=[VMEM] * 2,
        compiler_params=params(SCOPED),
        cost_estimate=cost(share * double * 4, share * double * 24),
        name="assemble",
    )(*pieces)


def exchange(value, flips):
    count = lax.axis_size("dp")
    return lax.ppermute(value, "dp", [(source, source ^ flips) for source in range(count)])


def relative_rows(matrix, order, index):
    bits = len(order)
    block = matrix.shape[0] >> bits
    split = matrix.reshape((2,) * bits + (block, matrix.shape[1]))
    axes = [bits - 1 - bit for bit in order]
    split = jnp.transpose(split, axes + [bits, bits + 1])
    for axis, bit in enumerate(order):
        split = jnp.where((index >> bit) & 1 == 1, jnp.flip(split, axis), split)
    return split.reshape(matrix.shape)


def scatter_sum(left, right, order):
    total = left.shape[0]
    arrived = []
    for step in range(len(order) + 1):
        low = total >> (step + 1) if step < len(order) else 0
        high = total >> step
        part = dot(left[low:high], right)
        for other in arrived:
            part = part + other[low:high].astype(floating)
        if step == len(order):
            return part
        arrived.append(exchange(part.astype(bfloat), 1 << order[step]))


def halving_grads(kept, low, slots, right, index, count):
    width = low.shape[1]
    order = list(range(count.bit_length() - 1))
    hidden, normed, attended, normed_ffn = (relative_rows(one.T, order, index) for one in kept)
    quarter = index & 3
    places = jnp.arange(4) ^ quarter
    dgate = jnp.concatenate(list(jnp.stack(slots[:4])[places]), axis=1)
    dup = jnp.concatenate(list(jnp.stack(slots[4:])[places]), axis=1)
    grad_down = scatter_sum(hidden, low, order)
    grad_gate = scatter_sum(normed_ffn, dgate, order)
    grad_up = scatter_sum(normed_ffn, dup, order)
    grad_out = scatter_sum(attended, right[:, :width], order)
    grad_qkv = scatter_sum(normed, right[:, width:], order)
    grads = [grad_down, grad_gate, grad_up, grad_out] + [grad_qkv[:, place * width : (place + 1) * width] for place in range(3)]
    return [one[None] for one in grads]


def after(values, *earlier):
    return lax.optimization_barrier((values, earlier))[0]


def gather_start(value):
    return [value, exchange(value, 1), exchange(value, 2)]


def gather_end(pieces, *earlier):
    return pieces + [exchange(after(pieces[2], *earlier), 1)]


def swapped(pieces):
    return [pieces[0]] + [exchange(pieces[flips], flips) for flips in (1, 2, 3)]


def sum_once(pair, *earlier):
    send, keep = pair
    arrived = after(exchange(send, 4), *earlier)
    return keep[0] + arrived[0].astype(floating), (keep[1] + arrived[1].astype(floating)).astype(bfloat)


def sum_twice(held, passed, *earlier):
    return held + after(exchange(passed, 8), *earlier).astype(floating)


def sum_over(value, bits):
    for bit in range(bits):
        value = value + exchange(value, 1 << bit)
    return value


def quarter_grads(normed_ffn, kept, slots, right, down_pair, index):
    width = normed_ffn[0].shape[1]
    share = width // 16
    block = 4 * share
    whole = [(0, width, 0, width)]
    gates = swapped(slots[:4])
    ups = swapped(list(after(slots[4:], right)))
    down_sums = sum_once(down_pair, right)
    gate_pair = quarter_product(normed_ffn, gates, whole, block, [right, down_sums[1]], "product_gate")
    grad_down = sum_twice(*down_sums)
    rights = gather_start(after(right, gate_pair[0], grad_down, ups[1:]))
    gate_sums = sum_once(gate_pair)
    up_pair = quarter_product(normed_ffn, ups, whole, block, [gate_sums[1], grad_down], "product_up")
    up_sums = sum_once(up_pair)
    gate_tile = sum_twice(*gate_sums).astype(bfloat)
    rights = gather_end(rights, up_sums[1], gate_tile)
    halves = (
        [(width, block, 0, width), (width + block, block, width, width)], [(width + block, block, 2 * width, 2 * width)])
    first_send, first_keep, small, *second_pair = attn_product(kept, rights, halves, share, [up_sums[1], gate_tile])
    held, first_passed, small = first_sum(first_keep, exchange(first_send, 4), small)
    up_tile = sum_twice(*up_sums, first_passed).astype(bfloat)
    quarter = index & 3
    gate_tile = after(gate_tile, first_passed)
    pieces = [
        jnp.concatenate(
            [lax.dynamic_slice_in_dim(tile, (slot ^ quarter) * share, share, axis=0) for tile in (gate_tile, up_tile)], axis=1)
        for slot in range(4)
    ]
    pieces = swapped(pieces)
    grad_out, grad_query, small = first_end(held, exchange(first_passed, 8), small)
    second_sums = sum_once(second_pair, first_passed)
    grad_gate, grad_up = assemble(list(after(pieces, second_sums[1], small)))
    held, passed = second_sums
    passed = exchange(passed, 8)
    grads = [grad_down[None], grad_gate, grad_up, grad_out, grad_query]
    for span in (slice(0, width), slice(width, 2 * width)):
        grads.append((held[:, span] + passed[:, span].astype(floating))[None])
    return grads, small


def local(states_in, out_grad, counts, segments, mixing, correction, gain_attn, w_query, w_key, w_value, w_attn_out, gain_ffn,
          w_gate, w_up, w_down):
    weights = (w_query, w_key, w_value, w_attn_out, w_gate, w_up, w_down)
    width = gain_attn.shape[1]
    index = lax.axis_index("dp")
    count = lax.axis_size("dp")
    fast = count == 16
    message, *weights = forward_lite(states_in, segments, mixing, correction, gain_attn, gain_ffn, weights)
    message = lax.ppermute(message, "section", [(0, 1), (1, 0)])
    (x, states, queries, key_rows, value_rows, probs, active, middle, one, two, change, *kept) = forward(
        fast, states_in, message, segments, mixing, correction, gain_attn, gain_ffn, weights)
    before = []
    if fast:
        kept, normed_ffn = swapped(kept[:4]), kept[4]
        before = kept[1:]
    message = relay_backward(out_grad, counts, correction, mixing, gain_ffn, gain_attn, one, two, middle, queries, key_rows,
                             value_rows, probs, active, weights)
    message = lax.ppermute(message, "section", [(0, 1), (1, 0)])
    g_in, low = start(message, out_grad, counts, correction, [])
    *slots, grad_middle, grad_att, ffn_gain = ffn_backward(g_in, low, correction, gain_ffn, middle, one, two, before, weights)
    before = slots[0]
    if fast:
        lows = gather_end(gather_start(low), before)
        beside, across = (one[:, width + width // 2 :] for one in kept[1:3])
        normed_ffn = gather_end([normed_ffn, beside, across], before)
        down_pair = quarter_product(kept, lows, [(0, width, 0, width)], width // 4, [before], "product_down")
        before = down_pair[0]
    state_grads, right, small = attn_backward(x, g_in, grad_middle, grad_att, active, change, queries, key_rows, value_rows, probs,
                                              ffn_gain, gain_attn, mixing, correction, before, weights)
    if fast:
        grads, small = quarter_grads(normed_ffn, kept, slots, right, down_pair, index)
    else:
        grads = halving_grads(kept, low, slots, right[: low.shape[0]], index, count)
        small = sum_over(small, count.bit_length() - 1)
    grad_down, grad_gate, grad_up, grad_out, grad_query, grad_key, grad_value = grads
    share = width // count
    gains = lax.dynamic_slice(small, (0, index * share), (2, share))
    sums = jnp.sum(small[2:], axis=1)
    return (
        states,
        state_grads,
        sums[:4].reshape(1, 2, 2),
        sums[4:].reshape(1, 2),
        gains[0:1],
        grad_query,
        grad_key,
        grad_value,
        grad_out,
        gains[1:2],
        grad_gate,
        grad_up,
        grad_down,
    )


def solution(mesh):
    rows = P("dp", None)
    matrix = P("section", None, None)
    vector = P("section", None)
    share = P("section", "dp", None)
    gain_share = P("section", "dp")
    in_specs = (rows, rows, P("dp"), rows, matrix, vector, vector, matrix, matrix, matrix, matrix, vector, matrix, matrix, matrix)
    out_specs = (share, share, matrix, vector, gain_share, share, share, share, share, gain_share, share, share, share)
    return jax.shard_map(local, mesh=mesh, in_specs=in_specs, out_specs=out_specs, check_vma=False)
```

```python
import functools

import jax
import jax.numpy as jnp
from jax import lax
from jax.experimental import pallas as pl
from jax.experimental.pallas import tpu as pltpu
from jax.sharding import PartitionSpec as P

HEAD_DIM = 64
PAIR = 2 * HEAD_DIM
EPSILON = 1e-06
MASKED = -1e30
SCALE = HEAD_DIM ** (-0.5)
GELU_A = 0.7978845608028654
GELU_B = 0.044715
EXTRA = 16
AHEAD = 3
SCOPED = 12
bfloat = jnp.bfloat16
floating = jnp.float32

VMEM = pl.BlockSpec(memory_space=pltpu.VMEM)
SMEM = pl.BlockSpec(memory_space=pltpu.SMEM)
ANY = pl.BlockSpec(memory_space=pltpu.MemorySpace.HBM)


def dot(a, b):
    return jnp.dot(a, b, preferred_element_type=floating)


def dot_t(a, b):
    return lax.dot_general(a, b, (((1,), (1,)), ((), ())), preferred_element_type=floating)


def t_dot(a, b):
    return lax.dot_general(a, b, (((0,), (0,)), ((), ())), preferred_element_type=floating)


def params(mebibytes):
    return pltpu.CompilerParams(vmem_limit_bytes=mebibytes * 1024 * 1024)


def cost(flops, moved):
    return pl.CostEstimate(flops=flops // 1000, bytes_accessed=moved // 1000, transcendentals=0)


def scalar_rows(values, rows, width):
    lane = lax.broadcasted_iota(jnp.int32, (rows, width), 1)
    row = lax.broadcasted_iota(jnp.int32, (rows, width), 0)
    whole = jnp.zeros((rows, width), floating)
    for place, value in enumerate(values):
        whole = jnp.where(lane == place, value, whole)
    high = whole.astype(bfloat).astype(floating)
    middle = (whole - high).astype(bfloat).astype(floating)
    low = whole - high - middle
    part = jnp.where(row == 0, high, jnp.where(row == 1, middle, jnp.where(row == 2, low, 0.0)))
    return part.astype(bfloat)


def spread(value):
    high = value.astype(bfloat).astype(floating)
    middle = (value - high).astype(bfloat).astype(floating)
    low = value - high - middle
    top = jnp.concatenate([high, middle], axis=1)
    bottom = jnp.concatenate([low, jnp.zeros_like(low)], axis=1)
    return jnp.concatenate([top, bottom], axis=0).astype(bfloat)


def gathered_parts(block):
    block = block.astype(floating)
    width = block.shape[1] // 2
    return block[:8, :width] + block[:8, width:] + block[8:, :width]


def read_scalars(block, count):
    lane = lax.broadcasted_iota(jnp.int32, block.shape, 1)
    return [jnp.sum(jnp.where(lane == place, block, 0.0)) for place in range(count)]


def rms_scale(values):
    return lax.rsqrt(jnp.mean(values * values, axis=-1, keepdims=True) + EPSILON)


def lane_mask(length):
    return lax.broadcasted_iota(jnp.int32, (length, PAIR), 1) < HEAD_DIM


def stack_heads(block, first):
    zero = jnp.zeros_like(block)
    return jnp.concatenate([jnp.where(first, block, zero), jnp.where(first, zero, block)], axis=0)


def gelu_wave(gate):
    return jnp.tanh(GELU_A * (gate + GELU_B * gate * gate * gate))


def relative(blocks, index):
    low = (index & 1) == 1
    high = (index >> 1) == 1
    once = [jnp.where(low, blocks[place ^ 1], blocks[place]) for place in range(4)]
    return [jnp.where(high, once[place ^ 2], once[place]) for place in range(4)]


def attention(q_ref, k_ref, v_ref, seg_ref, att_ref, p_ref):
    length = seg_ref.shape[1]
    rows = q_ref.shape[0] // length
    pairs = q_ref.shape[1] // PAIR
    first = lane_mask(length)
    later = lax.broadcasted_iota(jnp.int32, (length, length), 0)
    earlier = lax.broadcasted_iota(jnp.int32, (length, length), 1)
    for row in range(rows):
        documents = jnp.broadcast_to(seg_ref[row : row + 1, :], (length, length)).astype(floating)
        allowed = (earlier <= later) & (documents == documents.T)
        allowed = jnp.concatenate([allowed, allowed], axis=0)
        span = slice(row * length, (row + 1) * length)
        for pair in range(pairs):
            heads = slice(pair * PAIR, (pair + 1) * PAIR)
            stacked = stack_heads(q_ref[span, heads], first)
            scores = jnp.where(allowed, dot_t(stacked, k_ref[span, heads]) * SCALE, MASKED)
            powers = jnp.exp(scores - jnp.max(scores, axis=-1, keepdims=True))
            probs = powers / jnp.sum(powers, axis=-1, keepdims=True)
            if p_ref is not None:
                p_ref[row * pairs + pair] = probs
            mixed = dot(probs.astype(bfloat), v_ref[span, heads])
            att_ref[span, heads] = jnp.where(first, mixed[:length], mixed[length:]).astype(bfloat)


def in_hbm(value):
    return pltpu.with_memory_space_constraint(value, pltpu.MemorySpace.HBM)


def forward_lite_kernel(x_any, seg_any, mix_any, cor_any, ga_any, gf_any, wq, wk, wv, wo, wg, wu, wd,
                        out_ref, wq_s, wk_s, wv_s, wo_s, wg_s, wu_s, wd_s,
                        x_in, seg_ref, mix_ref, cor_ref, ga_ref, gf_ref, q_ref, k_ref, v_ref, act_ref,
                        nrm_ref, att_ref, nf_ref, acc, sem, small_sem):
    tokens, width = act_ref.shape
    chunk = width
    pieces = wg.shape[2] // chunk
    small = [
        pltpu.make_async_copy(source, target, small_sem.at[place])
        for place, (source, target) in enumerate(
            ((x_any, x_in), (mix_any, mix_ref), (ga_any, ga_ref), (seg_any, seg_ref), (gf_any, gf_ref), (cor_any, cor_ref))
        )
    ]
    pairs = [(wq, wq_s), (wk, wk_s), (wv, wv_s), (wo, wo_s)]
    for piece in range(pieces):
        span = pl.ds(piece * chunk, chunk)
        pairs += [
            (wg.at[:, :, span], wg_s.at[:, :, span]), (wu.at[:, :, span], wu_s.at[:, :, span]), (wd.at[:, span, :], wd_s.at[:, span, :])
        ]
    queue = [pltpu.make_async_copy(source, target, sem.at[place]) for place, (source, target) in enumerate(pairs)]
    for copy in small + queue[:AHEAD]:
        copy.start()
    state = [0]

    def arrive():
        queue[state[0]].wait()
        if state[0] + AHEAD < len(queue):
            queue[state[0] + AHEAD].start()
        state[0] += 1

    for copy in small:
        copy.wait()
    section = lax.axis_index("section")
    mix = [[mix_ref[0, i, j] for j in range(2)] for i in range(2)]
    cor = [cor_ref[0, i] for i in range(2)]
    xa = x_in[:, :width].astype(floating)
    xb = x_in[:, width:].astype(floating)
    own_a = jnp.where(section == 0, mix[0][0], mix[1][0])
    own_b = jnp.where(section == 0, mix[0][1], mix[1][1])
    active = jnp.where(section == 0, xa, xb) + (own_a * xa + own_b * xb)
    act_ref[...] = active
    nrm_ref[...] = (active * rms_scale(active) * ga_ref[...]).astype(bfloat)
    for weight, target in zip((wq_s, wk_s, wv_s), (q_ref, k_ref, v_ref)):
        arrive()
        target[...] = dot(nrm_ref[...], weight[0]).astype(bfloat)
    attention(q_ref, k_ref, v_ref, seg_ref, att_ref, None)
    arrive()
    middle = act_ref[...] + dot(att_ref[...], wo_s[0])
    acc[...] = middle - act_ref[...]
    nf_ref[...] = (middle * rms_scale(middle) * gf_ref[...]).astype(bfloat)
    for piece in range(pieces):
        span = slice(piece * chunk, (piece + 1) * chunk)
        arrive()
        gate = dot(nf_ref[...], wg_s[0, :, span])
        arrive()
        upward = dot(nf_ref[...], wu_s[0, :, span])
        hidden = (0.5 * gate * (1.0 + gelu_wave(gate)) * upward).astype(bfloat)
        arrive()
        acc[...] += dot(hidden, wd_s[0, span, :])
    out_ref[:tokens, :] = acc[...].astype(bfloat)
    out_ref[tokens:, :] = scalar_rows(mix[0] + mix[1] + cor, EXTRA, width)


def forward_lite(x_in, segments, mixing, correction, gain_attn, gain_ffn, weights):
    tokens = x_in.shape[0]
    width = gain_attn.shape[1]
    size = sum(weight.size for weight in weights)
    narrow = pltpu.VMEM((tokens, width), bfloat)
    wide = pltpu.VMEM((tokens, width), floating)
    args = (x_in, segments, mixing, correction, gain_attn, gain_ffn) + weights
    scratch = [
        pltpu.VMEM(x_in.shape, bfloat), pltpu.VMEM(segments.shape, jnp.int32), pltpu.SMEM(mixing.shape, floating),
        pltpu.SMEM(correction.shape, floating), pltpu.VMEM(gain_attn.shape, floating), pltpu.VMEM(gain_ffn.shape, floating),
        narrow, narrow, narrow, wide, narrow, narrow, narrow, wide,
    ]
    scratch += [pltpu.SemaphoreType.DMA((4 + 3 * (weights[4].shape[2] // width),)), pltpu.SemaphoreType.DMA((6,))]
    return pl.pallas_call(
        forward_lite_kernel,
        out_shape=[jax.ShapeDtypeStruct((tokens + EXTRA, width), bfloat)]
        + [jax.ShapeDtypeStruct(weight.shape, bfloat) for weight in weights],
        in_specs=[ANY] * len(args),
        out_specs=[VMEM] * 8,
        scratch_shapes=scratch,
        compiler_params=params(SCOPED),
        cost_estimate=cost(2 * tokens * size, 2 * size),
        name="forward_lite",
    )(*[in_hbm(one) for one in args])


def forward_kernel(fast, x_in, message, seg_ref, mix_ref, cor_ref, ga_ref, gf_ref, wq, wk, wv, wo, wg, wu, wd,
                   x_ref, out_ref, q_ref, k_ref, v_ref, p_ref, act_ref, mid_ref, one_ref, two_ref, chg_ref, *refs):
    kept = refs[:4]
    nf_ref = refs[-4]
    nrm_ref, att_ref, acc = refs[-3:]
    tokens, width = act_ref.shape
    chunk = width
    pieces = wg.shape[2] // chunk
    section = lax.axis_index("section")
    quarter = lax.axis_index("dp") & 3
    mix = [[mix_ref[0, i, j] for j in range(2)] for i in range(2)]
    cor = [cor_ref[0, i] for i in range(2)]
    xa = x_in[:, :width].astype(floating)
    xb = x_in[:, width:].astype(floating)
    got = read_scalars(message[tokens : tokens + EXTRA, :PAIR].astype(floating), 6)
    moved = message[:tokens, :].astype(floating)
    sent_a = (xa + (got[0] * xa + got[1] * xb) + got[4] * moved).astype(bfloat)
    sent_b = (xb + (got[2] * xa + got[3] * xb) + got[5] * moved).astype(bfloat)
    x_ref[:, :width] = jnp.where(section == 0, x_in[:, :width], sent_a)
    x_ref[:, width:] = jnp.where(section == 0, x_in[:, width:], sent_b)
    xa = x_ref[:, :width].astype(floating)
    xb = x_ref[:, width:].astype(floating)
    own_a = jnp.where(section == 0, mix[0][0], mix[1][0])
    own_b = jnp.where(section == 0, mix[0][1], mix[1][1])
    active = jnp.where(section == 0, xa, xb) + (own_a * xa + own_b * xb)
    act_ref[...] = active
    nrm_ref[...] = (active * rms_scale(active) * ga_ref[...]).astype(bfloat)
    for weight, target in zip((wq, wk, wv), (q_ref, k_ref, v_ref)):
        target[...] = dot(nrm_ref[...], weight[0]).astype(bfloat)

    def keep_quarters(values, base):
        share = width // 16
        for far in range(4):
            blocks = [values[:, (4 * far + near) * share : (4 * far + near + 1) * share] for near in range(4)]
            for slot, block in enumerate(relative(blocks, quarter)):
                kept[slot][:, base + far * share : base + (far + 1) * share] = block

    attention(q_ref, k_ref, v_ref, seg_ref, att_ref, p_ref)
    middle = act_ref[...] + dot(att_ref[...], wo[0])
    mid_ref[...] = middle
    nf_ref[...] = (middle * rms_scale(middle) * gf_ref[...]).astype(bfloat)
    if fast:
        keep_quarters(att_ref[...], width)
        keep_quarters(nrm_ref[...], width + width // 4)
        for slot in (1, 2):
            kept[slot][:, width + width // 2 :] = nf_ref[...]
    else:
        kept[1][...] = nrm_ref[...]
        kept[2][...] = att_ref[...]
    for piece in range(pieces):
        span = slice(piece * chunk, (piece + 1) * chunk)
        gate = dot(nf_ref[...], wg[0, :, span])
        upward = dot(nf_ref[...], wu[0, :, span])
        wave = gelu_wave(gate)
        half = 0.5 * (1.0 + wave)
        value = gate * half
        hidden = (value * upward).astype(bfloat)
        slope = half + 0.5 * gate * (1.0 - wave * wave) * (GELU_A * (1.0 + 3.0 * GELU_B * gate * gate))
        one_ref[piece] = upward * slope
        two_ref[piece] = value
        if fast:
            share = chunk // 4
            blocks = [hidden[:, near * share : (near + 1) * share] for near in range(4)]
            for slot, block in enumerate(relative(blocks, quarter)):
                kept[slot][:, piece * share : (piece + 1) * share] = block
        else:
            kept[0][:, span] = hidden
        down = dot(hidden, wd[0, span, :])
        if piece == 0:
            acc[...] = down
        else:
            acc[...] += down
    change = mid_ref[...] + acc[...] - act_ref[...]
    chg_ref[...] = change
    xa = x_ref[:, :width].astype(floating)
    xb = x_ref[:, width:].astype(floating)
    out_ref[0, :, :width] = (xa + (mix[0][0] * xa + mix[0][1] * xb) + cor[0] * change).astype(bfloat)
    out_ref[0, :, width:] = (xb + (mix[1][0] * xa + mix[1][1] * xb) + cor[1] * change).astype(bfloat)


def forward(fast, x_in, message, segments, mixing, correction, gain_attn, gain_ffn, weights):
    tokens = x_in.shape[0]
    length = segments.shape[1]
    width = gain_attn.shape[1]
    hidden_width = weights[4].shape[2]
    size = sum(weight.size for weight in weights)
    shape = jax.ShapeDtypeStruct
    narrow = ((tokens, width), bfloat)
    wide = ((tokens, width), floating)
    probs = ((tokens // length * (width // PAIR), 2 * length, length), floating)
    if fast:
        short, long = (((tokens, columns), bfloat) for columns in (width + width // 2, 2 * width + width // 2))
        kept = [short, long, long, short, narrow]
    else:
        kept = [((tokens, hidden_width), bfloat), narrow, narrow, narrow]
    ffn = ((hidden_width // width, tokens, width), floating)
    outs = [((tokens, 2 * width), bfloat), ((1, tokens, 2 * width), bfloat), narrow, narrow, narrow, probs, wide, wide,
            ffn, ffn, wide] + kept
    return pl.pallas_call(
        lambda *refs: forward_kernel(fast, *refs),
        out_shape=[shape(*one) for one in outs],
        in_specs=[VMEM, VMEM, VMEM, SMEM, SMEM, VMEM, VMEM] + [VMEM] * 7,
        out_specs=[VMEM] * len(outs),
        scratch_shapes=[pltpu.VMEM(*narrow)] * 2 + [pltpu.VMEM(*wide)],
        compiler_params=params(SCOPED),
        cost_estimate=cost(2 * tokens * size, 2 * size),
        name="forward_full",
    )(x_in, message, segments, mixing, correction, gain_attn, gain_ffn, *weights)


def start_rows(message, grad_ref, counts_ref, cor_ref, g_ref, low_ref):
    tokens, width = low_ref.shape
    rows = counts_ref.shape[0]
    length = tokens // rows
    section = lax.axis_index("section")
    if message is not None:
        got = read_scalars(message[tokens : tokens + EXTRA, :PAIR].astype(floating), 4)
    place = lax.broadcasted_iota(jnp.int32, (length, width), 0)
    for row in range(rows):
        span = slice(row * length, (row + 1) * length)
        valid = place < counts_ref[row]
        own_a = jnp.where(valid, grad_ref[span, :width].astype(floating), 0.0)
        own_b = jnp.where(valid, grad_ref[span, width:].astype(floating), 0.0)
        if message is not None:
            later_b = own_b + message[span, :].astype(floating)
            far_a = own_a + (got[0] * own_a + got[2] * later_b)
            far_b = later_b + (got[1] * own_a + got[3] * later_b)
            own_a = jnp.where(section == 0, far_a, own_a).astype(bfloat).astype(floating)
            own_b = jnp.where(section == 0, far_b, own_b).astype(bfloat).astype(floating)
        g_ref[span, :width] = own_a.astype(bfloat)
        g_ref[span, width:] = own_b.astype(bfloat)
        low_ref[span, :] = (cor_ref[0, 0] * own_a + cor_ref[0, 1] * own_b).astype(bfloat)


def start(message, out_grad, counts, correction, before):
    tokens = out_grad.shape[0]
    width = message.shape[1]
    shape = jax.ShapeDtypeStruct
    return pl.pallas_call(
        lambda *refs: start_rows(*refs[:4], *refs[-2:]),
        out_shape=[shape((tokens, 2 * width), bfloat), shape((tokens, width), bfloat)],
        in_specs=[VMEM, VMEM, SMEM, SMEM] + [ANY] * len(before),
        out_specs=[VMEM, VMEM],
        compiler_params=params(SCOPED),
        cost_estimate=cost(tokens * width * 20, tokens * width * 12),
        name="backward_start",
    )(message, out_grad, counts, correction, *before)


def norm_backward(values, gain, grad_normed, with_gain):
    inverse = rms_scale(values)
    grad_gain = jnp.sum(grad_normed * values * inverse, axis=0, keepdims=True) if with_gain else None
    weighted = grad_normed * gain
    grad_values = inverse * weighted - values * inverse**3 * jnp.mean(weighted * values, axis=-1, keepdims=True)
    return grad_gain, grad_values


def ffn_steps(low_ref, one, two, wg, wu, wd, acc, emit):
    width = wd.shape[2]
    quarter = lax.axis_index("dp") & 3
    for step in range(4):
        piece = (3 - step) ^ quarter
        span = pl.ds(pl.multiple_of(piece * width, width), width)
        grad_hidden = dot_t(low_ref[...], wd[0, span, :])
        dgate = (grad_hidden * one[piece]).astype(bfloat)
        dup = (grad_hidden * two[piece]).astype(bfloat)
        emit(3 - step, dgate, dup)
        total = dot_t(dgate, wg[0, :, span]) + dot_t(dup, wu[0, :, span])
        if step == 0:
            acc[...] = total
        else:
            acc[...] += total


def ffn_kernel(g_in, low_ref, cor_ref, gf_ref, mid_ref, one, two, wg, wu, wd, *refs):
    slots = refs[-12:-4]
    dmid_ref, datt_ref, gain_ref, acc = refs[-4:]
    width = gf_ref.shape[1]

    def emit(slot, dgate, dup):
        slots[slot][...] = dgate
        slots[4 + slot][...] = dup

    ffn_steps(low_ref, one, two, wg, wu, wd, acc, emit)
    grad_gain, grad_values = norm_backward(mid_ref[...], gf_ref[...], acc[...], True)
    block = cor_ref[0, 0] * g_in[:, :width].astype(floating) + cor_ref[0, 1] * g_in[:, width:].astype(floating)
    grad_middle = block + grad_values
    dmid_ref[...] = grad_middle
    datt_ref[...] = grad_middle.astype(bfloat)
    gain_ref[...] = grad_gain


def ffn_backward(g_in, low, correction, gain_ffn, middle, one, two, before, weights):
    tokens = g_in.shape[0]
    width = gain_ffn.shape[1]
    shape = jax.ShapeDtypeStruct
    return pl.pallas_call(
        ffn_kernel,
        out_shape=[shape((tokens, width), bfloat)] * 8
        + [shape((tokens, width), floating), shape((tokens, width), bfloat), shape((1, width), floating)],
        in_specs=[VMEM, VMEM, SMEM] + [VMEM] * 7 + [ANY] * len(before),
        out_specs=[VMEM] * 11,
        scratch_shapes=[pltpu.VMEM((tokens, width), floating)],
        compiler_params=params(SCOPED),
        cost_estimate=cost(2 * tokens * 3 * weights[4].size, 2 * 3 * weights[4].size),
        name="backward_ffn",
    )(g_in, low, correction, gain_ffn, middle, one, two, *weights[4:], *before)


def attn_steps(q_ref, k_ref, v_ref, p_ref, do_ref, parts):
    tokens, width = do_ref.shape
    length = p_ref.shape[2]
    rows = tokens // length
    pairs = width // PAIR
    first = lane_mask(length)
    for row in range(rows):
        span = slice(row * length, (row + 1) * length)
        for pair in range(pairs):
            heads = slice(pair * PAIR, (pair + 1) * PAIR)
            probs = p_ref[row * pairs + pair]
            grad_out = stack_heads(do_ref[span, heads], first)
            grad_value = t_dot(probs.astype(bfloat), grad_out)
            grad_probs = dot_t(grad_out, v_ref[span, heads])
            carried = jnp.sum(probs * grad_probs, axis=-1, keepdims=True)
            grad_scores = (probs * (grad_probs - carried)).astype(bfloat)
            grad_query = dot(grad_scores, k_ref[span, heads])
            grad_query = jnp.where(first, grad_query[:length], grad_query[length:])
            grad_key = t_dot(grad_scores, stack_heads(q_ref[span, heads], first))
            for (part, base), value in zip(parts, (grad_query * SCALE, grad_key * SCALE, grad_value)):
                part[span, base + pair * PAIR : base + (pair + 1) * PAIR] = value.astype(bfloat)


def normed_grad(parts, rows, width, wq, wk, wv):
    return sum(dot_t(part[:rows, base : base + width], weight[0]) for (part, base), weight in zip(parts, (wq, wk, wv)))


def attn_kernel(datt_ref, q_ref, k_ref, v_ref, p_ref, gfg_ref, ga_ref, x_ref, g_in, dmid_ref, act_ref, chg_ref, mix_ref, cor_ref,
                wq, wk, wv, wo, before,
                grad_ref, right_ref, small_ref, do_ref):
    tokens, width = datt_ref.shape
    right_ref[:tokens, :width] = datt_ref[...]
    do_ref[...] = dot_t(datt_ref[...], wo[0]).astype(bfloat)
    parts = (right_ref, width), (right_ref, 2 * width), (right_ref, 3 * width)
    attn_steps(q_ref, k_ref, v_ref, p_ref, do_ref, parts)
    grad_normed = normed_grad(parts, tokens, width, wq, wk, wv)
    grad_gain, grad_values = norm_backward(act_ref[...], ga_ref[...], grad_normed, True)
    section = lax.axis_index("section")
    mix = [[mix_ref[0, i, j] for j in range(2)] for i in range(2)]
    cor = [cor_ref[0, i] for i in range(2)]
    out_a = g_in[:, :width].astype(floating)
    out_b = g_in[:, width:].astype(floating)
    grad_active = dmid_ref[...] + grad_values - (cor[0] * out_a + cor[1] * out_b)
    pred_a = out_a + jnp.where(section == 0, grad_active, 0.0)
    pred_b = out_b + jnp.where(section == 0, 0.0, grad_active)
    grad_ref[0, :, :width] = (pred_a + (mix[0][0] * pred_a + mix[1][0] * pred_b)).astype(bfloat)
    grad_ref[0, :, width:] = (pred_b + (mix[0][1] * pred_a + mix[1][1] * pred_b)).astype(bfloat)
    xa = x_ref[:, :width].astype(floating)
    xb = x_ref[:, width:].astype(floating)
    small_ref[0:1, :] = grad_gain
    small_ref[1:2, :] = gfg_ref[...]
    place = 2
    for pred in (pred_a, pred_b):
        for state in (xa, xb):
            small_ref[place : place + 1, :] = jnp.sum(pred * state, axis=0, keepdims=True)
            place += 1
    for out in (out_a, out_b):
        small_ref[place : place + 1, :] = jnp.sum(out * chg_ref[...], axis=0, keepdims=True)
        place += 1
    right_ref[tokens:, : 2 * width] = spread(small_ref[...])
    right_ref[tokens:, 2 * width :] = jnp.zeros((right_ref.shape[0] - tokens, 2 * width), bfloat)


def attn_backward(x, g_in, grad_middle, grad_att, active, change, queries, key_rows, value_rows, probs, ffn_gain, gain_attn,
                  mixing, correction, before, weights):
    tokens, width = active.shape
    shape = jax.ShapeDtypeStruct
    return pl.pallas_call(
        attn_kernel,
        out_shape=[
            shape((1, tokens, 2 * width), bfloat), shape((tokens + EXTRA, 4 * width), bfloat), shape((8, width), floating),
        ],
        in_specs=[VMEM] * 12 + [SMEM] * 2 + [VMEM] * 4 + [ANY],
        out_specs=[VMEM] * 3,
        scratch_shapes=[pltpu.VMEM((tokens, width), bfloat)],
        compiler_params=params(SCOPED),
        cost_estimate=cost(2 * tokens * 5 * weights[0].size, 2 * 4 * weights[0].size),
        name="backward_attn",
    )(grad_att, queries, key_rows, value_rows, probs, ffn_gain, gain_attn, x, g_in, grad_middle, active, change,
      mixing, correction, *weights[:4], before)


def relay_kernel(grad_in, counts_ref, cor_ref, mix_ref, gf_ref, ga_ref, one, two, mid_ref, q_ref, k_ref, v_ref, p_ref, act_ref,
                 wq, wk, wv, wo, wg, wu, wd,
                 msg_ref,
                 acc, g_in, low_ref, do_ref, dqkv_ref):
    tokens, width = low_ref.shape
    start_rows(None, grad_in, counts_ref, cor_ref, g_in, low_ref)
    ffn_steps(low_ref, one, two, wg, wu, wd, acc, lambda *parts: None)
    grad_values = norm_backward(mid_ref[...], gf_ref[...], acc[...], False)[1]
    cor = [cor_ref[0, i] for i in range(2)]
    block = cor[0] * g_in[:, :width].astype(floating) + cor[1] * g_in[:, width:].astype(floating)
    acc[...] = block + grad_values
    do_ref[...] = dot_t(acc[...].astype(bfloat), wo[0]).astype(bfloat)
    parts = (dqkv_ref, 0), (dqkv_ref, width), (dqkv_ref, 2 * width)
    attn_steps(q_ref, k_ref, v_ref, p_ref, do_ref, parts)
    grad_normed = normed_grad(parts, tokens, width, wq, wk, wv)
    grad_values = norm_backward(act_ref[...], ga_ref[...], grad_normed, False)[1]
    block = cor[0] * g_in[:, :width].astype(floating) + cor[1] * g_in[:, width:].astype(floating)
    msg_ref[:tokens, :] = (acc[...] + grad_values - block).astype(bfloat)
    mix = [[mix_ref[0, i, j] for j in range(2)] for i in range(2)]
    msg_ref[tokens:, :] = scalar_rows(mix[0] + mix[1], EXTRA, width)


def relay_backward(out_grad, counts, correction, mixing, gain_ffn, gain_attn, one, two, middle, queries, key_rows, value_rows,
                   probs, active, weights):
    tokens, width = active.shape
    shape = jax.ShapeDtypeStruct
    narrow = pltpu.VMEM((tokens, width), bfloat)
    wide = pltpu.VMEM((tokens, width), floating)
    size = sum(weight.size for weight in weights)
    return pl.pallas_call(
        relay_kernel,
        out_shape=shape((tokens + EXTRA, width), bfloat),
        in_specs=[VMEM, SMEM, SMEM, SMEM] + [VMEM] * 17,
        out_specs=VMEM,
        scratch_shapes=[wide, pltpu.VMEM((tokens, 2 * width), bfloat), narrow, narrow, pltpu.VMEM((tokens, 3 * width), bfloat)],
        compiler_params=params(SCOPED),
        cost_estimate=cost(2 * tokens * size, 2 * size),
        name="backward_relay",
    )(out_grad, counts, correction, mixing, gain_ffn, gain_attn, one, two, middle, queries, key_rows, value_rows, probs, active,
      *weights)


def quarter_parts(products, block, lefts, rights, own_ref, far_ref, keep_ref):
    tokens = lefts[0].shape[0]
    index = lax.axis_index("dp")
    near = (index >> 2) & 1
    far = (index >> 3) & 1
    for left_at, left_wide, right_at, right_wide in products:
        rows = slice(left_at, left_at + left_wide)
        span = slice(right_at, right_at + right_wide)
        total = sum(t_dot(left[:, rows], right[:tokens, span]) for left, right in zip(lefts, rights))
        for place in range(4):
            part = total[place * block : (place + 1) * block, :]
            slot = (place >> 1) ^ far
            mine = (place & 1) == near

            @pl.when(mine)
            def _():
                keep_ref[slot, :, span] = part

            @pl.when(jnp.logical_and(jnp.logical_not(mine), slot == 0))
            def _():
                own_ref[:block, span] = part.astype(bfloat)

            @pl.when(jnp.logical_and(jnp.logical_not(mine), slot == 1))
            def _():
                far_ref[:block, span] = part.astype(bfloat)


def quarter_product(lefts, rights, block, before, name):
    rows, wide = lefts[0].shape[0], rights[0].shape[1]
    shape = jax.ShapeDtypeStruct
    products = [(0, 4 * block, 0, wide)]
    return pl.pallas_call(
        lambda *refs: quarter_parts(products, block, refs[:4], refs[4:8], *refs[-3:]),
        out_shape=[shape((block, wide), bfloat), shape((block, wide), bfloat), shape((2, block, wide), floating)],
        in_specs=[VMEM] * 8 + [ANY] * len(before),
        out_specs=[VMEM] * 3,
        compiler_params=params(SCOPED),
        cost_estimate=cost(32 * rows * block * wide, 16 * block * wide),
        name=name,
    )(*lefts, *rights, *before)


def attn_product_kernel(products, block, refs):
    lefts, rights = refs[:4], refs[4:8]
    own_ref, far_ref, keep_ref, small_ref = refs[-4:]
    tokens = lefts[0].shape[0]
    quarter_parts(products, block, lefts, rights, own_ref, far_ref, keep_ref)
    half = far_ref.shape[1] // 2
    small = sum(gathered_parts(right[tokens:, :half]) for right in rights)
    small_ref[...] = small
    far_ref[block:, :half] = spread(small)
    far_ref[block:, half:] = jnp.zeros((EXTRA, half), bfloat)


def attn_product(lefts, rights, products, block, before):
    wide = rights[0].shape[1]
    shape = jax.ShapeDtypeStruct
    return pl.pallas_call(
        lambda *refs: attn_product_kernel(products, block, refs),
        out_shape=[shape((block, wide), bfloat), shape((block + EXTRA, wide), bfloat), shape((2, block, wide), floating),
                   shape((8, wide // 4), floating)],
        in_specs=[VMEM] * 8 + [ANY] * len(before),
        out_specs=[VMEM] * 4,
        compiler_params=params(SCOPED),
        cost_estimate=cost(wide, wide),
        name="product_attn",
    )(*lefts, *rights, *before)


def attn_sum_kernel(keep_ref, came_ref, small_ref, passed_ref, sums_ref):
    block, wide = keep_ref.shape[1:]
    half = wide // 2
    passed_ref[:block, :] = (keep_ref[1] + came_ref[:block, :].astype(floating)).astype(bfloat)
    small = small_ref[...] + gathered_parts(came_ref[block:, :half])
    sums_ref[...] = small
    passed_ref[block:, :half] = spread(small)
    passed_ref[block:, half:] = jnp.zeros((EXTRA, half), bfloat)


def attn_sum(keep, came, small):
    shape = jax.ShapeDtypeStruct
    return pl.pallas_call(
        attn_sum_kernel,
        out_shape=[shape(came.shape, bfloat), shape(small.shape, floating)],
        in_specs=[VMEM] * 3,
        out_specs=[VMEM] * 2,
        compiler_params=params(SCOPED),
        cost_estimate=cost(came.size, came.size),
        name="attn_sum",
    )(keep, came, small)


def attn_end_kernel(keep_ref, own_ref, came_ref, small_ref, *out_refs):
    block, wide = own_ref.shape
    width = wide // 4
    for place in range(4):
        span = slice(place * width, (place + 1) * width)
        total = keep_ref[0, :, span] + own_ref[:, span].astype(floating)
        out_refs[place][0] = total + came_ref[:block, span].astype(floating)
    out_refs[4][...] = small_ref[...] + gathered_parts(came_ref[block:, : 2 * width])


def attn_end(keep, own, came, small):
    block, wide = own.shape
    shape = jax.ShapeDtypeStruct
    return pl.pallas_call(
        attn_end_kernel,
        out_shape=[shape((1, block, wide // 4), floating)] * 4 + [shape(small.shape, floating)],
        in_specs=[VMEM] * 4,
        out_specs=[VMEM] * 5,
        compiler_params=params(SCOPED),
        cost_estimate=cost(own.size, own.size),
        name="attn_end",
    )(keep, own, came, small)


def assemble_kernel(own, one, two, three, gate_ref, up_ref):
    quarter = lax.axis_index("dp") & 3
    width = own.shape[1] // 2
    for slot, piece in enumerate((own, one, two, three)):
        span = pl.ds(pl.multiple_of((slot ^ quarter) * width, width), width)
        gate_ref[0, :, span] = piece[:, :width].astype(floating)
        up_ref[0, :, span] = piece[:, width:].astype(floating)


def assemble(pieces):
    share, double = pieces[0].shape
    shape = jax.ShapeDtypeStruct((1, share, 2 * double), floating)
    return pl.pallas_call(
        assemble_kernel,
        out_shape=[shape, shape],
        in_specs=[VMEM] * 4,
        out_specs=[VMEM] * 2,
        compiler_params=params(SCOPED),
        cost_estimate=cost(share * double * 4, share * double * 24),
        name="assemble",
    )(*pieces)


def exchange(value, flips):
    count = lax.axis_size("dp")
    return lax.ppermute(value, "dp", [(source, source ^ flips) for source in range(count)])


def relative_rows(matrix, order, index):
    bits = len(order)
    block = matrix.shape[0] >> bits
    split = matrix.reshape((2,) * bits + (block, matrix.shape[1]))
    axes = [bits - 1 - bit for bit in order]
    split = jnp.transpose(split, axes + [bits, bits + 1])
    for axis, bit in enumerate(order):
        split = jnp.where((index >> bit) & 1 == 1, jnp.flip(split, axis), split)
    return split.reshape(matrix.shape)


def scatter_sum(left, right, order):
    total = left.shape[0]
    arrived = []
    for step in range(len(order) + 1):
        low = total >> (step + 1) if step < len(order) else 0
        high = total >> step
        part = dot(left[low:high], right)
        for other in arrived:
            part = part + other[low:high].astype(floating)
        if step == len(order):
            return part
        arrived.append(exchange(part.astype(bfloat), 1 << order[step]))


def halving_grads(kept, low, slots, right, index, count):
    width = low.shape[1]
    order = list(range(count.bit_length() - 1))
    hidden, normed, attended, normed_ffn = (relative_rows(one.T, order, index) for one in kept)
    quarter = index & 3
    places = jnp.arange(4) ^ quarter
    dgate = jnp.concatenate(list(jnp.stack(slots[:4])[places]), axis=1)
    dup = jnp.concatenate(list(jnp.stack(slots[4:])[places]), axis=1)
    grad_down = scatter_sum(hidden, low, order)
    grad_gate = scatter_sum(normed_ffn, dgate, order)
    grad_up = scatter_sum(normed_ffn, dup, order)
    grad_out = scatter_sum(attended, right[:, :width], order)
    grad_qkv = scatter_sum(normed, right[:, width:], order)
    grads = [grad_down, grad_gate, grad_up, grad_out] + [grad_qkv[:, place * width : (place + 1) * width] for place in range(3)]
    return [one[None] for one in grads]


def after(values, *earlier):
    return lax.optimization_barrier((values, earlier))[0]


def gather_start(value):
    return [value, exchange(value, 1), exchange(value, 2)]


def gather_end(pieces, *earlier):
    return pieces + [exchange(after(pieces[2], *earlier), 1)]


def swapped(pieces):
    return [pieces[0]] + [exchange(pieces[flips], flips) for flips in (1, 2, 3)]


def sum_once(product, *earlier):
    own, far, keep = product
    passed = keep[1] + after(exchange(far, 4), *earlier).astype(floating)
    return exchange(own, 4), passed.astype(bfloat)


def sum_twice(product, own, came):
    return product[2][0] + own.astype(floating) + came.astype(floating)


def sum_over(value, bits):
    for bit in range(bits):
        value = value + exchange(value, 1 << bit)
    return value


def quarter_grads(normed_ffn, kept, slots, right, down, index):
    width = normed_ffn[0].shape[1]
    share = width // 16
    block = 4 * share
    gates = swapped(slots[:4])
    ups = swapped(list(after(slots[4:], right)))
    down_own, down_passed = sum_once(down, right)
    gate = quarter_product(normed_ffn, gates, block, [right, down_passed, down_own], "product_gate")
    down_came = exchange(down_passed, 8)
    gate_own, gate_passed = sum_once(gate)
    rights = gather_start(after(right, down_came, ups[1:], gate_passed))
    up = quarter_product(normed_ffn, ups, block, [gate[0], down_came], "product_up")
    grad_down = sum_twice(down, down_own, down_came)
    gate_came = exchange(gate_passed, 8)
    up_own, up_passed = sum_once(up)
    up_came = exchange(up_passed, 8)
    rights = gather_end(rights, up_came, gate_came, gate_own)
    products = [(width, block, 0, width), (width + block, block, width, 3 * width)]
    own, far, keep, small = attn_product(kept, rights, products, share, [up_own])
    passed, small = attn_sum(keep, exchange(far, 4), small)
    own = exchange(own, 4)
    up_came, gate_came = after((up_came, gate_came), passed)
    tiles = [sum_twice(gate, gate_own, gate_came).astype(bfloat), sum_twice(up, up_own, up_came).astype(bfloat)]
    quarter = index & 3
    pieces = [
        jnp.concatenate([lax.dynamic_slice_in_dim(tile, (slot ^ quarter) * share, share, axis=0) for tile in tiles], axis=1)
        for slot in range(4)
    ]
    grad_gate, grad_up = assemble(swapped(pieces))
    came = after(exchange(passed, 8), grad_gate)
    *attn_grads, small = attn_end(keep, own, came, small)
    return [grad_down[None], grad_gate, grad_up] + attn_grads, small


def local(states_in, out_grad, counts, segments, mixing, correction, gain_attn, w_query, w_key, w_value, w_attn_out, gain_ffn,
          w_gate, w_up, w_down):
    weights = (w_query, w_key, w_value, w_attn_out, w_gate, w_up, w_down)
    width = gain_attn.shape[1]
    index = lax.axis_index("dp")
    count = lax.axis_size("dp")
    fast = count == 16
    message, *weights = forward_lite(states_in, segments, mixing, correction, gain_attn, gain_ffn, weights)
    message = lax.ppermute(message, "section", [(0, 1), (1, 0)])
    (x, states, queries, key_rows, value_rows, probs, active, middle, one, two, change, *kept) = forward(
        fast, states_in, message, segments, mixing, correction, gain_attn, gain_ffn, weights)
    before = []
    if fast:
        kept, normed_ffn = swapped(kept[:4]), kept[4]
        before = kept[1:]
    message = relay_backward(out_grad, counts, correction, mixing, gain_ffn, gain_attn, one, two, middle, queries, key_rows,
                             value_rows, probs, active, weights)
    message = lax.ppermute(message, "section", [(0, 1), (1, 0)])
    g_in, low = start(message, out_grad, counts, correction, [])
    *slots, grad_middle, grad_att, ffn_gain = ffn_backward(g_in, low, correction, gain_ffn, middle, one, two, before, weights)
    before = slots[0]
    if fast:
        lows = gather_end(gather_start(low), before)
        beside, across = (one[:, width + width // 2 :] for one in kept[1:3])
        normed_ffn = gather_end([normed_ffn, beside, across], before)
        down = quarter_product(kept, lows, width // 4, [before], "product_down")
        before = down[0]
    state_grads, right, small = attn_backward(x, g_in, grad_middle, grad_att, active, change, queries, key_rows, value_rows, probs,
                                              ffn_gain, gain_attn, mixing, correction, before, weights)
    if fast:
        grads, small = quarter_grads(normed_ffn, kept, slots, right, down, index)
    else:
        grads = halving_grads(kept, low, slots, right[: low.shape[0]], index, count)
        small = sum_over(small, count.bit_length() - 1)
    grad_down, grad_gate, grad_up, grad_out, grad_query, grad_key, grad_value = grads
    share = width // count
    gains = lax.dynamic_slice(small, (0, index * share), (2, share))
    sums = jnp.sum(small[2:], axis=1)
    return (
        states,
        state_grads,
        sums[:4].reshape(1, 2, 2),
        sums[4:].reshape(1, 2),
        gains[0:1],
        grad_query,
        grad_key,
        grad_value,
        grad_out,
        gains[1:2],
        grad_gate,
        grad_up,
        grad_down,
    )


def solution(mesh):
    rows = P("dp", None)
    matrix = P("section", None, None)
    vector = P("section", None)
    share = P("section", "dp", None)
    gain_share = P("section", "dp")
    in_specs = (rows, rows, P("dp"), rows, matrix, vector, vector, matrix, matrix, matrix, matrix, vector, matrix, matrix, matrix)
    out_specs = (share, share, matrix, vector, gain_share, share, share, share, share, gain_share, share, share, share)
    return jax.shard_map(local, mesh=mesh, in_specs=in_specs, out_specs=out_specs, check_vma=False)
```

```python
import functools

import jax
import jax.numpy as jnp
from jax import lax
from jax.experimental import pallas as pl
from jax.experimental.pallas import tpu as pltpu
from jax.sharding import PartitionSpec as P

HEAD_DIM = 64
PAIR = 2 * HEAD_DIM
EPSILON = 1e-06
MASKED = -1e30
SCALE = HEAD_DIM ** (-0.5)
GELU_A = 0.7978845608028654
GELU_B = 0.044715
EXTRA = 16
SCOPED = 12
bfloat = jnp.bfloat16
floating = jnp.float32

VMEM = pl.BlockSpec(memory_space=pltpu.VMEM)
SMEM = pl.BlockSpec(memory_space=pltpu.SMEM)
ANY = pl.BlockSpec(memory_space=pltpu.MemorySpace.HBM)


def dot(a, b):
    return jnp.dot(a, b, preferred_element_type=floating)


def dot_t(a, b):
    return lax.dot_general(a, b, (((1,), (1,)), ((), ())), preferred_element_type=floating)


def t_dot(a, b):
    return lax.dot_general(a, b, (((0,), (0,)), ((), ())), preferred_element_type=floating)


def params(mebibytes):
    return pltpu.CompilerParams(vmem_limit_bytes=mebibytes * 1024 * 1024)


def cost(flops, moved):
    return pl.CostEstimate(flops=flops // 1000, bytes_accessed=moved // 1000, transcendentals=0)


def scalar_rows(values, rows, width):
    lane = lax.broadcasted_iota(jnp.int32, (rows, width), 1)
    row = lax.broadcasted_iota(jnp.int32, (rows, width), 0)
    whole = jnp.zeros((rows, width), floating)
    for place, value in enumerate(values):
        whole = jnp.where(lane == place, value, whole)
    high = whole.astype(bfloat).astype(floating)
    middle = (whole - high).astype(bfloat).astype(floating)
    low = whole - high - middle
    part = jnp.where(row == 0, high, jnp.where(row == 1, middle, jnp.where(row == 2, low, 0.0)))
    return part.astype(bfloat)


def spread(value):
    high = value.astype(bfloat).astype(floating)
    middle = (value - high).astype(bfloat).astype(floating)
    low = value - high - middle
    top = jnp.concatenate([high, middle], axis=1)
    bottom = jnp.concatenate([low, jnp.zeros_like(low)], axis=1)
    return jnp.concatenate([top, bottom], axis=0).astype(bfloat)


def gathered_parts(block):
    block = block.astype(floating)
    width = block.shape[1] // 2
    return block[:8, :width] + block[:8, width:] + block[8:, :width]


def read_scalars(block, count):
    lane = lax.broadcasted_iota(jnp.int32, block.shape, 1)
    return [jnp.sum(jnp.where(lane == place, block, 0.0)) for place in range(count)]


def rms_scale(values):
    return lax.rsqrt(jnp.mean(values * values, axis=-1, keepdims=True) + EPSILON)


def lane_mask(length):
    return lax.broadcasted_iota(jnp.int32, (length, PAIR), 1) < HEAD_DIM


def stack_heads(block, first):
    zero = jnp.zeros_like(block)
    return jnp.concatenate([jnp.where(first, block, zero), jnp.where(first, zero, block)], axis=0)


def gelu_wave(gate):
    return jnp.tanh(GELU_A * (gate + GELU_B * gate * gate * gate))


def relative(blocks, index):
    low = (index & 1) == 1
    high = (index >> 1) == 1
    once = [jnp.where(low, blocks[place ^ 1], blocks[place]) for place in range(4)]
    return [jnp.where(high, once[place ^ 2], once[place]) for place in range(4)]


def attention(q_ref, k_ref, v_ref, seg_ref, att_ref, p_ref):
    length = seg_ref.shape[1]
    rows = q_ref.shape[0] // length
    pairs = q_ref.shape[1] // PAIR
    first = lane_mask(length)
    later = lax.broadcasted_iota(jnp.int32, (length, length), 0)
    earlier = lax.broadcasted_iota(jnp.int32, (length, length), 1)
    for row in range(rows):
        documents = jnp.broadcast_to(seg_ref[row : row + 1, :], (length, length)).astype(floating)
        allowed = (earlier <= later) & (documents == documents.T)
        allowed = jnp.concatenate([allowed, allowed], axis=0)
        span = slice(row * length, (row + 1) * length)
        for pair in range(pairs):
            heads = slice(pair * PAIR, (pair + 1) * PAIR)
            stacked = stack_heads(q_ref[span, heads], first)
            scores = jnp.where(allowed, dot_t(stacked, k_ref[span, heads]) * SCALE, MASKED)
            powers = jnp.exp(scores - jnp.max(scores, axis=-1, keepdims=True))
            probs = powers / jnp.sum(powers, axis=-1, keepdims=True)
            if p_ref is not None:
                p_ref[row * pairs + pair] = probs
            mixed = dot(probs.astype(bfloat), v_ref[span, heads])
            att_ref[span, heads] = jnp.where(first, mixed[:length], mixed[length:]).astype(bfloat)


def in_hbm(value):
    return pltpu.with_memory_space_constraint(value, pltpu.MemorySpace.HBM)


def forward_lite_kernel(x_any, seg_any, mix_any, cor_any, ga_any, gf_any, wq, wk, wv, wo, wg, wu, wd,
                        out_ref, wq_s, wk_s, wv_s, wo_s, wg_s, wu_s, wd_s,
                        x_in, seg_ref, mix_ref, cor_ref, ga_ref, gf_ref, q_ref, k_ref, v_ref, act_ref,
                        nrm_ref, att_ref, nf_ref, acc, sem, small_sem):
    tokens, width = act_ref.shape
    chunk = width
    pieces = wg.shape[2] // chunk
    small = [
        pltpu.make_async_copy(source, target, small_sem.at[place])
        for place, (source, target) in enumerate(
            ((x_any, x_in), (mix_any, mix_ref), (ga_any, ga_ref), (seg_any, seg_ref), (gf_any, gf_ref), (cor_any, cor_ref))
        )
    ]
    pairs = [(wq, wq_s), (wk, wk_s), (wv, wv_s), (wo, wo_s)]
    queue = [pltpu.make_async_copy(source, target, sem.at[place]) for place, (source, target) in enumerate(pairs)]

    def group(piece):
        span = pl.ds(pl.multiple_of(piece * chunk, chunk), chunk)
        places = ((wg, wg_s, (slice(None), slice(None), span)), (wu, wu_s, (slice(None), slice(None), span)),
                  (wd, wd_s, (slice(None), span, slice(None))))
        return [
            pltpu.make_async_copy(source.at[where], target.at[where], sem.at[4 + 3 * piece + place])
            for place, (source, target, where) in enumerate(places)
        ]

    def start_group(piece):
        for copy in group(piece):
            copy.start()

    for copy in small + queue:
        copy.start()
    start_group(0)
    for copy in small:
        copy.wait()
    section = lax.axis_index("section")
    mix = [[mix_ref[0, i, j] for j in range(2)] for i in range(2)]
    cor = [cor_ref[0, i] for i in range(2)]
    xa = x_in[:, :width].astype(floating)
    xb = x_in[:, width:].astype(floating)
    own_a = jnp.where(section == 0, mix[0][0], mix[1][0])
    own_b = jnp.where(section == 0, mix[0][1], mix[1][1])
    active = jnp.where(section == 0, xa, xb) + (own_a * xa + own_b * xb)
    act_ref[...] = active
    nrm_ref[...] = (active * rms_scale(active) * ga_ref[...]).astype(bfloat)
    for copy, weight, target in zip(queue, (wq_s, wk_s, wv_s), (q_ref, k_ref, v_ref)):
        copy.wait()
        target[...] = dot(nrm_ref[...], weight[0]).astype(bfloat)
    start_group(1)
    attention(q_ref, k_ref, v_ref, seg_ref, att_ref, None)
    for piece in range(2, pieces):
        start_group(piece)
    queue[3].wait()
    middle = act_ref[...] + dot(att_ref[...], wo_s[0])
    acc[...] = middle - act_ref[...]
    nf_ref[...] = (middle * rms_scale(middle) * gf_ref[...]).astype(bfloat)

    def one_piece(piece, carry):
        span = pl.ds(pl.multiple_of(piece * chunk, chunk), chunk)
        waits = group(piece)
        waits[0].wait()
        gate = dot(nf_ref[...], wg_s[0, :, span])
        waits[1].wait()
        upward = dot(nf_ref[...], wu_s[0, :, span])
        hidden = (0.5 * gate * (1.0 + gelu_wave(gate)) * upward).astype(bfloat)
        waits[2].wait()
        acc[...] += dot(hidden, wd_s[0, span, :])
        return carry

    lax.fori_loop(0, pieces, one_piece, 0)
    out_ref[:tokens, :] = acc[...].astype(bfloat)
    out_ref[tokens:, :] = scalar_rows(mix[0] + mix[1] + cor, EXTRA, width)


def forward_lite(x_in, segments, mixing, correction, gain_attn, gain_ffn, weights):
    tokens = x_in.shape[0]
    width = gain_attn.shape[1]
    size = sum(weight.size for weight in weights)
    narrow = pltpu.VMEM((tokens, width), bfloat)
    wide = pltpu.VMEM((tokens, width), floating)
    args = (x_in, segments, mixing, correction, gain_attn, gain_ffn) + weights
    scratch = [
        pltpu.VMEM(x_in.shape, bfloat), pltpu.VMEM(segments.shape, jnp.int32), pltpu.SMEM(mixing.shape, floating),
        pltpu.SMEM(correction.shape, floating), pltpu.VMEM(gain_attn.shape, floating), pltpu.VMEM(gain_ffn.shape, floating),
        narrow, narrow, narrow, wide, narrow, narrow, narrow, wide,
    ]
    scratch += [pltpu.SemaphoreType.DMA((4 + 3 * (weights[4].shape[2] // width),)), pltpu.SemaphoreType.DMA((6,))]
    return pl.pallas_call(
        forward_lite_kernel,
        out_shape=[jax.ShapeDtypeStruct((tokens + EXTRA, width), bfloat)]
        + [jax.ShapeDtypeStruct(weight.shape, bfloat) for weight in weights],
        in_specs=[ANY] * len(args),
        out_specs=[VMEM] * 8,
        scratch_shapes=scratch,
        compiler_params=params(SCOPED),
        cost_estimate=cost(2 * tokens * size, 2 * size),
        name="forward_lite",
    )(*[in_hbm(one) for one in args])


def forward_kernel(fast, x_in, message, seg_ref, mix_ref, cor_ref, ga_ref, gf_ref, wq, wk, wv, wo, wg, wu, wd,
                   x_ref, out_ref, q_ref, k_ref, v_ref, p_ref, act_ref, mid_ref, one_ref, two_ref, chg_ref, *refs):
    kept = refs[:4]
    nf_ref = refs[-4]
    nrm_ref, att_ref, acc = refs[-3:]
    tokens, width = act_ref.shape
    chunk = width
    pieces = wg.shape[2] // chunk
    section = lax.axis_index("section")
    quarter = lax.axis_index("dp") & 3
    mix = [[mix_ref[0, i, j] for j in range(2)] for i in range(2)]
    cor = [cor_ref[0, i] for i in range(2)]
    xa = x_in[:, :width].astype(floating)
    xb = x_in[:, width:].astype(floating)
    got = read_scalars(message[tokens : tokens + EXTRA, :PAIR].astype(floating), 6)
    moved = message[:tokens, :].astype(floating)
    sent_a = (xa + (got[0] * xa + got[1] * xb) + got[4] * moved).astype(bfloat)
    sent_b = (xb + (got[2] * xa + got[3] * xb) + got[5] * moved).astype(bfloat)
    x_ref[:, :width] = jnp.where(section == 0, x_in[:, :width], sent_a)
    x_ref[:, width:] = jnp.where(section == 0, x_in[:, width:], sent_b)
    xa = x_ref[:, :width].astype(floating)
    xb = x_ref[:, width:].astype(floating)
    own_a = jnp.where(section == 0, mix[0][0], mix[1][0])
    own_b = jnp.where(section == 0, mix[0][1], mix[1][1])
    active = jnp.where(section == 0, xa, xb) + (own_a * xa + own_b * xb)
    act_ref[...] = active
    nrm_ref[...] = (active * rms_scale(active) * ga_ref[...]).astype(bfloat)
    for weight, target in zip((wq, wk, wv), (q_ref, k_ref, v_ref)):
        target[...] = dot(nrm_ref[...], weight[0]).astype(bfloat)

    def keep_quarters(values, base):
        share = width // 16
        for far in range(4):
            blocks = [values[:, (4 * far + near) * share : (4 * far + near + 1) * share] for near in range(4)]
            for slot, block in enumerate(relative(blocks, quarter)):
                target, start = (kept[slot], width + base) if slot < 3 else (refs[4], base)
                target[:, start + far * share : start + (far + 1) * share] = block

    attention(q_ref, k_ref, v_ref, seg_ref, att_ref, p_ref)
    middle = act_ref[...] + dot(att_ref[...], wo[0])
    mid_ref[...] = middle
    nf_ref[...] = (middle * rms_scale(middle) * gf_ref[...]).astype(bfloat)
    if fast:
        keep_quarters(att_ref[...], 0)
        keep_quarters(nrm_ref[...], width // 4)
        for slot in (1, 2):
            kept[slot][:, width + width // 2 :] = nf_ref[...]
    else:
        kept[1][...] = nrm_ref[...]
        kept[2][...] = att_ref[...]
    for piece in range(pieces):
        span = slice(piece * chunk, (piece + 1) * chunk)
        gate = dot(nf_ref[...], wg[0, :, span])
        upward = dot(nf_ref[...], wu[0, :, span])
        wave = gelu_wave(gate)
        half = 0.5 * (1.0 + wave)
        value = gate * half
        hidden = (value * upward).astype(bfloat)
        slope = half + 0.5 * gate * (1.0 - wave * wave) * (GELU_A * (1.0 + 3.0 * GELU_B * gate * gate))
        one_ref[piece] = upward * slope
        two_ref[piece] = value
        if fast:
            share = chunk // 4
            blocks = [hidden[:, near * share : (near + 1) * share] for near in range(4)]
            for slot, block in enumerate(relative(blocks, quarter)):
                kept[slot][:, piece * share : (piece + 1) * share] = block
        else:
            kept[0][:, span] = hidden
        down = dot(hidden, wd[0, span, :])
        if piece == 0:
            acc[...] = down
        else:
            acc[...] += down
    change = mid_ref[...] + acc[...] - act_ref[...]
    chg_ref[...] = change
    xa = x_ref[:, :width].astype(floating)
    xb = x_ref[:, width:].astype(floating)
    out_ref[0, :, :width] = (xa + (mix[0][0] * xa + mix[0][1] * xb) + cor[0] * change).astype(bfloat)
    out_ref[0, :, width:] = (xb + (mix[1][0] * xa + mix[1][1] * xb) + cor[1] * change).astype(bfloat)


def forward(fast, x_in, message, segments, mixing, correction, gain_attn, gain_ffn, weights):
    tokens = x_in.shape[0]
    length = segments.shape[1]
    width = gain_attn.shape[1]
    hidden_width = weights[4].shape[2]
    size = sum(weight.size for weight in weights)
    shape = jax.ShapeDtypeStruct
    narrow = ((tokens, width), bfloat)
    wide = ((tokens, width), floating)
    probs = ((tokens // length * (width // PAIR), 2 * length, length), floating)
    if fast:
        short, long = (((tokens, columns), bfloat) for columns in (width + width // 2, 2 * width + width // 2))
        kept = [short, long, long, narrow, ((tokens, width // 2), bfloat), narrow]
    else:
        kept = [((tokens, hidden_width), bfloat), narrow, narrow, narrow]
    ffn = ((hidden_width // width, tokens, width), floating)
    outs = [((tokens, 2 * width), bfloat), ((1, tokens, 2 * width), bfloat), narrow, narrow, narrow, probs, wide, wide,
            ffn, ffn, wide] + kept
    return pl.pallas_call(
        lambda *refs: forward_kernel(fast, *refs),
        out_shape=[shape(*one) for one in outs],
        in_specs=[VMEM, VMEM, VMEM, SMEM, SMEM, VMEM, VMEM] + [VMEM] * 7,
        out_specs=[VMEM] * len(outs),
        scratch_shapes=[pltpu.VMEM(*narrow)] * 2 + [pltpu.VMEM(*wide)],
        compiler_params=params(SCOPED),
        cost_estimate=cost(2 * tokens * size, 2 * size),
        name="forward_full",
    )(x_in, message, segments, mixing, correction, gain_attn, gain_ffn, *weights)


def start_rows(message, grad_ref, counts_ref, cor_ref, g_ref, low_ref):
    tokens, width = low_ref.shape
    rows = counts_ref.shape[0]
    length = tokens // rows
    section = lax.axis_index("section")
    if message is not None:
        got = read_scalars(message[tokens : tokens + EXTRA, :PAIR].astype(floating), 4)
    place = lax.broadcasted_iota(jnp.int32, (length, width), 0)
    for row in range(rows):
        span = slice(row * length, (row + 1) * length)
        valid = place < counts_ref[row]
        own_a = jnp.where(valid, grad_ref[span, :width].astype(floating), 0.0)
        own_b = jnp.where(valid, grad_ref[span, width:].astype(floating), 0.0)
        if message is not None:
            later_b = own_b + message[span, :].astype(floating)
            far_a = own_a + (got[0] * own_a + got[2] * later_b)
            far_b = later_b + (got[1] * own_a + got[3] * later_b)
            own_a = jnp.where(section == 0, far_a, own_a).astype(bfloat).astype(floating)
            own_b = jnp.where(section == 0, far_b, own_b).astype(bfloat).astype(floating)
        g_ref[span, :width] = own_a.astype(bfloat)
        g_ref[span, width:] = own_b.astype(bfloat)
        low_ref[span, :] = (cor_ref[0, 0] * own_a + cor_ref[0, 1] * own_b).astype(bfloat)


def start(message, out_grad, counts, correction, before):
    tokens = out_grad.shape[0]
    width = message.shape[1]
    shape = jax.ShapeDtypeStruct
    return pl.pallas_call(
        lambda *refs: start_rows(*refs[:4], *refs[-2:]),
        out_shape=[shape((tokens, 2 * width), bfloat), shape((tokens, width), bfloat)],
        in_specs=[VMEM, VMEM, SMEM, SMEM] + [ANY] * len(before),
        out_specs=[VMEM, VMEM],
        compiler_params=params(SCOPED),
        cost_estimate=cost(tokens * width * 20, tokens * width * 12),
        name="backward_start",
    )(message, out_grad, counts, correction, *before)


def norm_backward(values, gain, grad_normed, with_gain):
    inverse = rms_scale(values)
    grad_gain = jnp.sum(grad_normed * values * inverse, axis=0, keepdims=True) if with_gain else None
    weighted = grad_normed * gain
    grad_values = inverse * weighted - values * inverse**3 * jnp.mean(weighted * values, axis=-1, keepdims=True)
    return grad_gain, grad_values


def ffn_steps(low_ref, one, two, wg, wu, wd, acc, emit):
    width = wd.shape[2]
    quarter = lax.axis_index("dp") & 3
    for step in range(4):
        piece = (3 - step) ^ quarter
        span = pl.ds(pl.multiple_of(piece * width, width), width)
        grad_hidden = dot_t(low_ref[...], wd[0, span, :])
        dgate = (grad_hidden * one[piece]).astype(bfloat)
        dup = (grad_hidden * two[piece]).astype(bfloat)
        emit(3 - step, dgate, dup)
        total = dot_t(dgate, wg[0, :, span]) + dot_t(dup, wu[0, :, span])
        if step == 0:
            acc[...] = total
        else:
            acc[...] += total


def ffn_kernel(g_in, low_ref, cor_ref, gf_ref, mid_ref, one, two, wg, wu, wd, *refs):
    slots = refs[-12:-4]
    dmid_ref, datt_ref, gain_ref, acc = refs[-4:]
    width = gf_ref.shape[1]

    def emit(slot, dgate, dup):
        slots[slot][...] = dgate
        slots[4 + slot][...] = dup

    ffn_steps(low_ref, one, two, wg, wu, wd, acc, emit)
    grad_gain, grad_values = norm_backward(mid_ref[...], gf_ref[...], acc[...], True)
    block = cor_ref[0, 0] * g_in[:, :width].astype(floating) + cor_ref[0, 1] * g_in[:, width:].astype(floating)
    grad_middle = block + grad_values
    dmid_ref[...] = grad_middle
    datt_ref[...] = grad_middle.astype(bfloat)
    gain_ref[...] = grad_gain


def ffn_backward(g_in, low, correction, gain_ffn, middle, one, two, before, weights):
    tokens = g_in.shape[0]
    width = gain_ffn.shape[1]
    shape = jax.ShapeDtypeStruct
    return pl.pallas_call(
        ffn_kernel,
        out_shape=[shape((tokens, width), bfloat)] * 8
        + [shape((tokens, width), floating), shape((tokens, width), bfloat), shape((1, width), floating)],
        in_specs=[VMEM, VMEM, SMEM] + [VMEM] * 7 + [ANY] * len(before),
        out_specs=[VMEM] * 11,
        scratch_shapes=[pltpu.VMEM((tokens, width), floating)],
        compiler_params=params(SCOPED),
        cost_estimate=cost(2 * tokens * 3 * weights[4].size, 2 * 3 * weights[4].size),
        name="backward_ffn",
    )(g_in, low, correction, gain_ffn, middle, one, two, *weights[4:], *before)


def attn_steps(q_ref, k_ref, v_ref, p_ref, do_ref, parts):
    tokens, width = do_ref.shape
    length = p_ref.shape[2]
    rows = tokens // length
    pairs = width // PAIR
    first = lane_mask(length)
    for row in range(rows):
        span = slice(row * length, (row + 1) * length)
        for pair in range(pairs):
            heads = slice(pair * PAIR, (pair + 1) * PAIR)
            probs = p_ref[row * pairs + pair]
            grad_out = stack_heads(do_ref[span, heads], first)
            grad_value = t_dot(probs.astype(bfloat), grad_out)
            grad_probs = dot_t(grad_out, v_ref[span, heads])
            carried = jnp.sum(probs * grad_probs, axis=-1, keepdims=True)
            grad_scores = (probs * (grad_probs - carried)).astype(bfloat)
            grad_query = dot(grad_scores, k_ref[span, heads])
            grad_query = jnp.where(first, grad_query[:length], grad_query[length:])
            grad_key = t_dot(grad_scores, stack_heads(q_ref[span, heads], first))
            for (part, base), value in zip(parts, (grad_query * SCALE, grad_key * SCALE, grad_value)):
                part[span, base + pair * PAIR : base + (pair + 1) * PAIR] = value.astype(bfloat)


def normed_grad(parts, rows, width, wq, wk, wv):
    return sum(dot_t(part[:rows, base : base + width], weight[0]) for (part, base), weight in zip(parts, (wq, wk, wv)))


def attn_kernel(datt_ref, q_ref, k_ref, v_ref, p_ref, gfg_ref, ga_ref, x_ref, g_in, dmid_ref, act_ref, chg_ref, mix_ref, cor_ref,
                wq, wk, wv, wo, before,
                grad_ref, right_ref, small_ref, do_ref):
    tokens, width = datt_ref.shape
    right_ref[:tokens, :width] = datt_ref[...]
    do_ref[...] = dot_t(datt_ref[...], wo[0]).astype(bfloat)
    parts = (right_ref, width), (right_ref, 2 * width), (right_ref, 3 * width)
    attn_steps(q_ref, k_ref, v_ref, p_ref, do_ref, parts)
    grad_normed = normed_grad(parts, tokens, width, wq, wk, wv)
    grad_gain, grad_values = norm_backward(act_ref[...], ga_ref[...], grad_normed, True)
    section = lax.axis_index("section")
    mix = [[mix_ref[0, i, j] for j in range(2)] for i in range(2)]
    cor = [cor_ref[0, i] for i in range(2)]
    out_a = g_in[:, :width].astype(floating)
    out_b = g_in[:, width:].astype(floating)
    grad_active = dmid_ref[...] + grad_values - (cor[0] * out_a + cor[1] * out_b)
    pred_a = out_a + jnp.where(section == 0, grad_active, 0.0)
    pred_b = out_b + jnp.where(section == 0, 0.0, grad_active)
    grad_ref[0, :, :width] = (pred_a + (mix[0][0] * pred_a + mix[1][0] * pred_b)).astype(bfloat)
    grad_ref[0, :, width:] = (pred_b + (mix[0][1] * pred_a + mix[1][1] * pred_b)).astype(bfloat)
    xa = x_ref[:, :width].astype(floating)
    xb = x_ref[:, width:].astype(floating)
    small_ref[0:1, :] = grad_gain
    small_ref[1:2, :] = gfg_ref[...]
    place = 2
    for pred in (pred_a, pred_b):
        for state in (xa, xb):
            small_ref[place : place + 1, :] = jnp.sum(pred * state, axis=0, keepdims=True)
            place += 1
    for out in (out_a, out_b):
        small_ref[place : place + 1, :] = jnp.sum(out * chg_ref[...], axis=0, keepdims=True)
        place += 1
    right_ref[tokens:, : 2 * width] = spread(small_ref[...])
    right_ref[tokens:, 2 * width :] = jnp.zeros((right_ref.shape[0] - tokens, 2 * width), bfloat)


def attn_backward(x, g_in, grad_middle, grad_att, active, change, queries, key_rows, value_rows, probs, ffn_gain, gain_attn,
                  mixing, correction, before, weights):
    tokens, width = active.shape
    shape = jax.ShapeDtypeStruct
    return pl.pallas_call(
        attn_kernel,
        out_shape=[
            shape((1, tokens, 2 * width), bfloat), shape((tokens + EXTRA, 4 * width), bfloat), shape((8, width), floating),
        ],
        in_specs=[VMEM] * 12 + [SMEM] * 2 + [VMEM] * 4 + [ANY],
        out_specs=[VMEM] * 3,
        scratch_shapes=[pltpu.VMEM((tokens, width), bfloat)],
        compiler_params=params(SCOPED),
        cost_estimate=cost(2 * tokens * 5 * weights[0].size, 2 * 4 * weights[0].size),
        name="backward_attn",
    )(grad_att, queries, key_rows, value_rows, probs, ffn_gain, gain_attn, x, g_in, grad_middle, active, change,
      mixing, correction, *weights[:4], before)


def relay_kernel(grad_in, counts_ref, cor_ref, mix_ref, gf_ref, ga_ref, one, two, mid_ref, q_ref, k_ref, v_ref, p_ref, act_ref,
                 wq, wk, wv, wo, wg, wu, wd,
                 msg_ref,
                 acc, g_in, low_ref, do_ref, dqkv_ref):
    tokens, width = low_ref.shape
    start_rows(None, grad_in, counts_ref, cor_ref, g_in, low_ref)
    acc[...] = jnp.zeros_like(acc)

    def one_piece(piece, carry):
        span = pl.ds(pl.multiple_of(piece * width, width), width)
        grad_hidden = dot_t(low_ref[...], wd[0, span, :])
        dgate = (grad_hidden * one[piece]).astype(bfloat)
        dup = (grad_hidden * two[piece]).astype(bfloat)
        acc[...] += dot_t(dgate, wg[0, :, span]) + dot_t(dup, wu[0, :, span])
        return carry

    lax.fori_loop(0, one.shape[0], one_piece, 0)
    grad_values = norm_backward(mid_ref[...], gf_ref[...], acc[...], False)[1]
    cor = [cor_ref[0, i] for i in range(2)]
    block = cor[0] * g_in[:, :width].astype(floating) + cor[1] * g_in[:, width:].astype(floating)
    acc[...] = block + grad_values
    do_ref[...] = dot_t(acc[...].astype(bfloat), wo[0]).astype(bfloat)
    parts = (dqkv_ref, 0), (dqkv_ref, width), (dqkv_ref, 2 * width)
    attn_steps(q_ref, k_ref, v_ref, p_ref, do_ref, parts)
    grad_normed = normed_grad(parts, tokens, width, wq, wk, wv)
    grad_values = norm_backward(act_ref[...], ga_ref[...], grad_normed, False)[1]
    block = cor[0] * g_in[:, :width].astype(floating) + cor[1] * g_in[:, width:].astype(floating)
    msg_ref[:tokens, :] = (acc[...] + grad_values - block).astype(bfloat)
    mix = [[mix_ref[0, i, j] for j in range(2)] for i in range(2)]
    msg_ref[tokens:, :] = scalar_rows(mix[0] + mix[1], EXTRA, width)


def relay_backward(out_grad, counts, correction, mixing, gain_ffn, gain_attn, one, two, middle, queries, key_rows, value_rows,
                   probs, active, weights):
    tokens, width = active.shape
    shape = jax.ShapeDtypeStruct
    narrow = pltpu.VMEM((tokens, width), bfloat)
    wide = pltpu.VMEM((tokens, width), floating)
    size = sum(weight.size for weight in weights)
    return pl.pallas_call(
        relay_kernel,
        out_shape=shape((tokens + EXTRA, width), bfloat),
        in_specs=[VMEM, SMEM, SMEM, SMEM] + [VMEM] * 17,
        out_specs=VMEM,
        scratch_shapes=[wide, pltpu.VMEM((tokens, 2 * width), bfloat), narrow, narrow, pltpu.VMEM((tokens, 3 * width), bfloat)],
        compiler_params=params(SCOPED),
        cost_estimate=cost(2 * tokens * size, 2 * size),
        name="backward_relay",
    )(out_grad, counts, correction, mixing, gain_ffn, gain_attn, one, two, middle, queries, key_rows, value_rows, probs, active,
      *weights)


def quarter_kernel(base, products, block, refs):
    count = 4
    lefts = refs[:count]
    rights = refs[count : 2 * count]
    send_ref, keep_ref = refs[-2:]
    quarter_parts(base, products, block, lefts, rights, send_ref, keep_ref)


def quarter_parts(base, products, block, lefts, rights, send_ref, keep_ref):
    tokens = lefts[0].shape[0]
    tail = lefts[0].shape[1] - lefts[-1].shape[1]
    index = lax.axis_index("dp")
    near = (index >> 2) & 1
    far = (index >> 3) & 1
    for left_at, left_wide, right_at, right_wide in products:
        columns = slice(right_at, right_at + right_wide)
        total = 0.0
        for left, right in zip(lefts, rights):
            at = left_at if left.shape[1] > left_at else left_at - tail
            total = total + t_dot(left[:, at : at + left_wide], right[:tokens, columns])
        span = slice(right_at - base, right_at - base + right_wide)
        for place in range(4):
            part = total[place * block : (place + 1) * block, :]
            slot = (place >> 1) ^ far
            mine = (place & 1) == near

            @pl.when(mine)
            def _():
                keep_ref[slot, :, span] = part

            @pl.when(jnp.logical_not(mine))
            def _():
                send_ref[slot, :, span] = part.astype(bfloat)


def attn_product_kernel(halves, block, refs):
    lefts, rights = refs[:4], refs[4:8]
    first_send, first_keep, small_ref, second_send, second_keep, stage = refs[-6:]
    tokens = lefts[0].shape[0]
    wide = first_keep.shape[2]
    quarter_parts(0, halves[0], block, lefts, rights, stage, first_keep)
    first_send[:block, :] = stage[0]
    first_send[block : 2 * block, :] = stage[1]
    small = sum(gathered_parts(right[tokens:, :wide]) for right in rights)
    small_ref[...] = small
    first_send[2 * block :, :] = spread(small)
    quarter_parts(wide, halves[1], block, lefts, rights, second_send, second_keep)


def attn_product(lefts, rights, halves, block, before):
    wide = rights[0].shape[1] // 2
    shape = jax.ShapeDtypeStruct
    send, keep = shape((2, block, wide), bfloat), shape((2, block, wide), floating)
    return pl.pallas_call(
        lambda *refs: attn_product_kernel(halves, block, refs),
        out_shape=[shape((2 * block + EXTRA, wide), bfloat), keep, shape((8, wide // 2), floating), send, keep],
        in_specs=[VMEM] * 8 + [ANY] * len(before),
        out_specs=[VMEM] * 5,
        scratch_shapes=[pltpu.VMEM(send.shape, bfloat)],
        compiler_params=params(SCOPED),
        cost_estimate=cost(wide, wide),
        name="product_attn",
    )(*lefts, *rights, *before)


def first_sum_kernel(keep_ref, came_ref, small_ref, held_ref, passed_ref, sums_ref):
    block = held_ref.shape[0]
    held_ref[...] = keep_ref[0] + came_ref[:block, :].astype(floating)
    passed_ref[:block, :] = (keep_ref[1] + came_ref[block : 2 * block, :].astype(floating)).astype(bfloat)
    small = small_ref[...] + gathered_parts(came_ref[2 * block :, :])
    sums_ref[...] = small
    passed_ref[block:, :] = spread(small)


def first_sum(keep, came, small):
    _, block, wide = keep.shape
    shape = jax.ShapeDtypeStruct
    return pl.pallas_call(
        first_sum_kernel,
        out_shape=[shape((block, wide), floating), shape((block + EXTRA, wide), bfloat), shape(small.shape, floating)],
        in_specs=[VMEM] * 3,
        out_specs=[VMEM] * 3,
        compiler_params=params(SCOPED),
        cost_estimate=cost(wide, wide),
        name="first_sum",
    )(keep, came, small)


def first_end_kernel(held_ref, came_ref, small_ref, left_ref, right_ref, sums_ref):
    block, wide = held_ref.shape
    left_ref[0] = held_ref[:, : wide // 2] + came_ref[:block, : wide // 2].astype(floating)
    right_ref[0] = held_ref[:, wide // 2 :] + came_ref[:block, wide // 2 :].astype(floating)
    sums_ref[...] = small_ref[...] + gathered_parts(came_ref[block:, :])


def first_end(held, came, small):
    block, wide = held.shape
    shape = jax.ShapeDtypeStruct
    return pl.pallas_call(
        first_end_kernel,
        out_shape=[shape((1, block, wide // 2), floating)] * 2 + [shape(small.shape, floating)],
        in_specs=[VMEM] * 3,
        out_specs=[VMEM] * 3,
        compiler_params=params(SCOPED),
        cost_estimate=cost(wide, wide),
        name="first_end",
    )(held, came, small)


def quarter_product(lefts, rights, products, block, before, name):
    base = products[0][2]
    wide = sum(one[3] for one in products)
    shape = jax.ShapeDtypeStruct
    flops = sum(2 * 4 * lefts[0].shape[0] * one[1] * one[3] for one in products)
    return pl.pallas_call(
        lambda *refs: quarter_kernel(base, products, block, refs),
        out_shape=[shape((2, block, wide), bfloat), shape((2, block, wide), floating)],
        in_specs=[VMEM] * 8 + [ANY] * len(before),
        out_specs=[VMEM, VMEM],
        compiler_params=params(SCOPED),
        cost_estimate=cost(flops, 12 * block * wide),
        name=name,
    )(*lefts, *rights, *before)


def assemble_kernel(own, one, two, three, gate_ref, up_ref):
    quarter = lax.axis_index("dp") & 3
    width = own.shape[1] // 2
    for slot, piece in enumerate((own, one, two, three)):
        span = pl.ds(pl.multiple_of((slot ^ quarter) * width, width), width)
        gate_ref[0, :, span] = piece[:, :width].astype(floating)
        up_ref[0, :, span] = piece[:, width:].astype(floating)


def assemble(pieces):
    share, double = pieces[0].shape
    shape = jax.ShapeDtypeStruct((1, share, 2 * double), floating)
    return pl.pallas_call(
        assemble_kernel,
        out_shape=[shape, shape],
        in_specs=[VMEM] * 4,
        out_specs=[VMEM] * 2,
        compiler_params=params(SCOPED),
        cost_estimate=cost(share * double * 4, share * double * 24),
        name="assemble",
    )(*pieces)


def exchange(value, flips):
    count = lax.axis_size("dp")
    return lax.ppermute(value, "dp", [(source, source ^ flips) for source in range(count)])


def relative_rows(matrix, order, index):
    bits = len(order)
    block = matrix.shape[0] >> bits
    split = matrix.reshape((2,) * bits + (block, matrix.shape[1]))
    axes = [bits - 1 - bit for bit in order]
    split = jnp.transpose(split, axes + [bits, bits + 1])
    for axis, bit in enumerate(order):
        split = jnp.where((index >> bit) & 1 == 1, jnp.flip(split, axis), split)
    return split.reshape(matrix.shape)


def scatter_sum(left, right, order):
    total = left.shape[0]
    arrived = []
    for step in range(len(order) + 1):
        low = total >> (step + 1) if step < len(order) else 0
        high = total >> step
        part = dot(left[low:high], right)
        for other in arrived:
            part = part + other[low:high].astype(floating)
        if step == len(order):
            return part
        arrived.append(exchange(part.astype(bfloat), 1 << order[step]))


def halving_grads(kept, low, slots, right, index, count):
    width = low.shape[1]
    order = list(range(count.bit_length() - 1))
    hidden, normed, attended, normed_ffn = (relative_rows(one.T, order, index) for one in kept)
    quarter = index & 3
    places = jnp.arange(4) ^ quarter
    dgate = jnp.concatenate(list(jnp.stack(slots[:4])[places]), axis=1)
    dup = jnp.concatenate(list(jnp.stack(slots[4:])[places]), axis=1)
    grad_down = scatter_sum(hidden, low, order)
    grad_gate = scatter_sum(normed_ffn, dgate, order)
    grad_up = scatter_sum(normed_ffn, dup, order)
    grad_out = scatter_sum(attended, right[:, :width], order)
    grad_qkv = scatter_sum(normed, right[:, width:], order)
    grads = [grad_down, grad_gate, grad_up, grad_out] + [grad_qkv[:, place * width : (place + 1) * width] for place in range(3)]
    return [one[None] for one in grads]


def after(values, *earlier):
    return lax.optimization_barrier((values, earlier))[0]


def gather_start(value):
    return [value, exchange(value, 1), exchange(value, 2)]


def gather_end(pieces, *earlier):
    return pieces + [exchange(after(pieces[2], *earlier), 1)]


def swapped(pieces):
    return [pieces[0]] + [exchange(pieces[flips], flips) for flips in (1, 2, 3)]


def sum_once(pair, *earlier):
    send, keep = pair
    arrived = after(exchange(send, 4), *earlier)
    return keep[0] + arrived[0].astype(floating), (keep[1] + arrived[1].astype(floating)).astype(bfloat)


def sum_twice(held, passed, *earlier):
    return held + after(exchange(passed, 8), *earlier).astype(floating)


def sum_over(value, bits):
    for bit in range(bits):
        value = value + exchange(value, 1 << bit)
    return value


def quarter_grads(normed_ffn, kept, nearby, slots, right, down_pair, index):
    width = normed_ffn[0].shape[1]
    share = width // 16
    block = 4 * share
    whole = [(0, width, 0, width)]
    gates = swapped(slots[:4])
    ups, nearby = after((slots[4:], nearby), right)
    ups, nearby = swapped(list(ups)), exchange(nearby, 3)
    down_sums = sum_once(down_pair, right)
    gate_pair = quarter_product(normed_ffn, gates, whole, block, [right, down_sums[1]], "product_gate")
    grad_down = sum_twice(*down_sums)
    rights = gather_start(after(right, gate_pair[0], grad_down, ups[1:], nearby))
    gate_sums = sum_once(gate_pair)
    up_pair = quarter_product(normed_ffn, ups, whole, block, [gate_sums[1], grad_down], "product_up")
    up_sums = sum_once(up_pair)
    gate_tile = sum_twice(*gate_sums).astype(bfloat)
    rights = gather_end(rights, up_sums[1], gate_tile)
    halves = (
        [(width, block, 0, width), (width + block, block, width, width)], [(width + block, block, 2 * width, 2 * width)])
    before = [up_sums[1], gate_tile]
    first_send, first_keep, small, *second_pair = attn_product(kept[:3] + [nearby], rights, halves, share, before)
    held, first_passed, small = first_sum(first_keep, exchange(first_send, 4), small)
    up_tile = sum_twice(*up_sums, first_passed).astype(bfloat)
    quarter = index & 3
    gate_tile = after(gate_tile, first_passed)
    pieces = [
        jnp.concatenate(
            [lax.dynamic_slice_in_dim(tile, (slot ^ quarter) * share, share, axis=0) for tile in (gate_tile, up_tile)], axis=1)
        for slot in range(4)
    ]
    pieces = swapped(pieces)
    grad_out, grad_query, small = first_end(held, exchange(first_passed, 8), small)
    second_sums = sum_once(second_pair, first_passed)
    grad_gate, grad_up = assemble(list(after(pieces, second_sums[1], small)))
    held, passed = second_sums
    passed = exchange(passed, 8)
    grads = [grad_down[None], grad_gate, grad_up, grad_out, grad_query]
    for span in (slice(0, width), slice(width, 2 * width)):
        grads.append((held[:, span] + passed[:, span].astype(floating))[None])
    return grads, small


def local(states_in, out_grad, counts, segments, mixing, correction, gain_attn, w_query, w_key, w_value, w_attn_out, gain_ffn,
          w_gate, w_up, w_down):
    weights = (w_query, w_key, w_value, w_attn_out, w_gate, w_up, w_down)
    width = gain_attn.shape[1]
    index = lax.axis_index("dp")
    count = lax.axis_size("dp")
    fast = count == 16
    message, *weights = forward_lite(states_in, segments, mixing, correction, gain_attn, gain_ffn, weights)
    message = lax.ppermute(message, "section", [(0, 1), (1, 0)])
    (x, states, queries, key_rows, value_rows, probs, active, middle, one, two, change, *kept) = forward(
        fast, states_in, message, segments, mixing, correction, gain_attn, gain_ffn, weights)
    before = []
    if fast:
        kept, nearby, normed_ffn = swapped(kept[:4]), kept[4], kept[5]
        before = kept[1:]
    message = relay_backward(out_grad, counts, correction, mixing, gain_ffn, gain_attn, one, two, middle, queries, key_rows,
                             value_rows, probs, active, weights)
    message = lax.ppermute(message, "section", [(0, 1), (1, 0)])
    g_in, low = start(message, out_grad, counts, correction, [])
    *slots, grad_middle, grad_att, ffn_gain = ffn_backward(g_in, low, correction, gain_ffn, middle, one, two, before, weights)
    before = slots[0]
    if fast:
        lows = gather_end(gather_start(low), before)
        beside, across = (one[:, width + width // 2 :] for one in kept[1:3])
        normed_ffn = gather_end([normed_ffn, beside, across], before)
        down_pair = quarter_product(kept, lows, [(0, width, 0, width)], width // 4, [before], "product_down")
        before = down_pair[0]
    state_grads, right, small = attn_backward(x, g_in, grad_middle, grad_att, active, change, queries, key_rows, value_rows, probs,
                                              ffn_gain, gain_attn, mixing, correction, before, weights)
    if fast:
        grads, small = quarter_grads(normed_ffn, kept, nearby, slots, right, down_pair, index)
    else:
        grads = halving_grads(kept, low, slots, right[: low.shape[0]], index, count)
        small = sum_over(small, count.bit_length() - 1)
    grad_down, grad_gate, grad_up, grad_out, grad_query, grad_key, grad_value = grads
    share = width // count
    gains = lax.dynamic_slice(small, (0, index * share), (2, share))
    sums = jnp.sum(small[2:], axis=1)
    return (
        states,
        state_grads,
        sums[:4].reshape(1, 2, 2),
        sums[4:].reshape(1, 2),
        gains[0:1],
        grad_query,
        grad_key,
        grad_value,
        grad_out,
        gains[1:2],
        grad_gate,
        grad_up,
        grad_down,
    )


def solution(mesh):
    rows = P("dp", None)
    matrix = P("section", None, None)
    vector = P("section", None)
    share = P("section", "dp", None)
    gain_share = P("section", "dp")
    in_specs = (rows, rows, P("dp"), rows, matrix, vector, vector, matrix, matrix, matrix, matrix, vector, matrix, matrix, matrix)
    out_specs = (share, share, matrix, vector, gain_share, share, share, share, share, gain_share, share, share, share)
    return jax.shard_map(local, mesh=mesh, in_specs=in_specs, out_specs=out_specs, check_vma=False)
```

```python
import functools

import jax
import jax.numpy as jnp
from jax import lax
from jax.experimental import pallas as pl
from jax.experimental.pallas import tpu as pltpu
from jax.sharding import PartitionSpec as P

HEAD_DIM = 64
PAIR = 2 * HEAD_DIM
EPSILON = 1e-06
MASKED = -1e30
SCALE = HEAD_DIM ** (-0.5)
GELU_A = 0.7978845608028654
GELU_B = 0.044715
EXTRA = 16
CHUNK = 256
SCOPED = 12
bfloat = jnp.bfloat16
floating = jnp.float32

VMEM = pl.BlockSpec(memory_space=pltpu.VMEM)
SMEM = pl.BlockSpec(memory_space=pltpu.SMEM)
ANY = pl.BlockSpec(memory_space=pltpu.MemorySpace.HBM)


def dot(a, b):
    return jnp.dot(a, b, preferred_element_type=floating)


def dot_t(a, b):
    return lax.dot_general(a, b, (((1,), (1,)), ((), ())), preferred_element_type=floating)


def t_dot(a, b):
    return lax.dot_general(a, b, (((0,), (0,)), ((), ())), preferred_element_type=floating)


def params(mebibytes):
    return pltpu.CompilerParams(vmem_limit_bytes=mebibytes * 1024 * 1024)


def cost(flops, moved):
    return pl.CostEstimate(flops=flops // 1000, bytes_accessed=moved // 1000, transcendentals=0)


def scalar_rows(values, rows, width):
    lane = lax.broadcasted_iota(jnp.int32, (rows, width), 1)
    row = lax.broadcasted_iota(jnp.int32, (rows, width), 0)
    whole = jnp.zeros((rows, width), floating)
    for place, value in enumerate(values):
        whole = jnp.where(lane == place, value, whole)
    high = whole.astype(bfloat).astype(floating)
    middle = (whole - high).astype(bfloat).astype(floating)
    low = whole - high - middle
    part = jnp.where(row == 0, high, jnp.where(row == 1, middle, jnp.where(row == 2, low, 0.0)))
    return part.astype(bfloat)


def spread(value):
    high = value.astype(bfloat).astype(floating)
    middle = (value - high).astype(bfloat).astype(floating)
    low = value - high - middle
    top = jnp.concatenate([high, middle], axis=1)
    bottom = jnp.concatenate([low, jnp.zeros_like(low)], axis=1)
    return jnp.concatenate([top, bottom], axis=0).astype(bfloat)


def gathered_parts(block):
    block = block.astype(floating)
    width = block.shape[1] // 2
    return block[:8, :width] + block[:8, width:] + block[8:, :width]


def read_scalars(block, count):
    lane = lax.broadcasted_iota(jnp.int32, block.shape, 1)
    return [jnp.sum(jnp.where(lane == place, block, 0.0)) for place in range(count)]


def rms_scale(values):
    return lax.rsqrt(jnp.mean(values * values, axis=-1, keepdims=True) + EPSILON)


def lane_mask(length):
    return lax.broadcasted_iota(jnp.int32, (length, PAIR), 1) < HEAD_DIM


def stack_heads(block, first):
    zero = jnp.zeros_like(block)
    return jnp.concatenate([jnp.where(first, block, zero), jnp.where(first, zero, block)], axis=0)


def gelu_wave(gate):
    return jnp.tanh(GELU_A * (gate + GELU_B * gate * gate * gate))


def relative(blocks, index):
    low = (index & 1) == 1
    high = (index >> 1) == 1
    once = [jnp.where(low, blocks[place ^ 1], blocks[place]) for place in range(4)]
    return [jnp.where(high, once[place ^ 2], once[place]) for place in range(4)]


def attention(q_ref, k_ref, v_ref, seg_ref, att_ref, p_ref):
    length = seg_ref.shape[1]
    rows = q_ref.shape[0] // length
    pairs = q_ref.shape[1] // PAIR
    first = lane_mask(length)
    later = lax.broadcasted_iota(jnp.int32, (length, length), 0)
    earlier = lax.broadcasted_iota(jnp.int32, (length, length), 1)
    for row in range(rows):
        documents = jnp.broadcast_to(seg_ref[row : row + 1, :], (length, length)).astype(floating)
        allowed = (earlier <= later) & (documents == documents.T)
        allowed = jnp.concatenate([allowed, allowed], axis=0)
        span = slice(row * length, (row + 1) * length)
        for pair in range(pairs):
            heads = slice(pair * PAIR, (pair + 1) * PAIR)
            stacked = stack_heads(q_ref[span, heads], first)
            scores = jnp.where(allowed, dot_t(stacked, k_ref[span, heads]) * SCALE, MASKED)
            powers = jnp.exp(scores - jnp.max(scores, axis=-1, keepdims=True))
            probs = powers / jnp.sum(powers, axis=-1, keepdims=True)
            if p_ref is not None:
                p_ref[row * pairs + pair] = probs
            mixed = dot(probs.astype(bfloat), v_ref[span, heads])
            att_ref[span, heads] = jnp.where(first, mixed[:length], mixed[length:]).astype(bfloat)


def in_hbm(value):
    return pltpu.with_memory_space_constraint(value, pltpu.MemorySpace.HBM)


def forward_lite_kernel(x_any, seg_any, mix_any, cor_any, ga_any, gf_any, wq, wk, wv, wo, wg, wu, wd,
                        out_ref, wq_s, wk_s, wv_s, wo_s, wg_s, wu_s, wd_s,
                        x_in, seg_ref, mix_ref, cor_ref, ga_ref, gf_ref, q_ref, k_ref, v_ref, act_ref,
                        nrm_ref, att_ref, nf_ref, acc, sem, small_sem):
    tokens, width = act_ref.shape
    chunk = width
    pieces = wg.shape[2] // chunk
    small = [
        pltpu.make_async_copy(source, target, small_sem.at[place])
        for place, (source, target) in enumerate(
            ((x_any, x_in), (mix_any, mix_ref), (ga_any, ga_ref), (seg_any, seg_ref), (gf_any, gf_ref), (cor_any, cor_ref))
        )
    ]
    pairs = [(wq, wq_s), (wk, wk_s), (wv, wv_s), (wo, wo_s)]
    queue = [pltpu.make_async_copy(source, target, sem.at[place]) for place, (source, target) in enumerate(pairs)]

    def group(piece):
        span = pl.ds(pl.multiple_of(piece * chunk, chunk), chunk)
        places = ((wg, wg_s, (slice(None), slice(None), span)), (wu, wu_s, (slice(None), slice(None), span)),
                  (wd, wd_s, (slice(None), span, slice(None))))
        return [
            pltpu.make_async_copy(source.at[where], target.at[where], sem.at[4 + 3 * piece + place])
            for place, (source, target, where) in enumerate(places)
        ]

    def start_group(piece):
        for copy in group(piece):
            copy.start()

    for copy in small + queue:
        copy.start()
    start_group(0)
    for copy in small:
        copy.wait()
    section = lax.axis_index("section")
    mix = [[mix_ref[0, i, j] for j in range(2)] for i in range(2)]
    cor = [cor_ref[0, i] for i in range(2)]
    xa = x_in[:, :width].astype(floating)
    xb = x_in[:, width:].astype(floating)
    own_a = jnp.where(section == 0, mix[0][0], mix[1][0])
    own_b = jnp.where(section == 0, mix[0][1], mix[1][1])
    active = jnp.where(section == 0, xa, xb) + (own_a * xa + own_b * xb)
    act_ref[...] = active
    nrm_ref[...] = (active * rms_scale(active) * ga_ref[...]).astype(bfloat)
    for copy, weight, target in zip(queue, (wq_s, wk_s, wv_s), (q_ref, k_ref, v_ref)):
        copy.wait()
        target[...] = dot(nrm_ref[...], weight[0]).astype(bfloat)
    start_group(1)
    attention(q_ref, k_ref, v_ref, seg_ref, att_ref, None)
    for piece in range(2, pieces):
        start_group(piece)
    queue[3].wait()
    middle = act_ref[...] + dot(att_ref[...], wo_s[0])
    acc[...] = middle - act_ref[...]
    nf_ref[...] = (middle * rms_scale(middle) * gf_ref[...]).astype(bfloat)

    def one_piece(piece, carry):
        span = pl.ds(pl.multiple_of(piece * chunk, chunk), chunk)
        waits = group(piece)
        waits[0].wait()
        gate = dot(nf_ref[...], wg_s[0, :, span])
        waits[1].wait()
        upward = dot(nf_ref[...], wu_s[0, :, span])
        hidden = (0.5 * gate * (1.0 + gelu_wave(gate)) * upward).astype(bfloat)
        waits[2].wait()
        acc[...] += dot(hidden, wd_s[0, span, :])
        return carry

    lax.fori_loop(0, pieces, one_piece, 0)
    out_ref[:tokens, :] = acc[...].astype(bfloat)
    out_ref[tokens:, :] = scalar_rows(mix[0] + mix[1] + cor, EXTRA, width)


def forward_lite(x_in, segments, mixing, correction, gain_attn, gain_ffn, weights):
    tokens = x_in.shape[0]
    width = gain_attn.shape[1]
    size = sum(weight.size for weight in weights)
    narrow = pltpu.VMEM((tokens, width), bfloat)
    wide = pltpu.VMEM((tokens, width), floating)
    args = (x_in, segments, mixing, correction, gain_attn, gain_ffn) + weights
    scratch = [
        pltpu.VMEM(x_in.shape, bfloat), pltpu.VMEM(segments.shape, jnp.int32), pltpu.SMEM(mixing.shape, floating),
        pltpu.SMEM(correction.shape, floating), pltpu.VMEM(gain_attn.shape, floating), pltpu.VMEM(gain_ffn.shape, floating),
        narrow, narrow, narrow, wide, narrow, narrow, narrow, wide,
    ]
    scratch += [pltpu.SemaphoreType.DMA((4 + 3 * (weights[4].shape[2] // width),)), pltpu.SemaphoreType.DMA((6,))]
    return pl.pallas_call(
        forward_lite_kernel,
        out_shape=[jax.ShapeDtypeStruct((tokens + EXTRA, width), bfloat)]
        + [jax.ShapeDtypeStruct(weight.shape, bfloat) for weight in weights],
        in_specs=[ANY] * len(args),
        out_specs=[VMEM] * 8,
        scratch_shapes=scratch,
        compiler_params=params(SCOPED),
        cost_estimate=cost(2 * tokens * size, 2 * size),
        name="forward_lite",
    )(*[in_hbm(one) for one in args])


def forward_kernel(fast, x_in, message, seg_ref, mix_ref, cor_ref, ga_ref, gf_ref, wq, wk, wv, wo, wg, wu, wd,
                   x_ref, out_ref, q_ref, k_ref, v_ref, p_ref, act_ref, mid_ref, one_ref, two_ref, chg_ref, *refs):
    kept = refs[:4]
    nf_ref = refs[-4]
    nrm_ref, att_ref, acc = refs[-3:]
    tokens, width = act_ref.shape
    chunk = width
    pieces = wg.shape[2] // chunk
    section = lax.axis_index("section")
    quarter = lax.axis_index("dp") & 3
    mix = [[mix_ref[0, i, j] for j in range(2)] for i in range(2)]
    cor = [cor_ref[0, i] for i in range(2)]
    xa = x_in[:, :width].astype(floating)
    xb = x_in[:, width:].astype(floating)
    got = read_scalars(message[tokens : tokens + EXTRA, :PAIR].astype(floating), 6)
    moved = message[:tokens, :].astype(floating)
    sent_a = (xa + (got[0] * xa + got[1] * xb) + got[4] * moved).astype(bfloat)
    sent_b = (xb + (got[2] * xa + got[3] * xb) + got[5] * moved).astype(bfloat)
    x_ref[:, :width] = jnp.where(section == 0, x_in[:, :width], sent_a)
    x_ref[:, width:] = jnp.where(section == 0, x_in[:, width:], sent_b)
    xa = x_ref[:, :width].astype(floating)
    xb = x_ref[:, width:].astype(floating)
    own_a = jnp.where(section == 0, mix[0][0], mix[1][0])
    own_b = jnp.where(section == 0, mix[0][1], mix[1][1])
    active = jnp.where(section == 0, xa, xb) + (own_a * xa + own_b * xb)
    act_ref[...] = active
    nrm_ref[...] = (active * rms_scale(active) * ga_ref[...]).astype(bfloat)
    for weight, target in zip((wq, wk, wv), (q_ref, k_ref, v_ref)):
        target[...] = dot(nrm_ref[...], weight[0]).astype(bfloat)

    def keep_quarters(values, base):
        share = width // 16
        for far in range(4):
            blocks = [values[:, (4 * far + near) * share : (4 * far + near + 1) * share] for near in range(4)]
            for slot, block in enumerate(relative(blocks, quarter)):
                target, start = (kept[slot], width + base) if slot < 3 else (refs[4], base)
                target[:, start + far * share : start + (far + 1) * share] = block

    attention(q_ref, k_ref, v_ref, seg_ref, att_ref, p_ref)
    middle = act_ref[...] + dot(att_ref[...], wo[0])
    mid_ref[...] = middle
    nf_ref[...] = (middle * rms_scale(middle) * gf_ref[...]).astype(bfloat)
    if fast:
        keep_quarters(att_ref[...], 0)
        keep_quarters(nrm_ref[...], width // 4)
        for slot in (1, 2):
            kept[slot][:, width + width // 2 :] = nf_ref[...]
    else:
        kept[1][...] = nrm_ref[...]
        kept[2][...] = att_ref[...]
    for piece in range(pieces):
        span = slice(piece * chunk, (piece + 1) * chunk)
        gate = dot(nf_ref[...], wg[0, :, span])
        upward = dot(nf_ref[...], wu[0, :, span])
        wave = gelu_wave(gate)
        half = 0.5 * (1.0 + wave)
        value = gate * half
        hidden = (value * upward).astype(bfloat)
        slope = half + 0.5 * gate * (1.0 - wave * wave) * (GELU_A * (1.0 + 3.0 * GELU_B * gate * gate))
        one_ref[piece] = upward * slope
        two_ref[piece] = value
        if fast:
            share = chunk // 4
            blocks = [hidden[:, near * share : (near + 1) * share] for near in range(4)]
            for slot, block in enumerate(relative(blocks, quarter)):
                kept[slot][:, piece * share : (piece + 1) * share] = block
        else:
            kept[0][:, span] = hidden
        down = dot(hidden, wd[0, span, :])
        if piece == 0:
            acc[...] = down
        else:
            acc[...] += down
    change = mid_ref[...] + acc[...] - act_ref[...]
    chg_ref[...] = change
    xa = x_ref[:, :width].astype(floating)
    xb = x_ref[:, width:].astype(floating)
    out_ref[0, :, :width] = (xa + (mix[0][0] * xa + mix[0][1] * xb) + cor[0] * change).astype(bfloat)
    out_ref[0, :, width:] = (xb + (mix[1][0] * xa + mix[1][1] * xb) + cor[1] * change).astype(bfloat)


def forward(fast, x_in, message, segments, mixing, correction, gain_attn, gain_ffn, weights):
    tokens = x_in.shape[0]
    length = segments.shape[1]
    width = gain_attn.shape[1]
    hidden_width = weights[4].shape[2]
    size = sum(weight.size for weight in weights)
    shape = jax.ShapeDtypeStruct
    narrow = ((tokens, width), bfloat)
    wide = ((tokens, width), floating)
    probs = ((tokens // length * (width // PAIR), 2 * length, length), floating)
    if fast:
        short, long = (((tokens, columns), bfloat) for columns in (width + width // 2, 2 * width + width // 2))
        kept = [short, long, long, narrow, ((tokens, width // 2), bfloat), narrow]
    else:
        kept = [((tokens, hidden_width), bfloat), narrow, narrow, narrow]
    ffn = ((hidden_width // width, tokens, width), floating)
    outs = [((tokens, 2 * width), bfloat), ((1, tokens, 2 * width), bfloat), narrow, narrow, narrow, probs, wide, wide,
            ffn, ffn, wide] + kept
    return pl.pallas_call(
        lambda *refs: forward_kernel(fast, *refs),
        out_shape=[shape(*one) for one in outs],
        in_specs=[VMEM, VMEM, VMEM, SMEM, SMEM, VMEM, VMEM] + [VMEM] * 7,
        out_specs=[VMEM] * len(outs),
        scratch_shapes=[pltpu.VMEM(*narrow)] * 2 + [pltpu.VMEM(*wide)],
        compiler_params=params(SCOPED),
        cost_estimate=cost(2 * tokens * size, 2 * size),
        name="forward_full",
    )(x_in, message, segments, mixing, correction, gain_attn, gain_ffn, *weights)


def start_rows(message, grad_ref, counts_ref, cor_ref, g_ref, low_ref):
    tokens, width = low_ref.shape
    rows = counts_ref.shape[0]
    length = tokens // rows
    section = lax.axis_index("section")
    if message is not None:
        got = read_scalars(message[tokens : tokens + EXTRA, :PAIR].astype(floating), 4)
    place = lax.broadcasted_iota(jnp.int32, (tokens, width), 0)
    valid = place < counts_ref[0]
    for row in range(1, rows):
        valid = valid | ((place >= row * length) & (place < row * length + counts_ref[row]))
    own_a = jnp.where(valid, grad_ref[:, :width].astype(floating), 0.0)
    own_b = jnp.where(valid, grad_ref[:, width:].astype(floating), 0.0)
    if message is not None:
        later_b = own_b + message[:tokens, :].astype(floating)
        far_a = own_a + (got[0] * own_a + got[2] * later_b)
        far_b = later_b + (got[1] * own_a + got[3] * later_b)
        own_a = jnp.where(section == 0, far_a, own_a).astype(bfloat).astype(floating)
        own_b = jnp.where(section == 0, far_b, own_b).astype(bfloat).astype(floating)
    g_ref[:, :width] = own_a.astype(bfloat)
    g_ref[:, width:] = own_b.astype(bfloat)
    low_ref[...] = (cor_ref[0, 0] * own_a + cor_ref[0, 1] * own_b).astype(bfloat)


def start(message, out_grad, counts, correction, before):
    tokens = out_grad.shape[0]
    width = message.shape[1]
    shape = jax.ShapeDtypeStruct
    return pl.pallas_call(
        lambda *refs: start_rows(*refs[:4], *refs[-2:]),
        out_shape=[shape((tokens, 2 * width), bfloat), shape((tokens, width), bfloat)],
        in_specs=[VMEM, VMEM, SMEM, SMEM] + [ANY] * len(before),
        out_specs=[VMEM, VMEM],
        compiler_params=params(SCOPED),
        cost_estimate=cost(tokens * width * 20, tokens * width * 12),
        name="backward_start",
    )(message, out_grad, counts, correction, *before)


def norm_backward(values, gain, grad_normed, with_gain):
    inverse = rms_scale(values)
    grad_gain = jnp.sum(grad_normed * values * inverse, axis=0, keepdims=True) if with_gain else None
    weighted = grad_normed * gain
    grad_values = inverse * weighted - values * inverse**3 * jnp.mean(weighted * values, axis=-1, keepdims=True)
    return grad_gain, grad_values


def ffn_steps(low_ref, one, two, wg, wu, wd, acc, emit):
    width = wd.shape[2]
    quarter = lax.axis_index("dp") & 3
    for step in range(4):
        piece = (3 - step) ^ quarter
        span = pl.ds(pl.multiple_of(piece * width, width), width)
        grad_hidden = dot_t(low_ref[...], wd[0, span, :])
        dgate = (grad_hidden * one[piece]).astype(bfloat)
        dup = (grad_hidden * two[piece]).astype(bfloat)
        emit(3 - step, dgate, dup)
        total = dot_t(dgate, wg[0, :, span]) + dot_t(dup, wu[0, :, span])
        if step == 0:
            acc[...] = total
        else:
            acc[...] += total


def ffn_kernel(g_in, low_ref, cor_ref, gf_ref, mid_ref, one, two, wg, wu, wd, *refs):
    slots = refs[-12:-4]
    dmid_ref, datt_ref, gain_ref, acc = refs[-4:]
    width = gf_ref.shape[1]

    def emit(slot, dgate, dup):
        slots[slot][...] = dgate
        slots[4 + slot][...] = dup

    ffn_steps(low_ref, one, two, wg, wu, wd, acc, emit)
    grad_gain, grad_values = norm_backward(mid_ref[...], gf_ref[...], acc[...], True)
    block = cor_ref[0, 0] * g_in[:, :width].astype(floating) + cor_ref[0, 1] * g_in[:, width:].astype(floating)
    grad_middle = block + grad_values
    dmid_ref[...] = grad_middle
    datt_ref[...] = grad_middle.astype(bfloat)
    gain_ref[...] = grad_gain


def ffn_backward(g_in, low, correction, gain_ffn, middle, one, two, before, weights):
    tokens = g_in.shape[0]
    width = gain_ffn.shape[1]
    shape = jax.ShapeDtypeStruct
    return pl.pallas_call(
        ffn_kernel,
        out_shape=[shape((tokens, width), bfloat)] * 8
        + [shape((tokens, width), floating), shape((tokens, width), bfloat), shape((1, width), floating)],
        in_specs=[VMEM, VMEM, SMEM] + [VMEM] * 7 + [ANY] * len(before),
        out_specs=[VMEM] * 11,
        scratch_shapes=[pltpu.VMEM((tokens, width), floating)],
        compiler_params=params(SCOPED),
        cost_estimate=cost(2 * tokens * 3 * weights[4].size, 2 * 3 * weights[4].size),
        name="backward_ffn",
    )(g_in, low, correction, gain_ffn, middle, one, two, *weights[4:], *before)


def attn_steps(q_ref, k_ref, v_ref, p_ref, do_ref, parts):
    tokens, width = do_ref.shape
    length = p_ref.shape[2]
    rows = tokens // length
    pairs = width // PAIR
    first = lane_mask(length)
    for row in range(rows):
        span = slice(row * length, (row + 1) * length)
        for pair in range(pairs):
            heads = slice(pair * PAIR, (pair + 1) * PAIR)
            probs = p_ref[row * pairs + pair]
            grad_out = stack_heads(do_ref[span, heads], first)
            grad_value = t_dot(probs.astype(bfloat), grad_out)
            grad_probs = dot_t(grad_out, v_ref[span, heads])
            carried = jnp.sum(probs * grad_probs, axis=-1, keepdims=True)
            grad_scores = (probs * (grad_probs - carried)).astype(bfloat)
            grad_query = dot(grad_scores, k_ref[span, heads])
            grad_query = jnp.where(first, grad_query[:length], grad_query[length:])
            grad_key = t_dot(grad_scores, stack_heads(q_ref[span, heads], first))
            for (part, base), value in zip(parts, (grad_query * SCALE, grad_key * SCALE, grad_value)):
                part[span, base + pair * PAIR : base + (pair + 1) * PAIR] = value.astype(bfloat)


def normed_grad(parts, rows, width, wq, wk, wv):
    return sum(dot_t(part[:rows, base : base + width], weight[0]) for (part, base), weight in zip(parts, (wq, wk, wv)))


def attn_kernel(datt_ref, q_ref, k_ref, v_ref, p_ref, gfg_ref, ga_ref, x_ref, g_in, dmid_ref, act_ref, chg_ref, mix_ref, cor_ref,
                wq, wk, wv, wo, before,
                grad_ref, right_ref, small_ref, do_ref):
    tokens, width = datt_ref.shape
    right_ref[:tokens, :width] = datt_ref[...]
    do_ref[...] = dot_t(datt_ref[...], wo[0]).astype(bfloat)
    parts = (right_ref, width), (right_ref, 2 * width), (right_ref, 3 * width)
    attn_steps(q_ref, k_ref, v_ref, p_ref, do_ref, parts)
    grad_normed = normed_grad(parts, tokens, width, wq, wk, wv)
    grad_gain, grad_values = norm_backward(act_ref[...], ga_ref[...], grad_normed, True)
    section = lax.axis_index("section")
    mix = [[mix_ref[0, i, j] for j in range(2)] for i in range(2)]
    cor = [cor_ref[0, i] for i in range(2)]
    out_a = g_in[:, :width].astype(floating)
    out_b = g_in[:, width:].astype(floating)
    grad_active = dmid_ref[...] + grad_values - (cor[0] * out_a + cor[1] * out_b)
    pred_a = out_a + jnp.where(section == 0, grad_active, 0.0)
    pred_b = out_b + jnp.where(section == 0, 0.0, grad_active)
    grad_ref[0, :, :width] = (pred_a + (mix[0][0] * pred_a + mix[1][0] * pred_b)).astype(bfloat)
    grad_ref[0, :, width:] = (pred_b + (mix[0][1] * pred_a + mix[1][1] * pred_b)).astype(bfloat)
    xa = x_ref[:, :width].astype(floating)
    xb = x_ref[:, width:].astype(floating)
    small_ref[0:1, :] = grad_gain
    small_ref[1:2, :] = gfg_ref[...]
    place = 2
    for pred in (pred_a, pred_b):
        for state in (xa, xb):
            small_ref[place : place + 1, :] = jnp.sum(pred * state, axis=0, keepdims=True)
            place += 1
    for out in (out_a, out_b):
        small_ref[place : place + 1, :] = jnp.sum(out * chg_ref[...], axis=0, keepdims=True)
        place += 1
    right_ref[tokens:, : 2 * width] = spread(small_ref[...])
    right_ref[tokens:, 2 * width :] = jnp.zeros((right_ref.shape[0] - tokens, 2 * width), bfloat)


def attn_backward(x, g_in, grad_middle, grad_att, active, change, queries, key_rows, value_rows, probs, ffn_gain, gain_attn,
                  mixing, correction, before, weights):
    tokens, width = active.shape
    shape = jax.ShapeDtypeStruct
    return pl.pallas_call(
        attn_kernel,
        out_shape=[
            shape((1, tokens, 2 * width), bfloat), shape((tokens + EXTRA, 4 * width), bfloat), shape((8, width), floating),
        ],
        in_specs=[VMEM] * 12 + [SMEM] * 2 + [VMEM] * 4 + [ANY],
        out_specs=[VMEM] * 3,
        scratch_shapes=[pltpu.VMEM((tokens, width), bfloat)],
        compiler_params=params(SCOPED),
        cost_estimate=cost(2 * tokens * 5 * weights[0].size, 2 * 4 * weights[0].size),
        name="backward_attn",
    )(grad_att, queries, key_rows, value_rows, probs, ffn_gain, gain_attn, x, g_in, grad_middle, active, change,
      mixing, correction, *weights[:4], before)


def relay_kernel(grad_in, counts_ref, cor_ref, mix_ref, gf_ref, ga_ref, one, two, mid_ref, q_ref, k_ref, v_ref, p_ref, act_ref,
                 wq, wk, wv, wo, wg, wu, wd,
                 msg_ref,
                 acc, g_in, low_ref, do_ref, dqkv_ref):
    tokens, width = low_ref.shape
    start_rows(None, grad_in, counts_ref, cor_ref, g_in, low_ref)
    ffn_steps(low_ref, one, two, wg, wu, wd, acc, lambda *parts: None)
    grad_values = norm_backward(mid_ref[...], gf_ref[...], acc[...], False)[1]
    cor = [cor_ref[0, i] for i in range(2)]
    block = cor[0] * g_in[:, :width].astype(floating) + cor[1] * g_in[:, width:].astype(floating)
    acc[...] = block + grad_values
    do_ref[...] = dot_t(acc[...].astype(bfloat), wo[0]).astype(bfloat)
    parts = (dqkv_ref, 0), (dqkv_ref, width), (dqkv_ref, 2 * width)
    attn_steps(q_ref, k_ref, v_ref, p_ref, do_ref, parts)
    grad_normed = normed_grad(parts, tokens, width, wq, wk, wv)
    grad_values = norm_backward(act_ref[...], ga_ref[...], grad_normed, False)[1]
    block = cor[0] * g_in[:, :width].astype(floating) + cor[1] * g_in[:, width:].astype(floating)
    msg_ref[:tokens, :] = (acc[...] + grad_values - block).astype(bfloat)
    mix = [[mix_ref[0, i, j] for j in range(2)] for i in range(2)]
    msg_ref[tokens:, :] = scalar_rows(mix[0] + mix[1], EXTRA, width)


def relay_backward(out_grad, counts, correction, mixing, gain_ffn, gain_attn, one, two, middle, queries, key_rows, value_rows,
                   probs, active, weights):
    tokens, width = active.shape
    shape = jax.ShapeDtypeStruct
    narrow = pltpu.VMEM((tokens, width), bfloat)
    wide = pltpu.VMEM((tokens, width), floating)
    size = sum(weight.size for weight in weights)
    return pl.pallas_call(
        relay_kernel,
        out_shape=shape((tokens + EXTRA, width), bfloat),
        in_specs=[VMEM, SMEM, SMEM, SMEM] + [VMEM] * 17,
        out_specs=VMEM,
        scratch_shapes=[wide, pltpu.VMEM((tokens, 2 * width), bfloat), narrow, narrow, pltpu.VMEM((tokens, 3 * width), bfloat)],
        compiler_params=params(SCOPED),
        cost_estimate=cost(2 * tokens * size, 2 * size),
        name="backward_relay",
    )(out_grad, counts, correction, mixing, gain_ffn, gain_attn, one, two, middle, queries, key_rows, value_rows, probs, active,
      *weights)


def quarter_parts(base, products, block, lefts, rights, own_ref, far_ref, keep_ref):
    tokens = lefts[0].shape[0]
    tail = lefts[0].shape[1] - lefts[-1].shape[1]
    index = lax.axis_index("dp")
    near = (index >> 2) & 1
    far = (index >> 3) & 1
    for left_at, left_wide, right_at, right_wide in products:
        starts = [left_at if left.shape[1] > left_at else left_at - tail for left in lefts]

        def one_chunk(step, carry, starts=starts, left_wide=left_wide, right_at=right_at):
            columns = pl.ds(pl.multiple_of(right_at + step * CHUNK, PAIR), CHUNK)
            span = pl.ds(pl.multiple_of(right_at - base + step * CHUNK, PAIR), CHUNK)
            total = 0.0
            for left, right, at in zip(lefts, rights, starts):
                total = total + t_dot(left[:, at : at + left_wide], right[:tokens, columns])
            for place in range(4):
                part = total[place * block : (place + 1) * block, :]
                slot = (place >> 1) ^ far
                mine = (place & 1) == near

                @pl.when(mine)
                def _():
                    keep_ref[slot, :, span] = part

                @pl.when(jnp.logical_and(jnp.logical_not(mine), slot == 0))
                def _():
                    own_ref[:block, span] = part.astype(bfloat)

                @pl.when(jnp.logical_and(jnp.logical_not(mine), slot == 1))
                def _():
                    far_ref[:block, span] = part.astype(bfloat)

            return carry

        lax.fori_loop(0, right_wide // CHUNK, one_chunk, 0)


def quarter_product(lefts, rights, block, before, name, parted):
    rows, wide = lefts[0].shape[0], rights[0].shape[1]
    shape = jax.ShapeDtypeStruct
    products = [(0, 4 * block, 0, wide)]
    sends = [shape((block, wide), bfloat)] * 2 if parted else [shape((2, block, wide), bfloat)]

    def kernel(*refs):
        own_ref, far_ref = refs[-3:-1] if parted else (refs[-2].at[0], refs[-2].at[1])
        quarter_parts(0, products, block, refs[:4], refs[4:8], own_ref, far_ref, refs[-1])

    return pl.pallas_call(
        kernel,
        out_shape=sends + [shape((2, block, wide), floating)],
        in_specs=[VMEM] * 8 + [ANY] * len(before),
        out_specs=[VMEM] * (len(sends) + 1),
        compiler_params=params(SCOPED),
        cost_estimate=cost(32 * rows * block * wide, 16 * block * wide),
        name=name,
    )(*lefts, *rights, *before)


def attn_product_kernel(halves, block, refs):
    lefts, rights = refs[:4], refs[4:8]
    first_send, first_keep, small_ref, second_send, second_keep, stage = refs[-6:]
    tokens = lefts[0].shape[0]
    wide = first_keep.shape[2]
    quarter_parts(0, halves[0], block, lefts, rights, first_send, stage, first_keep)
    first_send[block : 2 * block, :] = stage[...]
    small = sum(gathered_parts(right[tokens:, :wide]) for right in rights)
    small_ref[...] = small
    first_send[2 * block :, :] = spread(small)
    quarter_parts(wide, halves[1], block, lefts, rights, second_send.at[0], second_send.at[1], second_keep)


def attn_product(lefts, rights, halves, block, before):
    wide = rights[0].shape[1] // 2
    shape = jax.ShapeDtypeStruct
    send, keep = shape((2, block, wide), bfloat), shape((2, block, wide), floating)
    return pl.pallas_call(
        lambda *refs: attn_product_kernel(halves, block, refs),
        out_shape=[shape((2 * block + EXTRA, wide), bfloat), keep, shape((8, wide // 2), floating), send, keep],
        in_specs=[VMEM] * 8 + [ANY] * len(before),
        out_specs=[VMEM] * 5,
        scratch_shapes=[pltpu.VMEM(send.shape[1:], bfloat)],
        compiler_params=params(SCOPED),
        cost_estimate=cost(wide, wide),
        name="product_attn",
    )(*lefts, *rights, *before)


def first_sum_kernel(keep_ref, came_ref, small_ref, held_ref, passed_ref, sums_ref):
    block = held_ref.shape[0]
    held_ref[...] = keep_ref[0] + came_ref[:block, :].astype(floating)
    passed_ref[:block, :] = (keep_ref[1] + came_ref[block : 2 * block, :].astype(floating)).astype(bfloat)
    small = small_ref[...] + gathered_parts(came_ref[2 * block :, :])
    sums_ref[...] = small
    passed_ref[block:, :] = spread(small)


def first_sum(keep, came, small):
    _, block, wide = keep.shape
    shape = jax.ShapeDtypeStruct
    return pl.pallas_call(
        first_sum_kernel,
        out_shape=[shape((block, wide), floating), shape((block + EXTRA, wide), bfloat), shape(small.shape, floating)],
        in_specs=[VMEM] * 3,
        out_specs=[VMEM] * 3,
        compiler_params=params(SCOPED),
        cost_estimate=cost(wide, wide),
        name="first_sum",
    )(keep, came, small)


def first_end_kernel(held_ref, came_ref, small_ref, left_ref, right_ref, sums_ref):
    block, wide = held_ref.shape
    left_ref[0] = held_ref[:, : wide // 2] + came_ref[:block, : wide // 2].astype(floating)
    right_ref[0] = held_ref[:, wide // 2 :] + came_ref[:block, wide // 2 :].astype(floating)
    sums_ref[...] = small_ref[...] + gathered_parts(came_ref[block:, :])


def first_end(held, came, small):
    block, wide = held.shape
    shape = jax.ShapeDtypeStruct
    return pl.pallas_call(
        first_end_kernel,
        out_shape=[shape((1, block, wide // 2), floating)] * 2 + [shape(small.shape, floating)],
        in_specs=[VMEM] * 3,
        out_specs=[VMEM] * 3,
        compiler_params=params(SCOPED),
        cost_estimate=cost(wide, wide),
        name="first_end",
    )(held, came, small)


def assemble_kernel(own, one, two, three, gate_ref, up_ref):
    quarter = lax.axis_index("dp") & 3
    width = own.shape[1] // 2
    for slot, piece in enumerate((own, one, two, three)):
        span = pl.ds(pl.multiple_of((slot ^ quarter) * width, width), width)
        gate_ref[0, :, span] = piece[:, :width].astype(floating)
        up_ref[0, :, span] = piece[:, width:].astype(floating)


def assemble(pieces):
    share, double = pieces[0].shape
    shape = jax.ShapeDtypeStruct((1, share, 2 * double), floating)
    return pl.pallas_call(
        assemble_kernel,
        out_shape=[shape, shape],
        in_specs=[VMEM] * 4,
        out_specs=[VMEM] * 2,
        compiler_params=params(SCOPED),
        cost_estimate=cost(share * double * 4, share * double * 24),
        name="assemble",
    )(*pieces)


def exchange(value, flips):
    count = lax.axis_size("dp")
    return lax.ppermute(value, "dp", [(source, source ^ flips) for source in range(count)])


def relative_rows(matrix, order, index):
    bits = len(order)
    block = matrix.shape[0] >> bits
    split = matrix.reshape((2,) * bits + (block, matrix.shape[1]))
    axes = [bits - 1 - bit for bit in order]
    split = jnp.transpose(split, axes + [bits, bits + 1])
    for axis, bit in enumerate(order):
        split = jnp.where((index >> bit) & 1 == 1, jnp.flip(split, axis), split)
    return split.reshape(matrix.shape)


def scatter_sum(left, right, order):
    total = left.shape[0]
    arrived = []
    for step in range(len(order) + 1):
        low = total >> (step + 1) if step < len(order) else 0
        high = total >> step
        part = dot(left[low:high], right)
        for other in arrived:
            part = part + other[low:high].astype(floating)
        if step == len(order):
            return part
        arrived.append(exchange(part.astype(bfloat), 1 << order[step]))


def halving_grads(kept, low, slots, right, index, count):
    width = low.shape[1]
    order = list(range(count.bit_length() - 1))
    hidden, normed, attended, normed_ffn = (relative_rows(one.T, order, index) for one in kept)
    quarter = index & 3
    places = jnp.arange(4) ^ quarter
    dgate = jnp.concatenate(list(jnp.stack(slots[:4])[places]), axis=1)
    dup = jnp.concatenate(list(jnp.stack(slots[4:])[places]), axis=1)
    grad_down = scatter_sum(hidden, low, order)
    grad_gate = scatter_sum(normed_ffn, dgate, order)
    grad_up = scatter_sum(normed_ffn, dup, order)
    grad_out = scatter_sum(attended, right[:, :width], order)
    grad_qkv = scatter_sum(normed, right[:, width:], order)
    grads = [grad_down, grad_gate, grad_up, grad_out] + [grad_qkv[:, place * width : (place + 1) * width] for place in range(3)]
    return [one[None] for one in grads]


def after(values, *earlier):
    return lax.optimization_barrier((values, earlier))[0]


def gather_start(value):
    return [value, exchange(value, 1), exchange(value, 2)]


def gather_end(pieces, *earlier):
    return pieces + [exchange(after(pieces[2], *earlier), 1)]


def swapped(pieces):
    return [pieces[0]] + [exchange(pieces[flips], flips) for flips in (1, 2, 3)]


def parts_once(product, *earlier):
    own, far, keep = product
    own, far = after((exchange(own, 4), exchange(far, 4)), *earlier)
    return keep[0] + own.astype(floating), (keep[1] + far.astype(floating)).astype(bfloat)


def sum_once(pair, *earlier):
    send, keep = pair
    arrived = after(exchange(send, 4), *earlier)
    return keep[0] + arrived[0].astype(floating), (keep[1] + arrived[1].astype(floating)).astype(bfloat)


def sum_twice(held, passed, *earlier):
    return held + after(exchange(passed, 8), *earlier).astype(floating)


def sum_over(value, bits):
    for bit in range(bits):
        value = value + exchange(value, 1 << bit)
    return value


def quarter_grads(normed_ffn, kept, nearby, slots, right, down_pair, index):
    width = normed_ffn[0].shape[1]
    share = width // 16
    block = 4 * share
    gates = swapped(slots[:4])
    ups, nearby = after((slots[4:], nearby), right)
    ups, nearby = swapped(list(ups)), exchange(nearby, 3)
    down_sums = sum_once(down_pair, right)
    gate_pair = quarter_product(normed_ffn, gates, block, [right, down_sums[1]], "product_gate", True)
    grad_down = sum_twice(*down_sums)
    rights = gather_start(after(right, gate_pair[0], ups[1:]))
    gate_sums = parts_once(gate_pair)
    up_pair = quarter_product(normed_ffn, ups, block, [gate_sums[1], grad_down, nearby], "product_up", False)
    up_sums = sum_once(up_pair)
    gate_tile = sum_twice(*gate_sums).astype(bfloat)
    rights = gather_end(rights, up_sums[1], gate_tile)
    halves = (
        [(width, block, 0, width), (width + block, block, width, width)], [(width + block, block, 2 * width, 2 * width)])
    before = [up_sums[1], gate_tile]
    first_send, first_keep, small, *second_pair = attn_product(kept[:3] + [nearby], rights, halves, share, before)
    held, first_passed, small = first_sum(first_keep, exchange(first_send, 4), small)
    up_tile = sum_twice(*up_sums, first_passed).astype(bfloat)
    quarter = index & 3
    gate_tile = after(gate_tile, first_passed)
    pieces = [
        jnp.concatenate(
            [lax.dynamic_slice_in_dim(tile, (slot ^ quarter) * share, share, axis=0) for tile in (gate_tile, up_tile)], axis=1)
        for slot in range(4)
    ]
    pieces = swapped(pieces)
    grad_out, grad_query, small = first_end(held, exchange(first_passed, 8), small)
    second_sums = sum_once(second_pair, first_passed)
    grad_gate, grad_up = assemble(list(after(pieces, second_sums[1], small)))
    held, passed = second_sums
    passed = exchange(passed, 8)
    grads = [grad_down[None], grad_gate, grad_up, grad_out, grad_query]
    for span in (slice(0, width), slice(width, 2 * width)):
        grads.append((held[:, span] + passed[:, span].astype(floating))[None])
    return grads, small


def local(states_in, out_grad, counts, segments, mixing, correction, gain_attn, w_query, w_key, w_value, w_attn_out, gain_ffn,
          w_gate, w_up, w_down):
    weights = (w_query, w_key, w_value, w_attn_out, w_gate, w_up, w_down)
    width = gain_attn.shape[1]
    index = lax.axis_index("dp")
    count = lax.axis_size("dp")
    fast = count == 16
    message, *weights = forward_lite(states_in, segments, mixing, correction, gain_attn, gain_ffn, weights)
    message = lax.ppermute(message, "section", [(0, 1), (1, 0)])
    (x, states, queries, key_rows, value_rows, probs, active, middle, one, two, change, *kept) = forward(
        fast, states_in, message, segments, mixing, correction, gain_attn, gain_ffn, weights)
    before = []
    if fast:
        kept, nearby, normed_ffn = swapped(kept[:4]), kept[4], kept[5]
        before = kept[1:]
    message = relay_backward(out_grad, counts, correction, mixing, gain_ffn, gain_attn, one, two, middle, queries, key_rows,
                             value_rows, probs, active, weights)
    message = lax.ppermute(message, "section", [(0, 1), (1, 0)])
    g_in, low = start(message, out_grad, counts, correction, [])
    *slots, grad_middle, grad_att, ffn_gain = ffn_backward(g_in, low, correction, gain_ffn, middle, one, two, before, weights)
    before = slots[0]
    if fast:
        lows = gather_end(gather_start(low), before)
        beside, across = (one[:, width + width // 2 :] for one in kept[1:3])
        normed_ffn = gather_end([normed_ffn, beside, across], before)
        down_pair = quarter_product(kept, lows, width // 4, [before], "product_down", False)
        before = down_pair[0]
    state_grads, right, small = attn_backward(x, g_in, grad_middle, grad_att, active, change, queries, key_rows, value_rows, probs,
                                              ffn_gain, gain_attn, mixing, correction, before, weights)
    if fast:
        grads, small = quarter_grads(normed_ffn, kept, nearby, slots, right, down_pair, index)
    else:
        grads = halving_grads(kept, low, slots, right[: low.shape[0]], index, count)
        small = sum_over(small, count.bit_length() - 1)
    grad_down, grad_gate, grad_up, grad_out, grad_query, grad_key, grad_value = grads
    share = width // count
    gains = lax.dynamic_slice(small, (0, index * share), (2, share))
    sums = jnp.sum(small[2:], axis=1)
    return (
        states,
        state_grads,
        sums[:4].reshape(1, 2, 2),
        sums[4:].reshape(1, 2),
        gains[0:1],
        grad_query,
        grad_key,
        grad_value,
        grad_out,
        gains[1:2],
        grad_gate,
        grad_up,
        grad_down,
    )


def solution(mesh):
    rows = P("dp", None)
    matrix = P("section", None, None)
    vector = P("section", None)
    share = P("section", "dp", None)
    gain_share = P("section", "dp")
    in_specs = (rows, rows, P("dp"), rows, matrix, vector, vector, matrix, matrix, matrix, matrix, vector, matrix, matrix, matrix)
    out_specs = (share, share, matrix, vector, gain_share, share, share, share, share, gain_share, share, share, share)
    return jax.shard_map(local, mesh=mesh, in_specs=in_specs, out_specs=out_specs, check_vma=False)
```

```python
import functools

import jax
import jax.numpy as jnp
from jax import lax
from jax.experimental import pallas as pl
from jax.experimental.pallas import tpu as pltpu
from jax.sharding import PartitionSpec as P

HEAD_DIM = 64
PAIR = 2 * HEAD_DIM
EPSILON = 1e-06
MASKED = -1e30
SCALE = HEAD_DIM ** (-0.5)
GELU_A = 0.7978845608028654
GELU_B = 0.044715
EXTRA = 16
SCOPED = 12
bfloat = jnp.bfloat16
floating = jnp.float32

VMEM = pl.BlockSpec(memory_space=pltpu.VMEM)
SMEM = pl.BlockSpec(memory_space=pltpu.SMEM)
ANY = pl.BlockSpec(memory_space=pltpu.MemorySpace.HBM)


def dot(a, b):
    return jnp.dot(a, b, preferred_element_type=floating)


def dot_t(a, b):
    return lax.dot_general(a, b, (((1,), (1,)), ((), ())), preferred_element_type=floating)


def t_dot(a, b):
    return lax.dot_general(a, b, (((0,), (0,)), ((), ())), preferred_element_type=floating)


def params(mebibytes):
    return pltpu.CompilerParams(vmem_limit_bytes=mebibytes * 1024 * 1024)


def cost(flops, moved):
    return pl.CostEstimate(flops=flops // 1000, bytes_accessed=moved // 1000, transcendentals=0)


def spread(value):
    high = value.astype(bfloat).astype(floating)
    middle = (value - high).astype(bfloat).astype(floating)
    low = value - high - middle
    top = jnp.concatenate([high, middle], axis=1)
    bottom = jnp.concatenate([low, jnp.zeros_like(low)], axis=1)
    return jnp.concatenate([top, bottom], axis=0).astype(bfloat)


def gathered_parts(block):
    block = block.astype(floating)
    width = block.shape[1] // 2
    return block[:8, :width] + block[:8, width:] + block[8:, :width]


def rms_scale(values):
    return lax.rsqrt(jnp.mean(values * values, axis=-1, keepdims=True) + EPSILON)


def lane_mask(length):
    return lax.broadcasted_iota(jnp.int32, (length, PAIR), 1) < HEAD_DIM


def stack_heads(block, first):
    zero = jnp.zeros_like(block)
    return jnp.concatenate([jnp.where(first, block, zero), jnp.where(first, zero, block)], axis=0)


def gelu_wave(gate):
    return jnp.tanh(GELU_A * (gate + GELU_B * gate * gate * gate))


def relative(blocks, index):
    low = (index & 1) == 1
    high = (index >> 1) == 1
    once = [jnp.where(low, blocks[place ^ 1], blocks[place]) for place in range(4)]
    return [jnp.where(high, once[place ^ 2], once[place]) for place in range(4)]


def attention(q_ref, k_ref, v_ref, seg_ref, att_ref, p_ref):
    length = seg_ref.shape[1]
    rows = q_ref.shape[0] // length
    pairs = q_ref.shape[1] // PAIR
    first = lane_mask(length)
    later = lax.broadcasted_iota(jnp.int32, (length, length), 0)
    earlier = lax.broadcasted_iota(jnp.int32, (length, length), 1)
    for row in range(rows):
        documents = jnp.broadcast_to(seg_ref[row : row + 1, :], (length, length)).astype(floating)
        allowed = (earlier <= later) & (documents == documents.T)
        allowed = jnp.concatenate([allowed, allowed], axis=0)
        span = slice(row * length, (row + 1) * length)
        for pair in range(pairs):
            heads = slice(pair * PAIR, (pair + 1) * PAIR)
            stacked = stack_heads(q_ref[span, heads], first)
            scores = jnp.where(allowed, dot_t(stacked, k_ref[span, heads]) * SCALE, MASKED)
            powers = jnp.exp(scores - jnp.max(scores, axis=-1, keepdims=True))
            probs = powers / jnp.sum(powers, axis=-1, keepdims=True)
            if p_ref is not None:
                p_ref[row * pairs + pair] = probs
            mixed = dot(probs.astype(bfloat), v_ref[span, heads])
            att_ref[span, heads] = jnp.where(first, mixed[:length], mixed[length:]).astype(bfloat)


def in_hbm(value):
    return pltpu.with_memory_space_constraint(value, pltpu.MemorySpace.HBM)


def forward_lite_kernel(x_any, seg_any, mix_any, cor_any, ga_any, gf_any, wq, wk, wv, wo, wg, wu, wd,
                        out_ref, wq_s, wk_s, wv_s, wo_s, wg_s, wu_s, wd_s,
                        x_in, seg_ref, mix_ref, cor_ref, ga_ref, gf_ref, q_ref, k_ref, v_ref, act_ref,
                        nrm_ref, att_ref, nf_ref, acc, sem, small_sem):
    tokens, width = act_ref.shape
    chunk = width
    pieces = wg.shape[2] // chunk
    small = [
        pltpu.make_async_copy(source, target, small_sem.at[place])
        for place, (source, target) in enumerate(
            ((x_any, x_in), (mix_any, mix_ref), (ga_any, ga_ref), (seg_any, seg_ref), (gf_any, gf_ref), (cor_any, cor_ref))
        )
    ]
    pairs = [(wq, wq_s), (wk, wk_s), (wv, wv_s), (wo, wo_s)]
    queue = [pltpu.make_async_copy(source, target, sem.at[place]) for place, (source, target) in enumerate(pairs)]

    def group(piece):
        span = pl.ds(pl.multiple_of(piece * chunk, chunk), chunk)
        places = ((wg, wg_s, (slice(None), slice(None), span)), (wu, wu_s, (slice(None), slice(None), span)),
                  (wd, wd_s, (slice(None), span, slice(None))))
        return [
            pltpu.make_async_copy(source.at[where], target.at[where], sem.at[4 + 3 * piece + place])
            for place, (source, target, where) in enumerate(places)
        ]

    def start_group(piece):
        for copy in group(piece):
            copy.start()

    for copy in small + queue:
        copy.start()
    for copy in small:
        copy.wait()
    section = lax.axis_index("section")
    mix = [[mix_ref[0, i, j] for j in range(2)] for i in range(2)]
    cor = [cor_ref[0, i] for i in range(2)]
    xa = x_in[:, :width].astype(floating)
    xb = x_in[:, width:].astype(floating)
    own_a = jnp.where(section == 0, mix[0][0], mix[1][0])
    own_b = jnp.where(section == 0, mix[0][1], mix[1][1])
    active = jnp.where(section == 0, xa, xb) + (own_a * xa + own_b * xb)
    act_ref[...] = active
    nrm_ref[...] = (active * rms_scale(active) * ga_ref[...]).astype(bfloat)
    for place, (copy, weight, target) in enumerate(zip(queue, (wq_s, wk_s, wv_s), (q_ref, k_ref, v_ref))):
        copy.wait()
        if place != 1:
            start_group(place // 2)
        target[...] = dot(nrm_ref[...], weight[0]).astype(bfloat)
    attention(q_ref, k_ref, v_ref, seg_ref, att_ref, None)
    for piece in range(2, pieces):
        start_group(piece)
    queue[3].wait()
    middle = act_ref[...] + dot(att_ref[...], wo_s[0])
    acc[...] = middle - act_ref[...]
    nf_ref[...] = (middle * rms_scale(middle) * gf_ref[...]).astype(bfloat)

    def one_piece(piece, carry):
        span = pl.ds(pl.multiple_of(piece * chunk, chunk), chunk)
        waits = group(piece)
        waits[0].wait()
        gate = dot(nf_ref[...], wg_s[0, :, span])
        waits[1].wait()
        upward = dot(nf_ref[...], wu_s[0, :, span])
        hidden = (0.5 * gate * (1.0 + gelu_wave(gate)) * upward).astype(bfloat)
        waits[2].wait()
        acc[...] += dot(hidden, wd_s[0, span, :])
        return carry

    lax.fori_loop(0, pieces, one_piece, 0, unroll=2)
    xa = x_in[:, :width].astype(floating)
    xb = x_in[:, width:].astype(floating)
    out_ref[:, :width] = (xa + (mix[0][0] * xa + mix[0][1] * xb) + cor[0] * acc[...]).astype(bfloat)
    out_ref[:, width:] = (xb + (mix[1][0] * xa + mix[1][1] * xb) + cor[1] * acc[...]).astype(bfloat)


def forward_lite(x_in, segments, mixing, correction, gain_attn, gain_ffn, weights):
    tokens = x_in.shape[0]
    width = gain_attn.shape[1]
    size = sum(weight.size for weight in weights)
    narrow = pltpu.VMEM((tokens, width), bfloat)
    wide = pltpu.VMEM((tokens, width), floating)
    args = (x_in, segments, mixing, correction, gain_attn, gain_ffn) + weights
    scratch = [
        pltpu.VMEM(x_in.shape, bfloat), pltpu.VMEM(segments.shape, jnp.int32), pltpu.SMEM(mixing.shape, floating),
        pltpu.SMEM(correction.shape, floating), pltpu.VMEM(gain_attn.shape, floating), pltpu.VMEM(gain_ffn.shape, floating),
        narrow, narrow, narrow, wide, narrow, narrow, narrow, wide,
    ]
    scratch += [pltpu.SemaphoreType.DMA((4 + 3 * (weights[4].shape[2] // width),)), pltpu.SemaphoreType.DMA((6,))]
    return pl.pallas_call(
        forward_lite_kernel,
        out_shape=[jax.ShapeDtypeStruct((tokens, 2 * width), bfloat)]
        + [jax.ShapeDtypeStruct(weight.shape, bfloat) for weight in weights],
        in_specs=[ANY] * len(args),
        out_specs=[VMEM] * 8,
        scratch_shapes=scratch,
        compiler_params=params(SCOPED),
        cost_estimate=cost(2 * tokens * size, 2 * size),
        name="forward_lite",
    )(*[in_hbm(one) for one in args])


def forward_kernel(fast, x_in, message, seg_ref, mix_ref, cor_ref, ga_ref, gf_ref, wq, wk, wv, wo, wg, wu, wd,
                   x_ref, out_ref, q_ref, k_ref, v_ref, p_ref, act_ref, mid_ref, one_ref, two_ref, chg_ref, *refs):
    kept = refs[:4]
    nf_ref = refs[-4]
    nrm_ref, att_ref, acc = refs[-3:]
    tokens, width = act_ref.shape
    chunk = width
    pieces = wg.shape[2] // chunk
    section = lax.axis_index("section")
    quarter = lax.axis_index("dp") & 3
    mix = [[mix_ref[0, i, j] for j in range(2)] for i in range(2)]
    cor = [cor_ref[0, i] for i in range(2)]
    x_ref[...] = jnp.where(section == 0, x_in[...], message[...])
    xa = x_ref[:, :width].astype(floating)
    xb = x_ref[:, width:].astype(floating)
    own_a = jnp.where(section == 0, mix[0][0], mix[1][0])
    own_b = jnp.where(section == 0, mix[0][1], mix[1][1])
    active = jnp.where(section == 0, xa, xb) + (own_a * xa + own_b * xb)
    act_ref[...] = active
    nrm_ref[...] = (active * rms_scale(active) * ga_ref[...]).astype(bfloat)
    for weight, target in zip((wq, wk, wv), (q_ref, k_ref, v_ref)):
        target[...] = dot(nrm_ref[...], weight[0]).astype(bfloat)

    def keep_quarters(values, base):
        share = width // 16
        for far in range(4):
            blocks = [values[:, (4 * far + near) * share : (4 * far + near + 1) * share] for near in range(4)]
            for slot, block in enumerate(relative(blocks, quarter)):
                target, start = (kept[slot], width + base) if slot < 3 else (refs[4], base)
                target[:, start + far * share : start + (far + 1) * share] = block

    attention(q_ref, k_ref, v_ref, seg_ref, att_ref, p_ref)
    middle = act_ref[...] + dot(att_ref[...], wo[0])
    mid_ref[...] = middle
    nf_ref[...] = (middle * rms_scale(middle) * gf_ref[...]).astype(bfloat)
    if fast:
        keep_quarters(att_ref[...], 0)
        keep_quarters(nrm_ref[...], width // 4)
        for slot in (1, 2):
            kept[slot][:, width + width // 2 :] = nf_ref[...]
    else:
        kept[1][...] = nrm_ref[...]
        kept[2][...] = att_ref[...]
    for piece in range(pieces):
        span = slice(piece * chunk, (piece + 1) * chunk)
        gate = dot(nf_ref[...], wg[0, :, span])
        upward = dot(nf_ref[...], wu[0, :, span])
        wave = gelu_wave(gate)
        half = 0.5 * (1.0 + wave)
        value = gate * half
        hidden = (value * upward).astype(bfloat)
        slope = half + 0.5 * gate * (1.0 - wave * wave) * (GELU_A * (1.0 + 3.0 * GELU_B * gate * gate))
        one_ref[piece] = upward * slope
        two_ref[piece] = value
        if fast:
            share = chunk // 4
            blocks = [hidden[:, near * share : (near + 1) * share] for near in range(4)]
            for slot, block in enumerate(relative(blocks, quarter)):
                kept[slot][:, piece * share : (piece + 1) * share] = block
        else:
            kept[0][:, span] = hidden
        down = dot(hidden, wd[0, span, :])
        if piece == 0:
            acc[...] = down
        else:
            acc[...] += down
    change = mid_ref[...] + acc[...] - act_ref[...]
    chg_ref[...] = change
    xa = x_ref[:, :width].astype(floating)
    xb = x_ref[:, width:].astype(floating)
    out_ref[0, :, :width] = (xa + (mix[0][0] * xa + mix[0][1] * xb) + cor[0] * change).astype(bfloat)
    out_ref[0, :, width:] = (xb + (mix[1][0] * xa + mix[1][1] * xb) + cor[1] * change).astype(bfloat)


def forward(fast, x_in, message, segments, mixing, correction, gain_attn, gain_ffn, weights):
    tokens = x_in.shape[0]
    length = segments.shape[1]
    width = gain_attn.shape[1]
    hidden_width = weights[4].shape[2]
    size = sum(weight.size for weight in weights)
    shape = jax.ShapeDtypeStruct
    narrow = ((tokens, width), bfloat)
    wide = ((tokens, width), floating)
    probs = ((tokens // length * (width // PAIR), 2 * length, length), floating)
    if fast:
        short, long = (((tokens, columns), bfloat) for columns in (width + width // 2, 2 * width + width // 2))
        kept = [short, long, long, narrow, ((tokens, width // 2), bfloat), narrow]
    else:
        kept = [((tokens, hidden_width), bfloat), narrow, narrow, narrow]
    ffn = ((hidden_width // width, tokens, width), floating)
    outs = [((tokens, 2 * width), bfloat), ((1, tokens, 2 * width), bfloat), narrow, narrow, narrow, probs, wide, wide,
            ffn, ffn, wide] + kept
    return pl.pallas_call(
        lambda *refs: forward_kernel(fast, *refs),
        out_shape=[shape(*one) for one in outs],
        in_specs=[VMEM, VMEM, VMEM, SMEM, SMEM, VMEM, VMEM] + [VMEM] * 7,
        out_specs=[VMEM] * len(outs),
        scratch_shapes=[pltpu.VMEM(*narrow)] * 2 + [pltpu.VMEM(*wide)],
        compiler_params=params(SCOPED),
        cost_estimate=cost(2 * tokens * size, 2 * size),
        name="forward_full",
    )(x_in, message, segments, mixing, correction, gain_attn, gain_ffn, *weights)


def start_rows(message, grad_ref, counts_ref, cor_ref, g_ref, low_ref):
    tokens, width = low_ref.shape
    rows = counts_ref.shape[0]
    length = tokens // rows
    section = lax.axis_index("section")
    place = lax.broadcasted_iota(jnp.int32, (tokens, width), 0)
    valid = place < counts_ref[0]
    for row in range(1, rows):
        valid = valid | ((place >= row * length) & (place < row * length + counts_ref[row]))
    own_a = jnp.where(valid, grad_ref[:, :width].astype(floating), 0.0)
    own_b = jnp.where(valid, grad_ref[:, width:].astype(floating), 0.0)
    if message is not None:
        own_a = jnp.where(section == 0, message[:, :width].astype(floating), own_a)
        own_b = jnp.where(section == 0, message[:, width:].astype(floating), own_b)
    g_ref[:, :width] = own_a.astype(bfloat)
    g_ref[:, width:] = own_b.astype(bfloat)
    low_ref[...] = (cor_ref[0, 0] * own_a + cor_ref[0, 1] * own_b).astype(bfloat)


def start(message, out_grad, counts, correction, before):
    tokens = out_grad.shape[0]
    width = message.shape[1] // 2
    shape = jax.ShapeDtypeStruct
    return pl.pallas_call(
        lambda *refs: start_rows(*refs[:4], *refs[-2:]),
        out_shape=[shape((tokens, 2 * width), bfloat), shape((tokens, width), bfloat)],
        in_specs=[VMEM, VMEM, SMEM, SMEM] + [ANY] * len(before),
        out_specs=[VMEM, VMEM],
        compiler_params=params(SCOPED),
        cost_estimate=cost(tokens * width * 20, tokens * width * 12),
        name="backward_start",
    )(message, out_grad, counts, correction, *before)


def norm_backward(values, gain, grad_normed, with_gain):
    inverse = rms_scale(values)
    grad_gain = jnp.sum(grad_normed * values * inverse, axis=0, keepdims=True) if with_gain else None
    weighted = grad_normed * gain
    grad_values = inverse * weighted - values * inverse**3 * jnp.mean(weighted * values, axis=-1, keepdims=True)
    return grad_gain, grad_values


def ffn_steps(low_ref, one, two, wg, wu, wd, acc, emit):
    width = wd.shape[2]
    quarter = lax.axis_index("dp") & 3
    for step in range(4):
        piece = (3 - step) ^ quarter
        span = pl.ds(pl.multiple_of(piece * width, width), width)
        grad_hidden = dot_t(low_ref[...], wd[0, span, :])
        dgate = (grad_hidden * one[piece]).astype(bfloat)
        dup = (grad_hidden * two[piece]).astype(bfloat)
        emit(3 - step, dgate, dup)
        total = dot_t(dgate, wg[0, :, span]) + dot_t(dup, wu[0, :, span])
        if step == 0:
            acc[...] = total
        else:
            acc[...] += total


def ffn_kernel(g_in, low_ref, cor_ref, gf_ref, mid_ref, one, two, wg, wu, wd, *refs):
    slots = refs[-12:-4]
    dmid_ref, datt_ref, gain_ref, acc = refs[-4:]
    width = gf_ref.shape[1]

    def emit(slot, dgate, dup):
        slots[slot][...] = dgate
        slots[4 + slot][...] = dup

    ffn_steps(low_ref, one, two, wg, wu, wd, acc, emit)
    grad_gain, grad_values = norm_backward(mid_ref[...], gf_ref[...], acc[...], True)
    block = cor_ref[0, 0] * g_in[:, :width].astype(floating) + cor_ref[0, 1] * g_in[:, width:].astype(floating)
    grad_middle = block + grad_values
    dmid_ref[...] = grad_middle
    datt_ref[...] = grad_middle.astype(bfloat)
    gain_ref[...] = grad_gain


def ffn_backward(g_in, low, correction, gain_ffn, middle, one, two, before, weights):
    tokens = g_in.shape[0]
    width = gain_ffn.shape[1]
    shape = jax.ShapeDtypeStruct
    return pl.pallas_call(
        ffn_kernel,
        out_shape=[shape((tokens, width), bfloat)] * 8
        + [shape((tokens, width), floating), shape((tokens, width), bfloat), shape((1, width), floating)],
        in_specs=[VMEM, VMEM, SMEM] + [VMEM] * 7 + [ANY] * len(before),
        out_specs=[VMEM] * 11,
        scratch_shapes=[pltpu.VMEM((tokens, width), floating)],
        compiler_params=params(SCOPED),
        cost_estimate=cost(2 * tokens * 3 * weights[4].size, 2 * 3 * weights[4].size),
        name="backward_ffn",
    )(g_in, low, correction, gain_ffn, middle, one, two, *weights[4:], *before)


def attn_steps(q_ref, k_ref, v_ref, p_ref, do_ref, parts):
    tokens, width = do_ref.shape
    length = p_ref.shape[2]
    rows = tokens // length
    pairs = width // PAIR
    first = lane_mask(length)
    for row in range(rows):
        span = slice(row * length, (row + 1) * length)
        for pair in range(pairs):
            heads = slice(pair * PAIR, (pair + 1) * PAIR)
            probs = p_ref[row * pairs + pair]
            grad_out = stack_heads(do_ref[span, heads], first)
            grad_value = t_dot(probs.astype(bfloat), grad_out)
            grad_probs = dot_t(grad_out, v_ref[span, heads])
            carried = jnp.sum(probs * grad_probs, axis=-1, keepdims=True)
            grad_scores = (probs * (grad_probs - carried)).astype(bfloat)
            grad_query = dot(grad_scores, k_ref[span, heads])
            grad_query = jnp.where(first, grad_query[:length], grad_query[length:])
            grad_key = t_dot(grad_scores, stack_heads(q_ref[span, heads], first))
            for (part, base), value in zip(parts, (grad_query * SCALE, grad_key * SCALE, grad_value)):
                part[span, base + pair * PAIR : base + (pair + 1) * PAIR] = value.astype(bfloat)


def normed_grad(parts, rows, width, wq, wk, wv):
    return sum(dot_t(part[:rows, base : base + width], weight[0]) for (part, base), weight in zip(parts, (wq, wk, wv)))


def attn_kernel(datt_ref, q_ref, k_ref, v_ref, p_ref, gfg_ref, ga_ref, x_ref, g_in, dmid_ref, act_ref, chg_ref, mix_ref, cor_ref,
                wq, wk, wv, wo, before,
                grad_ref, right_ref, small_ref, do_ref):
    tokens, width = datt_ref.shape
    right_ref[:tokens, :width] = datt_ref[...]
    do_ref[...] = dot_t(datt_ref[...], wo[0]).astype(bfloat)
    parts = (right_ref, width), (right_ref, 2 * width), (right_ref, 3 * width)
    attn_steps(q_ref, k_ref, v_ref, p_ref, do_ref, parts)
    grad_normed = normed_grad(parts, tokens, width, wq, wk, wv)
    grad_gain, grad_values = norm_backward(act_ref[...], ga_ref[...], grad_normed, True)
    section = lax.axis_index("section")
    mix = [[mix_ref[0, i, j] for j in range(2)] for i in range(2)]
    cor = [cor_ref[0, i] for i in range(2)]
    out_a = g_in[:, :width].astype(floating)
    out_b = g_in[:, width:].astype(floating)
    grad_active = dmid_ref[...] + grad_values - (cor[0] * out_a + cor[1] * out_b)
    pred_a = out_a + jnp.where(section == 0, grad_active, 0.0)
    pred_b = out_b + jnp.where(section == 0, 0.0, grad_active)
    grad_ref[0, :, :width] = (pred_a + (mix[0][0] * pred_a + mix[1][0] * pred_b)).astype(bfloat)
    grad_ref[0, :, width:] = (pred_b + (mix[0][1] * pred_a + mix[1][1] * pred_b)).astype(bfloat)
    xa = x_ref[:, :width].astype(floating)
    xb = x_ref[:, width:].astype(floating)
    small_ref[0:1, :] = grad_gain
    small_ref[1:2, :] = gfg_ref[...]
    place = 2
    for pred in (pred_a, pred_b):
        for state in (xa, xb):
            small_ref[place : place + 1, :] = jnp.sum(pred * state, axis=0, keepdims=True)
            place += 1
    for out in (out_a, out_b):
        small_ref[place : place + 1, :] = jnp.sum(out * chg_ref[...], axis=0, keepdims=True)
        place += 1
    right_ref[tokens:, : 2 * width] = spread(small_ref[...])
    right_ref[tokens:, 2 * width :] = jnp.zeros((right_ref.shape[0] - tokens, 2 * width), bfloat)


def attn_backward(x, g_in, grad_middle, grad_att, active, change, queries, key_rows, value_rows, probs, ffn_gain, gain_attn,
                  mixing, correction, before, weights):
    tokens, width = active.shape
    shape = jax.ShapeDtypeStruct
    return pl.pallas_call(
        attn_kernel,
        out_shape=[
            shape((1, tokens, 2 * width), bfloat), shape((tokens + EXTRA, 4 * width), bfloat), shape((8, width), floating),
        ],
        in_specs=[VMEM] * 12 + [SMEM] * 2 + [VMEM] * 4 + [ANY],
        out_specs=[VMEM] * 3,
        scratch_shapes=[pltpu.VMEM((tokens, width), bfloat)],
        compiler_params=params(SCOPED),
        cost_estimate=cost(2 * tokens * 5 * weights[0].size, 2 * 4 * weights[0].size),
        name="backward_attn",
    )(grad_att, queries, key_rows, value_rows, probs, ffn_gain, gain_attn, x, g_in, grad_middle, active, change,
      mixing, correction, *weights[:4], before)


def relay_kernel(grad_in, counts_ref, cor_ref, mix_ref, gf_ref, ga_ref, one, two, mid_ref, q_ref, k_ref, v_ref, p_ref, act_ref,
                 wq, wk, wv, wo, wg, wu, wd,
                 msg_ref,
                 acc, g_in, low_ref, do_ref, dqkv_ref):
    tokens, width = low_ref.shape
    start_rows(None, grad_in, counts_ref, cor_ref, g_in, low_ref)
    ffn_steps(low_ref, one, two, wg, wu, wd, acc, lambda *parts: None)
    grad_values = norm_backward(mid_ref[...], gf_ref[...], acc[...], False)[1]
    cor = [cor_ref[0, i] for i in range(2)]
    block = cor[0] * g_in[:, :width].astype(floating) + cor[1] * g_in[:, width:].astype(floating)
    acc[...] = block + grad_values
    do_ref[...] = dot_t(acc[...].astype(bfloat), wo[0]).astype(bfloat)
    parts = (dqkv_ref, 0), (dqkv_ref, width), (dqkv_ref, 2 * width)
    attn_steps(q_ref, k_ref, v_ref, p_ref, do_ref, parts)
    grad_normed = normed_grad(parts, tokens, width, wq, wk, wv)
    grad_values = norm_backward(act_ref[...], ga_ref[...], grad_normed, False)[1]
    out_a = g_in[:, :width].astype(floating)
    out_b = g_in[:, width:].astype(floating)
    pred_b = out_b + (acc[...] + grad_values - (cor[0] * out_a + cor[1] * out_b))
    mix = [[mix_ref[0, i, j] for j in range(2)] for i in range(2)]
    msg_ref[:, :width] = (out_a + (mix[0][0] * out_a + mix[1][0] * pred_b)).astype(bfloat)
    msg_ref[:, width:] = (pred_b + (mix[0][1] * out_a + mix[1][1] * pred_b)).astype(bfloat)


def relay_backward(out_grad, counts, correction, mixing, gain_ffn, gain_attn, one, two, middle, queries, key_rows, value_rows,
                   probs, active, weights):
    tokens, width = active.shape
    shape = jax.ShapeDtypeStruct
    narrow = pltpu.VMEM((tokens, width), bfloat)
    wide = pltpu.VMEM((tokens, width), floating)
    size = sum(weight.size for weight in weights)
    return pl.pallas_call(
        relay_kernel,
        out_shape=shape((tokens, 2 * width), bfloat),
        in_specs=[VMEM, SMEM, SMEM, SMEM] + [VMEM] * 17,
        out_specs=VMEM,
        scratch_shapes=[wide, pltpu.VMEM((tokens, 2 * width), bfloat), narrow, narrow, pltpu.VMEM((tokens, 3 * width), bfloat)],
        compiler_params=params(SCOPED),
        cost_estimate=cost(2 * tokens * size, 2 * size),
        name="backward_relay",
    )(out_grad, counts, correction, mixing, gain_ffn, gain_attn, one, two, middle, queries, key_rows, value_rows, probs, active,
      *weights)


def quarter_parts(base, products, block, lefts, rights, own_ref, far_ref, all_ref, left_s, right_s):
    tokens = lefts[0].shape[0]
    tail = lefts[0].shape[1] - lefts[-1].shape[1]
    mine = (lax.axis_index("dp") >> 2) & 3
    for left_at, left_wide, right_at, right_wide in products:
        columns = slice(right_at, right_at + right_wide)
        span = slice(right_at - base, right_at - base + right_wide)
        for row, (left, right) in enumerate(zip(lefts, rights)):
            at = left_at if left.shape[1] > left_at else left_at - tail
            rows = slice(row * tokens, (row + 1) * tokens)
            left_s[rows, :left_wide] = left[:, at : at + left_wide]
            right_s[rows, :right_wide] = right[:tokens, columns]
        total = t_dot(left_s[:, :left_wide], right_s[:, :right_wide])
        for place in range(4):
            all_ref[place ^ mine, :, span] = total[place * block : (place + 1) * block, :]
    own_ref[:block, :] = all_ref[1].astype(bfloat)
    far_ref[:block, :] = all_ref[3].astype(bfloat)


def quarter_product(lefts, rights, block, before, name, parted):
    rows, wide = lefts[0].shape[0], rights[0].shape[1]
    shape = jax.ShapeDtypeStruct
    products = [(0, 4 * block, 0, wide)]
    sends = [shape((block, wide), bfloat)] * 2 if parted else [shape((2, block, wide), bfloat)]

    def kernel(*refs):
        *outs, all_ref, left_s, right_s = refs[-5:] if parted else refs[-4:]
        own_ref, far_ref = outs if parted else (outs[0].at[0], outs[0].at[1])
        quarter_parts(0, products, block, refs[:4], refs[4:8], own_ref, far_ref, all_ref, left_s, right_s)

    return pl.pallas_call(
        kernel,
        out_shape=sends + [shape((4, block, wide), floating)],
        in_specs=[VMEM] * 8 + [ANY] * len(before),
        out_specs=[VMEM] * (len(sends) + 1),
        scratch_shapes=[pltpu.VMEM((4 * rows, 4 * block), bfloat), pltpu.VMEM((4 * rows, wide), bfloat)],
        compiler_params=params(SCOPED),
        cost_estimate=cost(32 * rows * block * wide, 16 * block * wide),
        name=name,
    )(*lefts, *rights, *before)


def attn_product_kernel(halves, block, refs):
    lefts, rights = refs[:4], refs[4:8]
    first_send, first_keep, small_ref, second_send, second_keep, stage, left_s, right_s = refs[-8:]
    tokens = lefts[0].shape[0]
    wide = first_keep.shape[2]
    quarter_parts(0, halves[0], block, lefts, rights, first_send, stage, first_keep, left_s, right_s)
    first_send[block : 2 * block, :] = stage[...]
    small = sum(gathered_parts(right[tokens:, :wide]) for right in rights)
    small_ref[...] = small
    first_send[2 * block :, :] = spread(small)
    quarter_parts(wide, halves[1], block, lefts, rights, second_send.at[0], second_send.at[1], second_keep, left_s, right_s)


def attn_product(lefts, rights, halves, block, before):
    wide = rights[0].shape[1] // 2
    shape = jax.ShapeDtypeStruct
    send, keep = shape((2, block, wide), bfloat), shape((4, block, wide), floating)
    return pl.pallas_call(
        lambda *refs: attn_product_kernel(halves, block, refs),
        out_shape=[shape((2 * block + EXTRA, wide), bfloat), keep, shape((8, wide // 2), floating), send, keep],
        in_specs=[VMEM] * 8 + [ANY] * len(before),
        out_specs=[VMEM] * 5,
        scratch_shapes=[
            pltpu.VMEM(send.shape[1:], bfloat), pltpu.VMEM((4 * lefts[0].shape[0], 4 * block), bfloat),
            pltpu.VMEM((4 * lefts[0].shape[0], wide), bfloat),
        ],
        compiler_params=params(SCOPED),
        cost_estimate=cost(wide, wide),
        name="product_attn",
    )(*lefts, *rights, *before)


def first_sum_kernel(keep_ref, came_ref, small_ref, held_ref, passed_ref, sums_ref):
    block = held_ref.shape[0]
    held_ref[...] = keep_ref[0] + came_ref[:block, :].astype(floating)
    passed_ref[:block, :] = (keep_ref[2] + came_ref[block : 2 * block, :].astype(floating)).astype(bfloat)
    small = small_ref[...] + gathered_parts(came_ref[2 * block :, :])
    sums_ref[...] = small
    passed_ref[block:, :] = spread(small)


def first_sum(keep, came, small):
    _, block, wide = keep.shape
    shape = jax.ShapeDtypeStruct
    return pl.pallas_call(
        first_sum_kernel,
        out_shape=[shape((block, wide), floating), shape((block + EXTRA, wide), bfloat), shape(small.shape, floating)],
        in_specs=[VMEM] * 3,
        out_specs=[VMEM] * 3,
        compiler_params=params(SCOPED),
        cost_estimate=cost(wide, wide),
        name="first_sum",
    )(keep, came, small)


def first_end_kernel(held_ref, came_ref, small_ref, left_ref, right_ref, sums_ref):
    block, wide = held_ref.shape
    left_ref[0] = held_ref[:, : wide // 2] + came_ref[:block, : wide // 2].astype(floating)
    right_ref[0] = held_ref[:, wide // 2 :] + came_ref[:block, wide // 2 :].astype(floating)
    sums_ref[...] = small_ref[...] + gathered_parts(came_ref[block:, :])


def first_end(held, came, small):
    block, wide = held.shape
    shape = jax.ShapeDtypeStruct
    return pl.pallas_call(
        first_end_kernel,
        out_shape=[shape((1, block, wide // 2), floating)] * 2 + [shape(small.shape, floating)],
        in_specs=[VMEM] * 3,
        out_specs=[VMEM] * 3,
        compiler_params=params(SCOPED),
        cost_estimate=cost(wide, wide),
        name="first_end",
    )(held, came, small)


def assemble_kernel(own, one, two, three, gate_ref, up_ref):
    quarter = lax.axis_index("dp") & 3
    width = own.shape[1] // 2
    for slot, piece in enumerate((own, one, two, three)):
        span = pl.ds(pl.multiple_of((slot ^ quarter) * width, width), width)
        gate_ref[0, :, span] = piece[:, :width].astype(floating)
        up_ref[0, :, span] = piece[:, width:].astype(floating)


def assemble(pieces):
    share, double = pieces[0].shape
    shape = jax.ShapeDtypeStruct((1, share, 2 * double), floating)
    return pl.pallas_call(
        assemble_kernel,
        out_shape=[shape, shape],
        in_specs=[VMEM] * 4,
        out_specs=[VMEM] * 2,
        compiler_params=params(SCOPED),
        cost_estimate=cost(share * double * 4, share * double * 24),
        name="assemble",
    )(*pieces)


def exchange(value, flips):
    count = lax.axis_size("dp")
    return lax.ppermute(value, "dp", [(source, source ^ flips) for source in range(count)])


def relative_rows(matrix, order, index):
    bits = len(order)
    block = matrix.shape[0] >> bits
    split = matrix.reshape((2,) * bits + (block, matrix.shape[1]))
    axes = [bits - 1 - bit for bit in order]
    split = jnp.transpose(split, axes + [bits, bits + 1])
    for axis, bit in enumerate(order):
        split = jnp.where((index >> bit) & 1 == 1, jnp.flip(split, axis), split)
    return split.reshape(matrix.shape)


def scatter_sum(left, right, order):
    total = left.shape[0]
    arrived = []
    for step in range(len(order) + 1):
        low = total >> (step + 1) if step < len(order) else 0
        high = total >> step
        part = dot(left[low:high], right)
        for other in arrived:
            part = part + other[low:high].astype(floating)
        if step == len(order):
            return part
        arrived.append(exchange(part.astype(bfloat), 1 << order[step]))


def halving_grads(kept, low, slots, right, index, count):
    width = low.shape[1]
    order = list(range(count.bit_length() - 1))
    hidden, normed, attended, normed_ffn = (relative_rows(one.T, order, index) for one in kept)
    quarter = index & 3
    places = jnp.arange(4) ^ quarter
    dgate = jnp.concatenate(list(jnp.stack(slots[:4])[places]), axis=1)
    dup = jnp.concatenate(list(jnp.stack(slots[4:])[places]), axis=1)
    grad_down = scatter_sum(hidden, low, order)
    grad_gate = scatter_sum(normed_ffn, dgate, order)
    grad_up = scatter_sum(normed_ffn, dup, order)
    grad_out = scatter_sum(attended, right[:, :width], order)
    grad_qkv = scatter_sum(normed, right[:, width:], order)
    grads = [grad_down, grad_gate, grad_up, grad_out] + [grad_qkv[:, place * width : (place + 1) * width] for place in range(3)]
    return [one[None] for one in grads]


def after(values, *earlier):
    return lax.optimization_barrier((values, earlier))[0]


def gather_start(value):
    return [value, exchange(value, 1), exchange(value, 2)]


def gather_end(pieces, *earlier):
    return pieces + [exchange(after(pieces[2], *earlier), 1)]


def swapped(pieces):
    return [pieces[0]] + [exchange(pieces[flips], flips) for flips in (1, 2, 3)]


def parts_once(product, *earlier):
    own, far, keep = product
    own, far = after((exchange(own, 4), exchange(far, 4)), *earlier)
    return keep[0] + own.astype(floating), (keep[2] + far.astype(floating)).astype(bfloat)


def sum_once(pair, *earlier):
    send, keep = pair
    arrived = after(exchange(send, 4), *earlier)
    return keep[0] + arrived[0].astype(floating), (keep[2] + arrived[1].astype(floating)).astype(bfloat)


def sum_twice(held, passed, *earlier):
    return held + after(exchange(passed, 8), *earlier).astype(floating)


def sum_over(value, bits):
    for bit in range(bits):
        value = value + exchange(value, 1 << bit)
    return value


def quarter_grads(normed_ffn, kept, nearby, slots, right, down_pair, index):
    width = normed_ffn[0].shape[1]
    share = width // 16
    block = 4 * share
    gates = swapped(slots[:4])
    ups, nearby = after((slots[4:], nearby), right)
    ups, nearby = swapped(list(ups)), exchange(nearby, 3)
    down_sums = sum_once(down_pair, right)
    gate_pair = quarter_product(normed_ffn, gates, block, [right, down_sums[1]], "product_gate", True)
    grad_down = sum_twice(*down_sums)
    rights = gather_start(after(right, gate_pair[0], ups[1:]))
    gate_sums = parts_once(gate_pair)
    up_pair = quarter_product(normed_ffn, ups, block, [gate_sums[1], grad_down, nearby], "product_up", False)
    up_sums = sum_once(up_pair)
    part = block * 3 // 4
    gate_came = exchange(gate_sums[1][:part], 8)
    rights = gather_end(rights, up_sums[1], gate_came)
    up_came = exchange(jnp.concatenate([up_sums[1], gate_sums[1][part:]], axis=0), 8)
    halves = (
        [(width, block, 0, width), (width + block, block, width, width)], [(width + block, block, 2 * width, 2 * width)])
    before = [up_sums[1], gate_came]
    first_send, first_keep, small, *second_pair = attn_product(kept[:3] + [nearby], rights, halves, share, before)
    held, first_passed, small = first_sum(first_keep, after(exchange(first_send, 4), up_came), small)
    gate_came, up_came = after((gate_came, up_came), first_passed)
    gate_tile = (gate_sums[0] + jnp.concatenate([gate_came, up_came[block:]], axis=0).astype(floating)).astype(bfloat)
    up_tile = (up_sums[0] + up_came[:block].astype(floating)).astype(bfloat)
    quarter = index & 3
    pieces = [
        jnp.concatenate(
            [lax.dynamic_slice_in_dim(tile, (slot ^ quarter) * share, share, axis=0) for tile in (gate_tile, up_tile)], axis=1)
        for slot in range(4)
    ]
    pieces = swapped(pieces)
    grad_out, grad_query, small = first_end(held, exchange(first_passed, 8), small)
    second_sums = sum_once(second_pair, first_passed)
    grad_gate, grad_up = assemble(list(after(pieces, second_sums[1], small)))
    return [grad_down[None], grad_gate, grad_up, grad_out, grad_query], (second_sums[0], exchange(second_sums[1], 8)), small


def local(states_in, out_grad, counts, segments, mixing, correction, gain_attn, w_query, w_key, w_value, w_attn_out, gain_ffn,
          w_gate, w_up, w_down):
    weights = (w_query, w_key, w_value, w_attn_out, w_gate, w_up, w_down)
    width = gain_attn.shape[1]
    index = lax.axis_index("dp")
    count = lax.axis_size("dp")
    fast = count == 16
    message, *weights = forward_lite(states_in, segments, mixing, correction, gain_attn, gain_ffn, weights)
    message = lax.ppermute(message, "section", [(0, 1), (1, 0)])
    (x, states, queries, key_rows, value_rows, probs, active, middle, one, two, change, *kept) = forward(
        fast, states_in, message, segments, mixing, correction, gain_attn, gain_ffn, weights)
    before = []
    if fast:
        kept, nearby, normed_ffn = swapped(kept[:4]), kept[4], kept[5]
        before = kept[1:]
    message = relay_backward(out_grad, counts, correction, mixing, gain_ffn, gain_attn, one, two, middle, queries, key_rows,
                             value_rows, probs, active, weights)
    message = lax.ppermute(message, "section", [(0, 1), (1, 0)])
    g_in, low = start(message, out_grad, counts, correction, before)
    *slots, grad_middle, grad_att, ffn_gain = ffn_backward(g_in, low, correction, gain_ffn, middle, one, two, [], weights)
    before = slots[0]
    if fast:
        lows = gather_end(gather_start(low), before)
        beside, across = (one[:, width + width // 2 :] for one in kept[1:3])
        normed_ffn = gather_end([normed_ffn, beside, across], before)
        down_pair = quarter_product(kept, lows, width // 4, [before], "product_down", False)
        before = down_pair[0]
    state_grads, right, small = attn_backward(x, g_in, grad_middle, grad_att, active, change, queries, key_rows, value_rows, probs,
                                              ffn_gain, gain_attn, mixing, correction, before, weights)
    if fast:
        grads, last, small = quarter_grads(normed_ffn, kept, nearby, slots, right, down_pair, index)
    else:
        grads = halving_grads(kept, low, slots, right[: low.shape[0]], index, count)
        small = sum_over(small, count.bit_length() - 1)
    share = width // count
    gains = lax.dynamic_slice(small, (0, index * share), (2, share))
    gains = gains[0:1], gains[1:2]
    sums = jnp.sum(small[2:], axis=1)
    sums = sums[:4].reshape(1, 2, 2), sums[4:].reshape(1, 2)
    if fast:
        came = after(last[1], gains, sums, grads)
        for span in (slice(0, width), slice(width, 2 * width)):
            grads.append((last[0][:, span] + came[:, span].astype(floating))[None])
    grad_down, grad_gate, grad_up, grad_out, grad_query, grad_key, grad_value = grads
    return (
        states,
        state_grads,
        sums[0],
        sums[1],
        gains[0],
        grad_query,
        grad_key,
        grad_value,
        grad_out,
        gains[1],
        grad_gate,
        grad_up,
        grad_down,
    )


def solution(mesh):
    rows = P("dp", None)
    matrix = P("section", None, None)
    vector = P("section", None)
    share = P("section", "dp", None)
    gain_share = P("section", "dp")
    in_specs = (rows, rows, P("dp"), rows, matrix, vector, vector, matrix, matrix, matrix, matrix, vector, matrix, matrix, matrix)
    out_specs = (share, share, matrix, vector, gain_share, share, share, share, share, gain_share, share, share, share)
    return jax.shard_map(local, mesh=mesh, in_specs=in_specs, out_specs=out_specs, check_vma=False)
```

```python
import functools

import jax
import jax.numpy as jnp
from jax import lax
from jax.experimental import pallas as pl
from jax.experimental.pallas import tpu as pltpu
from jax.sharding import PartitionSpec as P

HEAD_DIM = 64
PAIR = 2 * HEAD_DIM
EPSILON = 1e-06
MASKED = -1e30
SCALE = HEAD_DIM ** (-0.5)
GELU_A = 0.7978845608028654
GELU_B = 0.044715
EXTRA = 16
SCOPED = 12
bfloat = jnp.bfloat16
floating = jnp.float32

VMEM = pl.BlockSpec(memory_space=pltpu.VMEM)
SMEM = pl.BlockSpec(memory_space=pltpu.SMEM)
ANY = pl.BlockSpec(memory_space=pltpu.MemorySpace.HBM)


def dot(a, b):
    return jnp.dot(a, b, preferred_element_type=floating)


def dot_t(a, b):
    return lax.dot_general(a, b, (((1,), (1,)), ((), ())), preferred_element_type=floating)


def t_dot(a, b):
    return lax.dot_general(a, b, (((0,), (0,)), ((), ())), preferred_element_type=floating)


def params(mebibytes):
    return pltpu.CompilerParams(vmem_limit_bytes=mebibytes * 1024 * 1024)


def cost(flops, moved):
    return pl.CostEstimate(flops=flops // 1000, bytes_accessed=moved // 1000, transcendentals=0)


def spread(value):
    high = value.astype(bfloat).astype(floating)
    middle = (value - high).astype(bfloat).astype(floating)
    low = value - high - middle
    top = jnp.concatenate([high, middle], axis=1)
    bottom = jnp.concatenate([low, jnp.zeros_like(low)], axis=1)
    return jnp.concatenate([top, bottom], axis=0).astype(bfloat)


def gathered_parts(block):
    block = block.astype(floating)
    width = block.shape[1] // 2
    return block[:8, :width] + block[:8, width:] + block[8:, :width]


def rms_scale(values):
    return lax.rsqrt(jnp.mean(values * values, axis=-1, keepdims=True) + EPSILON)


def lane_mask(length):
    return lax.broadcasted_iota(jnp.int32, (length, PAIR), 1) < HEAD_DIM


def stack_heads(block, first):
    zero = jnp.zeros_like(block)
    return jnp.concatenate([jnp.where(first, block, zero), jnp.where(first, zero, block)], axis=0)


def gelu_wave(gate):
    return jnp.tanh(GELU_A * (gate + GELU_B * gate * gate * gate))


def relative(blocks, index):
    low = (index & 1) == 1
    high = (index >> 1) == 1
    once = [jnp.where(low, blocks[place ^ 1], blocks[place]) for place in range(4)]
    return [jnp.where(high, once[place ^ 2], once[place]) for place in range(4)]


def attention(q_ref, k_ref, v_ref, seg_ref, att_ref, p_ref):
    length = seg_ref.shape[1]
    rows = q_ref.shape[0] // length
    pairs = q_ref.shape[1] // PAIR
    first = lane_mask(length)
    later = lax.broadcasted_iota(jnp.int32, (length, length), 0)
    earlier = lax.broadcasted_iota(jnp.int32, (length, length), 1)
    for row in range(rows):
        documents = jnp.broadcast_to(seg_ref[row : row + 1, :], (length, length)).astype(floating)
        allowed = (earlier <= later) & (documents == documents.T)
        allowed = jnp.concatenate([allowed, allowed], axis=0)
        span = slice(row * length, (row + 1) * length)
        for pair in range(pairs):
            heads = slice(pair * PAIR, (pair + 1) * PAIR)
            stacked = stack_heads(q_ref[span, heads], first)
            scores = jnp.where(allowed, dot_t(stacked, k_ref[span, heads]) * SCALE, MASKED)
            powers = jnp.exp(scores - jnp.max(scores, axis=-1, keepdims=True))
            probs = powers / jnp.sum(powers, axis=-1, keepdims=True)
            if p_ref is not None:
                p_ref[row * pairs + pair] = probs
            mixed = dot(probs.astype(bfloat), v_ref[span, heads])
            att_ref[span, heads] = jnp.where(first, mixed[:length], mixed[length:]).astype(bfloat)


def in_hbm(value):
    return pltpu.with_memory_space_constraint(value, pltpu.MemorySpace.HBM)


def forward_lite_kernel(x_any, seg_any, mix_any, cor_any, ga_any, gf_any, wq, wk, wv, wo, wg, wu, wd,
                        out_ref, wq_s, wk_s, wv_s, wo_s, wg_s, wu_s, wd_s,
                        x_in, seg_ref, mix_ref, cor_ref, ga_ref, gf_ref, q_ref, k_ref, v_ref, act_ref,
                        nrm_ref, att_ref, nf_ref, acc, sem, small_sem):
    tokens, width = act_ref.shape
    chunk = width
    pieces = wg.shape[2] // chunk
    small = [
        pltpu.make_async_copy(source, target, small_sem.at[place])
        for place, (source, target) in enumerate(
            ((x_any, x_in), (mix_any, mix_ref), (ga_any, ga_ref), (seg_any, seg_ref), (gf_any, gf_ref), (cor_any, cor_ref))
        )
    ]
    pairs = [(wq, wq_s), (wk, wk_s), (wv, wv_s), (wo, wo_s)]
    queue = [pltpu.make_async_copy(source, target, sem.at[place]) for place, (source, target) in enumerate(pairs)]

    def group(piece):
        span = pl.ds(pl.multiple_of(piece * chunk, chunk), chunk)
        places = ((wg, wg_s, (slice(None), slice(None), span)), (wu, wu_s, (slice(None), slice(None), span)),
                  (wd, wd_s, (slice(None), span, slice(None))))
        return [
            pltpu.make_async_copy(source.at[where], target.at[where], sem.at[4 + 3 * piece + place])
            for place, (source, target, where) in enumerate(places)
        ]

    def start_group(piece):
        for copy in group(piece):
            copy.start()

    for copy in small + queue:
        copy.start()
    for copy in small:
        copy.wait()
    section = lax.axis_index("section")
    mix = [[mix_ref[0, i, j] for j in range(2)] for i in range(2)]
    cor = [cor_ref[0, i] for i in range(2)]
    xa = x_in[:, :width].astype(floating)
    xb = x_in[:, width:].astype(floating)
    own_a = jnp.where(section == 0, mix[0][0], mix[1][0])
    own_b = jnp.where(section == 0, mix[0][1], mix[1][1])
    active = jnp.where(section == 0, xa, xb) + (own_a * xa + own_b * xb)
    act_ref[...] = active
    nrm_ref[...] = (active * rms_scale(active) * ga_ref[...]).astype(bfloat)
    for place, (copy, weight, target) in enumerate(zip(queue, (wq_s, wk_s, wv_s), (q_ref, k_ref, v_ref))):
        copy.wait()
        if place != 1:
            start_group(place // 2)
        target[...] = dot(nrm_ref[...], weight[0]).astype(bfloat)
    attention(q_ref, k_ref, v_ref, seg_ref, att_ref, None)
    for piece in range(2, pieces):
        start_group(piece)
    queue[3].wait()
    middle = act_ref[...] + dot(att_ref[...], wo_s[0])
    acc[...] = middle - act_ref[...]
    nf_ref[...] = (middle * rms_scale(middle) * gf_ref[...]).astype(bfloat)

    def one_piece(piece, carry):
        span = pl.ds(pl.multiple_of(piece * chunk, chunk), chunk)
        waits = group(piece)
        waits[0].wait()
        gate = dot(nf_ref[...], wg_s[0, :, span])
        waits[1].wait()
        upward = dot(nf_ref[...], wu_s[0, :, span])
        hidden = (0.5 * gate * (1.0 + gelu_wave(gate)) * upward).astype(bfloat)
        waits[2].wait()
        acc[...] += dot(hidden, wd_s[0, span, :])
        return carry

    lax.fori_loop(0, pieces, one_piece, 0, unroll=2)
    xa = x_in[:, :width].astype(floating)
    xb = x_in[:, width:].astype(floating)
    out_ref[:, :width] = (xa + (mix[0][0] * xa + mix[0][1] * xb) + cor[0] * acc[...]).astype(bfloat)
    out_ref[:, width:] = (xb + (mix[1][0] * xa + mix[1][1] * xb) + cor[1] * acc[...]).astype(bfloat)


def forward_lite(x_in, segments, mixing, correction, gain_attn, gain_ffn, weights):
    tokens = x_in.shape[0]
    width = gain_attn.shape[1]
    size = sum(weight.size for weight in weights)
    narrow = pltpu.VMEM((tokens, width), bfloat)
    wide = pltpu.VMEM((tokens, width), floating)
    args = (x_in, segments, mixing, correction, gain_attn, gain_ffn) + weights
    scratch = [
        pltpu.VMEM(x_in.shape, bfloat), pltpu.VMEM(segments.shape, jnp.int32), pltpu.SMEM(mixing.shape, floating),
        pltpu.SMEM(correction.shape, floating), pltpu.VMEM(gain_attn.shape, floating), pltpu.VMEM(gain_ffn.shape, floating),
        narrow, narrow, narrow, wide, narrow, narrow, narrow, wide,
    ]
    scratch += [pltpu.SemaphoreType.DMA((4 + 3 * (weights[4].shape[2] // width),)), pltpu.SemaphoreType.DMA((6,))]
    return pl.pallas_call(
        forward_lite_kernel,
        out_shape=[jax.ShapeDtypeStruct((tokens, 2 * width), bfloat)]
        + [jax.ShapeDtypeStruct(weight.shape, bfloat) for weight in weights],
        in_specs=[ANY] * len(args),
        out_specs=[VMEM] * 8,
        scratch_shapes=scratch,
        compiler_params=params(SCOPED),
        cost_estimate=cost(2 * tokens * size, 2 * size),
        name="forward_lite",
    )(*[in_hbm(one) for one in args])


def forward_kernel(fast, x_in, message, seg_ref, mix_ref, cor_ref, ga_ref, gf_ref, wq, wk, wv, wo, wg, wu, wd,
                   x_ref, out_ref, q_ref, k_ref, v_ref, p_ref, act_ref, mid_ref, one_ref, two_ref, chg_ref, *refs):
    kept = refs[:4]
    nf_ref = refs[-4]
    nrm_ref, att_ref, acc = refs[-3:]
    tokens, width = act_ref.shape
    chunk = width
    pieces = wg.shape[2] // chunk
    section = lax.axis_index("section")
    quarter = lax.axis_index("dp") & 3
    mix = [[mix_ref[0, i, j] for j in range(2)] for i in range(2)]
    cor = [cor_ref[0, i] for i in range(2)]
    x_ref[...] = jnp.where(section == 0, x_in[...], message[...])
    xa = x_ref[:, :width].astype(floating)
    xb = x_ref[:, width:].astype(floating)
    own_a = jnp.where(section == 0, mix[0][0], mix[1][0])
    own_b = jnp.where(section == 0, mix[0][1], mix[1][1])
    active = jnp.where(section == 0, xa, xb) + (own_a * xa + own_b * xb)
    act_ref[...] = active
    nrm_ref[...] = (active * rms_scale(active) * ga_ref[...]).astype(bfloat)
    for weight, target in zip((wq, wk, wv), (q_ref, k_ref, v_ref)):
        target[...] = dot(nrm_ref[...], weight[0]).astype(bfloat)

    def keep_quarters(values, base):
        share = width // 16
        for far in range(4):
            blocks = [values[:, (4 * far + near) * share : (4 * far + near + 1) * share] for near in range(4)]
            for slot, block in enumerate(relative(blocks, quarter)):
                target, start = (kept[slot], width + base) if slot < 3 else (refs[4], base)
                target[:, start + far * share : start + (far + 1) * share] = block

    attention(q_ref, k_ref, v_ref, seg_ref, att_ref, p_ref)
    middle = act_ref[...] + dot(att_ref[...], wo[0])
    mid_ref[...] = middle
    nf_ref[...] = (middle * rms_scale(middle) * gf_ref[...]).astype(bfloat)
    if fast:
        keep_quarters(att_ref[...], 0)
        keep_quarters(nrm_ref[...], width // 4)
        for slot in (1, 2):
            kept[slot][:, width + width // 2 :] = nf_ref[...]
    else:
        kept[1][...] = nrm_ref[...]
        kept[2][...] = att_ref[...]
    for piece in range(pieces):
        span = slice(piece * chunk, (piece + 1) * chunk)
        gate = dot(nf_ref[...], wg[0, :, span])
        upward = dot(nf_ref[...], wu[0, :, span])
        wave = gelu_wave(gate)
        half = 0.5 * (1.0 + wave)
        value = gate * half
        hidden = (value * upward).astype(bfloat)
        slope = half + 0.5 * gate * (1.0 - wave * wave) * (GELU_A * (1.0 + 3.0 * GELU_B * gate * gate))
        one_ref[piece] = upward * slope
        two_ref[piece] = value
        if fast:
            share = chunk // 4
            blocks = [hidden[:, near * share : (near + 1) * share] for near in range(4)]
            for slot, block in enumerate(relative(blocks, quarter)):
                kept[slot][:, piece * share : (piece + 1) * share] = block
        else:
            kept[0][:, span] = hidden
        down = dot(hidden, wd[0, span, :])
        if piece == 0:
            acc[...] = down
        else:
            acc[...] += down
    change = mid_ref[...] + acc[...] - act_ref[...]
    chg_ref[...] = change
    xa = x_ref[:, :width].astype(floating)
    xb = x_ref[:, width:].astype(floating)
    out_ref[0, :, :width] = (xa + (mix[0][0] * xa + mix[0][1] * xb) + cor[0] * change).astype(bfloat)
    out_ref[0, :, width:] = (xb + (mix[1][0] * xa + mix[1][1] * xb) + cor[1] * change).astype(bfloat)


def forward(fast, x_in, message, segments, mixing, correction, gain_attn, gain_ffn, weights):
    tokens = x_in.shape[0]
    length = segments.shape[1]
    width = gain_attn.shape[1]
    hidden_width = weights[4].shape[2]
    size = sum(weight.size for weight in weights)
    shape = jax.ShapeDtypeStruct
    narrow = ((tokens, width), bfloat)
    wide = ((tokens, width), floating)
    probs = ((tokens // length * (width // PAIR), 2 * length, length), floating)
    if fast:
        short, long = (((tokens, columns), bfloat) for columns in (width + width // 2, 2 * width + width // 2))
        kept = [short, long, long, narrow, ((tokens, width // 2), bfloat), narrow]
    else:
        kept = [((tokens, hidden_width), bfloat), narrow, narrow, narrow]
    ffn = ((hidden_width // width, tokens, width), floating)
    outs = [((tokens, 2 * width), bfloat), ((1, tokens, 2 * width), bfloat), narrow, narrow, narrow, probs, wide, wide,
            ffn, ffn, wide] + kept
    return pl.pallas_call(
        lambda *refs: forward_kernel(fast, *refs),
        out_shape=[shape(*one) for one in outs],
        in_specs=[VMEM, VMEM, VMEM, SMEM, SMEM, VMEM, VMEM] + [VMEM] * 7,
        out_specs=[VMEM] * len(outs),
        scratch_shapes=[pltpu.VMEM(*narrow)] * 2 + [pltpu.VMEM(*wide)],
        compiler_params=params(SCOPED),
        cost_estimate=cost(2 * tokens * size, 2 * size),
        name="forward_full",
    )(x_in, message, segments, mixing, correction, gain_attn, gain_ffn, *weights)


def start_rows(message, grad_ref, counts_ref, cor_ref, g_ref, low_ref):
    tokens, width = low_ref.shape
    rows = counts_ref.shape[0]
    length = tokens // rows
    section = lax.axis_index("section")
    place = lax.broadcasted_iota(jnp.int32, (tokens, width), 0)
    valid = place < counts_ref[0]
    for row in range(1, rows):
        valid = valid | ((place >= row * length) & (place < row * length + counts_ref[row]))
    own_a = jnp.where(valid, grad_ref[:, :width].astype(floating), 0.0)
    own_b = jnp.where(valid, grad_ref[:, width:].astype(floating), 0.0)
    if message is not None:
        own_a = jnp.where(section == 0, message[:, :width].astype(floating), own_a)
        own_b = jnp.where(section == 0, message[:, width:].astype(floating), own_b)
    g_ref[:, :width] = own_a.astype(bfloat)
    g_ref[:, width:] = own_b.astype(bfloat)
    low_ref[...] = (cor_ref[0, 0] * own_a + cor_ref[0, 1] * own_b).astype(bfloat)


def start(message, out_grad, counts, correction, before):
    tokens = out_grad.shape[0]
    width = message.shape[1] // 2
    shape = jax.ShapeDtypeStruct
    return pl.pallas_call(
        lambda *refs: start_rows(*refs[:4], *refs[-2:]),
        out_shape=[shape((tokens, 2 * width), bfloat), shape((tokens, width), bfloat)],
        in_specs=[VMEM, VMEM, SMEM, SMEM] + [ANY] * len(before),
        out_specs=[VMEM, VMEM],
        compiler_params=params(SCOPED),
        cost_estimate=cost(tokens * width * 20, tokens * width * 12),
        name="backward_start",
    )(message, out_grad, counts, correction, *before)


def norm_backward(values, gain, grad_normed, with_gain):
    inverse = rms_scale(values)
    grad_gain = jnp.sum(grad_normed * values * inverse, axis=0, keepdims=True) if with_gain else None
    weighted = grad_normed * gain
    grad_values = inverse * weighted - values * inverse**3 * jnp.mean(weighted * values, axis=-1, keepdims=True)
    return grad_gain, grad_values


def ffn_steps(low_ref, one, two, wg, wu, wd, acc, emit):
    width = wd.shape[2]
    quarter = lax.axis_index("dp") & 3
    for step in range(4):
        piece = (3 - step) ^ quarter
        span = pl.ds(pl.multiple_of(piece * width, width), width)
        grad_hidden = dot_t(low_ref[...], wd[0, span, :])
        dgate = (grad_hidden * one[piece]).astype(bfloat)
        dup = (grad_hidden * two[piece]).astype(bfloat)
        emit(3 - step, dgate, dup)
        total = dot_t(dgate, wg[0, :, span]) + dot_t(dup, wu[0, :, span])
        if step == 0:
            acc[...] = total
        else:
            acc[...] += total


def ffn_kernel(g_in, low_ref, cor_ref, gf_ref, mid_ref, one, two, wg, wu, wd, *refs):
    slots = refs[-12:-4]
    dmid_ref, datt_ref, gain_ref, acc = refs[-4:]
    width = gf_ref.shape[1]

    def emit(slot, dgate, dup):
        slots[slot][...] = dgate
        slots[4 + slot][...] = dup

    ffn_steps(low_ref, one, two, wg, wu, wd, acc, emit)
    grad_gain, grad_values = norm_backward(mid_ref[...], gf_ref[...], acc[...], True)
    block = cor_ref[0, 0] * g_in[:, :width].astype(floating) + cor_ref[0, 1] * g_in[:, width:].astype(floating)
    grad_middle = block + grad_values
    dmid_ref[...] = grad_middle
    datt_ref[...] = grad_middle.astype(bfloat)
    gain_ref[...] = grad_gain


def ffn_backward(g_in, low, correction, gain_ffn, middle, one, two, before, weights):
    tokens = g_in.shape[0]
    width = gain_ffn.shape[1]
    shape = jax.ShapeDtypeStruct
    return pl.pallas_call(
        ffn_kernel,
        out_shape=[shape((tokens, width), bfloat)] * 8
        + [shape((tokens, width), floating), shape((tokens, width), bfloat), shape((1, width), floating)],
        in_specs=[VMEM, VMEM, SMEM] + [VMEM] * 7 + [ANY] * len(before),
        out_specs=[VMEM] * 11,
        scratch_shapes=[pltpu.VMEM((tokens, width), floating)],
        compiler_params=params(SCOPED),
        cost_estimate=cost(2 * tokens * 3 * weights[4].size, 2 * 3 * weights[4].size),
        name="backward_ffn",
    )(g_in, low, correction, gain_ffn, middle, one, two, *weights[4:], *before)


def attn_steps(q_ref, k_ref, v_ref, p_ref, do_ref, parts):
    tokens, width = do_ref.shape
    length = p_ref.shape[2]
    rows = tokens // length
    pairs = width // PAIR
    first = lane_mask(length)
    for row in range(rows):
        span = slice(row * length, (row + 1) * length)
        for pair in range(pairs):
            heads = slice(pair * PAIR, (pair + 1) * PAIR)
            probs = p_ref[row * pairs + pair]
            grad_out = stack_heads(do_ref[span, heads], first)
            grad_value = t_dot(probs.astype(bfloat), grad_out)
            grad_probs = dot_t(grad_out, v_ref[span, heads])
            carried = jnp.sum(probs * grad_probs, axis=-1, keepdims=True)
            grad_scores = (probs * (grad_probs - carried)).astype(bfloat)
            grad_query = dot(grad_scores, k_ref[span, heads])
            grad_query = jnp.where(first, grad_query[:length], grad_query[length:])
            grad_key = t_dot(grad_scores, stack_heads(q_ref[span, heads], first))
            for (part, base), value in zip(parts, (grad_query * SCALE, grad_key * SCALE, grad_value)):
                part[span, base + pair * PAIR : base + (pair + 1) * PAIR] = value.astype(bfloat)


def normed_grad(parts, rows, width, wq, wk, wv):
    return sum(dot_t(part[:rows, base : base + width], weight[0]) for (part, base), weight in zip(parts, (wq, wk, wv)))


def attn_kernel(datt_ref, q_ref, k_ref, v_ref, p_ref, gfg_ref, ga_ref, x_ref, g_in, dmid_ref, act_ref, chg_ref, mix_ref, cor_ref,
                wq, wk, wv, wo, before,
                grad_ref, right_ref, small_ref, do_ref):
    tokens, width = datt_ref.shape
    right_ref[:tokens, :width] = datt_ref[...]
    do_ref[...] = dot_t(datt_ref[...], wo[0]).astype(bfloat)
    parts = (right_ref, width), (right_ref, 2 * width), (right_ref, 3 * width)
    attn_steps(q_ref, k_ref, v_ref, p_ref, do_ref, parts)
    grad_normed = normed_grad(parts, tokens, width, wq, wk, wv)
    grad_gain, grad_values = norm_backward(act_ref[...], ga_ref[...], grad_normed, True)
    section = lax.axis_index("section")
    mix = [[mix_ref[0, i, j] for j in range(2)] for i in range(2)]
    cor = [cor_ref[0, i] for i in range(2)]
    out_a = g_in[:, :width].astype(floating)
    out_b = g_in[:, width:].astype(floating)
    grad_active = dmid_ref[...] + grad_values - (cor[0] * out_a + cor[1] * out_b)
    pred_a = out_a + jnp.where(section == 0, grad_active, 0.0)
    pred_b = out_b + jnp.where(section == 0, 0.0, grad_active)
    grad_ref[0, :, :width] = (pred_a + (mix[0][0] * pred_a + mix[1][0] * pred_b)).astype(bfloat)
    grad_ref[0, :, width:] = (pred_b + (mix[0][1] * pred_a + mix[1][1] * pred_b)).astype(bfloat)
    xa = x_ref[:, :width].astype(floating)
    xb = x_ref[:, width:].astype(floating)
    small_ref[0:1, :] = grad_gain
    small_ref[1:2, :] = gfg_ref[...]
    place = 2
    for pred in (pred_a, pred_b):
        for state in (xa, xb):
            small_ref[place : place + 1, :] = jnp.sum(pred * state, axis=0, keepdims=True)
            place += 1
    for out in (out_a, out_b):
        small_ref[place : place + 1, :] = jnp.sum(out * chg_ref[...], axis=0, keepdims=True)
        place += 1
    right_ref[tokens:, : 2 * width] = spread(small_ref[...])
    right_ref[tokens:, 2 * width :] = jnp.zeros((right_ref.shape[0] - tokens, 2 * width), bfloat)


def attn_backward(x, g_in, grad_middle, grad_att, active, change, queries, key_rows, value_rows, probs, ffn_gain, gain_attn,
                  mixing, correction, before, weights):
    tokens, width = active.shape
    shape = jax.ShapeDtypeStruct
    return pl.pallas_call(
        attn_kernel,
        out_shape=[
            shape((1, tokens, 2 * width), bfloat), shape((tokens + EXTRA, 4 * width), bfloat), shape((8, width), floating),
        ],
        in_specs=[VMEM] * 12 + [SMEM] * 2 + [VMEM] * 4 + [ANY],
        out_specs=[VMEM] * 3,
        scratch_shapes=[pltpu.VMEM((tokens, width), bfloat)],
        compiler_params=params(SCOPED),
        cost_estimate=cost(2 * tokens * 5 * weights[0].size, 2 * 4 * weights[0].size),
        name="backward_attn",
    )(grad_att, queries, key_rows, value_rows, probs, ffn_gain, gain_attn, x, g_in, grad_middle, active, change,
      mixing, correction, *weights[:4], before)


def relay_kernel(grad_in, counts_ref, cor_ref, mix_ref, gf_ref, ga_ref, one, two, mid_ref, q_ref, k_ref, v_ref, p_ref, act_ref,
                 wq, wk, wv, wo, wg, wu, wd,
                 msg_ref,
                 acc, g_in, low_ref, do_ref, dqkv_ref):
    tokens, width = low_ref.shape
    start_rows(None, grad_in, counts_ref, cor_ref, g_in, low_ref)
    ffn_steps(low_ref, one, two, wg, wu, wd, acc, lambda *parts: None)
    grad_values = norm_backward(mid_ref[...], gf_ref[...], acc[...], False)[1]
    cor = [cor_ref[0, i] for i in range(2)]
    block = cor[0] * g_in[:, :width].astype(floating) + cor[1] * g_in[:, width:].astype(floating)
    acc[...] = block + grad_values
    do_ref[...] = dot_t(acc[...].astype(bfloat), wo[0]).astype(bfloat)
    parts = (dqkv_ref, 0), (dqkv_ref, width), (dqkv_ref, 2 * width)
    attn_steps(q_ref, k_ref, v_ref, p_ref, do_ref, parts)
    grad_normed = normed_grad(parts, tokens, width, wq, wk, wv)
    grad_values = norm_backward(act_ref[...], ga_ref[...], grad_normed, False)[1]
    out_a = g_in[:, :width].astype(floating)
    out_b = g_in[:, width:].astype(floating)
    pred_b = out_b + (acc[...] + grad_values - (cor[0] * out_a + cor[1] * out_b))
    mix = [[mix_ref[0, i, j] for j in range(2)] for i in range(2)]
    msg_ref[:, :width] = (out_a + (mix[0][0] * out_a + mix[1][0] * pred_b)).astype(bfloat)
    msg_ref[:, width:] = (pred_b + (mix[0][1] * out_a + mix[1][1] * pred_b)).astype(bfloat)


def relay_backward(out_grad, counts, correction, mixing, gain_ffn, gain_attn, one, two, middle, queries, key_rows, value_rows,
                   probs, active, weights):
    tokens, width = active.shape
    shape = jax.ShapeDtypeStruct
    narrow = pltpu.VMEM((tokens, width), bfloat)
    wide = pltpu.VMEM((tokens, width), floating)
    size = sum(weight.size for weight in weights)
    return pl.pallas_call(
        relay_kernel,
        out_shape=shape((tokens, 2 * width), bfloat),
        in_specs=[VMEM, SMEM, SMEM, SMEM] + [VMEM] * 17,
        out_specs=VMEM,
        scratch_shapes=[wide, pltpu.VMEM((tokens, 2 * width), bfloat), narrow, narrow, pltpu.VMEM((tokens, 3 * width), bfloat)],
        compiler_params=params(SCOPED),
        cost_estimate=cost(2 * tokens * size, 2 * size),
        name="backward_relay",
    )(out_grad, counts, correction, mixing, gain_ffn, gain_attn, one, two, middle, queries, key_rows, value_rows, probs, active,
      *weights)


def quarter_parts(base, products, block, lefts, rights, own_ref, far_ref, all_ref, left_s, right_s):
    tokens = lefts[0].shape[0]
    tail = lefts[0].shape[1] - lefts[-1].shape[1]
    mine = (lax.axis_index("dp") >> 2) & 3
    for left_at, left_wide, right_at, right_wide in products:
        columns = slice(right_at, right_at + right_wide)
        span = slice(right_at - base, right_at - base + right_wide)
        for row, (left, right) in enumerate(zip(lefts, rights)):
            at = left_at if left.shape[1] > left_at else left_at - tail
            rows = slice(row * tokens, (row + 1) * tokens)
            left_s[rows, :left_wide] = left[:, at : at + left_wide]
            right_s[rows, :right_wide] = right[:tokens, columns]
        total = t_dot(left_s[:, :left_wide], right_s[:, :right_wide])
        for place in range(4):
            all_ref[place ^ mine, :, span] = total[place * block : (place + 1) * block, :]
    own_ref[:block, :] = all_ref[1].astype(bfloat)
    far_ref[:block, :] = all_ref[3].astype(bfloat)


def quarter_product(lefts, rights, block, before, name, parted):
    rows, wide = lefts[0].shape[0], rights[0].shape[1]
    shape = jax.ShapeDtypeStruct
    products = [(0, 4 * block, 0, wide)]
    sends = [shape((block, wide), bfloat)] * 2 if parted else [shape((2, block, wide), bfloat)]

    def kernel(*refs):
        *outs, all_ref, left_s, right_s = refs[-5:] if parted else refs[-4:]
        own_ref, far_ref = outs if parted else (outs[0].at[0], outs[0].at[1])
        quarter_parts(0, products, block, refs[:4], refs[4:8], own_ref, far_ref, all_ref, left_s, right_s)

    return pl.pallas_call(
        kernel,
        out_shape=sends + [shape((4, block, wide), floating)],
        in_specs=[VMEM] * 8 + [ANY] * len(before),
        out_specs=[VMEM] * (len(sends) + 1),
        scratch_shapes=[pltpu.VMEM((4 * rows, 4 * block), bfloat), pltpu.VMEM((4 * rows, wide), bfloat)],
        compiler_params=params(SCOPED),
        cost_estimate=cost(32 * rows * block * wide, 16 * block * wide),
        name=name,
    )(*lefts, *rights, *before)


def attn_product_kernel(halves, block, refs):
    lefts, rights = refs[:4], refs[4:8]
    first_send, first_keep, small_ref, second_send, second_keep, stage, left_s, right_s = refs[-8:]
    tokens = lefts[0].shape[0]
    wide = first_keep.shape[2]
    quarter_parts(0, halves[0], block, lefts, rights, first_send, stage, first_keep, left_s, right_s)
    first_send[block : 2 * block, :] = stage[...]
    small = sum(gathered_parts(right[tokens:, :wide]) for right in rights)
    small_ref[...] = small
    first_send[2 * block :, :] = spread(small)
    quarter_parts(wide, halves[1], block, lefts, rights, second_send.at[0], second_send.at[1], second_keep, left_s, right_s)


def attn_product(lefts, rights, halves, block, before):
    wide = rights[0].shape[1] // 2
    shape = jax.ShapeDtypeStruct
    send, keep = shape((2, block, wide), bfloat), shape((4, block, wide), floating)
    return pl.pallas_call(
        lambda *refs: attn_product_kernel(halves, block, refs),
        out_shape=[shape((2 * block + EXTRA, wide), bfloat), keep, shape((8, wide // 2), floating), send, keep],
        in_specs=[VMEM] * 8 + [ANY] * len(before),
        out_specs=[VMEM] * 5,
        scratch_shapes=[
            pltpu.VMEM(send.shape[1:], bfloat), pltpu.VMEM((4 * lefts[0].shape[0], 4 * block), bfloat),
            pltpu.VMEM((4 * lefts[0].shape[0], wide), bfloat),
        ],
        compiler_params=params(SCOPED),
        cost_estimate=cost(wide, wide),
        name="product_attn",
    )(*lefts, *rights, *before)


def first_sum_kernel(keep_ref, came_ref, small_ref, held_ref, passed_ref, sums_ref):
    block = held_ref.shape[0]
    held_ref[...] = keep_ref[0] + came_ref[:block, :].astype(floating)
    passed_ref[:block, :] = (keep_ref[2] + came_ref[block : 2 * block, :].astype(floating)).astype(bfloat)
    small = small_ref[...] + gathered_parts(came_ref[2 * block :, :])
    sums_ref[...] = small
    passed_ref[block:, :] = spread(small)


def first_sum(keep, came, small):
    _, block, wide = keep.shape
    shape = jax.ShapeDtypeStruct
    return pl.pallas_call(
        first_sum_kernel,
        out_shape=[shape((block, wide), floating), shape((block + EXTRA, wide), bfloat), shape(small.shape, floating)],
        in_specs=[VMEM] * 3,
        out_specs=[VMEM] * 3,
        compiler_params=params(SCOPED),
        cost_estimate=cost(wide, wide),
        name="first_sum",
    )(keep, came, small)


def first_end_kernel(held_ref, came_ref, small_ref, left_ref, right_ref, sums_ref):
    block, wide = held_ref.shape
    left_ref[0] = held_ref[:, : wide // 2] + came_ref[:block, : wide // 2].astype(floating)
    right_ref[0] = held_ref[:, wide // 2 :] + came_ref[:block, wide // 2 :].astype(floating)
    sums_ref[...] = small_ref[...] + gathered_parts(came_ref[block:, :])


def first_end(held, came, small):
    block, wide = held.shape
    shape = jax.ShapeDtypeStruct
    return pl.pallas_call(
        first_end_kernel,
        out_shape=[shape((1, block, wide // 2), floating)] * 2 + [shape(small.shape, floating)],
        in_specs=[VMEM] * 3,
        out_specs=[VMEM] * 3,
        compiler_params=params(SCOPED),
        cost_estimate=cost(wide, wide),
        name="first_end",
    )(held, came, small)


def assemble_kernel(own, one, two, three, gate_ref, up_ref):
    quarter = lax.axis_index("dp") & 3
    width = own.shape[1] // 2
    for slot, piece in enumerate((own, one, two, three)):
        span = pl.ds(pl.multiple_of((slot ^ quarter) * width, width), width)
        gate_ref[0, :, span] = piece[:, :width].astype(floating)
        up_ref[0, :, span] = piece[:, width:].astype(floating)


def assemble(pieces):
    share, double = pieces[0].shape
    shape = jax.ShapeDtypeStruct((1, share, 2 * double), floating)
    return pl.pallas_call(
        assemble_kernel,
        out_shape=[shape, shape],
        in_specs=[VMEM] * 4,
        out_specs=[VMEM] * 2,
        compiler_params=params(SCOPED),
        cost_estimate=cost(share * double * 4, share * double * 24),
        name="assemble",
    )(*pieces)


def exchange(value, flips):
    count = lax.axis_size("dp")
    return lax.ppermute(value, "dp", [(source, source ^ flips) for source in range(count)])


def relative_rows(matrix, order, index):
    bits = len(order)
    block = matrix.shape[0] >> bits
    split = matrix.reshape((2,) * bits + (block, matrix.shape[1]))
    axes = [bits - 1 - bit for bit in order]
    split = jnp.transpose(split, axes + [bits, bits + 1])
    for axis, bit in enumerate(order):
        split = jnp.where((index >> bit) & 1 == 1, jnp.flip(split, axis), split)
    return split.reshape(matrix.shape)


def scatter_sum(left, right, order):
    total = left.shape[0]
    arrived = []
    for step in range(len(order) + 1):
        low = total >> (step + 1) if step < len(order) else 0
        high = total >> step
        part = dot(left[low:high], right)
        for other in arrived:
            part = part + other[low:high].astype(floating)
        if step == len(order):
            return part
        arrived.append(exchange(part.astype(bfloat), 1 << order[step]))


def halving_grads(kept, low, slots, right, index, count):
    width = low.shape[1]
    order = list(range(count.bit_length() - 1))
    hidden, normed, attended, normed_ffn = (relative_rows(one.T, order, index) for one in kept)
    quarter = index & 3
    places = jnp.arange(4) ^ quarter
    dgate = jnp.concatenate(list(jnp.stack(slots[:4])[places]), axis=1)
    dup = jnp.concatenate(list(jnp.stack(slots[4:])[places]), axis=1)
    grad_down = scatter_sum(hidden, low, order)
    grad_gate = scatter_sum(normed_ffn, dgate, order)
    grad_up = scatter_sum(normed_ffn, dup, order)
    grad_out = scatter_sum(attended, right[:, :width], order)
    grad_qkv = scatter_sum(normed, right[:, width:], order)
    grads = [grad_down, grad_gate, grad_up, grad_out] + [grad_qkv[:, place * width : (place + 1) * width] for place in range(3)]
    return [one[None] for one in grads]


def after(values, *earlier):
    return lax.optimization_barrier((values, earlier))[0]


def gather_start(value):
    return [value, exchange(value, 1), exchange(value, 2)]


def gather_end(pieces, *earlier):
    return pieces + [exchange(after(pieces[2], *earlier), 1)]


def swapped(pieces):
    return [pieces[0]] + [exchange(pieces[flips], flips) for flips in (1, 2, 3)]


def parts_once(product, *earlier):
    own, far, keep = product
    own, far = after((exchange(own, 4), exchange(far, 4)), *earlier)
    return keep[0] + own.astype(floating), (keep[2] + far.astype(floating)).astype(bfloat)


def sum_once(pair, *earlier):
    send, keep = pair
    arrived = after(exchange(send, 4), *earlier)
    return keep[0] + arrived[0].astype(floating), (keep[2] + arrived[1].astype(floating)).astype(bfloat)


def sum_twice(held, passed, *earlier):
    return held + after(exchange(passed, 8), *earlier).astype(floating)


def sum_over(value, bits):
    for bit in range(bits):
        value = value + exchange(value, 1 << bit)
    return value


def quarter_grads(normed_ffn, kept, nearby, slots, right, down_pair, index):
    width = normed_ffn[0].shape[1]
    share = width // 16
    block = 4 * share
    gates = swapped(slots[:4])
    ups, nearby = after((slots[4:], nearby), right)
    ups, nearby = swapped(list(ups)), exchange(nearby, 3)
    down_sums = sum_once(down_pair, right)
    gate_pair = quarter_product(normed_ffn, gates, block, [right, down_sums[1]], "product_gate", True)
    grad_down = sum_twice(*down_sums)
    rights = gather_start(after(right, gate_pair[0], ups[1:]))
    gate_sums = parts_once(gate_pair)
    up_pair = quarter_product(normed_ffn, ups, block, [gate_sums[1], grad_down, nearby], "product_up", False)
    up_sums = sum_once(up_pair)
    part = block * 3 // 4
    gate_came = exchange(gate_sums[1][:part], 8)
    rights = gather_end(rights, up_sums[1], gate_came)
    up_came = exchange(jnp.concatenate([up_sums[1], gate_sums[1][part:]], axis=0), 8)
    halves = (
        [(width, block, 0, width), (width + block, block, width, width)], [(width + block, block, 2 * width, 2 * width)])
    before = [up_sums[1], gate_came]
    first_send, first_keep, small, *second_pair = attn_product(kept[:3] + [nearby], rights, halves, share, before)
    held, first_passed, small = first_sum(first_keep, after(exchange(first_send, 4), up_came), small)
    second_sums = sum_once(second_pair, first_passed)
    gate_came, up_came = after((gate_came, up_came), second_sums[1])
    gate_tile = (gate_sums[0] + jnp.concatenate([gate_came, up_came[block:]], axis=0).astype(floating)).astype(bfloat)
    up_tile = (up_sums[0] + up_came[:block].astype(floating)).astype(bfloat)
    quarter = index & 3
    pieces = [
        jnp.concatenate(
            [lax.dynamic_slice_in_dim(tile, (slot ^ quarter) * share, share, axis=0) for tile in (gate_tile, up_tile)], axis=1)
        for slot in range(4)
    ]
    pieces = swapped(pieces)
    grad_out, grad_query, small = first_end(held, exchange(first_passed, 8), small)
    grad_gate, grad_up = assemble(list(after(pieces, second_sums[1], small)))
    return [grad_down[None], grad_gate, grad_up, grad_out, grad_query], (second_sums[0], exchange(second_sums[1], 8)), small


def local(states_in, out_grad, counts, segments, mixing, correction, gain_attn, w_query, w_key, w_value, w_attn_out, gain_ffn,
          w_gate, w_up, w_down):
    weights = (w_query, w_key, w_value, w_attn_out, w_gate, w_up, w_down)
    width = gain_attn.shape[1]
    index = lax.axis_index("dp")
    count = lax.axis_size("dp")
    fast = count == 16
    message, *weights = forward_lite(states_in, segments, mixing, correction, gain_attn, gain_ffn, weights)
    message = lax.ppermute(message, "section", [(0, 1), (1, 0)])
    (x, states, queries, key_rows, value_rows, probs, active, middle, one, two, change, *kept) = forward(
        fast, states_in, message, segments, mixing, correction, gain_attn, gain_ffn, weights)
    before = []
    if fast:
        kept, nearby, normed_ffn = swapped(kept[:4]), kept[4], kept[5]
        before = kept[1:]
    message = relay_backward(out_grad, counts, correction, mixing, gain_ffn, gain_attn, one, two, middle, queries, key_rows,
                             value_rows, probs, active, weights)
    message = lax.ppermute(message, "section", [(0, 1), (1, 0)])
    g_in, low = start(message, out_grad, counts, correction, before)
    *slots, grad_middle, grad_att, ffn_gain = ffn_backward(g_in, low, correction, gain_ffn, middle, one, two, [], weights)
    before = slots[0]
    if fast:
        lows = gather_end(gather_start(low), before)
        beside, across = (one[:, width + width // 2 :] for one in kept[1:3])
        normed_ffn = gather_end([normed_ffn, beside, across], before)
        down_pair = quarter_product(kept, lows, width // 4, [before], "product_down", False)
        before = down_pair[0]
    state_grads, right, small = attn_backward(x, g_in, grad_middle, grad_att, active, change, queries, key_rows, value_rows, probs,
                                              ffn_gain, gain_attn, mixing, correction, before, weights)
    if fast:
        grads, last, small = quarter_grads(normed_ffn, kept, nearby, slots, right, down_pair, index)
    else:
        grads = halving_grads(kept, low, slots, right[: low.shape[0]], index, count)
        small = sum_over(small, count.bit_length() - 1)
    share = width // count
    gains = lax.dynamic_slice(small, (0, index * share), (2, share))
    gains = gains[0:1], gains[1:2]
    sums = jnp.sum(small[2:], axis=1)
    sums = sums[:4].reshape(1, 2, 2), sums[4:].reshape(1, 2)
    if fast:
        came = after(last[1], gains, sums, grads)
        for span in (slice(0, width), slice(width, 2 * width)):
            grads.append((last[0][:, span] + came[:, span].astype(floating))[None])
    grad_down, grad_gate, grad_up, grad_out, grad_query, grad_key, grad_value = grads
    return (
        states,
        state_grads,
        sums[0],
        sums[1],
        gains[0],
        grad_query,
        grad_key,
        grad_value,
        grad_out,
        gains[1],
        grad_gate,
        grad_up,
        grad_down,
    )


def solution(mesh):
    rows = P("dp", None)
    matrix = P("section", None, None)
    vector = P("section", None)
    share = P("section", "dp", None)
    gain_share = P("section", "dp")
    in_specs = (rows, rows, P("dp"), rows, matrix, vector, vector, matrix, matrix, matrix, matrix, vector, matrix, matrix, matrix)
    out_specs = (share, share, matrix, vector, gain_share, share, share, share, share, gain_share, share, share, share)
    return jax.shard_map(local, mesh=mesh, in_specs=in_specs, out_specs=out_specs, check_vma=False)
```

```python
import functools

import jax
import jax.numpy as jnp
from jax import lax
from jax.experimental import pallas as pl
from jax.experimental.pallas import tpu as pltpu
from jax.sharding import PartitionSpec as P

HEAD_DIM = 64
PAIR = 2 * HEAD_DIM
EPSILON = 1e-06
MASKED = -1e30
SCALE = HEAD_DIM ** (-0.5)
GELU_A = 0.7978845608028654
GELU_B = 0.044715
EXTRA = 16
SCOPED = 12
bfloat = jnp.bfloat16
floating = jnp.float32

VMEM = pl.BlockSpec(memory_space=pltpu.VMEM)
SMEM = pl.BlockSpec(memory_space=pltpu.SMEM)
ANY = pl.BlockSpec(memory_space=pltpu.MemorySpace.HBM)


def dot(a, b):
    return jnp.dot(a, b, preferred_element_type=floating)


def dot_t(a, b):
    return lax.dot_general(a, b, (((1,), (1,)), ((), ())), preferred_element_type=floating)


def t_dot(a, b):
    return lax.dot_general(a, b, (((0,), (0,)), ((), ())), preferred_element_type=floating)


def params(mebibytes):
    return pltpu.CompilerParams(vmem_limit_bytes=mebibytes * 1024 * 1024)


def cost(flops, moved):
    return pl.CostEstimate(flops=flops // 1000, bytes_accessed=moved // 1000, transcendentals=0)


def spread(value):
    high = value.astype(bfloat).astype(floating)
    middle = (value - high).astype(bfloat).astype(floating)
    low = value - high - middle
    top = jnp.concatenate([high, middle], axis=1)
    bottom = jnp.concatenate([low, jnp.zeros_like(low)], axis=1)
    return jnp.concatenate([top, bottom], axis=0).astype(bfloat)


def gathered_parts(block):
    block = block.astype(floating)
    width = block.shape[1] // 2
    return block[:8, :width] + block[:8, width:] + block[8:, :width]


def rms_scale(values):
    return lax.rsqrt(jnp.mean(values * values, axis=-1, keepdims=True) + EPSILON)


def lane_mask(length):
    return lax.broadcasted_iota(jnp.int32, (length, PAIR), 1) < HEAD_DIM


def stack_heads(block, first):
    zero = jnp.zeros_like(block)
    return jnp.concatenate([jnp.where(first, block, zero), jnp.where(first, zero, block)], axis=0)


def gelu_wave(gate):
    return jnp.tanh(GELU_A * (gate + GELU_B * gate * gate * gate))


def relative(blocks, index):
    low = (index & 1) == 1
    high = (index >> 1) == 1
    once = [jnp.where(low, blocks[place ^ 1], blocks[place]) for place in range(4)]
    return [jnp.where(high, once[place ^ 2], once[place]) for place in range(4)]


def attention(q_ref, k_ref, v_ref, seg_ref, att_ref, p_ref):
    length = seg_ref.shape[1]
    rows = q_ref.shape[0] // length
    pairs = q_ref.shape[1] // PAIR
    first = lane_mask(length)
    later = lax.broadcasted_iota(jnp.int32, (length, length), 0)
    earlier = lax.broadcasted_iota(jnp.int32, (length, length), 1)
    for row in range(rows):
        documents = jnp.broadcast_to(seg_ref[row : row + 1, :], (length, length)).astype(floating)
        allowed = (earlier <= later) & (documents == documents.T)
        allowed = jnp.concatenate([allowed, allowed], axis=0)
        span = slice(row * length, (row + 1) * length)
        for pair in range(pairs):
            heads = slice(pair * PAIR, (pair + 1) * PAIR)
            stacked = stack_heads(q_ref[span, heads], first)
            scores = jnp.where(allowed, dot_t(stacked, k_ref[span, heads]) * SCALE, MASKED)
            powers = jnp.exp(scores - jnp.max(scores, axis=-1, keepdims=True))
            probs = powers / jnp.sum(powers, axis=-1, keepdims=True)
            if p_ref is not None:
                p_ref[row * pairs + pair] = probs
            mixed = dot(probs.astype(bfloat), v_ref[span, heads])
            att_ref[span, heads] = jnp.where(first, mixed[:length], mixed[length:]).astype(bfloat)


def in_hbm(value):
    return pltpu.with_memory_space_constraint(value, pltpu.MemorySpace.HBM)


def forward_lite_kernel(x_any, seg_any, mix_any, cor_any, ga_any, gf_any, wq, wk, wv, wo, wg, wu, wd,
                        out_ref, wq_s, wk_s, wv_s, wo_s, wg_s, wu_s, wd_s,
                        x_in, seg_ref, mix_ref, cor_ref, ga_ref, gf_ref, q_ref, k_ref, v_ref, act_ref,
                        nrm_ref, att_ref, nf_ref, acc, sem, small_sem):
    tokens, width = act_ref.shape
    chunk = width
    pieces = wg.shape[2] // chunk
    small = [
        pltpu.make_async_copy(source, target, small_sem.at[place])
        for place, (source, target) in enumerate(
            ((x_any, x_in), (mix_any, mix_ref), (ga_any, ga_ref), (seg_any, seg_ref), (gf_any, gf_ref), (cor_any, cor_ref))
        )
    ]
    pairs = [(wq, wq_s), (wk, wk_s), (wv, wv_s), (wo, wo_s)]
    queue = [pltpu.make_async_copy(source, target, sem.at[place]) for place, (source, target) in enumerate(pairs)]

    def group(piece):
        span = pl.ds(pl.multiple_of(piece * chunk, chunk), chunk)
        places = ((wg, wg_s, (slice(None), slice(None), span)), (wu, wu_s, (slice(None), slice(None), span)),
                  (wd, wd_s, (slice(None), span, slice(None))))
        return [
            pltpu.make_async_copy(source.at[where], target.at[where], sem.at[4 + 3 * piece + place])
            for place, (source, target, where) in enumerate(places)
        ]

    def start_group(piece):
        for copy in group(piece):
            copy.start()

    for copy in small + queue:
        copy.start()
    for copy in small:
        copy.wait()
    section = lax.axis_index("section")
    mix = [[mix_ref[0, i, j] for j in range(2)] for i in range(2)]
    cor = [cor_ref[0, i] for i in range(2)]
    xa = x_in[:, :width].astype(floating)
    xb = x_in[:, width:].astype(floating)
    own_a = jnp.where(section == 0, mix[0][0], mix[1][0])
    own_b = jnp.where(section == 0, mix[0][1], mix[1][1])
    active = jnp.where(section == 0, xa, xb) + (own_a * xa + own_b * xb)
    act_ref[...] = active
    nrm_ref[...] = (active * rms_scale(active) * ga_ref[...]).astype(bfloat)
    for place, (copy, weight, target) in enumerate(zip(queue, (wq_s, wk_s, wv_s), (q_ref, k_ref, v_ref))):
        copy.wait()
        if place != 1:
            start_group(place // 2)
        target[...] = dot(nrm_ref[...], weight[0]).astype(bfloat)
    attention(q_ref, k_ref, v_ref, seg_ref, att_ref, None)
    for piece in range(2, pieces):
        start_group(piece)
    queue[3].wait()
    middle = act_ref[...] + dot(att_ref[...], wo_s[0])
    acc[...] = middle - act_ref[...]
    nf_ref[...] = (middle * rms_scale(middle) * gf_ref[...]).astype(bfloat)

    def one_piece(piece, carry):
        span = pl.ds(pl.multiple_of(piece * chunk, chunk), chunk)
        waits = group(piece)
        waits[0].wait()
        gate = dot(nf_ref[...], wg_s[0, :, span])
        waits[1].wait()
        upward = dot(nf_ref[...], wu_s[0, :, span])
        hidden = (0.5 * gate * (1.0 + gelu_wave(gate)) * upward).astype(bfloat)
        waits[2].wait()
        acc[...] += dot(hidden, wd_s[0, span, :])
        return carry

    lax.fori_loop(0, pieces, one_piece, 0, unroll=2)
    xa = x_in[:, :width].astype(floating)
    xb = x_in[:, width:].astype(floating)
    out_ref[:, :width] = (xa + (mix[0][0] * xa + mix[0][1] * xb) + cor[0] * acc[...]).astype(bfloat)
    out_ref[:, width:] = (xb + (mix[1][0] * xa + mix[1][1] * xb) + cor[1] * acc[...]).astype(bfloat)


def forward_lite(x_in, segments, mixing, correction, gain_attn, gain_ffn, weights):
    tokens = x_in.shape[0]
    width = gain_attn.shape[1]
    size = sum(weight.size for weight in weights)
    narrow = pltpu.VMEM((tokens, width), bfloat)
    wide = pltpu.VMEM((tokens, width), floating)
    args = (x_in, segments, mixing, correction, gain_attn, gain_ffn) + weights
    scratch = [
        pltpu.VMEM(x_in.shape, bfloat), pltpu.VMEM(segments.shape, jnp.int32), pltpu.SMEM(mixing.shape, floating),
        pltpu.SMEM(correction.shape, floating), pltpu.VMEM(gain_attn.shape, floating), pltpu.VMEM(gain_ffn.shape, floating),
        narrow, narrow, narrow, wide, narrow, narrow, narrow, wide,
    ]
    scratch += [pltpu.SemaphoreType.DMA((4 + 3 * (weights[4].shape[2] // width),)), pltpu.SemaphoreType.DMA((6,))]
    return pl.pallas_call(
        forward_lite_kernel,
        out_shape=[jax.ShapeDtypeStruct((tokens, 2 * width), bfloat)]
        + [jax.ShapeDtypeStruct(weight.shape, bfloat) for weight in weights],
        in_specs=[ANY] * len(args),
        out_specs=[VMEM] * 8,
        scratch_shapes=scratch,
        compiler_params=params(SCOPED),
        cost_estimate=cost(2 * tokens * size, 2 * size),
        name="forward_lite",
    )(*[in_hbm(one) for one in args])


def forward_kernel(fast, x_in, message, seg_ref, mix_ref, cor_ref, ga_ref, gf_ref, wq, wk, wv, wo, wg, wu, wd,
                   x_ref, out_ref, q_ref, k_ref, v_ref, p_ref, act_ref, mid_ref, one_ref, two_ref, chg_ref, *refs):
    kept = refs[:4]
    nf_ref = refs[-4]
    nrm_ref, att_ref, acc = refs[-3:]
    tokens, width = act_ref.shape
    chunk = width
    pieces = wg.shape[2] // chunk
    section = lax.axis_index("section")
    quarter = lax.axis_index("dp") & 3
    mix = [[mix_ref[0, i, j] for j in range(2)] for i in range(2)]
    cor = [cor_ref[0, i] for i in range(2)]
    x_ref[...] = jnp.where(section == 0, x_in[...], message[...])
    xa = x_ref[:, :width].astype(floating)
    xb = x_ref[:, width:].astype(floating)
    own_a = jnp.where(section == 0, mix[0][0], mix[1][0])
    own_b = jnp.where(section == 0, mix[0][1], mix[1][1])
    active = jnp.where(section == 0, xa, xb) + (own_a * xa + own_b * xb)
    act_ref[...] = active
    nrm_ref[...] = (active * rms_scale(active) * ga_ref[...]).astype(bfloat)
    for weight, target in zip((wq, wk, wv), (q_ref, k_ref, v_ref)):
        target[...] = dot(nrm_ref[...], weight[0]).astype(bfloat)

    def keep_quarters(values, base):
        share = width // 16
        for far in range(4):
            blocks = [values[:, (4 * far + near) * share : (4 * far + near + 1) * share] for near in range(4)]
            for slot, block in enumerate(relative(blocks, quarter)):
                target, start = (kept[slot], width + base) if slot < 3 else (refs[4], base)
                target[:, start + far * share : start + (far + 1) * share] = block

    attention(q_ref, k_ref, v_ref, seg_ref, att_ref, p_ref)
    middle = act_ref[...] + dot(att_ref[...], wo[0])
    mid_ref[...] = middle
    nf_ref[...] = (middle * rms_scale(middle) * gf_ref[...]).astype(bfloat)
    if fast:
        keep_quarters(att_ref[...], 0)
        keep_quarters(nrm_ref[...], width // 4)
        for slot in (1, 2):
            kept[slot][:, width + width // 2 :] = nf_ref[...]
    else:
        kept[1][...] = nrm_ref[...]
        kept[2][...] = att_ref[...]
    for piece in range(pieces):
        span = slice(piece * chunk, (piece + 1) * chunk)
        gate = dot(nf_ref[...], wg[0, :, span])
        upward = dot(nf_ref[...], wu[0, :, span])
        wave = gelu_wave(gate)
        half = 0.5 * (1.0 + wave)
        value = gate * half
        hidden = (value * upward).astype(bfloat)
        slope = half + 0.5 * gate * (1.0 - wave * wave) * (GELU_A * (1.0 + 3.0 * GELU_B * gate * gate))
        one_ref[piece] = upward * slope
        two_ref[piece] = value
        if fast:
            share = chunk // 4
            blocks = [hidden[:, near * share : (near + 1) * share] for near in range(4)]
            for slot, block in enumerate(relative(blocks, quarter)):
                kept[slot][:, piece * share : (piece + 1) * share] = block
        else:
            kept[0][:, span] = hidden
        down = dot(hidden, wd[0, span, :])
        if piece == 0:
            acc[...] = down
        else:
            acc[...] += down
    change = mid_ref[...] + acc[...] - act_ref[...]
    chg_ref[...] = change
    xa = x_ref[:, :width].astype(floating)
    xb = x_ref[:, width:].astype(floating)
    out_ref[0, :, :width] = (xa + (mix[0][0] * xa + mix[0][1] * xb) + cor[0] * change).astype(bfloat)
    out_ref[0, :, width:] = (xb + (mix[1][0] * xa + mix[1][1] * xb) + cor[1] * change).astype(bfloat)


def forward(fast, x_in, message, segments, mixing, correction, gain_attn, gain_ffn, weights):
    tokens = x_in.shape[0]
    length = segments.shape[1]
    width = gain_attn.shape[1]
    hidden_width = weights[4].shape[2]
    size = sum(weight.size for weight in weights)
    shape = jax.ShapeDtypeStruct
    narrow = ((tokens, width), bfloat)
    wide = ((tokens, width), floating)
    probs = ((tokens // length * (width // PAIR), 2 * length, length), floating)
    if fast:
        short, long = (((tokens, columns), bfloat) for columns in (width + width // 2, 2 * width + width // 2))
        kept = [short, long, long, narrow, ((tokens, width // 2), bfloat), narrow]
    else:
        kept = [((tokens, hidden_width), bfloat), narrow, narrow, narrow]
    ffn = ((hidden_width // width, tokens, width), floating)
    outs = [((tokens, 2 * width), bfloat), ((1, tokens, 2 * width), bfloat), narrow, narrow, narrow, probs, wide, wide,
            ffn, ffn, wide] + kept
    return pl.pallas_call(
        lambda *refs: forward_kernel(fast, *refs),
        out_shape=[shape(*one) for one in outs],
        in_specs=[VMEM, VMEM, VMEM, SMEM, SMEM, VMEM, VMEM] + [VMEM] * 7,
        out_specs=[VMEM] * len(outs),
        scratch_shapes=[pltpu.VMEM(*narrow)] * 2 + [pltpu.VMEM(*wide)],
        compiler_params=params(SCOPED),
        cost_estimate=cost(2 * tokens * size, 2 * size),
        name="forward_full",
    )(x_in, message, segments, mixing, correction, gain_attn, gain_ffn, *weights)


def start_rows(message, grad_ref, counts_ref, cor_ref, g_ref, low_ref):
    tokens, width = low_ref.shape
    rows = counts_ref.shape[0]
    length = tokens // rows
    section = lax.axis_index("section")
    place = lax.broadcasted_iota(jnp.int32, (tokens, width), 0)
    valid = place < counts_ref[0]
    for row in range(1, rows):
        valid = valid | ((place >= row * length) & (place < row * length + counts_ref[row]))
    own_a = jnp.where(valid, grad_ref[:, :width].astype(floating), 0.0)
    own_b = jnp.where(valid, grad_ref[:, width:].astype(floating), 0.0)
    if message is not None:
        own_a = jnp.where(section == 0, message[:, :width].astype(floating), own_a)
        own_b = jnp.where(section == 0, message[:, width:].astype(floating), own_b)
    g_ref[:, :width] = own_a.astype(bfloat)
    g_ref[:, width:] = own_b.astype(bfloat)
    low_ref[...] = (cor_ref[0, 0] * own_a + cor_ref[0, 1] * own_b).astype(bfloat)


def start(message, out_grad, counts, correction, before):
    tokens = out_grad.shape[0]
    width = message.shape[1] // 2
    shape = jax.ShapeDtypeStruct
    return pl.pallas_call(
        lambda *refs: start_rows(*refs[:4], *refs[-2:]),
        out_shape=[shape((tokens, 2 * width), bfloat), shape((tokens, width), bfloat)],
        in_specs=[VMEM, VMEM, SMEM, SMEM] + [ANY] * len(before),
        out_specs=[VMEM, VMEM],
        compiler_params=params(SCOPED),
        cost_estimate=cost(tokens * width * 20, tokens * width * 12),
        name="backward_start",
    )(message, out_grad, counts, correction, *before)


def norm_backward(values, gain, grad_normed, with_gain):
    inverse = rms_scale(values)
    grad_gain = jnp.sum(grad_normed * values * inverse, axis=0, keepdims=True) if with_gain else None
    weighted = grad_normed * gain
    grad_values = inverse * weighted - values * inverse**3 * jnp.mean(weighted * values, axis=-1, keepdims=True)
    return grad_gain, grad_values


def ffn_steps(low_ref, one, two, wg, wu, wd, acc, emit):
    width = wd.shape[2]
    quarter = lax.axis_index("dp") & 3
    for step in range(4):
        piece = (3 - step) ^ quarter
        span = pl.ds(pl.multiple_of(piece * width, width), width)
        grad_hidden = dot_t(low_ref[...], wd[0, span, :])
        dgate = (grad_hidden * one[piece]).astype(bfloat)
        dup = (grad_hidden * two[piece]).astype(bfloat)
        emit(3 - step, dgate, dup)
        total = dot_t(dgate, wg[0, :, span]) + dot_t(dup, wu[0, :, span])
        if step == 0:
            acc[...] = total
        else:
            acc[...] += total


def ffn_kernel(g_in, low_ref, cor_ref, gf_ref, mid_ref, one, two, wg, wu, wd, *refs):
    slots = refs[-12:-4]
    dmid_ref, datt_ref, gain_ref, acc = refs[-4:]
    width = gf_ref.shape[1]

    def emit(slot, dgate, dup):
        slots[slot][...] = dgate
        slots[4 + slot][...] = dup

    ffn_steps(low_ref, one, two, wg, wu, wd, acc, emit)
    grad_gain, grad_values = norm_backward(mid_ref[...], gf_ref[...], acc[...], True)
    block = cor_ref[0, 0] * g_in[:, :width].astype(floating) + cor_ref[0, 1] * g_in[:, width:].astype(floating)
    grad_middle = block + grad_values
    dmid_ref[...] = grad_middle
    datt_ref[...] = grad_middle.astype(bfloat)
    gain_ref[...] = grad_gain


def ffn_backward(g_in, low, correction, gain_ffn, middle, one, two, before, weights):
    tokens = g_in.shape[0]
    width = gain_ffn.shape[1]
    shape = jax.ShapeDtypeStruct
    return pl.pallas_call(
        ffn_kernel,
        out_shape=[shape((tokens, width), bfloat)] * 8
        + [shape((tokens, width), floating), shape((tokens, width), bfloat), shape((1, width), floating)],
        in_specs=[VMEM, VMEM, SMEM] + [VMEM] * 7 + [ANY] * len(before),
        out_specs=[VMEM] * 11,
        scratch_shapes=[pltpu.VMEM((tokens, width), floating)],
        compiler_params=params(SCOPED),
        cost_estimate=cost(2 * tokens * 3 * weights[4].size, 2 * 3 * weights[4].size),
        name="backward_ffn",
    )(g_in, low, correction, gain_ffn, middle, one, two, *weights[4:], *before)


def attn_steps(q_ref, k_ref, v_ref, p_ref, do_ref, parts):
    tokens, width = do_ref.shape
    length = p_ref.shape[2]
    rows = tokens // length
    pairs = width // PAIR
    first = lane_mask(length)
    for row in range(rows):
        span = slice(row * length, (row + 1) * length)
        for pair in range(pairs):
            heads = slice(pair * PAIR, (pair + 1) * PAIR)
            probs = p_ref[row * pairs + pair]
            grad_out = stack_heads(do_ref[span, heads], first)
            grad_value = t_dot(probs.astype(bfloat), grad_out)
            grad_probs = dot_t(grad_out, v_ref[span, heads])
            carried = jnp.sum(probs * grad_probs, axis=-1, keepdims=True)
            grad_scores = (probs * (grad_probs - carried)).astype(bfloat)
            grad_query = dot(grad_scores, k_ref[span, heads])
            grad_query = jnp.where(first, grad_query[:length], grad_query[length:])
            grad_key = t_dot(grad_scores, stack_heads(q_ref[span, heads], first))
            for (part, base), value in zip(parts, (grad_query * SCALE, grad_key * SCALE, grad_value)):
                part[span, base + pair * PAIR : base + (pair + 1) * PAIR] = value.astype(bfloat)


def normed_grad(parts, rows, width, wq, wk, wv):
    return sum(dot_t(part[:rows, base : base + width], weight[0]) for (part, base), weight in zip(parts, (wq, wk, wv)))


def attn_kernel(datt_ref, q_ref, k_ref, v_ref, p_ref, gfg_ref, ga_ref, x_ref, g_in, dmid_ref, act_ref, chg_ref, mix_ref, cor_ref,
                wq, wk, wv, wo, before,
                grad_ref, right_ref, small_ref, do_ref):
    tokens, width = datt_ref.shape
    right_ref[:tokens, :width] = datt_ref[...]
    do_ref[...] = dot_t(datt_ref[...], wo[0]).astype(bfloat)
    parts = (right_ref, width), (right_ref, 2 * width), (right_ref, 3 * width)
    attn_steps(q_ref, k_ref, v_ref, p_ref, do_ref, parts)
    grad_normed = normed_grad(parts, tokens, width, wq, wk, wv)
    grad_gain, grad_values = norm_backward(act_ref[...], ga_ref[...], grad_normed, True)
    section = lax.axis_index("section")
    mix = [[mix_ref[0, i, j] for j in range(2)] for i in range(2)]
    cor = [cor_ref[0, i] for i in range(2)]
    out_a = g_in[:, :width].astype(floating)
    out_b = g_in[:, width:].astype(floating)
    grad_active = dmid_ref[...] + grad_values - (cor[0] * out_a + cor[1] * out_b)
    pred_a = out_a + jnp.where(section == 0, grad_active, 0.0)
    pred_b = out_b + jnp.where(section == 0, 0.0, grad_active)
    grad_ref[0, :, :width] = (pred_a + (mix[0][0] * pred_a + mix[1][0] * pred_b)).astype(bfloat)
    grad_ref[0, :, width:] = (pred_b + (mix[0][1] * pred_a + mix[1][1] * pred_b)).astype(bfloat)
    xa = x_ref[:, :width].astype(floating)
    xb = x_ref[:, width:].astype(floating)
    small_ref[0:1, :] = grad_gain
    small_ref[1:2, :] = gfg_ref[...]
    place = 2
    for pred in (pred_a, pred_b):
        for state in (xa, xb):
            small_ref[place : place + 1, :] = jnp.sum(pred * state, axis=0, keepdims=True)
            place += 1
    for out in (out_a, out_b):
        small_ref[place : place + 1, :] = jnp.sum(out * chg_ref[...], axis=0, keepdims=True)
        place += 1
    right_ref[tokens:, : 2 * width] = spread(small_ref[...])
    right_ref[tokens:, 2 * width :] = jnp.zeros((right_ref.shape[0] - tokens, 2 * width), bfloat)


def attn_backward(x, g_in, grad_middle, grad_att, active, change, queries, key_rows, value_rows, probs, ffn_gain, gain_attn,
                  mixing, correction, before, weights):
    tokens, width = active.shape
    shape = jax.ShapeDtypeStruct
    return pl.pallas_call(
        attn_kernel,
        out_shape=[
            shape((1, tokens, 2 * width), bfloat), shape((tokens + EXTRA, 4 * width), bfloat), shape((8, width), floating),
        ],
        in_specs=[VMEM] * 12 + [SMEM] * 2 + [VMEM] * 4 + [ANY],
        out_specs=[VMEM] * 3,
        scratch_shapes=[pltpu.VMEM((tokens, width), bfloat)],
        compiler_params=params(SCOPED),
        cost_estimate=cost(2 * tokens * 5 * weights[0].size, 2 * 4 * weights[0].size),
        name="backward_attn",
    )(grad_att, queries, key_rows, value_rows, probs, ffn_gain, gain_attn, x, g_in, grad_middle, active, change,
      mixing, correction, *weights[:4], before)


def relay_kernel(grad_in, counts_ref, cor_ref, mix_ref, gf_ref, ga_ref, one, two, mid_ref, q_ref, k_ref, v_ref, p_ref, act_ref,
                 wq, wk, wv, wo, wg, wu, wd,
                 msg_ref,
                 acc, g_in, low_ref, do_ref, dqkv_ref):
    tokens, width = low_ref.shape
    start_rows(None, grad_in, counts_ref, cor_ref, g_in, low_ref)
    ffn_steps(low_ref, one, two, wg, wu, wd, acc, lambda *parts: None)
    grad_values = norm_backward(mid_ref[...], gf_ref[...], acc[...], False)[1]
    cor = [cor_ref[0, i] for i in range(2)]
    block = cor[0] * g_in[:, :width].astype(floating) + cor[1] * g_in[:, width:].astype(floating)
    acc[...] = block + grad_values
    do_ref[...] = dot_t(acc[...].astype(bfloat), wo[0]).astype(bfloat)
    parts = (dqkv_ref, 0), (dqkv_ref, width), (dqkv_ref, 2 * width)
    attn_steps(q_ref, k_ref, v_ref, p_ref, do_ref, parts)
    grad_normed = normed_grad(parts, tokens, width, wq, wk, wv)
    grad_values = norm_backward(act_ref[...], ga_ref[...], grad_normed, False)[1]
    out_a = g_in[:, :width].astype(floating)
    out_b = g_in[:, width:].astype(floating)
    pred_b = out_b + (acc[...] + grad_values - (cor[0] * out_a + cor[1] * out_b))
    mix = [[mix_ref[0, i, j] for j in range(2)] for i in range(2)]
    msg_ref[:, :width] = (out_a + (mix[0][0] * out_a + mix[1][0] * pred_b)).astype(bfloat)
    msg_ref[:, width:] = (pred_b + (mix[0][1] * out_a + mix[1][1] * pred_b)).astype(bfloat)


def relay_backward(out_grad, counts, correction, mixing, gain_ffn, gain_attn, one, two, middle, queries, key_rows, value_rows,
                   probs, active, weights):
    tokens, width = active.shape
    shape = jax.ShapeDtypeStruct
    narrow = pltpu.VMEM((tokens, width), bfloat)
    wide = pltpu.VMEM((tokens, width), floating)
    size = sum(weight.size for weight in weights)
    return pl.pallas_call(
        relay_kernel,
        out_shape=shape((tokens, 2 * width), bfloat),
        in_specs=[VMEM, SMEM, SMEM, SMEM] + [VMEM] * 17,
        out_specs=VMEM,
        scratch_shapes=[wide, pltpu.VMEM((tokens, 2 * width), bfloat), narrow, narrow, pltpu.VMEM((tokens, 3 * width), bfloat)],
        compiler_params=params(SCOPED),
        cost_estimate=cost(2 * tokens * size, 2 * size),
        name="backward_relay",
    )(out_grad, counts, correction, mixing, gain_ffn, gain_attn, one, two, middle, queries, key_rows, value_rows, probs, active,
      *weights)


def quarter_parts(base, products, block, lefts, rights, own_ref, far_ref, all_ref, left_s, right_s):
    tokens = lefts[0].shape[0]
    tail = lefts[0].shape[1] - lefts[-1].shape[1]
    mine = (lax.axis_index("dp") >> 2) & 3
    for left_at, left_wide, right_at, right_wide in products:
        columns = slice(right_at, right_at + right_wide)
        span = slice(right_at - base, right_at - base + right_wide)
        for row, (left, right) in enumerate(zip(lefts, rights)):
            at = left_at if left.shape[1] > left_at else left_at - tail
            rows = slice(row * tokens, (row + 1) * tokens)
            left_s[rows, :left_wide] = left[:, at : at + left_wide]
            right_s[rows, :right_wide] = right[:tokens, columns]
        total = t_dot(left_s[:, :left_wide], right_s[:, :right_wide])
        for place in range(4):
            all_ref[place ^ mine, :, span] = total[place * block : (place + 1) * block, :]
    own_ref[:block, :] = all_ref[1].astype(bfloat)
    far_ref[:block, :] = all_ref[3].astype(bfloat)


def quarter_product(lefts, rights, block, before, name, parted):
    rows, wide = lefts[0].shape[0], rights[0].shape[1]
    shape = jax.ShapeDtypeStruct
    products = [(0, 4 * block, 0, wide)]
    sends = [shape((block, wide), bfloat)] * 2 if parted else [shape((2, block, wide), bfloat)]

    def kernel(*refs):
        *outs, all_ref, left_s, right_s = refs[-5:] if parted else refs[-4:]
        own_ref, far_ref = outs if parted else (outs[0].at[0], outs[0].at[1])
        quarter_parts(0, products, block, refs[:4], refs[4:8], own_ref, far_ref, all_ref, left_s, right_s)

    return pl.pallas_call(
        kernel,
        out_shape=sends + [shape((4, block, wide), floating)],
        in_specs=[VMEM] * 8 + [ANY] * len(before),
        out_specs=[VMEM] * (len(sends) + 1),
        scratch_shapes=[pltpu.VMEM((4 * rows, 4 * block), bfloat), pltpu.VMEM((4 * rows, wide), bfloat)],
        compiler_params=params(SCOPED),
        cost_estimate=cost(32 * rows * block * wide, 16 * block * wide),
        name=name,
    )(*lefts, *rights, *before)


def attn_product_kernel(halves, block, refs):
    lefts, rights = refs[:4], refs[4:8]
    first_send, first_keep, small_ref, second_send, second_keep, stage, left_s, right_s = refs[-8:]
    tokens = lefts[0].shape[0]
    wide = first_keep.shape[2]
    quarter_parts(0, halves[0], block, lefts, rights, first_send, stage, first_keep, left_s, right_s)
    first_send[block : 2 * block, :] = stage[...]
    small = sum(gathered_parts(right[tokens:, :wide]) for right in rights)
    small_ref[...] = small
    first_send[2 * block :, :] = spread(small)
    quarter_parts(wide, halves[1], block, lefts, rights, second_send.at[0], second_send.at[1], second_keep, left_s, right_s)


def attn_product(lefts, rights, halves, block, before):
    wide = rights[0].shape[1] // 2
    shape = jax.ShapeDtypeStruct
    send, keep = shape((2, block, wide), bfloat), shape((4, block, wide), floating)
    return pl.pallas_call(
        lambda *refs: attn_product_kernel(halves, block, refs),
        out_shape=[shape((2 * block + EXTRA, wide), bfloat), keep, shape((8, wide // 2), floating), send, keep],
        in_specs=[VMEM] * 8 + [ANY] * len(before),
        out_specs=[VMEM] * 5,
        scratch_shapes=[
            pltpu.VMEM(send.shape[1:], bfloat), pltpu.VMEM((4 * lefts[0].shape[0], 4 * block), bfloat),
            pltpu.VMEM((4 * lefts[0].shape[0], wide), bfloat),
        ],
        compiler_params=params(SCOPED),
        cost_estimate=cost(wide, wide),
        name="product_attn",
    )(*lefts, *rights, *before)


def first_sum_kernel(keep_ref, came_ref, small_ref, held_ref, passed_ref, sums_ref):
    block = held_ref.shape[0]
    held_ref[...] = keep_ref[0] + came_ref[:block, :].astype(floating)
    passed_ref[:block, :] = (keep_ref[2] + came_ref[block : 2 * block, :].astype(floating)).astype(bfloat)
    small = small_ref[...] + gathered_parts(came_ref[2 * block :, :])
    sums_ref[...] = small
    passed_ref[block:, :] = spread(small)


def first_sum(keep, came, small):
    _, block, wide = keep.shape
    shape = jax.ShapeDtypeStruct
    return pl.pallas_call(
        first_sum_kernel,
        out_shape=[shape((block, wide), floating), shape((block + EXTRA, wide), bfloat), shape(small.shape, floating)],
        in_specs=[VMEM] * 3,
        out_specs=[VMEM] * 3,
        compiler_params=params(SCOPED),
        cost_estimate=cost(wide, wide),
        name="first_sum",
    )(keep, came, small)


def first_end_kernel(held_ref, came_ref, small_ref, left_ref, right_ref, sums_ref):
    block, wide = held_ref.shape
    left_ref[0] = held_ref[:, : wide // 2] + came_ref[:block, : wide // 2].astype(floating)
    right_ref[0] = held_ref[:, wide // 2 :] + came_ref[:block, wide // 2 :].astype(floating)
    sums_ref[...] = small_ref[...] + gathered_parts(came_ref[block:, :])


def first_end(held, came, small):
    block, wide = held.shape
    shape = jax.ShapeDtypeStruct
    return pl.pallas_call(
        first_end_kernel,
        out_shape=[shape((1, block, wide // 2), floating)] * 2 + [shape(small.shape, floating)],
        in_specs=[VMEM] * 3,
        out_specs=[VMEM] * 3,
        compiler_params=params(SCOPED),
        cost_estimate=cost(wide, wide),
        name="first_end",
    )(held, came, small)


def assemble_kernel(own, one, two, three, gate_ref, up_ref):
    quarter = lax.axis_index("dp") & 3
    width = own.shape[1] // 2
    for slot, piece in enumerate((own, one, two, three)):
        span = pl.ds(pl.multiple_of((slot ^ quarter) * width, width), width)
        gate_ref[0, :, span] = piece[:, :width].astype(floating)
        up_ref[0, :, span] = piece[:, width:].astype(floating)


def assemble(pieces):
    share, double = pieces[0].shape
    shape = jax.ShapeDtypeStruct((1, share, 2 * double), floating)
    return pl.pallas_call(
        assemble_kernel,
        out_shape=[shape, shape],
        in_specs=[VMEM] * 4,
        out_specs=[VMEM] * 2,
        compiler_params=params(SCOPED),
        cost_estimate=cost(share * double * 4, share * double * 24),
        name="assemble",
    )(*pieces)


def exchange(value, flips):
    count = lax.axis_size("dp")
    return lax.ppermute(value, "dp", [(source, source ^ flips) for source in range(count)])


def relative_rows(matrix, order, index):
    bits = len(order)
    block = matrix.shape[0] >> bits
    split = matrix.reshape((2,) * bits + (block, matrix.shape[1]))
    axes = [bits - 1 - bit for bit in order]
    split = jnp.transpose(split, axes + [bits, bits + 1])
    for axis, bit in enumerate(order):
        split = jnp.where((index >> bit) & 1 == 1, jnp.flip(split, axis), split)
    return split.reshape(matrix.shape)


def scatter_sum(left, right, order):
    total = left.shape[0]
    arrived = []
    for step in range(len(order) + 1):
        low = total >> (step + 1) if step < len(order) else 0
        high = total >> step
        part = dot(left[low:high], right)
        for other in arrived:
            part = part + other[low:high].astype(floating)
        if step == len(order):
            return part
        arrived.append(exchange(part.astype(bfloat), 1 << order[step]))


def halving_grads(kept, low, slots, right, index, count):
    width = low.shape[1]
    order = list(range(count.bit_length() - 1))
    hidden, normed, attended, normed_ffn = (relative_rows(one.T, order, index) for one in kept)
    quarter = index & 3
    places = jnp.arange(4) ^ quarter
    dgate = jnp.concatenate(list(jnp.stack(slots[:4])[places]), axis=1)
    dup = jnp.concatenate(list(jnp.stack(slots[4:])[places]), axis=1)
    grad_down = scatter_sum(hidden, low, order)
    grad_gate = scatter_sum(normed_ffn, dgate, order)
    grad_up = scatter_sum(normed_ffn, dup, order)
    grad_out = scatter_sum(attended, right[:, :width], order)
    grad_qkv = scatter_sum(normed, right[:, width:], order)
    grads = [grad_down, grad_gate, grad_up, grad_out] + [grad_qkv[:, place * width : (place + 1) * width] for place in range(3)]
    return [one[None] for one in grads]


def after(values, *earlier):
    return lax.optimization_barrier((values, earlier))[0]


def gather_start(value):
    return [value, exchange(value, 1), exchange(value, 2)]


def gather_end(pieces, *earlier):
    return pieces + [exchange(after(pieces[2], *earlier), 1)]


def swapped(pieces):
    return [pieces[0]] + [exchange(pieces[flips], flips) for flips in (1, 2, 3)]


def parts_once(product, *earlier):
    own, far, keep = product
    own, far = after((exchange(own, 4), exchange(far, 4)), *earlier)
    return keep[0] + own.astype(floating), (keep[2] + far.astype(floating)).astype(bfloat)


def sum_once(pair, *earlier):
    send, keep = pair
    arrived = after(exchange(send, 4), *earlier)
    return keep[0] + arrived[0].astype(floating), (keep[2] + arrived[1].astype(floating)).astype(bfloat)


def sum_twice(held, passed, *earlier):
    return held + after(exchange(passed, 8), *earlier).astype(floating)


def sum_over(value, bits):
    for bit in range(bits):
        value = value + exchange(value, 1 << bit)
    return value


def quarter_grads(normed_ffn, kept, nearby, slots, right, down_pair, index):
    width = normed_ffn[0].shape[1]
    share = width // 16
    block = 4 * share
    gates = swapped(slots[:4])
    ups, nearby = after((slots[4:], nearby), right)
    ups, nearby = swapped(list(ups)), exchange(nearby, 3)
    down_sums = sum_once(down_pair, right)
    gate_pair = quarter_product(normed_ffn, gates, block, [right, down_sums[1]], "product_gate", True)
    grad_down = sum_twice(*down_sums)
    rights = gather_start(after(right, gate_pair[0], ups[1:]))
    gate_sums = parts_once(gate_pair, grad_down)
    up_pair = quarter_product(normed_ffn, ups, block, [gate_sums[1], grad_down, nearby], "product_up", False)
    up_sums = sum_once(up_pair)
    part = block * 3 // 4
    gate_came = exchange(gate_sums[1][:part], 8)
    rights = gather_end(rights, up_sums[1], gate_came)
    up_came = exchange(jnp.concatenate([up_sums[1], gate_sums[1][part:]], axis=0), 8)
    halves = (
        [(width, block, 0, width), (width + block, block, width, width)], [(width + block, block, 2 * width, 2 * width)])
    before = [up_sums[1], gate_came]
    first_send, first_keep, small, *second_pair = attn_product(kept[:3] + [nearby], rights, halves, share, before)
    held, first_passed, small = first_sum(first_keep, after(exchange(first_send, 4), up_came), small)
    gate_came, up_came = after((gate_came, up_came), first_passed)
    gate_tile = (gate_sums[0] + jnp.concatenate([gate_came, up_came[block:]], axis=0).astype(floating)).astype(bfloat)
    up_tile = (up_sums[0] + up_came[:block].astype(floating)).astype(bfloat)
    quarter = index & 3
    pieces = [
        jnp.concatenate(
            [lax.dynamic_slice_in_dim(tile, (slot ^ quarter) * share, share, axis=0) for tile in (gate_tile, up_tile)], axis=1)
        for slot in range(4)
    ]
    pieces = swapped(pieces)
    grad_out, grad_query, small = first_end(held, exchange(first_passed, 8), small)
    second_sums = sum_once(second_pair, first_passed)
    grad_gate, grad_up = assemble(list(after(pieces, second_sums[1], small)))
    return [grad_down[None], grad_gate, grad_up, grad_out, grad_query], (second_sums[0], exchange(second_sums[1], 8)), small


def local(states_in, out_grad, counts, segments, mixing, correction, gain_attn, w_query, w_key, w_value, w_attn_out, gain_ffn,
          w_gate, w_up, w_down):
    weights = (w_query, w_key, w_value, w_attn_out, w_gate, w_up, w_down)
    width = gain_attn.shape[1]
    index = lax.axis_index("dp")
    count = lax.axis_size("dp")
    fast = count == 16
    message, *weights = forward_lite(states_in, segments, mixing, correction, gain_attn, gain_ffn, weights)
    message = lax.ppermute(message, "section", [(0, 1), (1, 0)])
    (x, states, queries, key_rows, value_rows, probs, active, middle, one, two, change, *kept) = forward(
        fast, states_in, message, segments, mixing, correction, gain_attn, gain_ffn, weights)
    before = []
    if fast:
        kept, nearby, normed_ffn = swapped(kept[:4]), kept[4], kept[5]
        before = kept[1:]
    message = relay_backward(out_grad, counts, correction, mixing, gain_ffn, gain_attn, one, two, middle, queries, key_rows,
                             value_rows, probs, active, weights)
    message = lax.ppermute(message, "section", [(0, 1), (1, 0)])
    g_in, low = start(message, out_grad, counts, correction, before)
    *slots, grad_middle, grad_att, ffn_gain = ffn_backward(g_in, low, correction, gain_ffn, middle, one, two, [], weights)
    before = slots[0]
    if fast:
        lows = gather_end(gather_start(low), before)
        beside, across = (one[:, width + width // 2 :] for one in kept[1:3])
        normed_ffn = gather_end([normed_ffn, beside, across], before)
        down_pair = quarter_product(kept, lows, width // 4, [before], "product_down", False)
        before = down_pair[0]
    state_grads, right, small = attn_backward(x, g_in, grad_middle, grad_att, active, change, queries, key_rows, value_rows, probs,
                                              ffn_gain, gain_attn, mixing, correction, before, weights)
    if fast:
        grads, last, small = quarter_grads(normed_ffn, kept, nearby, slots, right, down_pair, index)
    else:
        grads = halving_grads(kept, low, slots, right[: low.shape[0]], index, count)
        small = sum_over(small, count.bit_length() - 1)
    share = width // count
    gains = lax.dynamic_slice(small, (0, index * share), (2, share))
    gains = gains[0:1], gains[1:2]
    sums = jnp.sum(small[2:], axis=1)
    sums = sums[:4].reshape(1, 2, 2), sums[4:].reshape(1, 2)
    if fast:
        came = after(last[1], gains, sums, grads)
        for span in (slice(0, width), slice(width, 2 * width)):
            grads.append((last[0][:, span] + came[:, span].astype(floating))[None])
    grad_down, grad_gate, grad_up, grad_out, grad_query, grad_key, grad_value = grads
    return (
        states,
        state_grads,
        sums[0],
        sums[1],
        gains[0],
        grad_query,
        grad_key,
        grad_value,
        grad_out,
        gains[1],
        grad_gate,
        grad_up,
        grad_down,
    )


def solution(mesh):
    rows = P("dp", None)
    matrix = P("section", None, None)
    vector = P("section", None)
    share = P("section", "dp", None)
    gain_share = P("section", "dp")
    in_specs = (rows, rows, P("dp"), rows, matrix, vector, vector, matrix, matrix, matrix, matrix, vector, matrix, matrix, matrix)
    out_specs = (share, share, matrix, vector, gain_share, share, share, share, share, gain_share, share, share, share)
    return jax.shard_map(local, mesh=mesh, in_specs=in_specs, out_specs=out_specs, check_vma=False)
```

```python
import functools

import jax
import jax.numpy as jnp
from jax import lax
from jax.experimental import pallas as pl
from jax.experimental.pallas import tpu as pltpu
from jax.sharding import PartitionSpec as P

HEAD_DIM = 64
PAIR = 2 * HEAD_DIM
EPSILON = 1e-06
MASKED = -1e30
SCALE = HEAD_DIM ** (-0.5)
GELU_A = 0.7978845608028654
GELU_B = 0.044715
EXTRA = 16
SCOPED = 12
bfloat = jnp.bfloat16
floating = jnp.float32

VMEM = pl.BlockSpec(memory_space=pltpu.VMEM)
SMEM = pl.BlockSpec(memory_space=pltpu.SMEM)
ANY = pl.BlockSpec(memory_space=pltpu.MemorySpace.HBM)


def dot(a, b):
    return jnp.dot(a, b, preferred_element_type=floating)


def dot_t(a, b):
    return lax.dot_general(a, b, (((1,), (1,)), ((), ())), preferred_element_type=floating)


def t_dot(a, b):
    return lax.dot_general(a, b, (((0,), (0,)), ((), ())), preferred_element_type=floating)


def params(mebibytes):
    return pltpu.CompilerParams(vmem_limit_bytes=mebibytes * 1024 * 1024)


def cost(flops, moved):
    return pl.CostEstimate(flops=flops // 1000, bytes_accessed=moved // 1000, transcendentals=0)


def spread(value):
    high = value.astype(bfloat).astype(floating)
    middle = (value - high).astype(bfloat).astype(floating)
    low = value - high - middle
    top = jnp.concatenate([high, middle], axis=1)
    bottom = jnp.concatenate([low, jnp.zeros_like(low)], axis=1)
    return jnp.concatenate([top, bottom], axis=0).astype(bfloat)


def gathered_parts(block):
    block = block.astype(floating)
    width = block.shape[1] // 2
    return block[:8, :width] + block[:8, width:] + block[8:, :width]


def rms_scale(values):
    return lax.rsqrt(jnp.mean(values * values, axis=-1, keepdims=True) + EPSILON)


def lane_mask(length):
    return lax.broadcasted_iota(jnp.int32, (length, PAIR), 1) < HEAD_DIM


def stack_heads(block, first):
    zero = jnp.zeros_like(block)
    return jnp.concatenate([jnp.where(first, block, zero), jnp.where(first, zero, block)], axis=0)


def gelu_wave(gate):
    return jnp.tanh(GELU_A * (gate + GELU_B * gate * gate * gate))


def relative(blocks, index):
    low = (index & 1) == 1
    high = (index >> 1) == 1
    once = [jnp.where(low, blocks[place ^ 1], blocks[place]) for place in range(4)]
    return [jnp.where(high, once[place ^ 2], once[place]) for place in range(4)]


def attention(q_ref, k_ref, v_ref, seg_ref, att_ref, p_ref):
    length = seg_ref.shape[1]
    rows = q_ref.shape[0] // length
    pairs = q_ref.shape[1] // PAIR
    first = lane_mask(length)
    later = lax.broadcasted_iota(jnp.int32, (length, length), 0)
    earlier = lax.broadcasted_iota(jnp.int32, (length, length), 1)
    for row in range(rows):
        documents = jnp.broadcast_to(seg_ref[row : row + 1, :], (length, length)).astype(floating)
        allowed = (earlier <= later) & (documents == documents.T)
        allowed = jnp.concatenate([allowed, allowed], axis=0)
        span = slice(row * length, (row + 1) * length)
        for pair in range(pairs):
            heads = slice(pair * PAIR, (pair + 1) * PAIR)
            stacked = stack_heads(q_ref[span, heads], first)
            scores = jnp.where(allowed, dot_t(stacked, k_ref[span, heads]) * SCALE, MASKED)
            powers = jnp.exp(scores - jnp.max(scores, axis=-1, keepdims=True))
            probs = powers / jnp.sum(powers, axis=-1, keepdims=True)
            if p_ref is not None:
                p_ref[row * pairs + pair] = probs
            mixed = dot(probs.astype(bfloat), v_ref[span, heads])
            att_ref[span, heads] = jnp.where(first, mixed[:length], mixed[length:]).astype(bfloat)


def in_hbm(value):
    return pltpu.with_memory_space_constraint(value, pltpu.MemorySpace.HBM)


def forward_lite_kernel(x_any, seg_any, mix_any, cor_any, ga_any, gf_any, wq, wk, wv, wo, wg, wu, wd,
                        out_ref, wq_s, wk_s, wv_s, wo_s, wg_s, wu_s, wd_s,
                        x_in, seg_ref, mix_ref, cor_ref, ga_ref, gf_ref, q_ref, k_ref, v_ref, act_ref,
                        nrm_ref, att_ref, nf_ref, acc, sem, small_sem):
    tokens, width = act_ref.shape
    chunk = width
    pieces = wg.shape[2] // chunk
    small = [
        pltpu.make_async_copy(source, target, small_sem.at[place])
        for place, (source, target) in enumerate(
            ((x_any, x_in), (mix_any, mix_ref), (ga_any, ga_ref), (seg_any, seg_ref), (gf_any, gf_ref), (cor_any, cor_ref))
        )
    ]
    pairs = [(wq, wq_s), (wk, wk_s), (wv, wv_s), (wo, wo_s)]
    queue = [pltpu.make_async_copy(source, target, sem.at[place]) for place, (source, target) in enumerate(pairs)]

    def group(piece):
        span = pl.ds(pl.multiple_of(piece * chunk, chunk), chunk)
        places = ((wg, wg_s, (slice(None), slice(None), span)), (wu, wu_s, (slice(None), slice(None), span)),
                  (wd, wd_s, (slice(None), span, slice(None))))
        return [
            pltpu.make_async_copy(source.at[where], target.at[where], sem.at[4 + 3 * piece + place])
            for place, (source, target, where) in enumerate(places)
        ]

    def start_group(piece):
        for copy in group(piece):
            copy.start()

    for copy in small + queue:
        copy.start()
    for copy in small:
        copy.wait()
    section = lax.axis_index("section")
    mix = [[mix_ref[0, i, j] for j in range(2)] for i in range(2)]
    cor = [cor_ref[0, i] for i in range(2)]
    xa = x_in[:, :width].astype(floating)
    xb = x_in[:, width:].astype(floating)
    own_a = jnp.where(section == 0, mix[0][0], mix[1][0])
    own_b = jnp.where(section == 0, mix[0][1], mix[1][1])
    active = jnp.where(section == 0, xa, xb) + (own_a * xa + own_b * xb)
    act_ref[...] = active
    nrm_ref[...] = (active * rms_scale(active) * ga_ref[...]).astype(bfloat)
    for place, (copy, weight, target) in enumerate(zip(queue, (wq_s, wk_s, wv_s), (q_ref, k_ref, v_ref))):
        copy.wait()
        if place < 2:
            start_group(place)
        target[...] = dot(nrm_ref[...], weight[0]).astype(bfloat)
    attention(q_ref, k_ref, v_ref, seg_ref, att_ref, None)
    for piece in range(2, pieces):
        start_group(piece)
    queue[3].wait()
    middle = act_ref[...] + dot(att_ref[...], wo_s[0])
    acc[...] = middle - act_ref[...]
    nf_ref[...] = (middle * rms_scale(middle) * gf_ref[...]).astype(bfloat)

    def one_piece(piece, carry):
        span = pl.ds(pl.multiple_of(piece * chunk, chunk), chunk)
        waits = group(piece)
        waits[0].wait()
        gate = dot(nf_ref[...], wg_s[0, :, span])
        waits[1].wait()
        upward = dot(nf_ref[...], wu_s[0, :, span])
        hidden = (0.5 * gate * (1.0 + gelu_wave(gate)) * upward).astype(bfloat)
        waits[2].wait()
        acc[...] += dot(hidden, wd_s[0, span, :])
        return carry

    lax.fori_loop(0, pieces, one_piece, 0, unroll=2)
    xa = x_in[:, :width].astype(floating)
    xb = x_in[:, width:].astype(floating)
    out_ref[:, :width] = (xa + (mix[0][0] * xa + mix[0][1] * xb) + cor[0] * acc[...]).astype(bfloat)
    out_ref[:, width:] = (xb + (mix[1][0] * xa + mix[1][1] * xb) + cor[1] * acc[...]).astype(bfloat)


def forward_lite(x_in, segments, mixing, correction, gain_attn, gain_ffn, weights):
    tokens = x_in.shape[0]
    width = gain_attn.shape[1]
    size = sum(weight.size for weight in weights)
    narrow = pltpu.VMEM((tokens, width), bfloat)
    wide = pltpu.VMEM((tokens, width), floating)
    args = (x_in, segments, mixing, correction, gain_attn, gain_ffn) + weights
    scratch = [
        pltpu.VMEM(x_in.shape, bfloat), pltpu.VMEM(segments.shape, jnp.int32), pltpu.SMEM(mixing.shape, floating),
        pltpu.SMEM(correction.shape, floating), pltpu.VMEM(gain_attn.shape, floating), pltpu.VMEM(gain_ffn.shape, floating),
        narrow, narrow, narrow, wide, narrow, narrow, narrow, wide,
    ]
    scratch += [pltpu.SemaphoreType.DMA((4 + 3 * (weights[4].shape[2] // width),)), pltpu.SemaphoreType.DMA((6,))]
    return pl.pallas_call(
        forward_lite_kernel,
        out_shape=[jax.ShapeDtypeStruct((tokens, 2 * width), bfloat)]
        + [jax.ShapeDtypeStruct(weight.shape, bfloat) for weight in weights],
        in_specs=[ANY] * len(args),
        out_specs=[VMEM] * 8,
        scratch_shapes=scratch,
        compiler_params=params(SCOPED),
        cost_estimate=cost(2 * tokens * size, 2 * size),
        name="forward_lite",
    )(*[in_hbm(one) for one in args])


def forward_kernel(fast, x_in, message, seg_ref, mix_ref, cor_ref, ga_ref, gf_ref, wq, wk, wv, wo, wg, wu, wd,
                   x_ref, out_ref, q_ref, k_ref, v_ref, p_ref, act_ref, mid_ref, one_ref, two_ref, chg_ref, *refs):
    kept = refs[:4]
    nf_ref = refs[-4]
    nrm_ref, att_ref, acc = refs[-3:]
    tokens, width = act_ref.shape
    chunk = width
    pieces = wg.shape[2] // chunk
    section = lax.axis_index("section")
    quarter = lax.axis_index("dp") & 3
    mix = [[mix_ref[0, i, j] for j in range(2)] for i in range(2)]
    cor = [cor_ref[0, i] for i in range(2)]
    x_ref[...] = jnp.where(section == 0, x_in[...], message[...])
    xa = x_ref[:, :width].astype(floating)
    xb = x_ref[:, width:].astype(floating)
    own_a = jnp.where(section == 0, mix[0][0], mix[1][0])
    own_b = jnp.where(section == 0, mix[0][1], mix[1][1])
    active = jnp.where(section == 0, xa, xb) + (own_a * xa + own_b * xb)
    act_ref[...] = active
    nrm_ref[...] = (active * rms_scale(active) * ga_ref[...]).astype(bfloat)
    for weight, target in zip((wq, wk, wv), (q_ref, k_ref, v_ref)):
        target[...] = dot(nrm_ref[...], weight[0]).astype(bfloat)

    def keep_quarters(values, base):
        share = width // 16
        for far in range(4):
            blocks = [values[:, (4 * far + near) * share : (4 * far + near + 1) * share] for near in range(4)]
            for slot, block in enumerate(relative(blocks, quarter)):
                target, start = (kept[slot], width + base) if slot < 3 else (refs[4], base)
                target[:, start + far * share : start + (far + 1) * share] = block

    attention(q_ref, k_ref, v_ref, seg_ref, att_ref, p_ref)
    middle = act_ref[...] + dot(att_ref[...], wo[0])
    mid_ref[...] = middle
    nf_ref[...] = (middle * rms_scale(middle) * gf_ref[...]).astype(bfloat)
    if fast:
        keep_quarters(att_ref[...], 0)
        keep_quarters(nrm_ref[...], width // 4)
        for slot in (1, 2):
            kept[slot][:, width + width // 2 :] = nf_ref[...]
    else:
        kept[1][...] = nrm_ref[...]
        kept[2][...] = att_ref[...]
    for piece in range(pieces):
        span = slice(piece * chunk, (piece + 1) * chunk)
        gate = dot(nf_ref[...], wg[0, :, span])
        upward = dot(nf_ref[...], wu[0, :, span])
        wave = gelu_wave(gate)
        half = 0.5 * (1.0 + wave)
        value = gate * half
        hidden = (value * upward).astype(bfloat)
        slope = half + 0.5 * gate * (1.0 - wave * wave) * (GELU_A * (1.0 + 3.0 * GELU_B * gate * gate))
        one_ref[piece] = upward * slope
        two_ref[piece] = value
        if fast:
            share = chunk // 4
            blocks = [hidden[:, near * share : (near + 1) * share] for near in range(4)]
            for slot, block in enumerate(relative(blocks, quarter)):
                kept[slot][:, piece * share : (piece + 1) * share] = block
        else:
            kept[0][:, span] = hidden
        down = dot(hidden, wd[0, span, :])
        if piece == 0:
            acc[...] = down
        else:
            acc[...] += down
    change = mid_ref[...] + acc[...] - act_ref[...]
    chg_ref[...] = change
    xa = x_ref[:, :width].astype(floating)
    xb = x_ref[:, width:].astype(floating)
    out_ref[0, :, :width] = (xa + (mix[0][0] * xa + mix[0][1] * xb) + cor[0] * change).astype(bfloat)
    out_ref[0, :, width:] = (xb + (mix[1][0] * xa + mix[1][1] * xb) + cor[1] * change).astype(bfloat)


def forward(fast, x_in, message, segments, mixing, correction, gain_attn, gain_ffn, weights):
    tokens = x_in.shape[0]
    length = segments.shape[1]
    width = gain_attn.shape[1]
    hidden_width = weights[4].shape[2]
    size = sum(weight.size for weight in weights)
    shape = jax.ShapeDtypeStruct
    narrow = ((tokens, width), bfloat)
    wide = ((tokens, width), floating)
    probs = ((tokens // length * (width // PAIR), 2 * length, length), floating)
    if fast:
        short, long = (((tokens, columns), bfloat) for columns in (width + width // 2, 2 * width + width // 2))
        kept = [short, long, long, narrow, ((tokens, width // 2), bfloat), narrow]
    else:
        kept = [((tokens, hidden_width), bfloat), narrow, narrow, narrow]
    ffn = ((hidden_width // width, tokens, width), floating)
    outs = [((tokens, 2 * width), bfloat), ((1, tokens, 2 * width), bfloat), narrow, narrow, narrow, probs, wide, wide,
            ffn, ffn, wide] + kept
    return pl.pallas_call(
        lambda *refs: forward_kernel(fast, *refs),
        out_shape=[shape(*one) for one in outs],
        in_specs=[VMEM, VMEM, VMEM, SMEM, SMEM, VMEM, VMEM] + [VMEM] * 7,
        out_specs=[VMEM] * len(outs),
        scratch_shapes=[pltpu.VMEM(*narrow)] * 2 + [pltpu.VMEM(*wide)],
        compiler_params=params(SCOPED),
        cost_estimate=cost(2 * tokens * size, 2 * size),
        name="forward_full",
    )(x_in, message, segments, mixing, correction, gain_attn, gain_ffn, *weights)


def start_rows(message, grad_ref, counts_ref, cor_ref, g_ref, low_ref):
    tokens, width = low_ref.shape
    rows = counts_ref.shape[0]
    length = tokens // rows
    section = lax.axis_index("section")
    place = lax.broadcasted_iota(jnp.int32, (tokens, width), 0)
    valid = place < counts_ref[0]
    for row in range(1, rows):
        valid = valid | ((place >= row * length) & (place < row * length + counts_ref[row]))
    own_a = jnp.where(valid, grad_ref[:, :width].astype(floating), 0.0)
    own_b = jnp.where(valid, grad_ref[:, width:].astype(floating), 0.0)
    if message is not None:
        own_a = jnp.where(section == 0, message[:, :width].astype(floating), own_a)
        own_b = jnp.where(section == 0, message[:, width:].astype(floating), own_b)
    g_ref[:, :width] = own_a.astype(bfloat)
    g_ref[:, width:] = own_b.astype(bfloat)
    low_ref[...] = (cor_ref[0, 0] * own_a + cor_ref[0, 1] * own_b).astype(bfloat)


def start(message, out_grad, counts, correction, before):
    tokens = out_grad.shape[0]
    width = message.shape[1] // 2
    shape = jax.ShapeDtypeStruct
    return pl.pallas_call(
        lambda *refs: start_rows(*refs[:4], *refs[-2:]),
        out_shape=[shape((tokens, 2 * width), bfloat), shape((tokens, width), bfloat)],
        in_specs=[VMEM, VMEM, SMEM, SMEM] + [ANY] * len(before),
        out_specs=[VMEM, VMEM],
        compiler_params=params(SCOPED),
        cost_estimate=cost(tokens * width * 20, tokens * width * 12),
        name="backward_start",
    )(message, out_grad, counts, correction, *before)


def norm_backward(values, gain, grad_normed, with_gain):
    inverse = rms_scale(values)
    grad_gain = jnp.sum(grad_normed * values * inverse, axis=0, keepdims=True) if with_gain else None
    weighted = grad_normed * gain
    grad_values = inverse * weighted - values * inverse**3 * jnp.mean(weighted * values, axis=-1, keepdims=True)
    return grad_gain, grad_values


def ffn_steps(low_ref, one, two, wg, wu, wd, acc, emit):
    width = wd.shape[2]
    quarter = lax.axis_index("dp") & 3
    for step in range(4):
        piece = (3 - step) ^ quarter
        span = pl.ds(pl.multiple_of(piece * width, width), width)
        grad_hidden = dot_t(low_ref[...], wd[0, span, :])
        dgate = (grad_hidden * one[piece]).astype(bfloat)
        dup = (grad_hidden * two[piece]).astype(bfloat)
        emit(3 - step, dgate, dup)
        total = dot_t(dgate, wg[0, :, span]) + dot_t(dup, wu[0, :, span])
        if step == 0:
            acc[...] = total
        else:
            acc[...] += total


def ffn_kernel(g_in, low_ref, cor_ref, gf_ref, mid_ref, one, two, wg, wu, wd, *refs):
    slots = refs[-12:-4]
    dmid_ref, datt_ref, gain_ref, acc = refs[-4:]
    width = gf_ref.shape[1]

    def emit(slot, dgate, dup):
        slots[slot][...] = dgate
        slots[4 + slot][...] = dup

    ffn_steps(low_ref, one, two, wg, wu, wd, acc, emit)
    grad_gain, grad_values = norm_backward(mid_ref[...], gf_ref[...], acc[...], True)
    block = cor_ref[0, 0] * g_in[:, :width].astype(floating) + cor_ref[0, 1] * g_in[:, width:].astype(floating)
    grad_middle = block + grad_values
    dmid_ref[...] = grad_middle
    datt_ref[...] = grad_middle.astype(bfloat)
    gain_ref[...] = grad_gain


def ffn_backward(g_in, low, correction, gain_ffn, middle, one, two, before, weights):
    tokens = g_in.shape[0]
    width = gain_ffn.shape[1]
    shape = jax.ShapeDtypeStruct
    return pl.pallas_call(
        ffn_kernel,
        out_shape=[shape((tokens, width), bfloat)] * 8
        + [shape((tokens, width), floating), shape((tokens, width), bfloat), shape((1, width), floating)],
        in_specs=[VMEM, VMEM, SMEM] + [VMEM] * 7 + [ANY] * len(before),
        out_specs=[VMEM] * 11,
        scratch_shapes=[pltpu.VMEM((tokens, width), floating)],
        compiler_params=params(SCOPED),
        cost_estimate=cost(2 * tokens * 3 * weights[4].size, 2 * 3 * weights[4].size),
        name="backward_ffn",
    )(g_in, low, correction, gain_ffn, middle, one, two, *weights[4:], *before)


def attn_steps(q_ref, k_ref, v_ref, p_ref, do_ref, parts):
    tokens, width = do_ref.shape
    length = p_ref.shape[2]
    rows = tokens // length
    pairs = width // PAIR
    first = lane_mask(length)
    for row in range(rows):
        span = slice(row * length, (row + 1) * length)
        for pair in range(pairs):
            heads = slice(pair * PAIR, (pair + 1) * PAIR)
            probs = p_ref[row * pairs + pair]
            grad_out = stack_heads(do_ref[span, heads], first)
            grad_value = t_dot(probs.astype(bfloat), grad_out)
            grad_probs = dot_t(grad_out, v_ref[span, heads])
            carried = jnp.sum(probs * grad_probs, axis=-1, keepdims=True)
            grad_scores = (probs * (grad_probs - carried)).astype(bfloat)
            grad_query = dot(grad_scores, k_ref[span, heads])
            grad_query = jnp.where(first, grad_query[:length], grad_query[length:])
            grad_key = t_dot(grad_scores, stack_heads(q_ref[span, heads], first))
            for (part, base), value in zip(parts, (grad_query * SCALE, grad_key * SCALE, grad_value)):
                part[span, base + pair * PAIR : base + (pair + 1) * PAIR] = value.astype(bfloat)


def normed_grad(parts, rows, width, wq, wk, wv):
    return sum(dot_t(part[:rows, base : base + width], weight[0]) for (part, base), weight in zip(parts, (wq, wk, wv)))


def attn_kernel(datt_ref, q_ref, k_ref, v_ref, p_ref, gfg_ref, ga_ref, x_ref, g_in, dmid_ref, act_ref, chg_ref, mix_ref, cor_ref,
                wq, wk, wv, wo, before,
                grad_ref, right_ref, small_ref, do_ref):
    tokens, width = datt_ref.shape
    right_ref[:tokens, :width] = datt_ref[...]
    do_ref[...] = dot_t(datt_ref[...], wo[0]).astype(bfloat)
    parts = (right_ref, width), (right_ref, 2 * width), (right_ref, 3 * width)
    attn_steps(q_ref, k_ref, v_ref, p_ref, do_ref, parts)
    grad_normed = normed_grad(parts, tokens, width, wq, wk, wv)
    grad_gain, grad_values = norm_backward(act_ref[...], ga_ref[...], grad_normed, True)
    section = lax.axis_index("section")
    mix = [[mix_ref[0, i, j] for j in range(2)] for i in range(2)]
    cor = [cor_ref[0, i] for i in range(2)]
    out_a = g_in[:, :width].astype(floating)
    out_b = g_in[:, width:].astype(floating)
    grad_active = dmid_ref[...] + grad_values - (cor[0] * out_a + cor[1] * out_b)
    pred_a = out_a + jnp.where(section == 0, grad_active, 0.0)
    pred_b = out_b + jnp.where(section == 0, 0.0, grad_active)
    grad_ref[0, :, :width] = (pred_a + (mix[0][0] * pred_a + mix[1][0] * pred_b)).astype(bfloat)
    grad_ref[0, :, width:] = (pred_b + (mix[0][1] * pred_a + mix[1][1] * pred_b)).astype(bfloat)
    xa = x_ref[:, :width].astype(floating)
    xb = x_ref[:, width:].astype(floating)
    small_ref[0:1, :] = grad_gain
    small_ref[1:2, :] = gfg_ref[...]
    place = 2
    for pred in (pred_a, pred_b):
        for state in (xa, xb):
            small_ref[place : place + 1, :] = jnp.sum(pred * state, axis=0, keepdims=True)
            place += 1
    for out in (out_a, out_b):
        small_ref[place : place + 1, :] = jnp.sum(out * chg_ref[...], axis=0, keepdims=True)
        place += 1
    right_ref[tokens:, : 2 * width] = spread(small_ref[...])
    right_ref[tokens:, 2 * width :] = jnp.zeros((right_ref.shape[0] - tokens, 2 * width), bfloat)


def attn_backward(x, g_in, grad_middle, grad_att, active, change, queries, key_rows, value_rows, probs, ffn_gain, gain_attn,
                  mixing, correction, before, weights):
    tokens, width = active.shape
    shape = jax.ShapeDtypeStruct
    return pl.pallas_call(
        attn_kernel,
        out_shape=[
            shape((1, tokens, 2 * width), bfloat), shape((tokens + EXTRA, 4 * width), bfloat), shape((8, width), floating),
        ],
        in_specs=[VMEM] * 12 + [SMEM] * 2 + [VMEM] * 4 + [ANY],
        out_specs=[VMEM] * 3,
        scratch_shapes=[pltpu.VMEM((tokens, width), bfloat)],
        compiler_params=params(SCOPED),
        cost_estimate=cost(2 * tokens * 5 * weights[0].size, 2 * 4 * weights[0].size),
        name="backward_attn",
    )(grad_att, queries, key_rows, value_rows, probs, ffn_gain, gain_attn, x, g_in, grad_middle, active, change,
      mixing, correction, *weights[:4], before)


def relay_kernel(grad_in, counts_ref, cor_ref, mix_ref, gf_ref, ga_ref, one, two, mid_ref, q_ref, k_ref, v_ref, p_ref, act_ref,
                 wq, wk, wv, wo, wg, wu, wd,
                 msg_ref,
                 acc, g_in, low_ref, do_ref, dqkv_ref):
    tokens, width = low_ref.shape
    start_rows(None, grad_in, counts_ref, cor_ref, g_in, low_ref)
    ffn_steps(low_ref, one, two, wg, wu, wd, acc, lambda *parts: None)
    grad_values = norm_backward(mid_ref[...], gf_ref[...], acc[...], False)[1]
    cor = [cor_ref[0, i] for i in range(2)]
    block = cor[0] * g_in[:, :width].astype(floating) + cor[1] * g_in[:, width:].astype(floating)
    acc[...] = block + grad_values
    do_ref[...] = dot_t(acc[...].astype(bfloat), wo[0]).astype(bfloat)
    parts = (dqkv_ref, 0), (dqkv_ref, width), (dqkv_ref, 2 * width)
    attn_steps(q_ref, k_ref, v_ref, p_ref, do_ref, parts)
    grad_normed = normed_grad(parts, tokens, width, wq, wk, wv)
    grad_values = norm_backward(act_ref[...], ga_ref[...], grad_normed, False)[1]
    out_a = g_in[:, :width].astype(floating)
    out_b = g_in[:, width:].astype(floating)
    pred_b = out_b + (acc[...] + grad_values - (cor[0] * out_a + cor[1] * out_b))
    mix = [[mix_ref[0, i, j] for j in range(2)] for i in range(2)]
    msg_ref[:, :width] = (out_a + (mix[0][0] * out_a + mix[1][0] * pred_b)).astype(bfloat)
    msg_ref[:, width:] = (pred_b + (mix[0][1] * out_a + mix[1][1] * pred_b)).astype(bfloat)


def relay_backward(out_grad, counts, correction, mixing, gain_ffn, gain_attn, one, two, middle, queries, key_rows, value_rows,
                   probs, active, weights):
    tokens, width = active.shape
    shape = jax.ShapeDtypeStruct
    narrow = pltpu.VMEM((tokens, width), bfloat)
    wide = pltpu.VMEM((tokens, width), floating)
    size = sum(weight.size for weight in weights)
    return pl.pallas_call(
        relay_kernel,
        out_shape=shape((tokens, 2 * width), bfloat),
        in_specs=[VMEM, SMEM, SMEM, SMEM] + [VMEM] * 17,
        out_specs=VMEM,
        scratch_shapes=[wide, pltpu.VMEM((tokens, 2 * width), bfloat), narrow, narrow, pltpu.VMEM((tokens, 3 * width), bfloat)],
        compiler_params=params(SCOPED),
        cost_estimate=cost(2 * tokens * size, 2 * size),
        name="backward_relay",
    )(out_grad, counts, correction, mixing, gain_ffn, gain_attn, one, two, middle, queries, key_rows, value_rows, probs, active,
      *weights)


def quarter_parts(base, products, block, lefts, rights, own_ref, far_ref, all_ref, left_s, right_s):
    tokens = lefts[0].shape[0]
    tail = lefts[0].shape[1] - lefts[-1].shape[1]
    mine = (lax.axis_index("dp") >> 2) & 3
    for left_at, left_wide, right_at, right_wide in products:
        columns = slice(right_at, right_at + right_wide)
        span = slice(right_at - base, right_at - base + right_wide)
        for row, (left, right) in enumerate(zip(lefts, rights)):
            at = left_at if left.shape[1] > left_at else left_at - tail
            rows = slice(row * tokens, (row + 1) * tokens)
            left_s[rows, :left_wide] = left[:, at : at + left_wide]
            right_s[rows, :right_wide] = right[:tokens, columns]
        total = t_dot(left_s[:, :left_wide], right_s[:, :right_wide])
        for place in range(4):
            all_ref[place ^ mine, :, span] = total[place * block : (place + 1) * block, :]
    own_ref[:block, :] = all_ref[1].astype(bfloat)
    far_ref[:block, :] = all_ref[3].astype(bfloat)


def quarter_product(lefts, rights, block, before, name, parted):
    rows, wide = lefts[0].shape[0], rights[0].shape[1]
    shape = jax.ShapeDtypeStruct
    products = [(0, 4 * block, 0, wide)]
    sends = [shape((block, wide), bfloat)] * 2 if parted else [shape((2, block, wide), bfloat)]

    def kernel(*refs):
        *outs, all_ref, left_s, right_s = refs[-5:] if parted else refs[-4:]
        own_ref, far_ref = outs if parted else (outs[0].at[0], outs[0].at[1])
        quarter_parts(0, products, block, refs[:4], refs[4:8], own_ref, far_ref, all_ref, left_s, right_s)

    return pl.pallas_call(
        kernel,
        out_shape=sends + [shape((4, block, wide), floating)],
        in_specs=[VMEM] * 8 + [ANY] * len(before),
        out_specs=[VMEM] * (len(sends) + 1),
        scratch_shapes=[pltpu.VMEM((4 * rows, 4 * block), bfloat), pltpu.VMEM((4 * rows, wide), bfloat)],
        compiler_params=params(SCOPED),
        cost_estimate=cost(32 * rows * block * wide, 16 * block * wide),
        name=name,
    )(*lefts, *rights, *before)


def attn_product_kernel(halves, block, refs):
    lefts, rights = refs[:4], refs[4:8]
    first_send, first_keep, small_ref, second_send, second_keep, stage, left_s, right_s = refs[-8:]
    tokens = lefts[0].shape[0]
    wide = first_keep.shape[2]
    quarter_parts(0, halves[0], block, lefts, rights, first_send, stage, first_keep, left_s, right_s)
    first_send[block : 2 * block, :] = stage[...]
    small = sum(gathered_parts(right[tokens:, :wide]) for right in rights)
    small_ref[...] = small
    first_send[2 * block :, :] = spread(small)
    quarter_parts(wide, halves[1], block, lefts, rights, second_send.at[0], second_send.at[1], second_keep, left_s, right_s)


def attn_product(lefts, rights, halves, block, before):
    wide = rights[0].shape[1] // 2
    shape = jax.ShapeDtypeStruct
    send, keep = shape((2, block, wide), bfloat), shape((4, block, wide), floating)
    return pl.pallas_call(
        lambda *refs: attn_product_kernel(halves, block, refs),
        out_shape=[shape((2 * block + EXTRA, wide), bfloat), keep, shape((8, wide // 2), floating), send, keep],
        in_specs=[VMEM] * 8 + [ANY] * len(before),
        out_specs=[VMEM] * 5,
        scratch_shapes=[
            pltpu.VMEM(send.shape[1:], bfloat), pltpu.VMEM((4 * lefts[0].shape[0], 4 * block), bfloat),
            pltpu.VMEM((4 * lefts[0].shape[0], wide), bfloat),
        ],
        compiler_params=params(SCOPED),
        cost_estimate=cost(wide, wide),
        name="product_attn",
    )(*lefts, *rights, *before)


def first_sum_kernel(keep_ref, came_ref, small_ref, held_ref, passed_ref, sums_ref):
    block = held_ref.shape[0]
    held_ref[...] = keep_ref[0] + came_ref[:block, :].astype(floating)
    passed_ref[:block, :] = (keep_ref[2] + came_ref[block : 2 * block, :].astype(floating)).astype(bfloat)
    small = small_ref[...] + gathered_parts(came_ref[2 * block :, :])
    sums_ref[...] = small
    passed_ref[block:, :] = spread(small)


def first_sum(keep, came, small):
    _, block, wide = keep.shape
    shape = jax.ShapeDtypeStruct
    return pl.pallas_call(
        first_sum_kernel,
        out_shape=[shape((block, wide), floating), shape((block + EXTRA, wide), bfloat), shape(small.shape, floating)],
        in_specs=[VMEM] * 3,
        out_specs=[VMEM] * 3,
        compiler_params=params(SCOPED),
        cost_estimate=cost(wide, wide),
        name="first_sum",
    )(keep, came, small)


def first_end_kernel(held_ref, came_ref, small_ref, left_ref, right_ref, sums_ref):
    block, wide = held_ref.shape
    left_ref[0] = held_ref[:, : wide // 2] + came_ref[:block, : wide // 2].astype(floating)
    right_ref[0] = held_ref[:, wide // 2 :] + came_ref[:block, wide // 2 :].astype(floating)
    sums_ref[...] = small_ref[...] + gathered_parts(came_ref[block:, :])


def first_end(held, came, small):
    block, wide = held.shape
    shape = jax.ShapeDtypeStruct
    return pl.pallas_call(
        first_end_kernel,
        out_shape=[shape((1, block, wide // 2), floating)] * 2 + [shape(small.shape, floating)],
        in_specs=[VMEM] * 3,
        out_specs=[VMEM] * 3,
        compiler_params=params(SCOPED),
        cost_estimate=cost(wide, wide),
        name="first_end",
    )(held, came, small)


def assemble_kernel(own, one, two, three, gate_ref, up_ref):
    quarter = lax.axis_index("dp") & 3
    width = own.shape[1] // 2
    for slot, piece in enumerate((own, one, two, three)):
        span = pl.ds(pl.multiple_of((slot ^ quarter) * width, width), width)
        gate_ref[0, :, span] = piece[:, :width].astype(floating)
        up_ref[0, :, span] = piece[:, width:].astype(floating)


def assemble(pieces):
    share, double = pieces[0].shape
    shape = jax.ShapeDtypeStruct((1, share, 2 * double), floating)
    return pl.pallas_call(
        assemble_kernel,
        out_shape=[shape, shape],
        in_specs=[VMEM] * 4,
        out_specs=[VMEM] * 2,
        compiler_params=params(SCOPED),
        cost_estimate=cost(share * double * 4, share * double * 24),
        name="assemble",
    )(*pieces)


def exchange(value, flips):
    count = lax.axis_size("dp")
    return lax.ppermute(value, "dp", [(source, source ^ flips) for source in range(count)])


def relative_rows(matrix, order, index):
    bits = len(order)
    block = matrix.shape[0] >> bits
    split = matrix.reshape((2,) * bits + (block, matrix.shape[1]))
    axes = [bits - 1 - bit for bit in order]
    split = jnp.transpose(split, axes + [bits, bits + 1])
    for axis, bit in enumerate(order):
        split = jnp.where((index >> bit) & 1 == 1, jnp.flip(split, axis), split)
    return split.reshape(matrix.shape)


def scatter_sum(left, right, order):
    total = left.shape[0]
    arrived = []
    for step in range(len(order) + 1):
        low = total >> (step + 1) if step < len(order) else 0
        high = total >> step
        part = dot(left[low:high], right)
        for other in arrived:
            part = part + other[low:high].astype(floating)
        if step == len(order):
            return part
        arrived.append(exchange(part.astype(bfloat), 1 << order[step]))


def halving_grads(kept, low, slots, right, index, count):
    width = low.shape[1]
    order = list(range(count.bit_length() - 1))
    hidden, normed, attended, normed_ffn = (relative_rows(one.T, order, index) for one in kept)
    quarter = index & 3
    places = jnp.arange(4) ^ quarter
    dgate = jnp.concatenate(list(jnp.stack(slots[:4])[places]), axis=1)
    dup = jnp.concatenate(list(jnp.stack(slots[4:])[places]), axis=1)
    grad_down = scatter_sum(hidden, low, order)
    grad_gate = scatter_sum(normed_ffn, dgate, order)
    grad_up = scatter_sum(normed_ffn, dup, order)
    grad_out = scatter_sum(attended, right[:, :width], order)
    grad_qkv = scatter_sum(normed, right[:, width:], order)
    grads = [grad_down, grad_gate, grad_up, grad_out] + [grad_qkv[:, place * width : (place + 1) * width] for place in range(3)]
    return [one[None] for one in grads]


def after(values, *earlier):
    return lax.optimization_barrier((values, earlier))[0]


def gather_start(value):
    return [value, exchange(value, 1), exchange(value, 2)]


def gather_end(pieces, *earlier):
    return pieces + [exchange(after(pieces[2], *earlier), 1)]


def swapped(pieces):
    return [pieces[0]] + [exchange(pieces[flips], flips) for flips in (1, 2, 3)]


def parts_once(product, *earlier):
    own, far, keep = product
    own, far = after((exchange(own, 4), exchange(far, 4)), *earlier)
    return keep[0] + own.astype(floating), (keep[2] + far.astype(floating)).astype(bfloat)


def sum_once(pair, *earlier):
    send, keep = pair
    arrived = after(exchange(send, 4), *earlier)
    return keep[0] + arrived[0].astype(floating), (keep[2] + arrived[1].astype(floating)).astype(bfloat)


def sum_twice(held, passed, *earlier):
    return held + after(exchange(passed, 8), *earlier).astype(floating)


def sum_over(value, bits):
    for bit in range(bits):
        value = value + exchange(value, 1 << bit)
    return value


def quarter_grads(normed_ffn, kept, nearby, slots, right, down_pair, index):
    width = normed_ffn[0].shape[1]
    share = width // 16
    block = 4 * share
    gates = swapped(slots[:4])
    ups, nearby = after((slots[4:], nearby), right)
    ups, nearby = swapped(list(ups)), exchange(nearby, 3)
    down_sums = sum_once(down_pair, right)
    gate_pair = quarter_product(normed_ffn, gates, block, [right, down_sums[1]], "product_gate", True)
    grad_down = sum_twice(*down_sums)
    rights = gather_start(after(right, gate_pair[0], ups[1:]))
    gate_sums = parts_once(gate_pair, grad_down)
    up_pair = quarter_product(normed_ffn, ups, block, [gate_sums[1], grad_down, nearby], "product_up", False)
    up_sums = sum_once(up_pair)
    part = block * 3 // 4
    gate_came = exchange(gate_sums[1][:part], 8)
    rights = gather_end(rights, up_sums[1], gate_came)
    up_came = exchange(jnp.concatenate([up_sums[1], gate_sums[1][part:]], axis=0), 8)
    halves = (
        [(width, block, 0, width), (width + block, block, width, width)], [(width + block, block, 2 * width, 2 * width)])
    before = [up_sums[1], gate_came]
    first_send, first_keep, small, *second_pair = attn_product(kept[:3] + [nearby], rights, halves, share, before)
    held, first_passed, small = first_sum(first_keep, after(exchange(first_send, 4), up_came), small)
    gate_came, up_came = after((gate_came, up_came), first_passed)
    gate_tile = (gate_sums[0] + jnp.concatenate([gate_came, up_came[block:]], axis=0).astype(floating)).astype(bfloat)
    up_tile = (up_sums[0] + up_came[:block].astype(floating)).astype(bfloat)
    quarter = index & 3
    pieces = [
        jnp.concatenate(
            [lax.dynamic_slice_in_dim(tile, (slot ^ quarter) * share, share, axis=0) for tile in (gate_tile, up_tile)], axis=1)
        for slot in range(4)
    ]
    pieces = swapped(pieces)
    grad_out, grad_query, small = first_end(held, exchange(first_passed, 8), small)
    second_sums = sum_once(second_pair, first_passed)
    grad_gate, grad_up = assemble(list(after(pieces, second_sums[1], small)))
    return [grad_down[None], grad_gate, grad_up, grad_out, grad_query], (second_sums[0], exchange(second_sums[1], 8)), small


def local(states_in, out_grad, counts, segments, mixing, correction, gain_attn, w_query, w_key, w_value, w_attn_out, gain_ffn,
          w_gate, w_up, w_down):
    weights = (w_query, w_key, w_value, w_attn_out, w_gate, w_up, w_down)
    width = gain_attn.shape[1]
    index = lax.axis_index("dp")
    count = lax.axis_size("dp")
    fast = count == 16
    message, *weights = forward_lite(states_in, segments, mixing, correction, gain_attn, gain_ffn, weights)
    message = lax.ppermute(message, "section", [(0, 1), (1, 0)])
    (x, states, queries, key_rows, value_rows, probs, active, middle, one, two, change, *kept) = forward(
        fast, states_in, message, segments, mixing, correction, gain_attn, gain_ffn, weights)
    before = []
    if fast:
        kept, nearby, normed_ffn = swapped(kept[:4]), kept[4], kept[5]
        before = kept[1:]
    message = relay_backward(out_grad, counts, correction, mixing, gain_ffn, gain_attn, one, two, middle, queries, key_rows,
                             value_rows, probs, active, weights)
    message = lax.ppermute(message, "section", [(0, 1), (1, 0)])
    g_in, low = start(message, out_grad, counts, correction, before)
    *slots, grad_middle, grad_att, ffn_gain = ffn_backward(g_in, low, correction, gain_ffn, middle, one, two, [], weights)
    before = slots[0]
    if fast:
        lows = gather_end(gather_start(low), before)
        beside, across = (one[:, width + width // 2 :] for one in kept[1:3])
        normed_ffn = gather_end([normed_ffn, beside, across], before)
        down_pair = quarter_product(kept, lows, width // 4, [before], "product_down", False)
        before = down_pair[0]
    state_grads, right, small = attn_backward(x, g_in, grad_middle, grad_att, active, change, queries, key_rows, value_rows, probs,
                                              ffn_gain, gain_attn, mixing, correction, before, weights)
    if fast:
        grads, last, small = quarter_grads(normed_ffn, kept, nearby, slots, right, down_pair, index)
    else:
        grads = halving_grads(kept, low, slots, right[: low.shape[0]], index, count)
        small = sum_over(small, count.bit_length() - 1)
    share = width // count
    gains = lax.dynamic_slice(small, (0, index * share), (2, share))
    gains = gains[0:1], gains[1:2]
    sums = jnp.sum(small[2:], axis=1)
    sums = sums[:4].reshape(1, 2, 2), sums[4:].reshape(1, 2)
    if fast:
        came = after(last[1], gains, sums, grads)
        for span in (slice(0, width), slice(width, 2 * width)):
            grads.append((last[0][:, span] + came[:, span].astype(floating))[None])
    grad_down, grad_gate, grad_up, grad_out, grad_query, grad_key, grad_value = grads
    return (
        states,
        state_grads,
        sums[0],
        sums[1],
        gains[0],
        grad_query,
        grad_key,
        grad_value,
        grad_out,
        gains[1],
        grad_gate,
        grad_up,
        grad_down,
    )


def solution(mesh):
    rows = P("dp", None)
    matrix = P("section", None, None)
    vector = P("section", None)
    share = P("section", "dp", None)
    gain_share = P("section", "dp")
    in_specs = (rows, rows, P("dp"), rows, matrix, vector, vector, matrix, matrix, matrix, matrix, vector, matrix, matrix, matrix)
    out_specs = (share, share, matrix, vector, gain_share, share, share, share, share, gain_share, share, share, share)
    return jax.shard_map(local, mesh=mesh, in_specs=in_specs, out_specs=out_specs, check_vma=False)
```
